32 devices in a mesh: dp: 4 (over y, x), tensor: 8 (over z, core).
Axes of the slice: x: 2, y: 2, z: 4, core: 2. Of those that a mesh axis runs over, the one named last changes fastest.
Arguments:
- tokens: bfloat16 [8192, 2048], P(('dp', 'tensor')), may hold values from -6 to 6
- cotangent: bfloat16 [8192, 2048], P(('dp', 'tensor')), may hold values from -6 to 6
- first_norm_gain: float32 [2048], replicated, may hold values from 0.5 to 1.5
- w_qkv: bfloat16 [2048, 3, 2048], P(None, None, 'tensor'), may hold values from -0.125 to 0.125
- w_out: bfloat16 [2048, 2048], P('tensor'), may hold values from -0.75 to 0.75
- g_ln: float32 [2048], replicated, may hold values from 0.5 to 1.5
- b_ln: float32 [2048], replicated, may hold values from -3 to 3
- w_up: bfloat16 [2048, 8192], P(None, 'tensor'), may hold values from -0.125 to 0.125
- w_down: bfloat16 [8192, 2048], P('tensor'), may hold values from -0.0625 to 0.0625
- probs: float32 [8192], P(('dp', 'tensor')), may hold values from 0.2 to 1
- lengths: int32 [4, 8], P('dp'), may hold values from 1 to 1024, 2048 in all within a row
- head_count: int32 [4], P('dp'), may hold values from 4 to 16, as said below
- widths: int32 [8192], P('dp'), may hold values from 0 to 3, as said below
Outputs:
- out: bfloat16 [8192, 2048], P(('dp', 'tensor'))
- tokens_grad: float32 [8192, 2048], P(('dp', 'tensor'))
- probs_grad: float32 [8192], P(('dp', 'tensor'))
- g_rms_grad: float32 [2048], replicated
- w_qkv_grad: float32 [2048, 3, 2048], P('dp', None, 'tensor')
- w_out_grad: float32 [2048, 2048], P('tensor', 'dp')
- g_ln_grad: float32 [2048], replicated
- b_ln_grad: float32 [2048], replicated
- w_up_grad: float32 [2048, 8192], P('dp', 'tensor')
- w_down_grad: float32 [8192, 2048], P('tensor', 'dp')
The draws below stay inside these ranges and needn't reach their ends.
Inputs may be any that keep to these rules, and one draw needn't show every extreme that they name: `head_count`: each packed sequence's number of active heads is a multiple of 4. `widths`: in every packed sequence each width index is held by exactly 512 tokens.
All inputs are finite; a program needn't handle non-finite values.
Results may differ from the reference program's by a relative error of at most 0.025.
Values may be sent and summed in bfloat16 or wider, within the bound.
A program may use at most 192 MiB of HBM per device.

```python
import math
import jax
import jax.numpy as jnp
import numpy as np
from jax import lax

D = 2048
HEADS = 16
HDIM = 128
FF = 8192
SEQ_LEN = 2048
DOCS = 8
QBLOCK = 512
HD = 2048
MAXDOC = 1024
SEQS = 4
TOKENS = 8192
N_TENSOR = 8


def draw_head_count(key, part):
    levels = jax.random.randint(key, (SEQS,), 0, 4)
    levels = levels.at[0].set(3).at[SEQS - 1].set(0)
    return ((levels + 1) * (HEADS // 4)).astype(jnp.int32)


def draw_widths(key, part):
    pattern = jnp.arange(SEQ_LEN, dtype=jnp.int32) % 4
    keys = jax.random.split(jax.random.fold_in(key, 7), SEQS)
    rows = jax.vmap(lambda one: jax.random.permutation(one, pattern))(keys)
    return rows.reshape(TOKENS).astype(jnp.int32)


def block_scale(rng, extent, cuts, low, top_value):
    def one(axis_at, shards_of):
        heights = jax.random.uniform(jax.random.fold_in(jax.random.fold_in(rng, 6), axis_at), (shards_of,), jnp.float32, low / len(cuts), top_value / len(cuts))
        return jnp.repeat(jnp.exp(heights), extent[axis_at] // shards_of).reshape((-1,) + (1,) * (len(extent) - axis_at - 1))

    factor_of = one(*cuts[0])
    for cut in cuts[1:]:
        factor_of = factor_of * one(*cut)
    return factor_of


def profile(count, total, most, lean):
    weights = [(1 << 20) // math.isqrt(rank ** lean) + 1 for rank in range(2, count + 1)]
    rest, counts = total - most - (count - 1), [1] * (count - 1)
    while rest > 0:
        free = [i for i in range(count - 1) if counts[i] < most]
        mass, remaining = sum([weights[i] for i in free]), rest
        for i in free:
            addition = min(most - counts[i], max(1, remaining * weights[i] // mass), rest)
            counts[i] = counts[i] + addition
            rest = rest - addition
    return np.array([most] + counts)


def ragged(own_key, amount, total, most, skew):
    if amount == 2:
        one = jax.random.randint(own_key, (), max(1, total - most), min(most, total - 1) + 1)
        return jnp.stack([one, total - one])
    sizes = jnp.asarray(profile(amount, total, most, skew), jnp.int32)
    couples = (amount - 1) // 2
    giver, sink = sizes[1:1 + 2 * couples:2], sizes[2:2 + 2 * couples:2]
    slack = jnp.minimum(giver - 1, most - sink)
    shifted = jax.random.randint(jax.random.fold_in(own_key, 1), (couples,), 0, 1 << 20) % (slack + 1)
    sizes = sizes.at[1:1 + 2 * couples:2].set(giver - shifted).at[2:2 + 2 * couples:2].set(sink + shifted)
    return sizes[jax.random.permutation(jax.random.fold_in(own_key, 2), amount)]


def gaussian(own_key, shape, spread, reach, cuts=(), held_as=jnp.bfloat16):
    entries = spread * jax.random.normal(own_key, shape, jnp.float32)
    if cuts:
        entries = entries * block_scale(own_key, shape, cuts, -0.22, 0.18)
    return jnp.clip(entries, -reach, reach).astype(held_as)


def setup_inputs(seed: int = 0) -> dict:
    splits = jax.random.split(jax.random.key(seed), 14)
    return {
        "tokens": gaussian(splits[0], (TOKENS, D), 1.0, 6.0, ((0, 32),)),
        "cotangent": gaussian(splits[1], (TOKENS, D), 1.0, 6.0, ((0, 32),)),
        "first_norm_gain": jnp.clip(1.0 + 0.1 * jax.random.normal(splits[2], (D,), jnp.float32), 0.5, 1.5),
        "w_qkv": gaussian(splits[3], (D, 3, HD), D ** -0.5, 0.125, ((2, 8),)),
        "w_out": gaussian(splits[4], (HD, D), (HD // 32) ** -0.5, 0.75, ((0, 8),)),
        "g_ln": jnp.clip(1.0 + 0.1 * jax.random.normal(splits[5], (D,), jnp.float32), 0.5, 1.5),
        "b_ln": gaussian(splits[6], (D,), 0.5, 3.0, (), jnp.float32),
        "w_up": gaussian(splits[7], (D, FF), D ** -0.5, 0.125, ((1, 8),)),
        "w_down": gaussian(splits[8], (FF, D), FF ** -0.5, 0.0625, ((0, 8),)),
        "probs": jnp.clip(0.2 + 0.8 * jax.random.uniform(splits[9], (TOKENS,), jnp.float32) ** block_scale(splits[9], (TOKENS,), ((0, 32),), -0.2, 0.2), 0.2, 1.0),
        "lengths": jax.vmap(lambda own: ragged(own, DOCS, SEQ_LEN, MAXDOC, 2))(jax.random.split(splits[10], SEQS)).reshape((SEQS, DOCS)).astype(jnp.int32),
        "head_count": draw_head_count(jax.random.fold_in(splits[13], 71), 0),
        "widths": draw_widths(jax.random.fold_in(splits[13], 71), 0),
    }


@jax.custom_vjp
def low(v):
    return lax.optimization_barrier(v.astype(jnp.bfloat16)).astype(jnp.float32)

@jax.custom_vjp
def low_back(v):
    return v

def low_keep(v):
    return (low(v), None)

def low_pass(kept, grad):
    return (grad,)

def back_keep(v):
    return (v, None)

def back_low(kept, grad):
    return (low(grad),)
low.defvjp(low_keep, low_pass)
low_back.defvjp(back_keep, back_low)
EPSILON = 1e-05
NEGATIVE = -1e+30
PRECISE = lax.Precision.HIGHEST

def swap_halves(field):
    middle = field.shape[-1] // 2
    return jnp.concatenate([field[..., middle:], field[..., :middle]], axis=-1)

def rotate(field, cosines, sines):
    return field * cosines + swap_halves(field) * sines

def position_tables(doc_lengths, length_all):
    places = jnp.arange(length_all, dtype=jnp.int32)
    doc_ends = jnp.cumsum(doc_lengths).astype(jnp.int32)
    passed = (places[:, None] >= doc_ends[None, :]).astype(jnp.int32)
    starts = lax.optimization_barrier(jnp.sum(passed * doc_lengths[None, :], axis=1)).astype(jnp.int32)
    offsets = (places - starts).astype(jnp.float32)
    half_dim = HDIM // 2
    frequency = 10000.0 ** (-jnp.arange(half_dim, dtype=jnp.float32) / half_dim)
    angles = offsets[:, None] * frequency[None, :]
    cosines = jnp.concatenate([jnp.cos(angles), jnp.cos(angles)], axis=1)
    sines = jnp.concatenate([-jnp.sin(angles), jnp.sin(angles)], axis=1)
    return (places, starts, cosines, sines)

def one_sequence(layer_input, seq_widths, seq_probs, doc_lengths, count, weights):
    w_qkv, w_out, w_up, w_down, first_norm_gain, g_ln, b_ln = weights
    places, starts, cosines, sines = position_tables(doc_lengths, SEQ_LEN)
    cos_heads = cosines[:, None, :]
    sin_heads = sines[:, None, :]
    scaling = HDIM ** (-0.5)
    heads_here = HEADS // N_TENSOR
    columns = FF // N_TENSOR
    block_count = SEQ_LEN // QBLOCK
    normalized_rows = low(layer_input * lax.rsqrt(lax.optimization_barrier(jnp.mean(layer_input * layer_input, axis=1, keepdims=True)) + EPSILON) * first_norm_gain)
    qkv_groups = w_qkv.reshape(D, 3, N_TENSOR, heads_here * HDIM).transpose(2, 0, 1, 3)
    out_groups = w_out.reshape(N_TENSOR, heads_here * HDIM, D)

    def attend(running, members):
        group_id, w_in, w_mix = members
        source = low_back(normalized_rows)
        projected = low_back(jnp.einsum('td,dcf->tcf', source, w_in, precision=PRECISE))
        queries = low(rotate(projected[:, 0].reshape(SEQ_LEN, heads_here, HDIM), cos_heads, sin_heads))
        keys_rot = low(rotate(projected[:, 1].reshape(SEQ_LEN, heads_here, HDIM), cos_heads, sin_heads))
        values = low(projected[:, 2].reshape(SEQ_LEN, heads_here, HDIM))
        head_ids = group_id * heads_here + jnp.arange(heads_here, dtype=jnp.int32)
        active = (head_ids < count).astype(jnp.float32)

        def block(block_index):
            first_row = block_index * QBLOCK
            rows_q = lax.dynamic_slice_in_dim(queries, first_row, QBLOCK, 0)
            row_ids = lax.dynamic_slice_in_dim(places, first_row, QBLOCK, 0)
            row_starts = lax.dynamic_slice_in_dim(starts, first_row, QBLOCK, 0)
            allowed = (places[None, :] <= row_ids[:, None]) & (places[None, :] >= row_starts[:, None])
            raw_scores = jnp.einsum('qhe,khe->hqk', rows_q, keys_rot, precision=PRECISE) * scaling
            scores = low_back(jnp.where(allowed[None], raw_scores, NEGATIVE))
            highest = lax.optimization_barrier(jnp.max(scores, axis=-1, keepdims=True))
            exponent = jnp.exp(scores - highest)
            weights_b = low(exponent / lax.optimization_barrier(jnp.sum(exponent, axis=-1, keepdims=True)))
            return jnp.einsum('hqk,khe->qhe', weights_b, values, precision=PRECISE)
        attended = lax.map(jax.checkpoint(block), jnp.arange(block_count, dtype=jnp.int32))
        attended = attended.reshape(SEQ_LEN, heads_here, HDIM) * active[None, :, None]
        attended = low(low_back(attended)).reshape(SEQ_LEN, heads_here * HDIM)
        return (running + low(jnp.dot(attended, w_mix, precision=PRECISE)), None)
    attn_total, _ = lax.scan(attend, jnp.zeros((SEQ_LEN, D), jnp.float32), (jnp.arange(N_TENSOR, dtype=jnp.int32), qkv_groups, out_groups))
    resid = layer_input + low_back(attn_total)
    mean_h = lax.optimization_barrier(jnp.mean(resid, axis=1, keepdims=True))
    centred = resid - mean_h
    variance = lax.optimization_barrier(jnp.mean(centred * centred, axis=1, keepdims=True))
    normed_ln = low(centred * lax.rsqrt(variance + EPSILON) * g_ln + b_ln)
    up_groups = w_up.reshape(D, N_TENSOR, columns).transpose(1, 0, 2)
    down_groups = w_down.reshape(N_TENSOR, columns, D)
    limit = (seq_widths + 1) * (FF // 4)

    def feed(running, members):
        group_id, w_a, w_b = members
        hidden = low_back(jnp.dot(low_back(normed_ln), w_a, precision=PRECISE))
        column_ids = group_id * columns + jnp.arange(columns, dtype=jnp.int32)
        keep = (column_ids[None, :] < limit[:, None]).astype(jnp.float32)
        lifted = jnp.maximum(hidden, 0.0)
        squared = low(lifted * lifted * keep)
        return (running + low(jnp.dot(squared, w_b, precision=PRECISE)), None)
    ffn_total, _ = lax.scan(jax.checkpoint(feed), jnp.zeros((SEQ_LEN, D), jnp.float32), (jnp.arange(N_TENSOR, dtype=jnp.int32), up_groups, down_groups))
    return resid + seq_probs[:, None] * low_back(ffn_total)

def reference(tokens, cotangent, first_norm_gain, w_qkv, w_out, g_ln, b_ln, w_up, w_down, probs, lengths, head_count, widths):
    floats = (tokens.astype(jnp.float32), probs.astype(jnp.float32), first_norm_gain.astype(jnp.float32), w_qkv.astype(jnp.float32), w_out.astype(jnp.float32), g_ln.astype(jnp.float32), b_ln.astype(jnp.float32), w_up.astype(jnp.float32), w_down.astype(jnp.float32))

    def forward(layer_input, prob_all, gain_a, w_a, w_b, gain_b, bias_b, w_c, w_d):
        weights = (w_a, w_b, w_c, w_d, gain_a, gain_b, bias_b)

        def per_sequence(members):
            seq_x, seq_w, seq_p, seq_l, seq_c = members
            return one_sequence(seq_x, seq_w, seq_p, seq_l, seq_c, weights)
        result = lax.map(jax.checkpoint(per_sequence), (layer_input.reshape(SEQS, SEQ_LEN, D), widths.reshape(SEQS, SEQ_LEN), prob_all.reshape(SEQS, SEQ_LEN), lengths, head_count))
        return result.reshape(TOKENS, D)
    result, pull = jax.vjp(forward, *floats)
    grads = pull(cotangent.astype(jnp.float32))
    return (result.astype(jnp.bfloat16), grads[0], grads[1], grads[2], grads[3], grads[4], grads[5], grads[6], grads[7], grads[8])
```

```python
import functools

import jax
import jax.numpy as jnp
from jax import lax
from jax.experimental import pallas as pl
from jax.experimental.pallas import tpu as pltpu
from jax.sharding import PartitionSpec as P

HDIM = 128
FF = 8192
EPSILON = 1e-05
NEGATIVE = -1e30
MAXDOC = 1024
GROUPS = 4
QROWS = 256
MESH = pl.DeviceIdType.MESH
BF = jnp.bfloat16
F32 = jnp.float32
ANY = pl.BlockSpec(memory_space=pl.ANY)
VM = pl.BlockSpec(memory_space=pltpu.VMEM)
DMA = pltpu.SemaphoreType.DMA
NT = (((1,), (1,)), ((), ()))
TN = (((0,), (0,)), ((), ()))


def dot(a, b, dims=(((1,), (0,)), ((), ()))):
    return lax.dot_general(a, b, dims, preferred_element_type=F32)


class Line:
    def __init__(self, ranks, rows):
        self.ranks, self.chips, self.rows = ranks, ranks // 2, rows
        self.t = lax.axis_index("tensor")
        self.z, self.c = self.t // 2, lax.rem(self.t, 2)
        self.has_up, self.has_down = self.z < self.chips - 1, self.z > 0
        self.up = jnp.minimum(self.t + 2, ranks - 1)
        self.down = jnp.maximum(self.t - 2, 0)
        self.partner = self.t + 1 - 2 * self.c

    def barrier(self, dp_size=0):
        sem = pltpu.get_barrier_semaphore()
        pl.semaphore_signal(sem, inc=1, device_id={"tensor": self.partner}, device_id_type=MESH)

        @pl.when(self.has_up)
        def _():
            pl.semaphore_signal(sem, inc=1, device_id={"tensor": self.up}, device_id_type=MESH)

        @pl.when(self.has_down)
        def _():
            pl.semaphore_signal(sem, inc=1, device_id={"tensor": self.down}, device_id_type=MESH)

        d = lax.axis_index("dp")
        for step in range(1, dp_size):
            pl.semaphore_signal(
                sem, inc=1, device_id={"dp": lax.rem(d + step, dp_size)}, device_id_type=MESH
            )
        links = self.has_up.astype(jnp.int32) + self.has_down.astype(jnp.int32)
        pl.semaphore_wait(sem, 1 + max(dp_size - 1, 0) + links)

    def block(self, rank):
        return pl.ds(pl.multiple_of(rank * self.rows, self.rows), self.rows)


def copy_to(src, dst, send, recv, rank):
    return pltpu.make_async_remote_copy(
        src_ref=src,
        dst_ref=dst,
        send_sem=send,
        recv_sem=recv,
        device_id={"tensor": rank},
        device_id_type=MESH,
    )


class Gather:
    def __init__(self, line, own, full, send, recv, local):
        self.l, self.own, self.full = line, own, full
        self.send, self.recv, self.local = send, recv, local

    @staticmethod
    def scratch(ranks, groups):
        return [DMA((3, groups, ranks // 2)), DMA((groups, ranks)), DMA((groups,))]

    def copy(self, g, rank, way, own=False):
        l = self.l
        place = self.full.at[g, l.block(rank)]
        return copy_to(
            self.own.at[g] if own else place,
            place,
            self.send.at[way, g, rank // 2],
            self.recv.at[g, rank],
            (l.up, l.down, l.partner)[way],
        )

    def pass_on(self, g, rank, up, down, own=False):
        l = self.l
        if up:

            @pl.when(l.has_up)
            def _():
                self.copy(g, rank, 0, own).start()

        if down:

            @pl.when(l.has_down)
            def _():
                self.copy(g, rank, 1, own).start()

        self.copy(g, rank, 2, own).start()

    def begin(self, g):
        l = self.l
        self.pass_on(g, l.t, True, True, own=True)
        pltpu.make_async_copy(self.own.at[g], self.full.at[g, l.block(l.t)], self.local.at[g]).start()

    def hop(self, g, h):
        l = self.l

        @pl.when(l.z - h >= 0)
        def _():
            self.copy(g, l.t - 2 * h, 0).wait_recv()
            self.pass_on(g, l.t - 2 * h, True, False)

        @pl.when(l.z + h <= l.chips - 1)
        def _():
            self.copy(g, l.t + 2 * h, 1).wait_recv()
            self.pass_on(g, l.t + 2 * h, False, True)

    def arrived(self, g):
        l = self.l
        pltpu.make_async_copy(self.own.at[g], self.full.at[g, l.block(l.t)], self.local.at[g]).wait()
        for z in range(l.chips):
            self.copy(g, 2 * z + 1 - l.c, 2).wait_recv()

    def drain(self, g):
        l = self.l
        for z in range(l.chips):

            @pl.when(l.has_up & (l.z >= z))
            def _():
                self.copy(g, 2 * z + l.c, 0).wait_send()

            @pl.when(l.has_down & (l.z <= z))
            def _():
                self.copy(g, 2 * z + l.c, 1).wait_send()

            self.copy(g, 2 * z + l.c, 2).wait_send()


class Reduce:
    def __init__(self, line, part, near, far, acc, send, near_recv, far_recv):
        self.l, self.part, self.near, self.far, self.acc = line, part, near, far, acc
        self.send, self.near_recv, self.far_recv = send, near_recv, far_recv

    @staticmethod
    def scratch(ranks, groups, rows, width):
        chips = ranks // 2
        return [
            pltpu.VMEM((groups, ranks * rows, width), BF),
            pltpu.VMEM((groups, chips, rows, width), BF),
            pltpu.VMEM((groups, chips + 1, rows, width), BF),
            pltpu.VMEM((rows, width), F32),
            DMA((2, groups, chips)),
            DMA((groups, chips)),
            DMA((groups, chips + 1)),
        ]

    def to_partner(self, g, z):
        l = self.l
        return copy_to(
            self.part.at[g, l.block(2 * z + 1 - l.c)],
            self.near.at[g, z],
            self.send.at[0, g, z],
            self.near_recv.at[g, z],
            l.partner,
        )

    def along(self, g, z, up, receive=False):
        l = self.l
        at = l.z if receive else jnp.where(up, l.z + 1, l.z - 1)
        slot = z if up else jnp.where(z == at, l.chips, z)
        return copy_to(
            self.part.at[g, l.block(2 * z + l.c)],
            self.far.at[g, slot],
            self.send.at[1, g, z],
            self.far_recv.at[g, slot],
            l.up if up else l.down,
        ), slot

    def begin(self, g):
        for z in range(self.l.chips):
            self.to_partner(g, z).start()

    def join(self, g, z):
        self.to_partner(g, z).wait_recv()
        self.acc[...] = self.part[g, self.l.block(2 * z + self.l.c)].astype(F32) + self.near[
            g, z
        ].astype(F32)

    def add_far(self, g, z, up):
        copy, slot = self.along(g, z, up, receive=True)
        copy.wait_recv()
        self.acc[...] += self.far[g, slot].astype(F32)

    def step(self, g, d):
        l = self.l

        def send(z, up):
            self.join(g, z)

            @pl.when(l.has_down if up else l.has_up)
            def _():
                self.add_far(g, z, up)

            self.part[g, l.block(2 * z + l.c)] = self.acc[...].astype(BF)
            self.along(g, z, up)[0].start()

        @pl.when(l.z + d <= l.chips - 1)
        def _():
            send(l.z + d, True)

        @pl.when(l.z - d >= 0)
        def _():
            send(l.z - d, False)

    def last(self, g):
        l = self.l
        self.join(g, l.z)

        @pl.when(l.has_down)
        def _():
            self.add_far(g, l.z, True)

        @pl.when(l.has_up)
        def _():
            self.add_far(g, l.z, False)

    def drain(self, g):
        l = self.l
        for z in range(l.chips):
            self.to_partner(g, z).wait_send()

            @pl.when(l.z != z)
            def _():
                copy_to(
                    self.part.at[g, l.block(2 * z + l.c)],
                    self.far.at[g, z],
                    self.send.at[1, g, z],
                    self.far_recv.at[g, z],
                    l.partner,
                ).wait_send()


def within(value, limit, body):
    pl.when((value >= 0) & (value < limit))(lambda: body(value))


def swap_halves(field):
    return pltpu.roll(field, HDIM // 2, axis=1)


def call(body, ins, outs, scratch, ident, in_specs=None, out_specs=None, limit=60, flops=0, moved=0):
    return pl.pallas_call(
        body,
        out_shape=outs,
        in_specs=in_specs or [VM] * len(ins),
        out_specs=out_specs or [VM] * len(outs),
        scratch_shapes=scratch,
        compiler_params=pltpu.CompilerParams(
            collective_id=ident, has_side_effects=True, vmem_limit_bytes=limit << 20
        ),
        cost_estimate=pl.CostEstimate(flops=flops, bytes_accessed=moved, transcendentals=0),
    )(*ins)


def gather_project(normed, w_qkv, cosines, sines, ranks, width):
    groups, rows, model = normed.shape
    heads = width // HDIM

    def body(own, w, cos, sin, qkv, kept, full, w_v, g_send, g_recv, g_local, w_sem, kept_sem):
        line = Line(ranks, rows)
        load = pltpu.make_async_copy(w, w_v, w_sem)
        load.start()
        line.barrier()
        gather = Gather(line, own, full, g_send, g_recv, g_local)

        def keep(g):
            return pltpu.make_async_copy(full.at[g], kept.at[g], kept_sem.at[g])

        def project(g):
            gather.arrived(g)
            keep(g).start()
            x = full[g]
            c, s = cos[g], sin[g]
            for which in range(3):
                p = dot(x, w_v[which])
                for h in range(heads):
                    u = p[:, h * HDIM : (h + 1) * HDIM]
                    if which < 2:
                        u = u * c + swap_halves(u) * s
                    u = u.astype(BF)
                    at = (which * heads + h) * HDIM
                    for rank in range(ranks):
                        qkv[rank, g, :, at : at + HDIM] = u[rank * rows : (rank + 1) * rows]

        @pl.loop(0, groups + line.chips - 1)
        def _(i):
            within(i, groups, gather.begin)
            for h in range(1, line.chips):
                within(i - h, groups, functools.partial(gather.hop, h=h))

            @pl.when(i == line.chips - 1)
            def _():
                load.wait()

            within(i - line.chips + 1, groups, project)

        @pl.loop(0, groups)
        def _(g):
            keep(g).wait()
            gather.drain(g)

    return call(
        body,
        [normed, w_qkv, cosines, sines],
        [
            jax.ShapeDtypeStruct((ranks, groups, rows, 3 * width), BF),
            jax.ShapeDtypeStruct((groups, ranks * rows, model), BF),
        ],
        [
            pltpu.VMEM((groups, ranks * rows, model), BF),
            pltpu.VMEM(w_qkv.shape, BF),
            *Gather.scratch(ranks, groups),
            DMA,
            DMA((groups,)),
        ],
        0,
        in_specs=[VM, ANY, VM, VM],
        out_specs=[VM, ANY],
        flops=2 * ranks * groups * rows * model * 3 * width,
        moved=60 << 20,
    )


QBLOCK = 512


def swap_halves_x(field):
    middle = field.shape[-1] // 2
    return jnp.concatenate([field[..., middle:], field[..., :middle]], axis=-1)


def rotate(field, cosines, sines):
    return field * cosines + swap_halves_x(field) * sines


def rotate_back(field, cosines, sines):
    return field * cosines + swap_halves_x(field * sines)


def position_tables(doc_lengths, length_all):
    places = jnp.arange(length_all, dtype=jnp.int32)
    doc_ends = jnp.cumsum(doc_lengths)
    passed = (places[:, None] >= doc_ends[None, :]).astype(jnp.int32)
    starts = jnp.sum(passed * doc_lengths[None, :], axis=1)
    offsets = (places - starts).astype(jnp.float32)
    half_dim = HDIM // 2
    frequency = 10000.0 ** (-jnp.arange(half_dim, dtype=jnp.float32) / half_dim)
    angles = offsets[:, None] * frequency[None, :]
    cosines = jnp.concatenate([jnp.cos(angles), jnp.cos(angles)], axis=1)
    sines = jnp.concatenate([-jnp.sin(angles), jnp.sin(angles)], axis=1)
    return (places, starts, cosines, sines)


def shards(
    tokens,
    cotangent,
    first_norm_gain,
    w_qkv,
    w_out,
    g_ln,
    b_ln,
    w_up,
    w_down,
    probs,
    lengths,
    head_count,
    widths,
):
    length_all = widths.shape[0]
    heads_here = w_out.shape[0] // HDIM
    columns = w_up.shape[1]
    scaling = HDIM ** (-0.5)
    block_count = length_all // QBLOCK
    places, starts, cosines, sines = position_tables(lengths[0], length_all)
    cos_heads = cosines[:, None, :]
    sin_heads = sines[:, None, :]
    layer_input = tokens.astype(jnp.float32)
    root_mean_scale = lax.rsqrt(
        jnp.mean(layer_input * layer_input, axis=1, keepdims=True) + EPSILON
    )
    input_normalized = layer_input * root_mean_scale
    normalized_rows = (input_normalized * first_norm_gain).astype(jnp.bfloat16)
    ranks = length_all // tokens.shape[0]
    own_rows = tokens.shape[0] // GROUPS
    order = lambda a: a.reshape(ranks, GROUPS, own_rows, -1).swapaxes(0, 1).reshape(GROUPS, ranks * own_rows, -1)
    qkv, kept_x = gather_project(
        normalized_rows.reshape(GROUPS, own_rows, -1), w_qkv.transpose(1, 0, 2), order(cosines), order(sines), ranks, heads_here * HDIM
    )
    qkv = qkv.reshape(length_all, 3, heads_here, HDIM)
    queries, keys_rot, values = qkv[:, 0], qkv[:, 1], qkv[:, 2]
    gathered = kept_x.reshape(GROUPS, ranks, own_rows, -1).swapaxes(0, 1).reshape(length_all, -1)
    head_ids = lax.axis_index("tensor") * heads_here + jnp.arange(heads_here, dtype=jnp.int32)
    active = (head_ids < head_count[0]).astype(jnp.float32)

    def scores_of(block_index):
        first_row = block_index * QBLOCK
        rows_q = lax.dynamic_slice_in_dim(queries, first_row, QBLOCK, 0)
        row_ids = lax.dynamic_slice_in_dim(places, first_row, QBLOCK, 0)
        row_starts = lax.dynamic_slice_in_dim(starts, first_row, QBLOCK, 0)
        allowed = (places[None, :] <= row_ids[:, None]) & (places[None, :] >= row_starts[:, None])
        raw_scores = (
            jnp.einsum("qhe,khe->hqk", rows_q, keys_rot, preferred_element_type=jnp.float32)
            * scaling
        )
        return (rows_q, jnp.where(allowed[None], raw_scores, NEGATIVE))

    def forward_block(block_index):
        rows_q, scores = scores_of(block_index)
        highest = jnp.max(scores, axis=-1, keepdims=True)
        exponent = jnp.exp(scores - highest)
        summed = jnp.sum(exponent, axis=-1, keepdims=True)
        weights_b = (exponent / summed).astype(jnp.bfloat16)
        attended_b = jnp.einsum(
            "hqk,khe->qhe", weights_b, values, preferred_element_type=jnp.float32
        )
        return (attended_b, (highest + jnp.log(summed))[..., 0])

    attended, log_totals = lax.map(forward_block, jnp.arange(block_count, dtype=jnp.int32))
    attended = attended.reshape(length_all, heads_here, HDIM) * active[None, :, None]
    attended = attended.astype(jnp.bfloat16).reshape(length_all, heads_here * HDIM)
    attn_part = lax.psum_scatter(
        jnp.dot(attended, w_out, preferred_element_type=jnp.float32).astype(jnp.bfloat16),
        "tensor",
        scatter_dimension=0,
        tiled=True,
    ).astype(jnp.float32)
    resid = layer_input + attn_part
    mean_h = jnp.mean(resid, axis=1, keepdims=True)
    centred = resid - mean_h
    variance = jnp.mean(centred * centred, axis=1, keepdims=True)
    inv_std = lax.rsqrt(variance + EPSILON)
    lhat = centred * inv_std
    normed_ln = (lhat * g_ln + b_ln).astype(jnp.bfloat16)
    gathered_ln = lax.all_gather(normed_ln, "tensor", axis=0, tiled=True)
    hidden = jnp.dot(gathered_ln, w_up, preferred_element_type=jnp.float32)
    column_ids = lax.axis_index("tensor") * columns + jnp.arange(columns, dtype=jnp.int32)
    limit = (widths + 1) * (FF // 4)
    keep = (column_ids[None, :] < limit[:, None]).astype(jnp.float32)
    lifted = jnp.maximum(hidden, 0.0)
    squared = (lifted * lifted * keep).astype(jnp.bfloat16)
    ffn_part = lax.psum_scatter(
        jnp.dot(squared, w_down, preferred_element_type=jnp.float32).astype(jnp.bfloat16),
        "tensor",
        scatter_dimension=0,
        tiled=True,
    ).astype(jnp.float32)
    result = (resid + probs[:, None] * ffn_part).astype(jnp.bfloat16)
    grad_result = cotangent.astype(jnp.float32)
    probs_grad = jnp.sum(grad_result * ffn_part, axis=1)
    scaled_grad = (probs[:, None] * grad_result).astype(jnp.bfloat16)
    back_ffn = lax.all_gather(scaled_grad, "tensor", axis=0, tiled=True)
    w_down_grad = jnp.einsum("tf,td->fd", squared, back_ffn, preferred_element_type=jnp.float32)
    grad_squared = jnp.einsum("td,fd->tf", back_ffn, w_down, preferred_element_type=jnp.float32)
    grad_hidden = (grad_squared * keep * 2.0 * lifted).astype(jnp.bfloat16)
    source_ln = lax.all_gather(normed_ln, "tensor", axis=0, tiled=True)
    w_up_grad = jnp.einsum("td,tf->df", source_ln, grad_hidden, preferred_element_type=jnp.float32)
    grad_ln_in = lax.psum_scatter(
        jnp.einsum("tf,df->td", grad_hidden, w_up, preferred_element_type=jnp.float32).astype(
            jnp.bfloat16
        ),
        "tensor",
        scatter_dimension=0,
        tiled=True,
    ).astype(jnp.float32)
    g_ln_part = jnp.sum(grad_ln_in * lhat, axis=0)
    b_ln_part = jnp.sum(grad_ln_in, axis=0)
    grad_lhat = grad_ln_in * g_ln
    grad_resid = grad_result + inv_std * (
        grad_lhat
        - jnp.mean(grad_lhat, axis=1, keepdims=True)
        - lhat * jnp.mean(grad_lhat * lhat, axis=1, keepdims=True)
    )
    back_attn = lax.all_gather(grad_resid.astype(jnp.bfloat16), "tensor", axis=0, tiled=True)
    w_out_grad = jnp.einsum("tf,td->fd", attended, back_attn, preferred_element_type=jnp.float32)
    grad_attended = jnp.einsum(
        "td,fd->tf", back_attn, w_out, preferred_element_type=jnp.float32
    ).astype(jnp.bfloat16)
    grad_attended = (
        grad_attended.reshape(length_all, heads_here, HDIM)
        * active.astype(jnp.bfloat16)[None, :, None]
    )

    def backward_block(running, block_index):
        grad_keys, grad_values = running
        rows_q, scores = scores_of(block_index)
        rows_grad = lax.dynamic_slice_in_dim(grad_attended, block_index * QBLOCK, QBLOCK, 0)
        weights_f = jnp.exp(scores - log_totals[block_index][..., None])
        grad_values = grad_values + jnp.einsum(
            "hqk,qhe->khe",
            weights_f.astype(jnp.bfloat16),
            rows_grad,
            preferred_element_type=jnp.float32,
        )
        grad_weights = jnp.einsum(
            "qhe,khe->hqk", rows_grad, values, preferred_element_type=jnp.float32
        )
        inner_sum = jnp.sum(weights_f * grad_weights, axis=-1, keepdims=True)
        grad_scores = (weights_f * (grad_weights - inner_sum)).astype(jnp.bfloat16)
        grad_rows = (
            jnp.einsum("hqk,khe->qhe", grad_scores, keys_rot, preferred_element_type=jnp.float32)
            * scaling
        )
        grad_keys = (
            grad_keys
            + jnp.einsum("hqk,qhe->khe", grad_scores, rows_q, preferred_element_type=jnp.float32)
            * scaling
        )
        return ((grad_keys, grad_values), grad_rows)

    empty = jnp.zeros((length_all, heads_here, HDIM), jnp.float32)
    (grad_keys, grad_values), grad_queries = lax.scan(
        backward_block, (empty, empty), jnp.arange(block_count, dtype=jnp.int32)
    )
    grad_queries = grad_queries.reshape(length_all, heads_here, HDIM)
    grad_q_raw = rotate_back(grad_queries, cos_heads, sin_heads).astype(jnp.bfloat16)
    grad_k_raw = rotate_back(grad_keys, cos_heads, sin_heads).astype(jnp.bfloat16)
    grad_v_raw = grad_values.astype(jnp.bfloat16)
    grad_proj = jnp.stack([grad_q_raw, grad_k_raw, grad_v_raw], axis=1).reshape(
        length_all, 3, heads_here * HDIM
    )
    source_attn = gathered
    w_qkv_grad = jnp.einsum(
        "td,tcf->dcf", source_attn, grad_proj, preferred_element_type=jnp.float32
    )
    w_qkv_grad, w_out_grad, w_up_grad, w_down_grad = (
        lax.psum_scatter(
            w_qkv_grad.astype(jnp.bfloat16), "dp", scatter_dimension=0, tiled=True
        ).astype(jnp.float32),
        lax.psum_scatter(
            w_out_grad.astype(jnp.bfloat16), "dp", scatter_dimension=1, tiled=True
        ).astype(jnp.float32),
        lax.psum_scatter(
            w_up_grad.astype(jnp.bfloat16), "dp", scatter_dimension=0, tiled=True
        ).astype(jnp.float32),
        lax.psum_scatter(
            w_down_grad.astype(jnp.bfloat16), "dp", scatter_dimension=1, tiled=True
        ).astype(jnp.float32),
    )
    normalized_gradient = lax.psum_scatter(
        jnp.einsum("tcf,dcf->td", grad_proj, w_qkv, preferred_element_type=jnp.float32).astype(
            jnp.bfloat16
        ),
        "tensor",
        scatter_dimension=0,
        tiled=True,
    ).astype(jnp.float32)
    first_gain_partial = jnp.sum(normalized_gradient * input_normalized, axis=0)
    rescaled_gradient = normalized_gradient * first_norm_gain
    tokens_grad = grad_resid + root_mean_scale * (
        rescaled_gradient
        - input_normalized * jnp.mean(rescaled_gradient * input_normalized, axis=1, keepdims=True)
    )
    gain_terms = jnp.stack([first_gain_partial, g_ln_part, b_ln_part], axis=0)
    gain_totals = lax.psum(gain_terms, ("dp", "tensor"))
    return (
        result,
        tokens_grad,
        probs_grad,
        gain_totals[0],
        w_qkv_grad,
        w_out_grad,
        gain_totals[1],
        gain_totals[2],
        w_up_grad,
        w_down_grad,
    )


def solution(mesh):
    placed = (
        P(("dp", "tensor"), None),
        P(("dp", "tensor"), None),
        P(),
        P(None, None, "tensor"),
        P("tensor", None),
        P(),
        P(),
        P(None, "tensor"),
        P("tensor", None),
        P(("dp", "tensor")),
        P("dp", None),
        P("dp"),
        P("dp"),
    )
    return jax.shard_map(
        shards,
        mesh=mesh,
        in_specs=placed,
        out_specs=(
            P(("dp", "tensor"), None),
            P(("dp", "tensor"), None),
            P(("dp", "tensor")),
            P(),
            P("dp", None, "tensor"),
            P("tensor", "dp"),
            P(),
            P(),
            P("dp", "tensor"),
            P("tensor", "dp"),
        ),
        check_vma=False,
    )
```

```python
import functools

import jax
import jax.numpy as jnp
from jax import lax
from jax.experimental import pallas as pl
from jax.experimental.pallas import tpu as pltpu
from jax.sharding import PartitionSpec as P

HDIM = 128
FF = 8192
EPSILON = 1e-05
NEGATIVE = -1e30
MAXDOC = 1024
GROUPS = 4
QROWS = 256
MESH = pl.DeviceIdType.MESH
BF = jnp.bfloat16
F32 = jnp.float32
ANY = pl.BlockSpec(memory_space=pl.ANY)
VM = pl.BlockSpec(memory_space=pltpu.VMEM)
DMA = pltpu.SemaphoreType.DMA
NT = (((1,), (1,)), ((), ()))
TN = (((0,), (0,)), ((), ()))


def dot(a, b, dims=(((1,), (0,)), ((), ()))):
    return lax.dot_general(a, b, dims, preferred_element_type=F32)


class Line:
    def __init__(self, ranks, rows):
        self.ranks, self.chips, self.rows = ranks, ranks // 2, rows
        self.t = lax.axis_index("tensor")
        self.z, self.c = self.t // 2, lax.rem(self.t, 2)
        self.has_up, self.has_down = self.z < self.chips - 1, self.z > 0
        self.up = jnp.minimum(self.t + 2, ranks - 1)
        self.down = jnp.maximum(self.t - 2, 0)
        self.partner = self.t + 1 - 2 * self.c

    def barrier(self, dp_size=0):
        sem = pltpu.get_barrier_semaphore()
        pl.semaphore_signal(sem, inc=1, device_id={"tensor": self.partner}, device_id_type=MESH)

        @pl.when(self.has_up)
        def _():
            pl.semaphore_signal(sem, inc=1, device_id={"tensor": self.up}, device_id_type=MESH)

        @pl.when(self.has_down)
        def _():
            pl.semaphore_signal(sem, inc=1, device_id={"tensor": self.down}, device_id_type=MESH)

        d = lax.axis_index("dp")
        for step in range(1, dp_size):
            pl.semaphore_signal(
                sem, inc=1, device_id={"dp": lax.rem(d + step, dp_size)}, device_id_type=MESH
            )
        links = self.has_up.astype(jnp.int32) + self.has_down.astype(jnp.int32)
        pl.semaphore_wait(sem, 1 + max(dp_size - 1, 0) + links)

    def block(self, rank):
        return pl.ds(pl.multiple_of(rank * self.rows, self.rows), self.rows)


def copy_to(src, dst, send, recv, rank):
    return pltpu.make_async_remote_copy(
        src_ref=src,
        dst_ref=dst,
        send_sem=send,
        recv_sem=recv,
        device_id={"tensor": rank},
        device_id_type=MESH,
    )


class Gather:
    def __init__(self, line, own, full, send, recv, local):
        self.l, self.own, self.full = line, own, full
        self.send, self.recv, self.local = send, recv, local

    @staticmethod
    def scratch(ranks, groups):
        return [DMA((3, groups, ranks // 2)), DMA((groups, ranks)), DMA((groups,))]

    def copy(self, g, rank, way, own=False):
        l = self.l
        place = self.full.at[g, l.block(rank)]
        return copy_to(
            self.own.at[g] if own else place,
            place,
            self.send.at[way, g, rank // 2],
            self.recv.at[g, rank],
            (l.up, l.down, l.partner)[way],
        )

    def pass_on(self, g, rank, up, down, own=False):
        l = self.l
        if up:

            @pl.when(l.has_up)
            def _():
                self.copy(g, rank, 0, own).start()

        if down:

            @pl.when(l.has_down)
            def _():
                self.copy(g, rank, 1, own).start()

        self.copy(g, rank, 2, own).start()

    def begin(self, g):
        l = self.l
        self.pass_on(g, l.t, True, True, own=True)
        pltpu.make_async_copy(self.own.at[g], self.full.at[g, l.block(l.t)], self.local.at[g]).start()

    def hop(self, g, h):
        l = self.l

        @pl.when(l.z - h >= 0)
        def _():
            self.copy(g, l.t - 2 * h, 0).wait_recv()
            self.pass_on(g, l.t - 2 * h, True, False)

        @pl.when(l.z + h <= l.chips - 1)
        def _():
            self.copy(g, l.t + 2 * h, 1).wait_recv()
            self.pass_on(g, l.t + 2 * h, False, True)

    def arrived(self, g):
        l = self.l
        pltpu.make_async_copy(self.own.at[g], self.full.at[g, l.block(l.t)], self.local.at[g]).wait()
        for z in range(l.chips):
            self.copy(g, 2 * z + 1 - l.c, 2).wait_recv()

    def drain(self, g):
        l = self.l
        for z in range(l.chips):

            @pl.when(l.has_up & (l.z >= z))
            def _():
                self.copy(g, 2 * z + l.c, 0).wait_send()

            @pl.when(l.has_down & (l.z <= z))
            def _():
                self.copy(g, 2 * z + l.c, 1).wait_send()

            self.copy(g, 2 * z + l.c, 2).wait_send()


class Reduce:
    def __init__(self, line, part, near, far, acc, send, near_recv, far_recv):
        self.l, self.part, self.near, self.far, self.acc = line, part, near, far, acc
        self.send, self.near_recv, self.far_recv = send, near_recv, far_recv

    @staticmethod
    def scratch(ranks, groups, rows, width):
        chips = ranks // 2
        return [
            pltpu.VMEM((groups, ranks * rows, width), BF),
            pltpu.VMEM((groups, chips, rows, width), BF),
            pltpu.VMEM((groups, chips + 1, rows, width), BF),
            pltpu.VMEM((rows, width), F32),
            DMA((2, groups, chips)),
            DMA((groups, chips)),
            DMA((groups, chips + 1)),
        ]

    def to_partner(self, g, z):
        l = self.l
        return copy_to(
            self.part.at[g, l.block(2 * z + 1 - l.c)],
            self.near.at[g, z],
            self.send.at[0, g, z],
            self.near_recv.at[g, z],
            l.partner,
        )

    def along(self, g, z, up, receive=False):
        l = self.l
        at = l.z if receive else jnp.where(up, l.z + 1, l.z - 1)
        slot = z if up else jnp.where(z == at, l.chips, z)
        return copy_to(
            self.part.at[g, l.block(2 * z + l.c)],
            self.far.at[g, slot],
            self.send.at[1, g, z],
            self.far_recv.at[g, slot],
            l.up if up else l.down,
        ), slot

    def begin(self, g):
        for z in range(self.l.chips):
            self.to_partner(g, z).start()

    def join(self, g, z):
        self.to_partner(g, z).wait_recv()
        self.acc[...] = self.part[g, self.l.block(2 * z + self.l.c)].astype(F32) + self.near[
            g, z
        ].astype(F32)

    def add_far(self, g, z, up):
        copy, slot = self.along(g, z, up, receive=True)
        copy.wait_recv()
        self.acc[...] += self.far[g, slot].astype(F32)

    def step(self, g, d):
        l = self.l

        def send(z, up):
            self.join(g, z)

            @pl.when(l.has_down if up else l.has_up)
            def _():
                self.add_far(g, z, up)

            self.part[g, l.block(2 * z + l.c)] = self.acc[...].astype(BF)
            self.along(g, z, up)[0].start()

        @pl.when(l.z + d <= l.chips - 1)
        def _():
            send(l.z + d, True)

        @pl.when(l.z - d >= 0)
        def _():
            send(l.z - d, False)

    def last(self, g):
        l = self.l
        self.join(g, l.z)

        @pl.when(l.has_down)
        def _():
            self.add_far(g, l.z, True)

        @pl.when(l.has_up)
        def _():
            self.add_far(g, l.z, False)

    def drain(self, g):
        l = self.l
        for z in range(l.chips):
            self.to_partner(g, z).wait_send()

            @pl.when(l.z != z)
            def _():
                copy_to(
                    self.part.at[g, l.block(2 * z + l.c)],
                    self.far.at[g, z],
                    self.send.at[1, g, z],
                    self.far_recv.at[g, z],
                    l.partner,
                ).wait_send()


def within(value, limit, body):
    pl.when((value >= 0) & (value < limit))(lambda: body(value))


def swap_halves(field):
    return pltpu.roll(field, HDIM // 2, axis=1)


def call(body, ins, outs, scratch, ident, in_specs=None, out_specs=None, limit=60, flops=0, moved=0):
    return pl.pallas_call(
        body,
        out_shape=outs,
        in_specs=in_specs or [VM] * len(ins),
        out_specs=out_specs or [VM] * len(outs),
        scratch_shapes=scratch,
        compiler_params=pltpu.CompilerParams(
            collective_id=ident, has_side_effects=True, vmem_limit_bytes=limit << 20
        ),
        cost_estimate=pl.CostEstimate(flops=flops, bytes_accessed=moved, transcendentals=0),
    )(*ins)


def attend(qkv, starts, active, width):
    length, heads = qkv.shape[0], width // HDIM
    scaling = HDIM ** (-0.5)
    reach = MAXDOC // QROWS + 1

    def body(live, q, k, v, start, out, v_t):
        h = pl.program_id(0)

        @pl.when(live[h] == 0)
        def _():
            out[...] = jnp.zeros_like(out)

        @pl.when(live[h] != 0)
        def _():
            v_t[...] = v[...].T
            for i in range(length // QROWS):
                low, high = max(0, i + 1 - reach) * QROWS, (i + 1) * QROWS
                rows = slice(i * QROWS, high)
                weights = softmax_block(q[rows], k[low:high], start[:, rows], i * QROWS, low, scaling)
                out[rows] = dot(v_t[:, low:high], weights.astype(BF)).T.astype(BF)

    return pl.pallas_call(
        body,
        out_shape=jax.ShapeDtypeStruct((length, width), BF),
        grid_spec=pltpu.PrefetchScalarGridSpec(
            num_scalar_prefetch=1,
            grid=(heads,),
            in_specs=[
                pl.BlockSpec((length, HDIM), lambda h, live: (0, h)),
                pl.BlockSpec((length, HDIM), lambda h, live: (0, heads + h)),
                pl.BlockSpec((length, HDIM), lambda h, live: (0, 2 * heads + h)),
                pl.BlockSpec((1, length), lambda h, live: (0, 0)),
            ],
            out_specs=pl.BlockSpec((length, HDIM), lambda h, live: (0, h)),
            scratch_shapes=[pltpu.VMEM((HDIM, length), BF)],
        ),
        compiler_params=pltpu.CompilerParams(vmem_limit_bytes=32 << 20),
        cost_estimate=pl.CostEstimate(flops=4 << 30, bytes_accessed=4 << 20, transcendentals=0),
    )(active, qkv, qkv, qkv, starts)


def softmax_block(q, k, start, first_query, first_key, scaling):
    raw = dot(k, q, NT)
    keys = first_key + lax.broadcasted_iota(jnp.int32, raw.shape, 0)
    queries = first_query + lax.broadcasted_iota(jnp.int32, raw.shape, 1)
    raw = jnp.where((keys <= queries) & (keys >= start), raw * scaling, NEGATIVE)
    exponent = jnp.exp(raw - jnp.max(raw, axis=0, keepdims=True))
    return exponent * (1.0 / jnp.sum(exponent, axis=0, keepdims=True))


def attend_back(qkv, grad, starts, active, cosines, sines, width):
    length, heads = qkv.shape[0], width // HDIM
    scaling = HDIM ** (-0.5)
    reach = MAXDOC // QROWS + 1

    def body(live, q, k, v, g, start, cos, sin, g_q, g_k, g_v, k_t, sum_k, sum_v):
        h = pl.program_id(0)

        @pl.when(live[h] == 0)
        def _():
            g_q[...] = jnp.zeros_like(g_q)
            g_k[...] = jnp.zeros_like(g_k)
            g_v[...] = jnp.zeros_like(g_v)

        def rotate_back(d, rows):
            return (d * cos[rows] + swap_halves(d * sin[rows])).astype(BF)

        @pl.when(live[h] != 0)
        def _():
            k_t[...] = k[...].T
            sum_k[...] = jnp.zeros_like(sum_k)
            sum_v[...] = jnp.zeros_like(sum_v)
            for i in range(length // QROWS):
                low, high = max(0, i + 1 - reach) * QROWS, (i + 1) * QROWS
                rows, keys = slice(i * QROWS, high), slice(low, high)
                weights = softmax_block(q[rows], k[keys], start[:, rows], i * QROWS, low, scaling)
                sum_v[keys] += dot(weights.astype(BF), g[rows])
                g_weights = dot(v[keys], g[rows], NT)
                inner = jnp.sum(weights * g_weights, axis=0, keepdims=True)
                g_scores = (weights * (g_weights - inner)).astype(BF)
                sum_k[keys] += dot(g_scores, q[rows])
                g_q[rows] = rotate_back(dot(k_t[:, keys], g_scores).T * scaling, rows)
            for i in range(length // QROWS):
                rows = slice(i * QROWS, (i + 1) * QROWS)
                g_k[rows] = rotate_back(sum_k[rows] * scaling, rows)
                g_v[rows] = sum_v[rows].astype(BF)

    column = lambda n: pl.BlockSpec((length, HDIM), lambda h, live: (0, n * heads + h))
    table = pl.BlockSpec((length, HDIM), lambda h, live: (0, 0))
    return pl.pallas_call(
        body,
        out_shape=[jax.ShapeDtypeStruct((length, width), BF)] * 3,
        grid_spec=pltpu.PrefetchScalarGridSpec(
            num_scalar_prefetch=1,
            grid=(heads,),
            in_specs=[
                column(0),
                column(1),
                column(2),
                column(0),
                pl.BlockSpec((1, length), lambda h, live: (0, 0)),
                table,
                table,
            ],
            out_specs=[column(0)] * 3,
            scratch_shapes=[
                pltpu.VMEM((HDIM, length), BF),
                pltpu.VMEM((length, HDIM), F32),
                pltpu.VMEM((length, HDIM), F32),
            ],
        ),
        compiler_params=pltpu.CompilerParams(vmem_limit_bytes=48 << 20),
        cost_estimate=pl.CostEstimate(flops=10 << 30, bytes_accessed=8 << 20, transcendentals=0),
    )(active, qkv, qkv, qkv, grad, starts, cosines, sines)


def stream(line, groups, gather=None, arrived=None, reduce=None, produce=(), finish=None, lead=0):
    hops = line.chips - 1
    produce = list(produce)

    @pl.loop(0, groups + hops + (lead if reduce else 0))
    def _(i):
        if gather:
            within(i, groups, gather.begin)
        if reduce:

            def end(g):
                reduce.last(g)
                finish(g)

            within(i - lead - hops, groups, end)
        for n in range(hops):
            if gather:
                within(i - hops + n, groups, functools.partial(gather.hop, h=hops - n))
                if n == 0 and arrived:
                    within(i - hops, groups, arrived)
            if reduce and n:
                within(i - lead - hops + n, groups, functools.partial(reduce.step, d=n))
            for piece in produce[n * len(produce) // hops : (n + 1) * len(produce) // hops]:
                within(i - lead, groups, piece)
        if reduce:
            within(i - lead, groups, reduce.begin)
            within(i - lead, groups, functools.partial(reduce.step, d=hops))

    @pl.loop(0, groups)
    def _(g):
        if gather:
            gather.drain(g)
        if reduce:
            reduce.drain(g)


def gather_project(normed, w_qkv, cosines, sines, ranks, width):
    groups, rows, model = normed.shape
    heads = width // HDIM

    def body(own, w, cos, sin, qkv, kept, full, w_v, g_send, g_recv, g_local, w_sem, kept_sem):
        line = Line(ranks, rows)
        load = pltpu.make_async_copy(w, w_v, w_sem)
        load.start()
        line.barrier()
        gather = Gather(line, own, full, g_send, g_recv, g_local)

        def keep(g):
            return pltpu.make_async_copy(full.at[g], kept.at[g], kept_sem.at[g])

        def project(g):
            gather.arrived(g)
            keep(g).start()

            @pl.when(g == 0)
            def _():
                load.wait()

            x = full[g]
            c, s = cos[g], sin[g]
            for which in range(3):
                p = dot(x, w_v[which])
                for h in range(heads):
                    u = p[:, h * HDIM : (h + 1) * HDIM]
                    if which < 2:
                        u = u * c + swap_halves(u) * s
                    u = u.astype(BF)
                    at = (which * heads + h) * HDIM
                    for rank in range(ranks):
                        qkv[rank, g, :, at : at + HDIM] = u[rank * rows : (rank + 1) * rows]

        stream(line, groups, gather, arrived=project)

        @pl.loop(0, groups)
        def _(g):
            keep(g).wait()

    return call(
        body,
        [normed, w_qkv, cosines, sines],
        [
            jax.ShapeDtypeStruct((ranks, groups, rows, 3 * width), BF),
            jax.ShapeDtypeStruct((groups, ranks * rows, model), BF),
        ],
        [
            pltpu.VMEM((groups, ranks * rows, model), BF),
            pltpu.VMEM(w_qkv.shape, BF),
            *Gather.scratch(ranks, groups),
            DMA,
            DMA((groups,)),
        ],
        0,
        in_specs=[VM, ANY, VM, VM],
        out_specs=[VM, ANY],
        flops=2 * ranks * groups * rows * model * 3 * width,
        moved=60 << 20,
    )


def project_reduce(attended, w_out, own_grad, ranks):
    groups, rows, model = own_grad.shape
    width = w_out.shape[0]

    def body(a, w, own, total, kept, full, g_send, g_recv, g_local, part, near, far, acc, s1, s2, s3, kept_sem):
        line = Line(ranks, rows)
        line.barrier()
        gather = Gather(line, own, full, g_send, g_recv, g_local)
        reduce = Reduce(line, part, near, far, acc, s1, s2, s3)

        def keep(g):
            return pltpu.make_async_copy(full.at[g], kept.at[g], kept_sem.at[g])

        def arrived(g):
            gather.arrived(g)
            keep(g).start()

        def produce(g):
            x = a[:, g].reshape(ranks * rows, width)
            for n in range(0, model, 512):
                part[g, :, n : n + 512] = dot(x, w[:, n : n + 512]).astype(BF)

        def finish(g):
            total[g] = acc[...]

        stream(line, groups, gather, arrived, reduce, [produce], finish)

        @pl.loop(0, groups)
        def _(g):
            keep(g).wait()

    return call(
        body,
        [attended, w_out, own_grad],
        [
            jax.ShapeDtypeStruct((groups, rows, model), F32),
            jax.ShapeDtypeStruct((groups, ranks * rows, model), BF),
        ],
        [
            pltpu.VMEM((groups, ranks * rows, model), BF),
            *Gather.scratch(ranks, groups),
            *Reduce.scratch(ranks, groups, rows, model),
            DMA((groups,)),
        ],
        1,
        out_specs=[VM, ANY],
        flops=2 * ranks * groups * rows * model * width,
        moved=100 << 20,
    )


def feed(own_ln, branch_grad, w_up, w_down, limit, ranks):
    groups, rows, model = own_ln.shape
    columns = w_up.shape[1]
    tile = min(256, columns)
    tokens = ranks * rows

    def body(
        own, grad, up, down, lim, total, kept, squared, hidden_grad,
        full, g_send, g_recv, g_local, part, near, far, acc, s1, s2, s3,
        up_v, down_v, grad_v, lifted, w_sem, grad_sem, kept_sem,
    ):
        line = Line(ranks, rows)
        loads = [
            pltpu.make_async_copy(up, up_v, w_sem.at[0]),
            pltpu.make_async_copy(down, down_v, w_sem.at[1]),
        ]
        for load in loads:
            load.start()
        line.barrier()
        gather = Gather(line, own, full, g_send, g_recv, g_local)
        reduce = Reduce(line, part, near, far, acc, s1, s2, s3)
        first_column = line.t * columns

        def keep(g):
            return pltpu.make_async_copy(full.at[g], kept.at[g], kept_sem.at[g])

        def fetch(g):
            slot = lax.rem(g, 2)
            return pltpu.make_async_copy(grad.at[g], grad_v.at[slot], grad_sem.at[slot])

        fetch(0).start()

        def arrived(g):
            gather.arrived(g)
            keep(g).start()
            fetch(g).wait()

            @pl.when(g + 1 < groups)
            def _():
                fetch(g + 1).start()

            @pl.when(g == 0)
            def _():
                for load in loads:
                    load.wait()

        def forward(g):
            @pl.loop(0, columns // tile)
            def _(n):
                at = pl.ds(pl.multiple_of(n * tile, tile), tile)
                hidden = dot(full[g], up_v[:, at])
                ids = first_column + n * tile + lax.broadcasted_iota(jnp.int32, hidden.shape, 1)
                live = jnp.where(ids < lim[g], jnp.maximum(hidden, 0.0), 0.0)
                lifted[:, at] = live
                squared[g, :, at] = (live * live).astype(BF)

        def backward(g):
            slot = lax.rem(g, 2)

            @pl.loop(0, columns // tile)
            def _(n):
                at = pl.ds(pl.multiple_of(n * tile, tile), tile)
                back = dot(grad_v[slot], down_v[at, :], NT)
                hidden_grad[g, :, at] = (back * (2.0 * lifted[:, at])).astype(BF)

        def lower(g):
            @pl.loop(0, model // 256)
            def _(n):
                at = pl.ds(pl.multiple_of(n * 256, 256), 256)
                part[g, :, at] = dot(hidden_grad[g], up_v[at, :], NT).astype(BF)

        def finish(g):
            total[g] = acc[...]

        stream(line, groups, gather, arrived, reduce, [forward, backward, lower], finish, line.chips - 1)

        @pl.loop(0, groups)
        def _(g):
            keep(g).wait()

    return call(
        body,
        [own_ln, branch_grad, w_up, w_down, limit],
        [
            jax.ShapeDtypeStruct((groups, rows, model), F32),
            jax.ShapeDtypeStruct((groups, tokens, model), BF),
            jax.ShapeDtypeStruct((groups, tokens, columns), BF),
            jax.ShapeDtypeStruct((groups, tokens, columns), BF),
        ],
        [
            pltpu.VMEM((groups, tokens, model), BF),
            *Gather.scratch(ranks, groups),
            *Reduce.scratch(ranks, groups, rows, model),
            pltpu.VMEM(w_up.shape, BF),
            pltpu.VMEM(w_down.shape, BF),
            pltpu.VMEM((2, tokens, model), BF),
            pltpu.VMEM((tokens, columns), F32),
            DMA((2,)),
            DMA((2,)),
            DMA((groups,)),
        ],
        2,
        in_specs=[VM, ANY, ANY, ANY, VM],
        out_specs=[VM, ANY, VM, VM],
        flops=6 * groups * tokens * model * columns,
        moved=100 << 20,
    )


def feed_out(own_grad, squared, w_down, w_out, active, ranks):
    groups, rows, model = own_grad.shape
    columns, width = w_down.shape[0], w_out.shape[0]
    tokens = ranks * rows

    def body(
        own, sq, down, w, live, total, kept, grad,
        full, g_send, g_recv, g_local, part, near, far, acc, s1, s2, s3, kept_sem,
    ):
        line = Line(ranks, rows)
        line.barrier()
        gather = Gather(line, own, full, g_send, g_recv, g_local)
        reduce = Reduce(line, part, near, far, acc, s1, s2, s3)

        def keep(g):
            return pltpu.make_async_copy(full.at[g], kept.at[g], kept_sem.at[g])

        def arrived(g):
            gather.arrived(g)
            keep(g).start()
            back = (dot(full[g], w[...], NT) * live[...]).astype(BF)
            for rank in range(ranks):
                grad[rank, g] = back[rank * rows : (rank + 1) * rows]

        def produce(g):
            @pl.loop(0, model // 256)
            def _(n):
                at = pl.ds(pl.multiple_of(n * 256, 256), 256)
                part[g, :, at] = dot(sq[g], down[:, at]).astype(BF)

        def finish(g):
            total[g] = acc[...]

        stream(line, groups, gather, arrived, reduce, [produce], finish)

        @pl.loop(0, groups)
        def _(g):
            keep(g).wait()

    return call(
        body,
        [own_grad, squared, w_down, w_out, active],
        [
            jax.ShapeDtypeStruct((groups, rows, model), F32),
            jax.ShapeDtypeStruct((groups, tokens, model), BF),
            jax.ShapeDtypeStruct((ranks, groups, rows, width), BF),
        ],
        [
            pltpu.VMEM((groups, tokens, model), BF),
            *Gather.scratch(ranks, groups),
            *Reduce.scratch(ranks, groups, rows, model),
            DMA((groups,)),
        ],
        3,
        out_specs=[VM, ANY, VM],
        flops=2 * groups * tokens * model * (columns + width),
        moved=100 << 20,
    )


def project_back(grads, w_qkv, ranks):
    _, groups, rows, width = grads[0].shape
    model = w_qkv.shape[1]

    def body(g_q, g_k, g_v, w, total, part, near, far, acc, s1, s2, s3):
        line = Line(ranks, rows)
        line.barrier()
        reduce = Reduce(line, part, near, far, acc, s1, s2, s3)

        def produce(g):
            xs = [x[:, g].reshape(ranks * rows, width) for x in (g_q, g_k, g_v)]
            for n in range(0, model, 256):
                out = dot(xs[0], w[0, n : n + 256], NT)
                out += dot(xs[1], w[1, n : n + 256], NT)
                out += dot(xs[2], w[2, n : n + 256], NT)
                part[g, :, n : n + 256] = out.astype(BF)

        def finish(g):
            total[g] = acc[...]

        stream(line, groups, None, None, reduce, [produce], finish)

    return call(
        body,
        [*grads, w_qkv],
        [jax.ShapeDtypeStruct((groups, rows, model), F32)],
        Reduce.scratch(ranks, groups, rows, model),
        4,
        flops=6 * groups * ranks * rows * model * width,
        moved=60 << 20,
    )[0]

def position_tables(doc_lengths, length_all):
    places = jnp.arange(length_all, dtype=jnp.int32)
    doc_ends = jnp.cumsum(doc_lengths)
    passed = (places[:, None] >= doc_ends[None, :]).astype(jnp.int32)
    starts = jnp.sum(passed * doc_lengths[None, :], axis=1)
    offsets = (places - starts).astype(jnp.float32)
    half_dim = HDIM // 2
    frequency = 10000.0 ** (-jnp.arange(half_dim, dtype=jnp.float32) / half_dim)
    angles = offsets[:, None] * frequency[None, :]
    cosines = jnp.concatenate([jnp.cos(angles), jnp.cos(angles)], axis=1)
    sines = jnp.concatenate([-jnp.sin(angles), jnp.sin(angles)], axis=1)
    return (starts, cosines, sines)


def shards(
    tokens,
    cotangent,
    first_norm_gain,
    w_qkv,
    w_out,
    g_ln,
    b_ln,
    w_up,
    w_down,
    probs,
    lengths,
    head_count,
    widths,
):
    length_all = widths.shape[0]
    own_tokens, model = tokens.shape
    ranks = length_all // own_tokens
    groups, rows = GROUPS, own_tokens // GROUPS
    width = w_out.shape[0]
    heads_here = width // HDIM
    starts, cosines, sines = position_tables(lengths[0], length_all)
    starts = starts.reshape(1, length_all)

    def grouped(a):
        return a.reshape(ranks, groups, rows, -1).swapaxes(0, 1).reshape(groups, ranks * rows, -1)

    own = lambda a: a.reshape(groups, rows, model)
    flat = lambda a: a.reshape(-1, a.shape[-1])
    w_qkv_t = w_qkv.transpose(1, 0, 2)

    layer_input = tokens.astype(F32)
    root_mean_scale = lax.rsqrt(
        jnp.mean(layer_input * layer_input, axis=1, keepdims=True) + EPSILON
    )
    input_normalized = layer_input * root_mean_scale
    normalized_rows = (input_normalized * first_norm_gain).astype(BF)
    qkv, kept_x = gather_project(
        own(normalized_rows), w_qkv_t, grouped(cosines), grouped(sines), ranks, width
    )
    qkv = qkv.reshape(length_all, 3 * width)
    head_ids = lax.axis_index("tensor") * heads_here + jnp.arange(heads_here, dtype=jnp.int32)
    active = (head_ids < head_count[0]).astype(jnp.int32)
    attended = attend(qkv, starts, active, width)

    grad_result = cotangent.astype(F32)
    scaled_grad = (probs[:, None] * grad_result).astype(BF)
    attn_part, kept_ffn_grad = project_reduce(
        attended.reshape(ranks, groups, rows, width), w_out, own(scaled_grad), ranks
    )
    resid = layer_input + flat(attn_part)
    mean_h = jnp.mean(resid, axis=1, keepdims=True)
    centred = resid - mean_h
    variance = jnp.mean(centred * centred, axis=1, keepdims=True)
    inv_std = lax.rsqrt(variance + EPSILON)
    lhat = centred * inv_std
    normed_ln = (lhat * g_ln + b_ln).astype(BF)
    limit = grouped((widths + 1) * (FF // 4))
    grad_ln_in, kept_ln, squared, grad_hidden = feed(
        own(normed_ln), kept_ffn_grad, w_up, w_down, limit, ranks
    )
    grad_ln_in = flat(grad_ln_in)
    g_ln_part = jnp.sum(grad_ln_in * lhat, axis=0)
    b_ln_part = jnp.sum(grad_ln_in, axis=0)
    grad_lhat = grad_ln_in * g_ln
    grad_resid = grad_result + inv_std * (
        grad_lhat
        - jnp.mean(grad_lhat, axis=1, keepdims=True)
        - lhat * jnp.mean(grad_lhat * lhat, axis=1, keepdims=True)
    )
    live = jnp.repeat(active.astype(F32), HDIM).reshape(1, width)
    ffn_part, kept_attn_grad, grad_attended = feed_out(
        own(grad_resid.astype(BF)), squared, w_down, w_out, live, ranks
    )
    ffn_part = flat(ffn_part)
    result = (resid + probs[:, None] * ffn_part).astype(BF)
    probs_grad = jnp.sum(grad_result * ffn_part, axis=1)
    w_down_grad = dot(flat(squared), flat(kept_ffn_grad), TN)
    w_up_grad = dot(flat(kept_ln), flat(grad_hidden), TN)

    grad_proj = attend_back(
        qkv, grad_attended.reshape(length_all, width), starts, active, cosines, sines, width
    )
    w_out_grad = dot(flat(grouped(attended)), flat(kept_attn_grad), TN)
    w_qkv_grad = jnp.stack(
        [dot(flat(kept_x), flat(grouped(g)), TN) for g in grad_proj], axis=1
    )
    w_qkv_grad, w_out_grad, w_up_grad, w_down_grad = (
        lax.psum_scatter(w_qkv_grad.astype(BF), "dp", scatter_dimension=0, tiled=True).astype(F32),
        lax.psum_scatter(w_out_grad.astype(BF), "dp", scatter_dimension=1, tiled=True).astype(F32),
        lax.psum_scatter(w_up_grad.astype(BF), "dp", scatter_dimension=0, tiled=True).astype(F32),
        lax.psum_scatter(w_down_grad.astype(BF), "dp", scatter_dimension=1, tiled=True).astype(F32),
    )
    normalized_gradient = flat(
        project_back([g.reshape(ranks, groups, rows, width) for g in grad_proj], w_qkv_t, ranks)
    )
    first_gain_partial = jnp.sum(normalized_gradient * input_normalized, axis=0)
    rescaled_gradient = normalized_gradient * first_norm_gain
    tokens_grad = grad_resid + root_mean_scale * (
        rescaled_gradient
        - input_normalized * jnp.mean(rescaled_gradient * input_normalized, axis=1, keepdims=True)
    )
    gain_terms = jnp.stack([first_gain_partial, g_ln_part, b_ln_part], axis=0)
    gain_totals = lax.psum(gain_terms, ("dp", "tensor"))
    return (
        result,
        tokens_grad,
        probs_grad,
        gain_totals[0],
        w_qkv_grad,
        w_out_grad,
        gain_totals[1],
        gain_totals[2],
        w_up_grad,
        w_down_grad,
    )


def solution(mesh):
    placed = (
        P(("dp", "tensor"), None),
        P(("dp", "tensor"), None),
        P(),
        P(None, None, "tensor"),
        P("tensor", None),
        P(),
        P(),
        P(None, "tensor"),
        P("tensor", None),
        P(("dp", "tensor")),
        P("dp", None),
        P("dp"),
        P("dp"),
    )
    return jax.shard_map(
        shards,
        mesh=mesh,
        in_specs=placed,
        out_specs=(
            P(("dp", "tensor"), None),
            P(("dp", "tensor"), None),
            P(("dp", "tensor")),
            P(),
            P("dp", None, "tensor"),
            P("tensor", "dp"),
            P(),
            P(),
            P("dp", "tensor"),
            P("tensor", "dp"),
        ),
        check_vma=False,
    )
```

```python
import functools

import jax
import jax.numpy as jnp
from jax import lax
from jax.experimental import pallas as pl
from jax.experimental.pallas import tpu as pltpu
from jax.sharding import PartitionSpec as P

HDIM = 128
FF = 8192
EPSILON = 1e-05
NEGATIVE = -1e30
MAXDOC = 1024
GROUPS = 4
QROWS = 256
MESH = pl.DeviceIdType.MESH
BF = jnp.bfloat16
F32 = jnp.float32
ANY = pl.BlockSpec(memory_space=pl.ANY)
VM = pl.BlockSpec(memory_space=pltpu.VMEM)
DMA = pltpu.SemaphoreType.DMA
NT = (((1,), (1,)), ((), ()))
TN = (((0,), (0,)), ((), ()))


def dot(a, b, dims=(((1,), (0,)), ((), ()))):
    return lax.dot_general(a, b, dims, preferred_element_type=F32)


class Line:
    def __init__(self, ranks, rows):
        self.ranks, self.chips, self.rows = ranks, ranks // 2, rows
        self.t = lax.axis_index("tensor")
        self.z, self.c = self.t // 2, lax.rem(self.t, 2)
        self.has_up, self.has_down = self.z < self.chips - 1, self.z > 0
        self.up = jnp.minimum(self.t + 2, ranks - 1)
        self.down = jnp.maximum(self.t - 2, 0)
        self.partner = self.t + 1 - 2 * self.c

    def barrier(self, dp_size=0):
        sem = pltpu.get_barrier_semaphore()
        pl.semaphore_signal(sem, inc=1, device_id={"tensor": self.partner}, device_id_type=MESH)

        @pl.when(self.has_up)
        def _():
            pl.semaphore_signal(sem, inc=1, device_id={"tensor": self.up}, device_id_type=MESH)

        @pl.when(self.has_down)
        def _():
            pl.semaphore_signal(sem, inc=1, device_id={"tensor": self.down}, device_id_type=MESH)

        d = lax.axis_index("dp")
        for step in range(1, dp_size):
            pl.semaphore_signal(
                sem, inc=1, device_id={"dp": lax.rem(d + step, dp_size)}, device_id_type=MESH
            )
        links = self.has_up.astype(jnp.int32) + self.has_down.astype(jnp.int32)
        pl.semaphore_wait(sem, 1 + max(dp_size - 1, 0) + links)

    def barrier_all(self, dp_size):
        sem = pltpu.get_barrier_semaphore()
        for n in range(1, self.ranks):
            pl.semaphore_signal(
                sem, inc=1, device_id={"tensor": lax.rem(self.t + n, self.ranks)}, device_id_type=MESH
            )
        d = lax.axis_index("dp")
        for n in range(1, dp_size):
            pl.semaphore_signal(
                sem, inc=1, device_id={"dp": lax.rem(d + n, dp_size)}, device_id_type=MESH
            )
        pl.semaphore_wait(sem, self.ranks - 1 + dp_size - 1)

    def block(self, rank):
        return pl.ds(pl.multiple_of(rank * self.rows, self.rows), self.rows)


def copy_to(src, dst, send, recv, rank):
    return pltpu.make_async_remote_copy(
        src_ref=src,
        dst_ref=dst,
        send_sem=send,
        recv_sem=recv,
        device_id={"tensor": rank},
        device_id_type=MESH,
    )


class Gather:
    def __init__(self, line, own, full, send, recv, local):
        self.l, self.own, self.full = line, own, full
        self.send, self.recv, self.local = send, recv, local

    @staticmethod
    def scratch(ranks, groups):
        return [DMA((3, groups, ranks // 2)), DMA((groups, ranks)), DMA((groups,))]

    def copy(self, g, rank, way, own=False):
        l = self.l
        place = self.full.at[g, l.block(rank)]
        return copy_to(
            self.own.at[g] if own else place,
            place,
            self.send.at[way, g, rank // 2],
            self.recv.at[g, rank],
            (l.up, l.down, l.partner)[way],
        )

    def pass_on(self, g, rank, up, down, own=False):
        l = self.l
        if up:

            @pl.when(l.has_up)
            def _():
                self.copy(g, rank, 0, own).start()

        if down:

            @pl.when(l.has_down)
            def _():
                self.copy(g, rank, 1, own).start()

        self.copy(g, rank, 2, own).start()

    def begin(self, g):
        l = self.l
        self.pass_on(g, l.t, True, True, own=True)
        pltpu.make_async_copy(self.own.at[g], self.full.at[g, l.block(l.t)], self.local.at[g]).start()

    def hop(self, g, h):
        l = self.l

        @pl.when(l.z - h >= 0)
        def _():
            self.copy(g, l.t - 2 * h, 0).wait_recv()
            self.pass_on(g, l.t - 2 * h, True, False)

        @pl.when(l.z + h <= l.chips - 1)
        def _():
            self.copy(g, l.t + 2 * h, 1).wait_recv()
            self.pass_on(g, l.t + 2 * h, False, True)

    def arrived(self, g):
        l = self.l
        pltpu.make_async_copy(self.own.at[g], self.full.at[g, l.block(l.t)], self.local.at[g]).wait()
        for z in range(l.chips):
            self.copy(g, 2 * z + 1 - l.c, 2).wait_recv()

    def drain(self, g):
        l = self.l
        for z in range(l.chips):

            @pl.when(l.has_up & (l.z >= z))
            def _():
                self.copy(g, 2 * z + l.c, 0).wait_send()

            @pl.when(l.has_down & (l.z <= z))
            def _():
                self.copy(g, 2 * z + l.c, 1).wait_send()

            self.copy(g, 2 * z + l.c, 2).wait_send()


class Reduce:
    def __init__(self, line, part, near, far, acc, send, near_recv, far_recv):
        self.l, self.part, self.near, self.far, self.acc = line, part, near, far, acc
        self.send, self.near_recv, self.far_recv = send, near_recv, far_recv

    @staticmethod
    def scratch(ranks, groups, rows, width):
        chips = ranks // 2
        return [
            pltpu.VMEM((groups, ranks * rows, width), BF),
            pltpu.VMEM((groups, chips, rows, width), BF),
            pltpu.VMEM((groups, chips + 1, rows, width), BF),
            pltpu.VMEM((rows, width), F32),
            DMA((2, groups, chips)),
            DMA((groups, chips)),
            DMA((groups, chips + 1)),
        ]

    def to_partner(self, g, z):
        l = self.l
        return copy_to(
            self.part.at[g, l.block(2 * z + 1 - l.c)],
            self.near.at[g, z],
            self.send.at[0, g, z],
            self.near_recv.at[g, z],
            l.partner,
        )

    def along(self, g, z, up, receive=False):
        l = self.l
        at = l.z if receive else jnp.where(up, l.z + 1, l.z - 1)
        slot = z if up else jnp.where(z == at, l.chips, z)
        return copy_to(
            self.part.at[g, l.block(2 * z + l.c)],
            self.far.at[g, slot],
            self.send.at[1, g, z],
            self.far_recv.at[g, slot],
            l.up if up else l.down,
        ), slot

    def begin(self, g):
        for z in range(self.l.chips):
            self.to_partner(g, z).start()

    def join(self, g, z):
        self.to_partner(g, z).wait_recv()
        self.acc[...] = self.part[g, self.l.block(2 * z + self.l.c)].astype(F32) + self.near[
            g, z
        ].astype(F32)

    def add_far(self, g, z, up):
        copy, slot = self.along(g, z, up, receive=True)
        copy.wait_recv()
        self.acc[...] += self.far[g, slot].astype(F32)

    def step(self, g, d):
        l = self.l

        def send(z, up):
            self.join(g, z)

            @pl.when(l.has_down if up else l.has_up)
            def _():
                self.add_far(g, z, up)

            self.part[g, l.block(2 * z + l.c)] = self.acc[...].astype(BF)
            self.along(g, z, up)[0].start()

        @pl.when(l.z + d <= l.chips - 1)
        def _():
            send(l.z + d, True)

        @pl.when(l.z - d >= 0)
        def _():
            send(l.z - d, False)

    def last(self, g):
        l = self.l
        self.join(g, l.z)

        @pl.when(l.has_down)
        def _():
            self.add_far(g, l.z, True)

        @pl.when(l.has_up)
        def _():
            self.add_far(g, l.z, False)

    def drain(self, g):
        l = self.l
        for z in range(l.chips):
            self.to_partner(g, z).wait_send()

            @pl.when(l.z != z)
            def _():
                copy_to(
                    self.part.at[g, l.block(2 * z + l.c)],
                    self.far.at[g, z],
                    self.send.at[1, g, z],
                    self.far_recv.at[g, z],
                    l.partner,
                ).wait_send()


def within(value, limit, body):
    pl.when((value >= 0) & (value < limit))(lambda: body(value))


def swap_halves(field):
    return pltpu.roll(field, HDIM // 2, axis=1)


def call(body, ins, outs, scratch, ident, in_specs=None, out_specs=None, limit=60, flops=0, moved=0):
    return pl.pallas_call(
        body,
        out_shape=outs,
        in_specs=in_specs or [VM] * len(ins),
        out_specs=out_specs or [VM] * len(outs),
        scratch_shapes=scratch,
        compiler_params=pltpu.CompilerParams(
            collective_id=ident, has_side_effects=True, vmem_limit_bytes=limit << 20
        ),
        cost_estimate=pl.CostEstimate(flops=flops, bytes_accessed=moved, transcendentals=0),
    )(*ins)


def stream(line, groups, gather=None, arrived=None, reduce=None, produce=(), finish=None, lead=0, extra=None):
    hops = line.chips - 1
    produce = list(produce)
    turns = groups + hops + (lead if reduce else 0)

    @pl.loop(0, turns)
    def _(i):
        if gather:
            within(i, groups, gather.begin)
        if reduce:

            def end(g):
                reduce.last(g)
                finish(g)

            within(i - lead - hops, groups, end)
        for n in range(hops):
            if gather:
                within(i - hops + n, groups, functools.partial(gather.hop, h=hops - n))
                if n == 0 and arrived:
                    within(i - hops, groups, arrived)
            if reduce and n:
                within(i - lead - hops + n, groups, functools.partial(reduce.step, d=n))
            for piece in produce[n * len(produce) // hops : (n + 1) * len(produce) // hops]:
                within(i - lead, groups, piece)
        if reduce:
            within(i - lead, groups, reduce.begin)
            within(i - lead, groups, functools.partial(reduce.step, d=hops))
        if extra:
            within(i, min(extra[0], turns), extra[1])

    if extra:

        @pl.loop(min(extra[0], turns), extra[0])
        def _(i):
            extra[1](i)

    @pl.loop(0, groups)
    def _(g):
        if gather:
            gather.drain(g)
        if reduce:
            reduce.drain(g)


def starts_of(lengths, places):
    end, start = jnp.int32(0), jnp.zeros_like(places)
    for length in lengths:
        end = end + length
        start = start + jnp.where(places >= end, length, 0)
    return start


def softmax_block(q, k, start, first_query, first_key, scaling):
    raw = dot(k, q, NT)
    keys = first_key + lax.broadcasted_iota(jnp.int32, raw.shape, 0)
    queries = first_query + lax.broadcasted_iota(jnp.int32, raw.shape, 1)
    raw = jnp.where((keys <= queries) & (keys >= start), raw * scaling, NEGATIVE)
    exponent = jnp.exp(raw - jnp.max(raw, axis=0, keepdims=True))
    return exponent * (1.0 / jnp.sum(exponent, axis=0, keepdims=True))


def query_starts(lengths, first):
    places = first + lax.broadcasted_iota(jnp.int32, (8, QROWS), 1)
    return starts_of([lengths[0, n] for n in range(lengths.shape[1])], places)[:1]


def attend(qkv, lengths, active, width, groups, own_tokens):
    length, heads = qkv.shape[0], width // HDIM
    scaling = HDIM ** (-0.5)
    reach = MAXDOC // QROWS + 1
    rows_own = own_tokens // groups

    def body(live, docs, q, k, v, out, v_t):
        h = pl.program_id(0)

        @pl.when(live[h] == 0)
        def _():
            out[...] = jnp.zeros_like(out)

        @pl.when(live[h] != 0)
        def _():
            v_t[...] = v[...].T
            for i in range(length // QROWS):
                low, high = max(0, i + 1 - reach) * QROWS, (i + 1) * QROWS
                rows = slice(i * QROWS, high)
                start = query_starts(docs, i * QROWS)
                weights = softmax_block(q[rows], k[low:high], start, i * QROWS, low, scaling)
                done = dot(v_t[:, low:high], weights.astype(BF)).T.astype(BF)
                put_grouped(out, done, i * QROWS, own_tokens, rows_own)

    return pl.pallas_call(
        body,
        out_shape=jax.ShapeDtypeStruct((groups, length // groups, width), BF),
        grid_spec=pltpu.PrefetchScalarGridSpec(
            num_scalar_prefetch=2,
            grid=(heads,),
            in_specs=[
                pl.BlockSpec((length, HDIM), lambda h, live, docs: (0, h)),
                pl.BlockSpec((length, HDIM), lambda h, live, docs: (0, heads + h)),
                pl.BlockSpec((length, HDIM), lambda h, live, docs: (0, 2 * heads + h)),
            ],
            out_specs=pl.BlockSpec(
                (groups, length // groups, HDIM), lambda h, live, docs: (0, 0, h)
            ),
            scratch_shapes=[pltpu.VMEM((HDIM, length), BF)],
        ),
        compiler_params=pltpu.CompilerParams(vmem_limit_bytes=32 << 20),
        cost_estimate=pl.CostEstimate(flops=4 << 30, bytes_accessed=4 << 20, transcendentals=0),
    )(active, lengths, qkv, qkv, qkv)


def put_grouped(out, block, first, own_tokens, rows):
    for at in range(0, block.shape[0], rows):
        rank, inside = divmod(first + at, own_tokens)
        out[inside // rows, rank * rows : (rank + 1) * rows] = block[at : at + rows]


def attend_back(qkv, grad, lengths, active, cosines, sines, width, groups, own_tokens):
    length, heads = qkv.shape[0], width // HDIM
    scaling = HDIM ** (-0.5)
    reach = MAXDOC // QROWS + 1
    rows_own = own_tokens // groups

    def body(live, docs, q, k, v, g, cos, sin, g_q, g_k, g_v, k_t, sum_k, sum_v):
        h = pl.program_id(0)

        @pl.when(live[h] == 0)
        def _():
            g_q[...] = jnp.zeros_like(g_q)
            g_k[...] = jnp.zeros_like(g_k)
            g_v[...] = jnp.zeros_like(g_v)

        def rotate_back(d, rows):
            return (d * cos[rows] + swap_halves(d * sin[rows])).astype(BF)

        @pl.when(live[h] != 0)
        def _():
            k_t[...] = k[...].T
            sum_k[...] = jnp.zeros_like(sum_k)
            sum_v[...] = jnp.zeros_like(sum_v)
            for i in range(length // QROWS):
                low, high = max(0, i + 1 - reach) * QROWS, (i + 1) * QROWS
                rows, keys = slice(i * QROWS, high), slice(low, high)
                start = query_starts(docs, i * QROWS)
                weights = softmax_block(q[rows], k[keys], start, i * QROWS, low, scaling)
                sum_v[keys] += dot(weights.astype(BF), g[rows])
                g_weights = dot(v[keys], g[rows], NT)
                inner = jnp.sum(weights * g_weights, axis=0, keepdims=True)
                g_scores = (weights * (g_weights - inner)).astype(BF)
                sum_k[keys] += dot(g_scores, q[rows])
                back = rotate_back(dot(k_t[:, keys], g_scores).T * scaling, rows)
                put_grouped(g_q, back, i * QROWS, own_tokens, rows_own)
            for i in range(length // QROWS):
                rows = slice(i * QROWS, (i + 1) * QROWS)
                put_grouped(g_k, rotate_back(sum_k[rows] * scaling, rows), i * QROWS, own_tokens, rows_own)
                put_grouped(g_v, sum_v[rows].astype(BF), i * QROWS, own_tokens, rows_own)

    column = lambda n: pl.BlockSpec((length, HDIM), lambda h, live, docs: (0, n * heads + h))
    table = pl.BlockSpec((length, HDIM), lambda h, live, docs: (0, 0))
    return pl.pallas_call(
        body,
        out_shape=[jax.ShapeDtypeStruct((groups, length // groups, width), BF)] * 3,
        grid_spec=pltpu.PrefetchScalarGridSpec(
            num_scalar_prefetch=2,
            grid=(heads,),
            in_specs=[column(0), column(1), column(2), column(0), table, table],
            out_specs=[
                pl.BlockSpec((groups, length // groups, HDIM), lambda h, live, docs: (0, 0, h))
            ]
            * 3,
            scratch_shapes=[
                pltpu.VMEM((HDIM, length), BF),
                pltpu.VMEM((length, HDIM), F32),
                pltpu.VMEM((length, HDIM), F32),
            ],
        ),
        compiler_params=pltpu.CompilerParams(vmem_limit_bytes=48 << 20),
        cost_estimate=pl.CostEstimate(flops=10 << 30, bytes_accessed=8 << 20, transcendentals=0),
    )(active, lengths, qkv, qkv, qkv, grad, cosines, sines)


class Spread:
    def __init__(self, size, out, land, send, recv):
        self.size, self.out, self.land, self.send, self.recv = size, out, land, send, recv
        self.me = lax.axis_index("dp")

    def target(self, n):
        return lax.rem(self.me + n, self.size)

    def copy(self, n, source=None):
        place = self.me if source is None else source
        return pltpu.make_async_remote_copy(
            src_ref=self.out.at[n],
            dst_ref=self.land.at[place],
            send_sem=self.send.at[n],
            recv_sem=self.recv.at[n],
            device_id={"dp": self.target(n)},
            device_id_type=MESH,
        )

    def own(self):
        return pltpu.make_async_copy(self.out.at[0], self.land.at[self.me], self.send.at[0])

    def begin(self, n):
        @pl.when(n == 0)
        def _():
            self.own().start()

        @pl.when(n != 0)
        def _():
            self.copy(n).start()

    def end(self):
        self.own().wait()

        @pl.loop(1, self.size)
        def _(n):
            self.copy(n).wait_send()
            self.copy(n, lax.rem(self.me + self.size - n, self.size)).wait_recv()

    @staticmethod
    def scratch(size, shape):
        return [pltpu.VMEM((size, *shape), BF), DMA((size,)), DMA((size,))]


def row_mean(field):
    return jnp.mean(field, axis=1, keepdims=True)


def layer_norm(resid):
    centred = resid - row_mean(resid)
    inv_std = lax.rsqrt(row_mean(centred * centred) + EPSILON)
    return centred * inv_std, inv_std


def gather_project(tokens, gain, lengths, frequency, w_qkv, ranks, width):
    groups, rows, model = tokens.shape
    heads = width // HDIM
    shift = rows.bit_length() - 1

    def body(
        x_ref, gain_ref, docs, freq, w, qkv, kept, cos_out, sin_out,
        own, full, w_v, g_send, g_recv, g_local, w_sem, kept_sem,
    ):
        line = Line(ranks, rows)
        load = pltpu.make_async_copy(w, w_v, w_sem)
        load.start()

        @pl.loop(0, groups)
        def _(g):
            x = x_ref[g].astype(F32)
            own[g] = (x * lax.rsqrt(row_mean(x * x) + EPSILON) * gain_ref[...]).astype(BF)

        line.barrier()
        gather = Gather(line, own, full, g_send, g_recv, g_local)

        def keep(g):
            return pltpu.make_async_copy(full.at[g], kept.at[g], kept_sem.at[g])

        def project(g):
            r = lax.broadcasted_iota(jnp.int32, (ranks * rows, HDIM), 0)
            lane = lax.broadcasted_iota(jnp.int32, (ranks * rows, HDIM), 1)
            places = lax.shift_right_logical(r, shift) * (groups * rows) + g * rows + (r & (rows - 1))
            starts = starts_of([docs[0, n] for n in range(docs.shape[1])], places)
            angles = (places - starts).astype(F32) * freq[...]
            c = jnp.cos(angles)
            s = jnp.sin(angles)
            s = jnp.where(lane < HDIM // 2, -s, s)
            for rank in range(ranks):
                cos_out[rank, g] = c[rank * rows : (rank + 1) * rows]
                sin_out[rank, g] = s[rank * rows : (rank + 1) * rows]
            gather.arrived(g)
            keep(g).start()

            @pl.when(g == 0)
            def _():
                load.wait()

            x = full[g]
            for which in range(3):
                p = dot(x, w_v[which])
                for h in range(heads):
                    u = p[:, h * HDIM : (h + 1) * HDIM]
                    if which < 2:
                        u = u * c + swap_halves(u) * s
                    u = u.astype(BF)
                    at = (which * heads + h) * HDIM
                    for rank in range(ranks):
                        qkv[rank, g, :, at : at + HDIM] = u[rank * rows : (rank + 1) * rows]

        stream(line, groups, gather, arrived=project)

        @pl.loop(0, groups)
        def _(g):
            keep(g).wait()

    table = jax.ShapeDtypeStruct((ranks, groups, rows, HDIM), F32)
    return call(
        body,
        [tokens, gain, lengths, frequency, w_qkv],
        [
            jax.ShapeDtypeStruct((ranks, groups, rows, 3 * width), BF),
            jax.ShapeDtypeStruct((groups, ranks * rows, model), BF),
            table,
            table,
        ],
        [
            pltpu.VMEM((groups, rows, model), BF),
            pltpu.VMEM((groups, ranks * rows, model), BF),
            pltpu.VMEM(w_qkv.shape, BF),
            *Gather.scratch(ranks, groups),
            DMA,
            DMA((groups,)),
        ],
        0,
        in_specs=[VM, VM, pl.BlockSpec(memory_space=pltpu.SMEM), VM, ANY],
        out_specs=[VM, ANY, VM, VM],
        flops=2 * ranks * groups * rows * model * 3 * width,
        moved=60 << 20,
    )


def project_reduce(attended, w_out, tokens, cotangent, probs, g_ln, b_ln, ranks):
    groups, rows, model = cotangent.shape
    width = w_out.shape[0]

    def body(
        a, w, x, dy, p, gain, bias, resid, normed, kept,
        own, full, g_send, g_recv, g_local, part, near, far, acc, s1, s2, s3, kept_sem,
    ):
        line = Line(ranks, rows)

        @pl.loop(0, groups)
        def _(g):
            own[g] = (dy[g].astype(F32) * p[g, :, :1]).astype(BF)

        line.barrier()
        gather = Gather(line, own, full, g_send, g_recv, g_local)
        reduce = Reduce(line, part, near, far, acc, s1, s2, s3)

        def keep(g):
            return pltpu.make_async_copy(full.at[g], kept.at[g], kept_sem.at[g])

        def arrived(g):
            gather.arrived(g)
            keep(g).start()

        def produce(g):
            for n in range(0, model, 512):
                part[g, :, n : n + 512] = dot(a[g], w[:, n : n + 512]).astype(BF)

        def finish(g):
            resid[g] = x[g].astype(F32) + acc[...]
            lhat, _ = layer_norm(resid[g])
            normed[g] = (lhat * gain[...] + bias[...]).astype(BF)

        stream(line, groups, gather, arrived, reduce, [produce], finish)

        @pl.loop(0, groups)
        def _(g):
            keep(g).wait()

    return call(
        body,
        [attended, w_out, tokens, cotangent, probs, g_ln, b_ln],
        [
            jax.ShapeDtypeStruct((groups, rows, model), F32),
            jax.ShapeDtypeStruct((groups, rows, model), BF),
            jax.ShapeDtypeStruct((groups, ranks * rows, model), BF),
        ],
        [
            pltpu.VMEM((groups, rows, model), BF),
            pltpu.VMEM((groups, ranks * rows, model), BF),
            *Gather.scratch(ranks, groups),
            *Reduce.scratch(ranks, groups, rows, model),
            DMA((groups,)),
        ],
        1,
        out_specs=[VM, VM, ANY],
        flops=2 * ranks * groups * rows * model * width,
        moved=100 << 20,
    )


def feed(own_ln, branch_grad, w_up, w_down, widths, resid, cotangent, g_ln, ranks):
    groups, rows, model = own_ln.shape
    columns = w_up.shape[1]
    tile = min(256, columns)
    tokens = ranks * rows

    def body(
        own, grad, up, down, wide, res, dy, gain, grad_resid, grad_low, gains, kept, squared, hidden_grad,
        full, g_send, g_recv, g_local, part, near, far, acc, s1, s2, s3,
        up_v, down_v, grad_v, lifted, w_sem, grad_sem, kept_sem,
    ):
        line = Line(ranks, rows)
        loads = [
            pltpu.make_async_copy(up, up_v, w_sem.at[0]),
            pltpu.make_async_copy(down, down_v, w_sem.at[1]),
        ]
        for load in loads:
            load.start()
        gains[...] = jnp.zeros_like(gains)
        line.barrier()
        gather = Gather(line, own, full, g_send, g_recv, g_local)
        reduce = Reduce(line, part, near, far, acc, s1, s2, s3)
        first_column = line.t * columns

        def keep(g):
            return pltpu.make_async_copy(full.at[g], kept.at[g], kept_sem.at[g])

        def fetch(g):
            slot = lax.rem(g, 2)
            return pltpu.make_async_copy(grad.at[g], grad_v.at[slot], grad_sem.at[slot])

        fetch(0).start()

        def arrived(g):
            gather.arrived(g)
            keep(g).start()
            fetch(g).wait()

            @pl.when(g + 1 < groups)
            def _():
                fetch(g + 1).start()

            @pl.when(g == 0)
            def _():
                for load in loads:
                    load.wait()

        def forward(g):
            limit = (jnp.broadcast_to(wide[pl.ds(g, 1), :], (HDIM, tokens)).T[:, :1] + 1) * (FF // 4)

            @pl.loop(0, columns // tile)
            def _(n):
                at = pl.ds(pl.multiple_of(n * tile, tile), tile)
                hidden = dot(full[g], up_v[:, at])
                ids = first_column + n * tile + lax.broadcasted_iota(jnp.int32, hidden.shape, 1)
                live = jnp.where(ids < limit, jnp.maximum(hidden, 0.0), 0.0)
                lifted[:, at] = live
                squared[g, :, at] = (live * live).astype(BF)

        def backward(g):
            slot = lax.rem(g, 2)

            @pl.loop(0, columns // tile)
            def _(n):
                at = pl.ds(pl.multiple_of(n * tile, tile), tile)
                back = dot(grad_v[slot], down_v[at, :], NT)
                hidden_grad[g, :, at] = (back * (2.0 * lifted[:, at])).astype(BF)

        def lower(g):
            @pl.loop(0, model // 256)
            def _(n):
                at = pl.ds(pl.multiple_of(n * 256, 256), 256)
                part[g, :, at] = dot(hidden_grad[g], up_v[at, :], NT).astype(BF)

        def finish(g):
            lhat, inv_std = layer_norm(res[g])
            back = acc[...]
            gains[0:1] += jnp.sum(back * lhat, axis=0, keepdims=True)
            gains[1:2] += jnp.sum(back, axis=0, keepdims=True)
            back = back * gain[...]
            back = dy[g].astype(F32) + inv_std * (back - row_mean(back) - lhat * row_mean(back * lhat))
            grad_resid[g] = back
            grad_low[g] = back.astype(BF)

        stream(line, groups, gather, arrived, reduce, [forward, backward, lower], finish, line.chips - 1)

        @pl.loop(0, groups)
        def _(g):
            keep(g).wait()

    return call(
        body,
        [own_ln, branch_grad, w_up, w_down, widths, resid, cotangent, g_ln],
        [
            jax.ShapeDtypeStruct((groups, rows, model), F32),
            jax.ShapeDtypeStruct((groups, rows, model), BF),
            jax.ShapeDtypeStruct((2, model), F32),
            jax.ShapeDtypeStruct((groups, tokens, model), BF),
            jax.ShapeDtypeStruct((groups, tokens, columns), BF),
            jax.ShapeDtypeStruct((groups, tokens, columns), BF),
        ],
        [
            pltpu.VMEM((groups, tokens, model), BF),
            *Gather.scratch(ranks, groups),
            *Reduce.scratch(ranks, groups, rows, model),
            pltpu.VMEM(w_up.shape, BF),
            pltpu.VMEM(w_down.shape, BF),
            pltpu.VMEM((2, tokens, model), BF),
            pltpu.VMEM((tokens, columns), F32),
            DMA((2,)),
            DMA((2,)),
            DMA((groups,)),
        ],
        2,
        in_specs=[VM, ANY, ANY, ANY, VM, VM, VM, VM],
        out_specs=[VM, VM, VM, ANY, VM, VM],
        flops=6 * groups * tokens * model * columns,
        moved=100 << 20,
    )


def feed_out(
    own_grad, squared, hidden_grad, kept_ln, branch_grad, w_down, w_out, active, resid, cotangent, probs, ranks, sequences
):
    groups, rows, model = own_grad.shape
    columns, width = w_down.shape[0], w_out.shape[0]
    tokens = ranks * rows
    share = model // sequences

    def body(
        own, sq, hg, ln, bg, down, w, live, res, dy, p, result, probs_grad, kept, grad, land_down, land_up,
        full, g_send, g_recv, g_local, part, near, far, acc, s1, s2, s3, kept_sem,
        out_down, down_send, down_recv, out_up, up_send, up_recv, ln_v, bg_v, fetch_sem,
    ):
        line = Line(ranks, rows)
        gather = Gather(line, own, full, g_send, g_recv, g_local)
        reduce = Reduce(line, part, near, far, acc, s1, s2, s3)
        to_down = Spread(sequences, out_down, land_down, down_send, down_recv)
        to_up = Spread(sequences, out_up, land_up, up_send, up_recv)

        def keep(g):
            return pltpu.make_async_copy(full.at[g], kept.at[g], kept_sem.at[g])

        def arrived(g):
            gather.arrived(g)
            keep(g).start()
            back = (dot(full[g], w[...], NT) * live[...]).astype(BF)
            for rank in range(ranks):
                grad[rank, g] = back[rank * rows : (rank + 1) * rows]

        def produce(g):
            @pl.loop(0, model // 256)
            def _(n):
                at = pl.ds(pl.multiple_of(n * 256, 256), 256)
                part[g, :, at] = dot(sq[g], down[:, at]).astype(BF)

        def finish(g):
            ffn = acc[...]
            result[g] = (res[g] + p[g, :, :1] * ffn).astype(BF)
            probs_grad[g] = jnp.broadcast_to(
                jnp.sum(dy[g].astype(F32) * ffn, axis=1, keepdims=True), (rows, HDIM)
            )

        def fetches(turn):
            at = pl.multiple_of(to_up.target(lax.rem(turn + 1, sequences)) * share, share)
            return [
                pltpu.make_async_copy(source.at[:, :, pl.ds(at, share)], held, fetch_sem.at[n])
                for n, (source, held) in enumerate(((ln, ln_v), (bg, bg_v)))
            ]

        def weights(turn):
            n = lax.rem(turn + 1, sequences)
            for fetch in fetches(turn):
                fetch.wait()
            side = min(256, columns)

            @pl.loop(0, columns // side)
            def _(m):
                at = pl.ds(pl.multiple_of(m * side, side), side)
                out_down[n, at] = dot(
                    sq[:, :, at].reshape(groups * tokens, side), bg_v[...].reshape(groups * tokens, share), TN
                ).astype(BF)

            @pl.loop(0, share // 256)
            def _(m):
                at = pl.ds(pl.multiple_of(m * 256, 256), 256)
                out_up[n, at] = dot(
                    ln_v[:, :, at].reshape(groups * tokens, 256), hg[...].reshape(groups * tokens, columns), TN
                ).astype(BF)

            to_down.begin(n)
            to_up.begin(n)

            @pl.when(turn + 1 < sequences)
            def _():
                for fetch in fetches(turn + 1):
                    fetch.start()

        for fetch in fetches(0):
            fetch.start()
        line.barrier(sequences)
        stream(line, groups, gather, arrived, reduce, [produce], finish, extra=(sequences, weights))

        @pl.loop(0, groups)
        def _(g):
            keep(g).wait()

        to_down.end()
        to_up.end()

    return call(
        body,
        [own_grad, squared, hidden_grad, kept_ln, branch_grad, w_down, w_out, active, resid, cotangent, probs],
        [
            jax.ShapeDtypeStruct((groups, rows, model), BF),
            jax.ShapeDtypeStruct((groups, rows, HDIM), F32),
            jax.ShapeDtypeStruct((groups, tokens, model), BF),
            jax.ShapeDtypeStruct((ranks, groups, rows, width), BF),
            jax.ShapeDtypeStruct((sequences, columns, share), BF),
            jax.ShapeDtypeStruct((sequences, share, columns), BF),
        ],
        [
            pltpu.VMEM((groups, tokens, model), BF),
            *Gather.scratch(ranks, groups),
            *Reduce.scratch(ranks, groups, rows, model),
            DMA((groups,)),
            *Spread.scratch(sequences, (columns, share)),
            *Spread.scratch(sequences, (share, columns)),
            pltpu.VMEM((groups, tokens, share), BF),
            pltpu.VMEM((groups, tokens, share), BF),
            DMA((2,)),
        ],
        3,
        in_specs=[VM, VM, VM, ANY, ANY, VM, VM, VM, VM, VM, VM],
        out_specs=[VM, VM, ANY, VM, ANY, ANY],
        flops=2 * groups * tokens * model * (3 * columns + width),
        moved=100 << 20,
    )


def project_back(
    grads, w_qkv, kept_x, attended, attn_grad, tokens, gain, grad_resid, gains, ranks, sequences
):
    groups, tokens_all, width = grads[0].shape
    rows = tokens_all // ranks
    model = w_qkv.shape[1]
    share = model // sequences

    def body(
        g_q, g_k, g_v, w, xs, a, ga, x_ref, gain_ref, g_res, gain_parts, tokens_grad, totals, land_qkv, land_out,
        part, near, far, acc, s1, s2, s3,
        out_qkv, qkv_send, qkv_recv, out_out, out_send, out_recv, x_v, ga_v, fetch_sem,
        mine, terms, t_send, t_recv, sums, d_send, d_recv,
    ):
        line = Line(ranks, rows)
        reduce = Reduce(line, part, near, far, acc, s1, s2, s3)
        to_qkv = Spread(sequences, out_qkv, land_qkv, qkv_send, qkv_recv)
        to_out = Spread(sequences, out_out, land_out, out_send, out_recv)
        parts = (g_q, g_k, g_v)

        def produce(g):
            for n in range(0, model, 256):
                out = dot(g_q[g], w[0, n : n + 256], NT)
                out += dot(g_k[g], w[1, n : n + 256], NT)
                out += dot(g_v[g], w[2, n : n + 256], NT)
                part[g, :, n : n + 256] = out.astype(BF)

        mine[0:1] = jnp.zeros((1, model), F32)
        mine[1:3] = gain_parts[...]

        def finish(g):
            x = x_ref[g].astype(F32)
            scale = lax.rsqrt(row_mean(x * x) + EPSILON)
            hat = x * scale
            back = acc[...]
            mine[0:1] += jnp.sum(back * hat, axis=0, keepdims=True)
            back = back * gain_ref[...]
            tokens_grad[g] = g_res[g] + scale * (back - hat * row_mean(back * hat))

        def fetches(turn):
            at = pl.multiple_of(to_qkv.target(lax.rem(turn + 1, sequences)) * share, share)
            return [
                pltpu.make_async_copy(source.at[:, :, pl.ds(at, share)], held, fetch_sem.at[n])
                for n, (source, held) in enumerate(((xs, x_v), (ga, ga_v)))
            ]

        def weights(turn):
            n = lax.rem(turn + 1, sequences)
            for fetch in fetches(turn):
                fetch.wait()

            @pl.loop(0, share // 256)
            def _(m):
                at = pl.ds(pl.multiple_of(m * 256, 256), 256)
                x = x_v[:, :, at].reshape(groups * tokens_all, 256)
                for which in range(3):
                    out_qkv[n, which, at] = dot(
                        x, parts[which][...].reshape(groups * tokens_all, width), TN
                    ).astype(BF)

            out_out[n] = dot(
                a[...].reshape(groups * tokens_all, width), ga_v[...].reshape(groups * tokens_all, share), TN
            ).astype(BF)
            to_qkv.begin(n)
            to_out.begin(n)

            @pl.when(turn + 1 < sequences)
            def _():
                for fetch in fetches(turn + 1):
                    fetch.start()

        def to_rank(n, source=None):
            return copy_to(
                mine,
                terms.at[line.t if source is None else source],
                t_send.at[n],
                t_recv.at[n],
                lax.rem(line.t + n, ranks),
            )

        for fetch in fetches(0):
            fetch.start()
        line.barrier_all(sequences)
        stream(line, groups, None, None, reduce, [produce], finish, extra=(sequences, weights))

        @pl.loop(1, ranks)
        def _(n):
            to_rank(n).start()

        total = mine[...]
        terms[line.t] = total

        @pl.loop(1, ranks)
        def _(n):
            to_rank(n).wait_send()
            to_rank(n, lax.rem(line.t + ranks - n, ranks)).wait_recv()

        total = terms[0]
        for n in range(1, ranks):
            total += terms[n]
        me = lax.axis_index("dp")

        def to_sequence(n, source=None):
            return pltpu.make_async_remote_copy(
                src_ref=sums.at[me],
                dst_ref=sums.at[me if source is None else source],
                send_sem=d_send.at[n],
                recv_sem=d_recv.at[n],
                device_id={"dp": lax.rem(me + n, sequences)},
                device_id_type=MESH,
            )

        sums[me] = total

        @pl.loop(1, sequences)
        def _(n):
            to_sequence(n).start()

        to_qkv.end()
        to_out.end()

        @pl.loop(1, sequences)
        def _(n):
            to_sequence(n).wait_send()
            to_sequence(n, lax.rem(me + sequences - n, sequences)).wait_recv()

        total = sums[0]
        for n in range(1, sequences):
            total += sums[n]
        totals[...] = total

    return call(
        body,
        [*grads, w_qkv, kept_x, attended, attn_grad, tokens, gain, grad_resid, gains],
        [
            jax.ShapeDtypeStruct((groups, rows, model), F32),
            jax.ShapeDtypeStruct((3, model), F32),
            jax.ShapeDtypeStruct((sequences, 3, share, width), BF),
            jax.ShapeDtypeStruct((sequences, width, share), BF),
        ],
        [
            *Reduce.scratch(ranks, groups, rows, model),
            *Spread.scratch(sequences, (3, share, width)),
            *Spread.scratch(sequences, (width, share)),
            pltpu.VMEM((groups, tokens_all, share), BF),
            pltpu.VMEM((groups, tokens_all, share), BF),
            DMA((2,)),
            pltpu.VMEM((3, model), F32),
            pltpu.VMEM((ranks, 3, model), F32),
            DMA((ranks,)),
            DMA((ranks,)),
            pltpu.VMEM((sequences, 3, model), F32),
            DMA((sequences,)),
            DMA((sequences,)),
        ],
        4,
        in_specs=[VM, VM, VM, VM, ANY, VM, ANY, VM, VM, VM, VM],
        out_specs=[VM, VM, ANY, ANY],
        flops=12 * groups * tokens_all * model * width,
        moved=60 << 20,
    )


def shards(
    tokens,
    cotangent,
    first_norm_gain,
    w_qkv,
    w_out,
    g_ln,
    b_ln,
    w_up,
    w_down,
    probs,
    lengths,
    head_count,
    widths,
):
    length_all = widths.shape[0]
    own_tokens, model = tokens.shape
    ranks = length_all // own_tokens
    sequences = lax.axis_size("dp")
    groups, rows = GROUPS, own_tokens // GROUPS
    width = w_out.shape[0]
    heads_here = width // HDIM
    half = HDIM // 2
    frequency = 10000.0 ** (-jnp.arange(half, dtype=F32) / half)
    frequency = jnp.concatenate([frequency, frequency]).reshape(1, HDIM)
    w_qkv_t = w_qkv.transpose(1, 0, 2)
    x = tokens.reshape(groups, rows, model)
    dy = cotangent.reshape(groups, rows, model)
    first_norm_gain, g_ln, b_ln = (v.reshape(1, model) for v in (first_norm_gain, g_ln, b_ln))
    p = jnp.broadcast_to(probs.reshape(groups, rows, 1), (groups, rows, HDIM))
    head_ids = lax.axis_index("tensor") * heads_here + jnp.arange(heads_here, dtype=jnp.int32)
    active = (head_ids < head_count[0]).astype(jnp.int32)
    live = jnp.repeat(active.astype(F32), HDIM).reshape(1, width)
    wide = widths.reshape(ranks, groups, rows).swapaxes(0, 1).reshape(groups, ranks * rows)

    qkv, kept_x, cosines, sines = gather_project(
        x, first_norm_gain, lengths, frequency, w_qkv_t, ranks, width
    )
    qkv = qkv.reshape(length_all, 3 * width)
    cosines, sines = cosines.reshape(length_all, HDIM), sines.reshape(length_all, HDIM)
    attended = attend(qkv, lengths, active, width, groups, own_tokens)
    resid, normed_ln, kept_ffn_grad = project_reduce(
        attended, w_out, x, dy, p, g_ln, b_ln, ranks
    )
    grad_resid, grad_low, gains, kept_ln, squared, grad_hidden = feed(
        normed_ln, kept_ffn_grad, w_up, w_down, wide, resid, dy, g_ln, ranks
    )
    result, probs_grad, kept_attn_grad, grad_attended, land_down, land_up = feed_out(
        grad_low, squared, grad_hidden, kept_ln, kept_ffn_grad, w_down, w_out, live, resid, dy, p, ranks, sequences
    )
    grad_proj = attend_back(
        qkv,
        grad_attended.reshape(length_all, width),
        lengths,
        active,
        cosines,
        sines,
        width,
        groups,
        own_tokens,
    )
    tokens_grad, totals, land_qkv, land_out = project_back(
        grad_proj, w_qkv_t, kept_x, attended, kept_attn_grad, x, first_norm_gain, grad_resid, gains, ranks, sequences
    )
    add_up = lambda landed: jnp.sum(landed.astype(F32), axis=0)
    return (
        result.reshape(own_tokens, model),
        tokens_grad.reshape(own_tokens, model),
        probs_grad[:, :, 0].reshape(own_tokens),
        totals[0],
        add_up(land_qkv).transpose(1, 0, 2),
        add_up(land_out),
        totals[1],
        totals[2],
        add_up(land_up),
        add_up(land_down),
    )


def solution(mesh):
    placed = (
        P(("dp", "tensor"), None),
        P(("dp", "tensor"), None),
        P(),
        P(None, None, "tensor"),
        P("tensor", None),
        P(),
        P(),
        P(None, "tensor"),
        P("tensor", None),
        P(("dp", "tensor")),
        P("dp", None),
        P("dp"),
        P("dp"),
    )
    return jax.shard_map(
        shards,
        mesh=mesh,
        in_specs=placed,
        out_specs=(
            P(("dp", "tensor"), None),
            P(("dp", "tensor"), None),
            P(("dp", "tensor")),
            P(),
            P("dp", None, "tensor"),
            P("tensor", "dp"),
            P(),
            P(),
            P("dp", "tensor"),
            P("tensor", "dp"),
        ),
        check_vma=False,
    )
```

```python
import functools

import jax
import jax.numpy as jnp
from jax import lax
from jax.experimental import pallas as pl
from jax.experimental.pallas import tpu as pltpu
from jax.sharding import PartitionSpec as P

HDIM = 128
FF = 8192
EPSILON = 1e-05
NEGATIVE = -1e30
MAXDOC = 1024
GROUPS = 8
QROWS = 256
MESH = pl.DeviceIdType.MESH
BF = jnp.bfloat16
F32 = jnp.float32
ANY = pl.BlockSpec(memory_space=pl.ANY)
VM = pl.BlockSpec(memory_space=pltpu.VMEM)
DMA = pltpu.SemaphoreType.DMA
NT = (((1,), (1,)), ((), ()))
TN = (((0,), (0,)), ((), ()))


def dot(a, b, dims=(((1,), (0,)), ((), ()))):
    return lax.dot_general(a, b, dims, preferred_element_type=F32)


class Line:
    def __init__(self, ranks, rows):
        self.ranks, self.chips, self.rows = ranks, ranks // 2, rows
        self.t = lax.axis_index("tensor")
        self.z, self.c = self.t // 2, lax.rem(self.t, 2)
        self.has_up, self.has_down = self.z < self.chips - 1, self.z > 0
        self.up = jnp.minimum(self.t + 2, ranks - 1)
        self.down = jnp.maximum(self.t - 2, 0)
        self.partner = self.t + 1 - 2 * self.c

    def barrier(self, dp_size=0):
        sem = pltpu.get_barrier_semaphore()
        pl.semaphore_signal(sem, inc=1, device_id={"tensor": self.partner}, device_id_type=MESH)

        @pl.when(self.has_up)
        def _():
            pl.semaphore_signal(sem, inc=1, device_id={"tensor": self.up}, device_id_type=MESH)

        @pl.when(self.has_down)
        def _():
            pl.semaphore_signal(sem, inc=1, device_id={"tensor": self.down}, device_id_type=MESH)

        d = lax.axis_index("dp")
        for step in range(1, dp_size):
            pl.semaphore_signal(
                sem, inc=1, device_id={"dp": lax.rem(d + step, dp_size)}, device_id_type=MESH
            )
        links = self.has_up.astype(jnp.int32) + self.has_down.astype(jnp.int32)
        pl.semaphore_wait(sem, 1 + max(dp_size - 1, 0) + links)

    def barrier_all(self, dp_size):
        sem = pltpu.get_barrier_semaphore()
        for n in range(1, self.ranks):
            pl.semaphore_signal(
                sem, inc=1, device_id={"tensor": lax.rem(self.t + n, self.ranks)}, device_id_type=MESH
            )
        d = lax.axis_index("dp")
        for n in range(1, dp_size):
            pl.semaphore_signal(
                sem, inc=1, device_id={"dp": lax.rem(d + n, dp_size)}, device_id_type=MESH
            )
        pl.semaphore_wait(sem, self.ranks - 1 + dp_size - 1)

    def block(self, rank):
        return pl.ds(pl.multiple_of(rank * self.rows, self.rows), self.rows)


def copy_to(src, dst, send, recv, rank):
    return pltpu.make_async_remote_copy(
        src_ref=src,
        dst_ref=dst,
        send_sem=send,
        recv_sem=recv,
        device_id={"tensor": rank},
        device_id_type=MESH,
    )


class Gather:
    def __init__(self, line, own, full, send, recv, local):
        self.l, self.own, self.full = line, own, full
        self.send, self.recv, self.local = send, recv, local

    @staticmethod
    def scratch(ranks, groups):
        return [DMA((3, groups, ranks // 2)), DMA((groups, ranks)), DMA((groups,))]

    def copy(self, g, rank, way, own=False):
        l = self.l
        place = self.full.at[g, l.block(rank)]
        return copy_to(
            self.own.at[g] if own else place,
            place,
            self.send.at[way, g, rank // 2],
            self.recv.at[g, rank],
            (l.up, l.down, l.partner)[way],
        )

    def pass_on(self, g, rank, up, down, own=False):
        l = self.l
        if up:

            @pl.when(l.has_up)
            def _():
                self.copy(g, rank, 0, own).start()

        if down:

            @pl.when(l.has_down)
            def _():
                self.copy(g, rank, 1, own).start()

        self.copy(g, rank, 2, own).start()

    def begin(self, g):
        l = self.l
        self.pass_on(g, l.t, True, True, own=True)
        pltpu.make_async_copy(self.own.at[g], self.full.at[g, l.block(l.t)], self.local.at[g]).start()

    def hop(self, g, h):
        l = self.l

        @pl.when(l.z - h >= 0)
        def _():
            self.copy(g, l.t - 2 * h, 0).wait_recv()
            self.pass_on(g, l.t - 2 * h, True, False)

        @pl.when(l.z + h <= l.chips - 1)
        def _():
            self.copy(g, l.t + 2 * h, 1).wait_recv()
            self.pass_on(g, l.t + 2 * h, False, True)

    def arrived(self, g):
        l = self.l
        pltpu.make_async_copy(self.own.at[g], self.full.at[g, l.block(l.t)], self.local.at[g]).wait()
        for z in range(l.chips):
            self.copy(g, 2 * z + 1 - l.c, 2).wait_recv()

    def drain(self, g):
        l = self.l
        for z in range(l.chips):

            @pl.when(l.has_up & (l.z >= z))
            def _():
                self.copy(g, 2 * z + l.c, 0).wait_send()

            @pl.when(l.has_down & (l.z <= z))
            def _():
                self.copy(g, 2 * z + l.c, 1).wait_send()

            self.copy(g, 2 * z + l.c, 2).wait_send()


class Reduce:
    def __init__(self, line, part, near, far, acc, send, near_recv, far_recv):
        self.l, self.part, self.near, self.far, self.acc = line, part, near, far, acc
        self.send, self.near_recv, self.far_recv = send, near_recv, far_recv

    @staticmethod
    def scratch(ranks, groups, rows, width):
        chips = ranks // 2
        return [
            pltpu.VMEM((groups, ranks * rows, width), BF),
            pltpu.VMEM((groups, chips, rows, width), BF),
            pltpu.VMEM((groups, chips + 1, rows, width), BF),
            pltpu.VMEM((rows, width), F32),
            DMA((2, groups, chips)),
            DMA((groups, chips)),
            DMA((groups, chips + 1)),
        ]

    def to_partner(self, g, z):
        l = self.l
        return copy_to(
            self.part.at[g, l.block(2 * z + 1 - l.c)],
            self.near.at[g, z],
            self.send.at[0, g, z],
            self.near_recv.at[g, z],
            l.partner,
        )

    def along(self, g, z, up, receive=False):
        l = self.l
        at = l.z if receive else jnp.where(up, l.z + 1, l.z - 1)
        slot = z if up else jnp.where(z == at, l.chips, z)
        return copy_to(
            self.part.at[g, l.block(2 * z + l.c)],
            self.far.at[g, slot],
            self.send.at[1, g, z],
            self.far_recv.at[g, slot],
            l.up if up else l.down,
        ), slot

    def begin(self, g):
        for z in range(self.l.chips):
            self.to_partner(g, z).start()

    def summed(self, g, z, slots):
        total = self.part[g, self.l.block(2 * z + self.l.c)].astype(F32) + self.near[g, z].astype(F32)
        for slot in slots:
            total += self.far[g, slot].astype(F32)
        return total

    def step(self, g, d):
        l = self.l

        def send(z, up):
            self.to_partner(g, z).wait_recv()
            further = l.has_down if up else l.has_up

            @pl.when(further)
            def _():
                copy, slot = self.along(g, z, up, receive=True)
                copy.wait_recv()
                self.part[g, l.block(2 * z + l.c)] = self.summed(g, z, [slot]).astype(BF)

            @pl.when(jnp.logical_not(further))
            def _():
                self.part[g, l.block(2 * z + l.c)] = self.summed(g, z, []).astype(BF)

            self.along(g, z, up)[0].start()

        @pl.when(l.z + d <= l.chips - 1)
        def _():
            send(l.z + d, True)

        @pl.when(l.z - d >= 0)
        def _():
            send(l.z - d, False)

    def last(self, g):
        l = self.l
        self.to_partner(g, l.z).wait_recv()

        @pl.when(l.has_down & l.has_up)
        def _():
            self.along(g, l.z, True, receive=True)[0].wait_recv()
            self.along(g, l.z, False, receive=True)[0].wait_recv()
            self.acc[...] = self.summed(g, l.z, [l.z, l.chips])

        @pl.when(jnp.logical_not(l.has_up))
        def _():
            self.along(g, l.z, True, receive=True)[0].wait_recv()
            self.acc[...] = self.summed(g, l.z, [l.z])

        @pl.when(jnp.logical_not(l.has_down))
        def _():
            self.along(g, l.z, False, receive=True)[0].wait_recv()
            self.acc[...] = self.summed(g, l.z, [l.chips])

    def drain(self, g):
        l = self.l
        for z in range(l.chips):
            self.to_partner(g, z).wait_send()

            @pl.when(l.z != z)
            def _():
                copy_to(
                    self.part.at[g, l.block(2 * z + l.c)],
                    self.far.at[g, z],
                    self.send.at[1, g, z],
                    self.far_recv.at[g, z],
                    l.partner,
                ).wait_send()


def within(value, limit, body):
    pl.when((value >= 0) & (value < limit))(lambda: body(value))


def swap_halves(field):
    return pltpu.roll(field, HDIM // 2, axis=1)


def call(body, ins, outs, scratch, ident, in_specs=None, out_specs=None, limit=60, flops=0, moved=0, aliases=None):
    return pl.pallas_call(
        body,
        out_shape=outs,
        in_specs=in_specs or [VM] * len(ins),
        out_specs=out_specs or [VM] * len(outs),
        scratch_shapes=scratch,
        compiler_params=pltpu.CompilerParams(
            collective_id=ident, has_side_effects=True, vmem_limit_bytes=limit << 20
        ),
        input_output_aliases=aliases or {},
        cost_estimate=pl.CostEstimate(flops=flops, bytes_accessed=moved, transcendentals=0),
    )(*ins)


def stream(line, groups, gather=None, arrived=None, reduce=None, produce=(), finish=None, lead=0, extra=None):
    hops = line.chips - 1
    produce = list(produce)
    turns = groups + hops + (lead if reduce else 0)

    @pl.loop(0, turns)
    def _(i):
        if reduce:

            def end(g):
                reduce.last(g)
                finish(g)

            within(i - lead - hops, groups, end)
        for n in range(hops):
            if gather:
                within(i - hops + n, groups, functools.partial(gather.hop, h=hops - n))
                if n == 0 and arrived:
                    within(i - hops, groups, arrived)
            if reduce and n:
                within(i - lead - hops + n, groups, functools.partial(reduce.step, d=n))
            if gather and n == hops - 1:
                within(i, groups, gather.begin)
            for piece in produce[n * len(produce) // hops : (n + 1) * len(produce) // hops]:
                within(i - lead, groups, piece)
        if reduce:
            within(i - lead, groups, reduce.begin)
            within(i - lead, groups, functools.partial(reduce.step, d=hops))
        if extra:
            within(i, min(extra[0], turns), extra[1])

    if extra:

        @pl.loop(min(extra[0], turns), extra[0])
        def _(i):
            extra[1](i)

    @pl.loop(0, groups)
    def _(g):
        if gather:
            gather.drain(g)
        if reduce:
            reduce.drain(g)


def starts_of(lengths, places):
    end, start = jnp.int32(0), jnp.zeros_like(places)
    for length in lengths:
        end = end + length
        start = start + jnp.where(places >= end, length, 0)
    return start


def softmax_block(q, k, start, first_query, first_key, scaling):
    raw = dot(k, q, NT)
    keys = first_key + lax.broadcasted_iota(jnp.int32, raw.shape, 0)
    queries = first_query + lax.broadcasted_iota(jnp.int32, raw.shape, 1)
    raw = jnp.where((keys <= queries) & (keys >= start), raw * scaling, NEGATIVE)
    exponent = jnp.exp(raw - jnp.max(raw, axis=0, keepdims=True))
    return exponent * (1.0 / jnp.sum(exponent, axis=0, keepdims=True))


def query_starts(lengths, first):
    places = first + lax.broadcasted_iota(jnp.int32, (8, QROWS), 1)
    return starts_of([lengths[0, n] for n in range(lengths.shape[1])], places)[:1]


def attend(qkv, lengths, active, width, groups, own_tokens):
    length, heads = qkv.shape[0], width // HDIM
    scaling = HDIM ** (-0.5)
    reach = MAXDOC // QROWS + 1
    rows_own = own_tokens // groups

    def body(live, docs, q, k, v, out, v_t):
        h = pl.program_id(0)

        @pl.when(live[h] == 0)
        def _():
            out[...] = jnp.zeros_like(out)

        @pl.when(live[h] != 0)
        def _():
            v_t[...] = v[...].T
            for i in range(length // QROWS):
                low, high = max(0, i + 1 - reach) * QROWS, (i + 1) * QROWS
                rows = slice(i * QROWS, high)
                start = query_starts(docs, i * QROWS)
                weights = softmax_block(q[rows], k[low:high], start, i * QROWS, low, scaling)
                done = dot(v_t[:, low:high], weights.astype(BF)).T.astype(BF)
                put_grouped(out, done, i * QROWS, own_tokens, rows_own)

    return pl.pallas_call(
        body,
        out_shape=jax.ShapeDtypeStruct((groups, length // groups, width), BF),
        grid_spec=pltpu.PrefetchScalarGridSpec(
            num_scalar_prefetch=2,
            grid=(heads,),
            in_specs=[
                pl.BlockSpec((length, HDIM), lambda h, live, docs: (0, h)),
                pl.BlockSpec((length, HDIM), lambda h, live, docs: (0, heads + h)),
                pl.BlockSpec((length, HDIM), lambda h, live, docs: (0, 2 * heads + h)),
            ],
            out_specs=pl.BlockSpec(
                (groups, length // groups, HDIM), lambda h, live, docs: (0, 0, h)
            ),
            scratch_shapes=[pltpu.VMEM((HDIM, length), BF)],
        ),
        compiler_params=pltpu.CompilerParams(vmem_limit_bytes=32 << 20),
        cost_estimate=pl.CostEstimate(flops=4 << 30, bytes_accessed=4 << 20, transcendentals=0),
    )(active, lengths, qkv, qkv, qkv)


def put_grouped(out, block, first, own_tokens, rows):
    for at in range(0, block.shape[0], rows):
        rank, inside = divmod(first + at, own_tokens)
        out[inside // rows, rank * rows : (rank + 1) * rows] = block[at : at + rows]


def attend_back(qkv, grad, lengths, active, cosines, sines, width, groups, own_tokens):
    length, heads = qkv.shape[0], width // HDIM
    scaling = HDIM ** (-0.5)
    reach = MAXDOC // QROWS + 1
    rows_own = own_tokens // groups

    def body(live, docs, q, k, v, g, cos, sin, g_q, g_k, g_v, k_t, sum_k, sum_v):
        h = pl.program_id(0)

        @pl.when(live[h] == 0)
        def _():
            g_q[...] = jnp.zeros_like(g_q)
            g_k[...] = jnp.zeros_like(g_k)
            g_v[...] = jnp.zeros_like(g_v)

        def rotate_back(d, rows):
            return (d * cos[rows] + swap_halves(d * sin[rows])).astype(BF)

        @pl.when(live[h] != 0)
        def _():
            k_t[...] = k[...].T
            sum_k[...] = jnp.zeros_like(sum_k)
            sum_v[...] = jnp.zeros_like(sum_v)
            for i in range(length // QROWS):
                low, high = max(0, i + 1 - reach) * QROWS, (i + 1) * QROWS
                rows, keys = slice(i * QROWS, high), slice(low, high)
                start = query_starts(docs, i * QROWS)
                weights = softmax_block(q[rows], k[keys], start, i * QROWS, low, scaling)
                sum_v[keys] += dot(weights.astype(BF), g[rows])
                g_weights = dot(v[keys], g[rows], NT)
                inner = jnp.sum(weights * g_weights, axis=0, keepdims=True)
                g_scores = (weights * (g_weights - inner)).astype(BF)
                sum_k[keys] += dot(g_scores, q[rows])
                back = rotate_back(dot(k_t[:, keys], g_scores).T * scaling, rows)
                put_grouped(g_q, back, i * QROWS, own_tokens, rows_own)
            for i in range(length // QROWS):
                rows = slice(i * QROWS, (i + 1) * QROWS)
                put_grouped(g_k, rotate_back(sum_k[rows] * scaling, rows), i * QROWS, own_tokens, rows_own)
                put_grouped(g_v, sum_v[rows].astype(BF), i * QROWS, own_tokens, rows_own)

    column = lambda n: pl.BlockSpec((length, HDIM), lambda h, live, docs: (0, n * heads + h))
    table = pl.BlockSpec((length, HDIM), lambda h, live, docs: (0, 0))
    return pl.pallas_call(
        body,
        out_shape=[jax.ShapeDtypeStruct((groups, length // groups, width), BF)] * 3,
        grid_spec=pltpu.PrefetchScalarGridSpec(
            num_scalar_prefetch=2,
            grid=(heads,),
            in_specs=[column(0), column(1), column(2), column(0), table, table],
            out_specs=[
                pl.BlockSpec((groups, length // groups, HDIM), lambda h, live, docs: (0, 0, h))
            ]
            * 3,
            scratch_shapes=[
                pltpu.VMEM((HDIM, length), BF),
                pltpu.VMEM((length, HDIM), F32),
                pltpu.VMEM((length, HDIM), F32),
            ],
        ),
        compiler_params=pltpu.CompilerParams(vmem_limit_bytes=48 << 20),
        cost_estimate=pl.CostEstimate(flops=10 << 30, bytes_accessed=8 << 20, transcendentals=0),
    )(active, lengths, qkv, qkv, qkv, grad, cosines, sines)


class Spread:
    def __init__(self, size, out, land, send, recv, rows=None):
        self.size, self.out, self.land, self.send, self.recv = size, out, land, send, recv
        self.rows = rows
        self.me = lax.axis_index("dp")

    def target(self, n):
        return lax.rem(self.me + n, self.size)

    def copy(self, n, source=None):
        return pltpu.make_async_remote_copy(
            src_ref=self.out.at[n],
            dst_ref=self.place(self.me if source is None else source),
            send_sem=self.send.at[n],
            recv_sem=self.recv.at[n],
            device_id={"dp": self.target(n)},
            device_id_type=MESH,
        )

    def place(self, source):
        return self.land.at[source] if self.rows is None else self.land.at[source, self.rows]

    def own(self):
        return pltpu.make_async_copy(self.out.at[0], self.place(self.me), self.send.at[0])

    def begin(self, n):
        @pl.when(n == 0)
        def _():
            self.own().start()

        @pl.when(n != 0)
        def _():
            self.copy(n).start()

    def end(self):
        self.own().wait()

        @pl.loop(1, self.size)
        def _(n):
            self.copy(n).wait_send()
            self.copy(n, lax.rem(self.me + self.size - n, self.size)).wait_recv()

    @staticmethod
    def scratch(size, shape):
        return [pltpu.VMEM((size, *shape), BF), DMA((size,)), DMA((size,))]


class Loads:
    def __init__(self, pairs, sems):
        self.copies = [
            pltpu.make_async_copy(source, held, sems.at[n]) for n, (source, held) in enumerate(pairs)
        ]
        for copy in self.copies:
            copy.start()

    def need(self, first, *which):
        @pl.when(first)
        def _():
            for n in which:
                self.copies[n].wait()


class Store:
    def __init__(self, held, out, sems, at=lambda ref, g: ref.at[g]):
        self.held, self.out, self.sems, self.at = held, out, sems, at

    def copy(self, g):
        return pltpu.make_async_copy(self.at(self.held, g), self.at(self.out, g), self.sems.at[g])

    def put(self, g):
        self.copy(g).start()

    def end(self, g):
        self.copy(g).wait()


def scratch_of(*arrays):
    return [pltpu.VMEM(a.shape, a.dtype) for a in arrays]


def row_mean(field):
    return jnp.mean(field, axis=1, keepdims=True)


def layer_norm(resid):
    centred = resid - row_mean(resid)
    inv_std = lax.rsqrt(row_mean(centred * centred) + EPSILON)
    return centred * inv_std, inv_std


def gather_project(tokens, gain, lengths, frequency, w_qkv, ranks, width):
    groups, rows, model = tokens.shape
    heads = width // HDIM
    shift = rows.bit_length() - 1

    def body(
        x_ref, gain_ref, docs, freq, w, qkv, kept, cos_out, sin_out,
        own, full, w_v, qkv_v, cos_v, sin_v, g_send, g_recv, g_local, w_sem, kept_sem, out_sem,
    ):
        line = Line(ranks, rows)
        loads = Loads([(w, w_v)], w_sem)

        @pl.loop(0, groups)
        def _(g):
            x = x_ref[g].astype(F32)
            own[g] = (x * lax.rsqrt(row_mean(x * x) + EPSILON) * gain_ref[...]).astype(BF)

        line.barrier()
        gather = Gather(line, own, full, g_send, g_recv, g_local)
        stores = [Store(full, kept, kept_sem)] + [
            Store(held, out, out_sem.at[n], lambda ref, g: ref.at[:, g])
            for n, (held, out) in enumerate(((qkv_v, qkv), (cos_v, cos_out), (sin_v, sin_out)))
        ]

        def project(g):
            r = lax.broadcasted_iota(jnp.int32, (ranks * rows, HDIM), 0)
            lane = lax.broadcasted_iota(jnp.int32, (ranks * rows, HDIM), 1)
            places = lax.shift_right_logical(r, shift) * (groups * rows) + g * rows + (r & (rows - 1))
            starts = starts_of([docs[0, n] for n in range(docs.shape[1])], places)
            angles = (places - starts).astype(F32) * freq[...]
            c = jnp.cos(angles)
            s = jnp.sin(angles)
            s = jnp.where(lane < HDIM // 2, -s, s)
            for rank in range(ranks):
                cos_v[rank, g] = c[rank * rows : (rank + 1) * rows]
                sin_v[rank, g] = s[rank * rows : (rank + 1) * rows]
            gather.arrived(g)
            loads.need(g == 0, 0)
            x = full[g]
            for which in range(3):
                p = dot(x, w_v[which])
                for h in range(heads):
                    u = p[:, h * HDIM : (h + 1) * HDIM]
                    if which < 2:
                        u = u * c + swap_halves(u) * s
                    u = u.astype(BF)
                    at = (which * heads + h) * HDIM
                    for rank in range(ranks):
                        qkv_v[rank, g, :, at : at + HDIM] = u[rank * rows : (rank + 1) * rows]
            for store in stores:
                store.put(g)

        stream(line, groups, gather, arrived=project)

        @pl.loop(0, groups)
        def _(g):
            for store in stores:
                store.end(g)

    table = jax.ShapeDtypeStruct((ranks, groups, rows, HDIM), F32)
    projected = jax.ShapeDtypeStruct((ranks, groups, rows, 3 * width), BF)
    return call(
        body,
        [tokens, gain, lengths, frequency, w_qkv],
        [projected, jax.ShapeDtypeStruct((groups, ranks * rows, model), BF), table, table],
        [
            pltpu.VMEM((groups, rows, model), BF),
            pltpu.VMEM((groups, ranks * rows, model), BF),
            *scratch_of(w_qkv, projected, table, table),
            *Gather.scratch(ranks, groups),
            DMA((1,)),
            DMA((groups,)),
            DMA((3, groups)),
        ],
        0,
        in_specs=[VM, VM, pl.BlockSpec(memory_space=pltpu.SMEM), VM, ANY],
        out_specs=[ANY, ANY, ANY, ANY],
        flops=2 * ranks * groups * rows * model * 3 * width,
        moved=60 << 20,
    )


def project_reduce(attended, w_out, tokens, cotangent, probs, g_ln, b_ln, ranks):
    groups, rows, model = cotangent.shape
    width = w_out.shape[0]

    def body(
        a, w, x, dy, p, gain, bias, resid, normed, kept,
        own, full, x_v, resid_v, normed_v, g_send, g_recv, g_local, part, near, far, acc, s1, s2, s3,
        x_sem, kept_sem, resid_sem, normed_sem,
    ):
        line = Line(ranks, rows)
        loads = Loads([(x, x_v)], x_sem)

        @pl.loop(0, groups)
        def _(g):
            own[g] = (dy[g].astype(F32) * p[g, :, :1]).astype(BF)

        line.barrier()
        gather = Gather(line, own, full, g_send, g_recv, g_local)
        reduce = Reduce(line, part, near, far, acc, s1, s2, s3)
        keep = Store(full, kept, kept_sem)
        stores = [Store(resid_v, resid, resid_sem), Store(normed_v, normed, normed_sem)]

        def arrived(g):
            gather.arrived(g)
            keep.put(g)

        def produce(g):
            for n in range(0, model, 512):
                part[g, :, n : n + 512] = dot(a[g], w[:, n : n + 512]).astype(BF)

        def finish(g):
            loads.need(g == 0, 0)
            total = x_v[g].astype(F32) + acc[...]
            resid_v[g] = total
            lhat, _ = layer_norm(total)
            normed_v[g] = (lhat * gain[...] + bias[...]).astype(BF)
            for store in stores:
                store.put(g)

        stream(line, groups, gather, arrived, reduce, [produce], finish)

        @pl.loop(0, groups)
        def _(g):
            for store in (keep, *stores):
                store.end(g)

    kept = jax.ShapeDtypeStruct((groups, ranks * rows, model), BF)
    resid = jax.ShapeDtypeStruct((groups, rows, model), F32)
    own = jax.ShapeDtypeStruct((groups, rows, model), BF)
    return call(
        body,
        [attended, w_out, tokens, cotangent, probs, g_ln, b_ln],
        [resid, own, kept],
        [
            *scratch_of(own, kept, tokens, resid, own),
            *Gather.scratch(ranks, groups),
            *Reduce.scratch(ranks, groups, rows, model),
            DMA((1,)),
            *[DMA((groups,))] * 3,
        ],
        1,
        in_specs=[VM, VM, ANY, VM, VM, VM, VM],
        out_specs=[ANY, ANY, ANY],
        flops=2 * ranks * groups * rows * model * width,
        moved=100 << 20,
    )


def feed(own_ln, branch_grad, w_up, w_down, widths, resid, cotangent, g_ln, ranks):
    groups, rows, model = own_ln.shape
    columns = w_up.shape[1]
    tile = min(256, columns)
    tokens = ranks * rows

    def body(
        own, grad, up, down, wide, res, dy, gain, grad_resid, grad_low, gains, kept, squared, hidden_grad,
        full, g_send, g_recv, g_local, part, near, far, acc, s1, s2, s3,
        up_v, down_v, res_v, dy_v, grad_v, lifted, squared_v, hidden_v, high_v, low_v, w_sem, grad_sem, out_sem,
    ):
        line = Line(ranks, rows)
        loads = Loads([(up, up_v), (down, down_v), (res, res_v), (dy, dy_v)], w_sem)
        gains[...] = jnp.zeros_like(gains)
        line.barrier()
        gather = Gather(line, own, full, g_send, g_recv, g_local)
        reduce = Reduce(line, part, near, far, acc, s1, s2, s3)
        first_column = line.t * columns
        keep, keep_squared, keep_hidden, keep_high, keep_low = (
            Store(held, out, out_sem.at[n])
            for n, (held, out) in enumerate(
                (
                    (full, kept),
                    (squared_v, squared),
                    (hidden_v, hidden_grad),
                    (high_v, grad_resid),
                    (low_v, grad_low),
                )
            )
        )

        def fetch(g):
            slot = lax.rem(g, 2)
            return pltpu.make_async_copy(grad.at[g], grad_v.at[slot], grad_sem.at[slot])

        fetch(0).start()

        def arrived(g):
            gather.arrived(g)
            keep.put(g)
            fetch(g).wait()

            @pl.when(g + 1 < groups)
            def _():
                fetch(g + 1).start()

            loads.need(g == 0, 0, 1)

        def forward(g):
            limit = (jnp.broadcast_to(wide[pl.ds(g, 1), :], (HDIM, tokens)).T[:, :1] + 1) * (FF // 4)

            @pl.loop(0, columns // tile)
            def _(n):
                at = pl.ds(pl.multiple_of(n * tile, tile), tile)
                hidden = dot(full[g], up_v[:, at])
                ids = first_column + n * tile + lax.broadcasted_iota(jnp.int32, hidden.shape, 1)
                live = jnp.where(ids < limit, jnp.maximum(hidden, 0.0), 0.0)
                lifted[:, at] = live
                squared_v[g, :, at] = (live * live).astype(BF)

            keep_squared.put(g)

        def backward(g):
            slot = lax.rem(g, 2)

            @pl.loop(0, columns // tile)
            def _(n):
                at = pl.ds(pl.multiple_of(n * tile, tile), tile)
                back = dot(grad_v[slot], down_v[at, :], NT)
                hidden_v[g, :, at] = (back * (2.0 * lifted[:, at])).astype(BF)

            keep_hidden.put(g)

        def lower(g):
            @pl.loop(0, model // 256)
            def _(n):
                at = pl.ds(pl.multiple_of(n * 256, 256), 256)
                part[g, :, at] = dot(hidden_v[g], up_v[at, :], NT).astype(BF)

        def finish(g):
            loads.need(g == 0, 2, 3)
            lhat, inv_std = layer_norm(res_v[g])
            back = acc[...]
            gains[0:1] += jnp.sum(back * lhat, axis=0, keepdims=True)
            gains[1:2] += jnp.sum(back, axis=0, keepdims=True)
            back = back * gain[...]
            back = dy_v[g].astype(F32) + inv_std * (back - row_mean(back) - lhat * row_mean(back * lhat))
            high_v[g] = back
            low_v[g] = back.astype(BF)
            keep_high.put(g)
            keep_low.put(g)

        stream(line, groups, gather, arrived, reduce, [forward, backward, lower], finish, line.chips - 1)

        @pl.loop(0, groups)
        def _(g):
            for store in (keep, keep_squared, keep_hidden, keep_high, keep_low):
                store.end(g)

    high = jax.ShapeDtypeStruct((groups, rows, model), F32)
    low = jax.ShapeDtypeStruct((groups, rows, model), BF)
    kept = jax.ShapeDtypeStruct((groups, tokens, model), BF)
    hidden = jax.ShapeDtypeStruct((groups, tokens, columns), BF)
    return call(
        body,
        [own_ln, branch_grad, w_up, w_down, widths, resid, cotangent, g_ln],
        [high, low, jax.ShapeDtypeStruct((2, model), F32), kept, hidden, hidden],
        [
            *scratch_of(kept),
            *Gather.scratch(ranks, groups),
            *Reduce.scratch(ranks, groups, rows, model),
            *scratch_of(w_up, w_down, resid, cotangent),
            pltpu.VMEM((2, tokens, model), BF),
            pltpu.VMEM((tokens, columns), F32),
            *scratch_of(hidden, hidden, high, low),
            DMA((4,)),
            DMA((2,)),
            DMA((5, groups)),
        ],
        2,
        in_specs=[VM, ANY, ANY, ANY, VM, ANY, ANY, VM],
        out_specs=[ANY, ANY, VM, ANY, ANY, ANY],
        flops=6 * groups * tokens * model * columns,
        moved=100 << 20,
    )


def hidden_weights(spread, inputs, hidden, first, turn_of, columns):
    n = turn_of
    side = min(256, spread.out.shape[1])

    @pl.loop(0, spread.out.shape[1] // side)
    def _(m):
        at = pl.ds(pl.multiple_of(first + m * side, side), side)
        to = pl.ds(pl.multiple_of(m * side, side), side)
        x = inputs[:, :, at]
        spread.out[n, to] = dot(
            x.reshape(x.shape[0] * x.shape[1], side), hidden[...].reshape(-1, columns), TN
        ).astype(BF)

    spread.begin(n)


def feed_out(
    own_grad, squared, hidden_grad, kept_ln, branch_grad, w_down, w_out, active, resid, cotangent, probs, ranks, sequences
):
    groups, rows, model = own_grad.shape
    columns, width = w_down.shape[0], w_out.shape[0]
    tokens = ranks * rows
    share = model // sequences
    half = share // 2

    def body(
        own, sq, hg, ln, bg, down, w, live, res, dy, p, result, probs_grad, kept, grad, land_down, land_up,
        full, g_send, g_recv, g_local, part, near, far, acc, s1, s2, s3, kept_sem,
        out_down, down_send, down_recv, out_up, up_send, up_recv, ln_v, bg_v, fetch_sem,
        sq_v, hg_v, down_v, res_v, dy_v, load_sem,
    ):
        line = Line(ranks, rows)
        gather = Gather(line, own, full, g_send, g_recv, g_local)
        reduce = Reduce(line, part, near, far, acc, s1, s2, s3)
        to_down = Spread(sequences, out_down, land_down, down_send, down_recv)
        to_up = Spread(sequences, out_up, land_up, up_send, up_recv, pl.ds(0, half))
        keep = Store(full, kept, kept_sem)

        def arrived(g):
            gather.arrived(g)
            keep.put(g)
            back = (dot(full[g], w[...], NT) * live[...]).astype(BF)
            for rank in range(ranks):
                grad[rank, g] = back[rank * rows : (rank + 1) * rows]

        def produce(g):
            loads.need(g == 0, 0, 1)

            @pl.loop(0, model // 256)
            def _(n):
                at = pl.ds(pl.multiple_of(n * 256, 256), 256)
                part[g, :, at] = dot(sq_v[g], down_v[:, at]).astype(BF)

        def finish(g):
            loads.need(g == 0, 3, 4)
            ffn = acc[...]
            result[g] = (res_v[g] + p[g, :, :1] * ffn).astype(BF)
            probs_grad[g] = jnp.broadcast_to(
                jnp.sum(dy_v[g].astype(F32) * ffn, axis=1, keepdims=True), (rows, HDIM)
            )

        def fetches(turn):
            at = pl.multiple_of(to_up.target(lax.rem(turn + 1, sequences)) * share, share)
            return [
                pltpu.make_async_copy(ln.at[:, :, pl.ds(at, half)], ln_v, fetch_sem.at[0]),
                pltpu.make_async_copy(bg.at[:, :, pl.ds(at, share)], bg_v, fetch_sem.at[1]),
            ]

        def weights(turn):
            n = lax.rem(turn + 1, sequences)
            loads.need(turn == 0, 2)
            for fetch in fetches(turn):
                fetch.wait()
            side = min(256, columns)

            @pl.loop(0, columns // side)
            def _(m):
                at = pl.ds(pl.multiple_of(m * side, side), side)
                out_down[n, at] = dot(
                    sq_v[:, :, at].reshape(groups * tokens, side), bg_v[...].reshape(groups * tokens, share), TN
                ).astype(BF)

            to_down.begin(n)
            hidden_weights(to_up, ln_v, hg_v, 0, n, columns)

            @pl.when(turn + 1 < sequences)
            def _():
                for fetch in fetches(turn + 1):
                    fetch.start()

        loads = Loads([(sq, sq_v), (down, down_v), (hg, hg_v), (res, res_v), (dy, dy_v)], load_sem)
        for fetch in fetches(0):
            fetch.start()
        line.barrier(sequences)
        stream(line, groups, gather, arrived, reduce, [produce], finish, extra=(sequences, weights))

        @pl.loop(0, groups)
        def _(g):
            keep.end(g)

        to_down.end()
        to_up.end()

    kept = jax.ShapeDtypeStruct((groups, tokens, model), BF)
    return call(
        body,
        [own_grad, squared, hidden_grad, kept_ln, branch_grad, w_down, w_out, active, resid, cotangent, probs],
        [
            jax.ShapeDtypeStruct((groups, rows, model), BF),
            jax.ShapeDtypeStruct((groups, rows, HDIM), F32),
            kept,
            jax.ShapeDtypeStruct((ranks, groups, rows, width), BF),
            jax.ShapeDtypeStruct((sequences, columns, share), BF),
            jax.ShapeDtypeStruct((sequences, share, columns), BF),
        ],
        [
            *scratch_of(kept),
            *Gather.scratch(ranks, groups),
            *Reduce.scratch(ranks, groups, rows, model),
            DMA((groups,)),
            *Spread.scratch(sequences, (columns, share)),
            *Spread.scratch(sequences, (half, columns)),
            pltpu.VMEM((groups, tokens, half), BF),
            pltpu.VMEM((groups, tokens, share), BF),
            DMA((2,)),
            *scratch_of(squared, hidden_grad, w_down, resid, cotangent),
            DMA((5,)),
        ],
        3,
        in_specs=[VM, ANY, ANY, ANY, ANY, ANY, VM, VM, ANY, ANY, VM],
        out_specs=[VM, VM, ANY, VM, ANY, ANY],
        flops=2 * groups * tokens * model * (3 * columns + width),
        moved=100 << 20,
    )


def project_back(
    grads, w_qkv, kept_x, attended, attn_grad, kept_ln, hidden_grad, landed_up, tokens, gain, grad_resid, gains, ranks, sequences
):
    groups, tokens_all, width = grads[0].shape
    rows = tokens_all // ranks
    model = w_qkv.shape[1]
    columns = hidden_grad.shape[2]
    share = model // sequences
    half = share // 2

    def body(
        g_q, g_k, g_v, w, xs, a, ga, ln, hg, up_in, x_ref, gain_ref, g_res, gain_parts,
        tokens_grad, totals, land_qkv, land_out, land_up,
        part, near, far, acc, s1, s2, s3,
        out_qkv, qkv_send, qkv_recv, out_out, out_send, out_recv, out_up, up_send, up_recv,
        x_v, ga_v, ln_v, fetch_sem, group_v, group_sem, w_v, a_v, hg_v, own_v, res_v, load_sem,
        mine, terms, t_send, t_recv, sums, d_send, d_recv,
    ):
        line = Line(ranks, rows)
        me = lax.axis_index("dp")
        reduce = Reduce(line, part, near, far, acc, s1, s2, s3)
        to_qkv = Spread(sequences, out_qkv, land_qkv, qkv_send, qkv_recv)
        to_out = Spread(sequences, out_out, land_out, out_send, out_recv)
        to_up = Spread(sequences, out_up, land_up, up_send, up_recv, pl.ds(half, half))
        parts = (g_q, g_k, g_v)
        loads = Loads([(w, w_v), (a, a_v), (hg, hg_v), (x_ref, own_v), (g_res, res_v)], load_sem)

        def group_fetch(g):
            slot = lax.rem(g, 2)
            return pltpu.make_async_copy(xs.at[g], group_v.at[slot], group_sem.at[slot])

        group_fetch(0).start()
        mine[0:1] = jnp.zeros((1, model), F32)
        mine[1:3] = gain_parts[...]

        def produce(g):
            loads.need(g == 0, 0)
            group_fetch(g).wait()

            @pl.when(g + 1 < groups)
            def _():
                group_fetch(g + 1).start()

            slot = lax.rem(g, 2)

            @pl.loop(0, model // 256)
            def _(n):
                at = pl.ds(pl.multiple_of(n * 256, 256), 256)
                out = dot(g_q[g], w_v[0, at], NT)
                out += dot(g_k[g], w_v[1, at], NT)
                out += dot(g_v[g], w_v[2, at], NT)
                part[g, :, at] = out.astype(BF)
                mine[0:1, at] += jnp.sum(out * group_v[slot, :, at].astype(F32), axis=0, keepdims=True)

        def finish(g):
            loads.need(g == 0, 3, 4)
            x = own_v[g].astype(F32)
            scale = lax.rsqrt(row_mean(x * x) + EPSILON)
            hat = x * scale
            back = acc[...] * gain_ref[...]
            tokens_grad[g] = res_v[g] + scale * (back - hat * row_mean(back * hat))

        def fetches(turn):
            at = pl.multiple_of(to_qkv.target(lax.rem(turn + 1, sequences)) * share, share)
            return [
                pltpu.make_async_copy(xs.at[:, :, pl.ds(at, share)], x_v, fetch_sem.at[0]),
                pltpu.make_async_copy(ga.at[:, :, pl.ds(at, share)], ga_v, fetch_sem.at[1]),
                pltpu.make_async_copy(ln.at[:, :, pl.ds(at + half, half)], ln_v, fetch_sem.at[2]),
            ]

        def weights(turn):
            n = lax.rem(turn + 1, sequences)
            loads.need(turn == 0, 1, 2)
            for fetch in fetches(turn):
                fetch.wait()
            hidden_weights(to_up, ln_v, hg_v, 0, n, columns)

            @pl.loop(0, share // 256)
            def _(m):
                at = pl.ds(pl.multiple_of(m * 256, 256), 256)
                x = x_v[:, :, at].reshape(groups * tokens_all, 256)
                for which in range(3):
                    out_qkv[n, which, at] = dot(
                        x, parts[which][...].reshape(groups * tokens_all, width), TN
                    ).astype(BF)

            out_out[n] = dot(
                a_v[...].reshape(groups * tokens_all, width), ga_v[...].reshape(groups * tokens_all, share), TN
            ).astype(BF)
            to_qkv.begin(n)
            to_out.begin(n)

            @pl.when(turn + 1 < sequences)
            def _():
                for fetch in fetches(turn + 1):
                    fetch.start()

        def to_rank(n, source=None):
            return copy_to(
                mine,
                terms.at[line.t if source is None else source],
                t_send.at[n],
                t_recv.at[n],
                lax.rem(line.t + n, ranks),
            )

        def to_sequence(n, source=None):
            return pltpu.make_async_remote_copy(
                src_ref=sums.at[me],
                dst_ref=sums.at[me if source is None else source],
                send_sem=d_send.at[n],
                recv_sem=d_recv.at[n],
                device_id={"dp": lax.rem(me + n, sequences)},
                device_id_type=MESH,
            )

        def beside(turn):
            within(turn, sequences, weights)

            @pl.when(turn == groups)
            def _():
                mine[0:1] = mine[0:1] / gain_ref[...]
                terms[line.t] = mine[...]

                @pl.loop(1, ranks)
                def _(n):
                    to_rank(n).start()

            @pl.when(turn == groups + 1)
            def _():
                @pl.loop(1, ranks)
                def _(n):
                    to_rank(n).wait_send()
                    to_rank(n, lax.rem(line.t + ranks - n, ranks)).wait_recv()

                total = terms[0]
                for n in range(1, ranks):
                    total += terms[n]
                sums[me] = total

                @pl.loop(1, sequences)
                def _(n):
                    to_sequence(n).start()

            @pl.when(turn == groups + 2)
            def _():
                @pl.loop(1, sequences)
                def _(n):
                    to_sequence(n).wait_send()
                    to_sequence(n, lax.rem(me + sequences - n, sequences)).wait_recv()

                total = sums[0]
                for n in range(1, sequences):
                    total += sums[n]
                totals[...] = total

        for fetch in fetches(0):
            fetch.start()
        line.barrier_all(sequences)
        stream(
            line, groups, None, None, reduce, [produce], finish, extra=(max(groups + 3, sequences), beside)
        )
        to_qkv.end()
        to_out.end()
        to_up.end()

    return call(
        body,
        [*grads, w_qkv, kept_x, attended, attn_grad, kept_ln, hidden_grad, landed_up, tokens, gain, grad_resid, gains],
        [
            jax.ShapeDtypeStruct((groups, rows, model), F32),
            jax.ShapeDtypeStruct((3, model), F32),
            jax.ShapeDtypeStruct((sequences, 3, share, width), BF),
            jax.ShapeDtypeStruct((sequences, width, share), BF),
            jax.ShapeDtypeStruct(landed_up.shape, BF),
        ],
        [
            *Reduce.scratch(ranks, groups, rows, model),
            *Spread.scratch(sequences, (3, share, width)),
            *Spread.scratch(sequences, (width, share)),
            *Spread.scratch(sequences, (half, columns)),
            pltpu.VMEM((groups, tokens_all, share), BF),
            pltpu.VMEM((groups, tokens_all, share), BF),
            pltpu.VMEM((groups, tokens_all, half), BF),
            DMA((3,)),
            pltpu.VMEM((2, tokens_all, model), BF),
            DMA((2,)),
            *scratch_of(w_qkv, attended, hidden_grad, tokens, grad_resid),
            DMA((5,)),
            pltpu.VMEM((3, model), F32),
            pltpu.VMEM((ranks, 3, model), F32),
            DMA((ranks,)),
            DMA((ranks,)),
            pltpu.VMEM((sequences, 3, model), F32),
            DMA((sequences,)),
            DMA((sequences,)),
        ],
        4,
        in_specs=[VM, VM, VM, ANY, ANY, ANY, ANY, ANY, ANY, ANY, ANY, VM, ANY, VM],
        out_specs=[VM, VM, ANY, ANY, ANY],
        flops=12 * groups * tokens_all * model * width,
        moved=60 << 20,
        aliases={9: 4},
    )


def shards(
    tokens,
    cotangent,
    first_norm_gain,
    w_qkv,
    w_out,
    g_ln,
    b_ln,
    w_up,
    w_down,
    probs,
    lengths,
    head_count,
    widths,
):
    length_all = widths.shape[0]
    own_tokens, model = tokens.shape
    ranks = length_all // own_tokens
    sequences = lax.axis_size("dp")
    groups, rows = GROUPS, own_tokens // GROUPS
    width = w_out.shape[0]
    heads_here = width // HDIM
    half = HDIM // 2
    frequency = 10000.0 ** (-jnp.arange(half, dtype=F32) / half)
    frequency = jnp.concatenate([frequency, frequency]).reshape(1, HDIM)
    w_qkv_t = w_qkv.transpose(1, 0, 2)
    x = tokens.reshape(groups, rows, model)
    dy = cotangent.reshape(groups, rows, model)
    first_norm_gain, g_ln, b_ln = (v.reshape(1, model) for v in (first_norm_gain, g_ln, b_ln))
    p = jnp.broadcast_to(probs.reshape(groups, rows, 1), (groups, rows, HDIM))
    head_ids = lax.axis_index("tensor") * heads_here + jnp.arange(heads_here, dtype=jnp.int32)
    active = (head_ids < head_count[0]).astype(jnp.int32)
    live = jnp.repeat(active.astype(F32), HDIM).reshape(1, width)
    wide = widths.reshape(ranks, groups, rows).swapaxes(0, 1).reshape(groups, ranks * rows)

    qkv, kept_x, cosines, sines = gather_project(
        x, first_norm_gain, lengths, frequency, w_qkv_t, ranks, width
    )
    qkv = qkv.reshape(length_all, 3 * width)
    cosines, sines = cosines.reshape(length_all, HDIM), sines.reshape(length_all, HDIM)
    attended = attend(qkv, lengths, active, width, groups, own_tokens)
    resid, normed_ln, kept_ffn_grad = project_reduce(
        attended, w_out, x, dy, p, g_ln, b_ln, ranks
    )
    grad_resid, grad_low, gains, kept_ln, squared, grad_hidden = feed(
        normed_ln, kept_ffn_grad, w_up, w_down, wide, resid, dy, g_ln, ranks
    )
    result, probs_grad, kept_attn_grad, grad_attended, land_down, land_up = feed_out(
        grad_low, squared, grad_hidden, kept_ln, kept_ffn_grad, w_down, w_out, live, resid, dy, p, ranks, sequences
    )
    grad_proj = attend_back(
        qkv,
        grad_attended.reshape(length_all, width),
        lengths,
        active,
        cosines,
        sines,
        width,
        groups,
        own_tokens,
    )
    tokens_grad, totals, land_qkv, land_out, land_up = project_back(
        grad_proj, w_qkv_t, kept_x, attended, kept_attn_grad, kept_ln, grad_hidden, land_up, x, first_norm_gain,
        grad_resid, gains, ranks, sequences,
    )
    add_up = lambda landed: jnp.sum(landed.astype(F32), axis=0)
    return (
        result.reshape(own_tokens, model),
        tokens_grad.reshape(own_tokens, model),
        probs_grad[:, :, 0].reshape(own_tokens),
        totals[0],
        add_up(land_qkv).transpose(1, 0, 2),
        add_up(land_out),
        totals[1],
        totals[2],
        add_up(land_up),
        add_up(land_down),
    )


def solution(mesh):
    placed = (
        P(("dp", "tensor"), None),
        P(("dp", "tensor"), None),
        P(),
        P(None, None, "tensor"),
        P("tensor", None),
        P(),
        P(),
        P(None, "tensor"),
        P("tensor", None),
        P(("dp", "tensor")),
        P("dp", None),
        P("dp"),
        P("dp"),
    )
    return jax.shard_map(
        shards,
        mesh=mesh,
        in_specs=placed,
        out_specs=(
            P(("dp", "tensor"), None),
            P(("dp", "tensor"), None),
            P(("dp", "tensor")),
            P(),
            P("dp", None, "tensor"),
            P("tensor", "dp"),
            P(),
            P(),
            P("dp", "tensor"),
            P("tensor", "dp"),
        ),
        check_vma=False,
    )
```

```python
import functools

import jax
import jax.numpy as jnp
from jax import lax
from jax.experimental import pallas as pl
from jax.experimental.pallas import tpu as pltpu
from jax.sharding import PartitionSpec as P

HDIM = 128
FF = 8192
EPSILON = 1e-05
NEGATIVE = -1e30
MAXDOC = 1024
GROUPS = 8
QROWS = 256
MESH = pl.DeviceIdType.MESH
BF = jnp.bfloat16
F32 = jnp.float32
ANY = pl.BlockSpec(memory_space=pl.ANY)
VM = pl.BlockSpec(memory_space=pltpu.VMEM)
DMA = pltpu.SemaphoreType.DMA
NT = (((1,), (1,)), ((), ()))
TN = (((0,), (0,)), ((), ()))


def dot(a, b, dims=(((1,), (0,)), ((), ()))):
    return lax.dot_general(a, b, dims, preferred_element_type=F32)


class Line:
    def __init__(self, ranks, rows):
        self.ranks, self.chips, self.rows = ranks, ranks // 2, rows
        self.t = lax.axis_index("tensor")
        self.z, self.c = self.t // 2, lax.rem(self.t, 2)
        self.has_up, self.has_down = self.z < self.chips - 1, self.z > 0
        self.up = jnp.minimum(self.t + 2, ranks - 1)
        self.down = jnp.maximum(self.t - 2, 0)
        self.partner = self.t + 1 - 2 * self.c

    def barrier(self, dp_size=0):
        sem = pltpu.get_barrier_semaphore()
        pl.semaphore_signal(sem, inc=1, device_id={"tensor": self.partner}, device_id_type=MESH)

        @pl.when(self.has_up)
        def _():
            pl.semaphore_signal(sem, inc=1, device_id={"tensor": self.up}, device_id_type=MESH)

        @pl.when(self.has_down)
        def _():
            pl.semaphore_signal(sem, inc=1, device_id={"tensor": self.down}, device_id_type=MESH)

        d = lax.axis_index("dp")
        for step in range(1, dp_size):
            pl.semaphore_signal(
                sem, inc=1, device_id={"dp": lax.rem(d + step, dp_size)}, device_id_type=MESH
            )
        links = self.has_up.astype(jnp.int32) + self.has_down.astype(jnp.int32)
        pl.semaphore_wait(sem, 1 + max(dp_size - 1, 0) + links)

    def barrier_all(self, dp_size):
        sem = pltpu.get_barrier_semaphore()
        for n in range(1, self.ranks):
            pl.semaphore_signal(
                sem, inc=1, device_id={"tensor": lax.rem(self.t + n, self.ranks)}, device_id_type=MESH
            )
        d = lax.axis_index("dp")
        for n in range(1, dp_size):
            pl.semaphore_signal(
                sem, inc=1, device_id={"dp": lax.rem(d + n, dp_size)}, device_id_type=MESH
            )
        pl.semaphore_wait(sem, self.ranks - 1 + dp_size - 1)


def copy_to(src, dst, send, recv, rank):
    return pltpu.make_async_remote_copy(
        src_ref=src,
        dst_ref=dst,
        send_sem=send,
        recv_sem=recv,
        device_id={"tensor": rank},
        device_id_type=MESH,
    )


class Gather:
    def __init__(self, line, full, send, recv, across_recv):
        self.l, self.full, self.send, self.recv, self.across_recv = line, full, send, recv, across_recv

    @staticmethod
    def scratch(ranks, groups):
        return [DMA((3, ranks // 2)), DMA((groups, ranks // 2)), DMA((groups,))]

    def along(self, g, z, up):
        l = self.l
        place = self.full.at[g, z, l.c]
        return copy_to(
            place,
            place,
            self.send.at[0 if up else 1, z],
            self.recv.at[0 if g == slice(None) else g, z],
            l.up if up else l.down,
        )

    def across(self, g, column):
        place = self.full.at[g, :, column]
        return copy_to(
            place, place, self.send.at[2, 0], self.across_recv.at[0 if g == slice(None) else g], self.l.partner
        )

    def pass_on(self, g, z, up):
        @pl.when(self.l.has_up if up else self.l.has_down)
        def _():
            self.along(g, z, up).start()

    def begin(self, g):
        self.pass_on(g, self.l.z, True)
        self.pass_on(g, self.l.z, False)

    def hop(self, g, h):
        l = self.l

        @pl.when(l.z - h >= 0)
        def _():
            self.along(g, l.z - h, True).wait_recv()
            self.pass_on(g, l.z - h, True)

        @pl.when(l.z + h <= l.chips - 1)
        def _():
            self.along(g, l.z + h, False).wait_recv()
            self.pass_on(g, l.z + h, False)

        if h == l.chips - 1:
            self.across(g, l.c).start()

    def arrived(self, g):
        self.across(g, 1 - self.l.c).wait_recv()

    def drain(self):
        l, every = self.l, slice(None)
        for z in range(l.chips):

            @pl.when(l.has_up & (l.z >= z))
            def _():
                self.along(every, z, True).wait_send()

            @pl.when(l.has_down & (l.z <= z))
            def _():
                self.along(every, z, False).wait_send()

        self.across(every, l.c).wait_send()


class Reduce:
    def __init__(self, line, part, near, far, acc, send, near_recv, far_recv):
        self.l, self.part, self.near, self.far, self.acc = line, part, near, far, acc
        self.send, self.near_recv, self.far_recv = send, near_recv, far_recv

    @staticmethod
    def scratch(ranks, groups, rows, width):
        chips = ranks // 2
        return [
            pltpu.VMEM((groups, chips, 2, rows, width), BF),
            pltpu.VMEM((groups, chips, rows, width), BF),
            pltpu.VMEM((groups, chips + 1, rows, width), BF),
            pltpu.VMEM((rows, width), F32),
            DMA((chips + 1,)),
            DMA((groups,)),
            DMA((groups, chips + 1)),
        ]

    def across(self, g):
        l = self.l
        one = 0 if g == slice(None) else g
        return copy_to(
            self.part.at[g, :, 1 - l.c],
            self.near.at[g],
            self.send.at[l.chips],
            self.near_recv.at[one],
            l.partner,
        )

    def along(self, g, z, up, receive=False):
        l = self.l
        at = l.z if receive else jnp.where(up, l.z + 1, l.z - 1)
        slot = z if up else jnp.where(z == at, l.chips, z)
        return copy_to(
            self.part.at[g, z, l.c],
            self.far.at[g, slot],
            self.send.at[z],
            self.far_recv.at[g, slot],
            l.up if up else l.down,
        ), slot

    def begin(self, g):
        self.across(g).start()

    def summed(self, g, z, slots):
        total = self.part[g, z, self.l.c].astype(F32) + self.near[g, z].astype(F32)
        for slot in slots:
            total += self.far[g, slot].astype(F32)
        return total

    def step(self, g, d):
        l = self.l
        if d == l.chips - 1:
            self.across(g).wait_recv()

        def send(z, up):
            further = l.has_down if up else l.has_up

            @pl.when(further)
            def _():
                copy, slot = self.along(g, z, up, receive=True)
                copy.wait_recv()
                self.part[g, z, l.c] = self.summed(g, z, [slot]).astype(BF)

            @pl.when(jnp.logical_not(further))
            def _():
                self.part[g, z, l.c] = self.summed(g, z, []).astype(BF)

            self.along(g, z, up)[0].start()

        @pl.when(l.z + d <= l.chips - 1)
        def _():
            send(l.z + d, True)

        @pl.when(l.z - d >= 0)
        def _():
            send(l.z - d, False)

    def last(self, g):
        l = self.l

        @pl.when(l.has_down & l.has_up)
        def _():
            self.along(g, l.z, True, receive=True)[0].wait_recv()
            self.along(g, l.z, False, receive=True)[0].wait_recv()
            self.acc[...] = self.summed(g, l.z, [l.z, l.chips])

        @pl.when(jnp.logical_not(l.has_up))
        def _():
            self.along(g, l.z, True, receive=True)[0].wait_recv()
            self.acc[...] = self.summed(g, l.z, [l.z])

        @pl.when(jnp.logical_not(l.has_down))
        def _():
            self.along(g, l.z, False, receive=True)[0].wait_recv()
            self.acc[...] = self.summed(g, l.z, [l.chips])

    def drain(self):
        l = self.l
        self.across(slice(None)).wait_send()
        for z in range(l.chips):

            @pl.when(l.z != z)
            def _():
                copy_to(
                    self.part.at[:, z, l.c],
                    self.far.at[:, z],
                    self.send.at[z],
                    self.far_recv.at[0, z],
                    l.partner,
                ).wait_send()


def within(value, limit, body):
    pl.when((value >= 0) & (value < limit))(lambda: body(value))


def swap_halves(field):
    return pltpu.roll(field, HDIM // 2, axis=1)


def call(body, ins, outs, scratch, ident, in_specs=None, out_specs=None, limit=60, flops=0, moved=0, aliases=None):
    return pl.pallas_call(
        body,
        out_shape=outs,
        in_specs=in_specs or [VM] * len(ins),
        out_specs=out_specs or [VM] * len(outs),
        scratch_shapes=scratch,
        compiler_params=pltpu.CompilerParams(
            collective_id=ident, has_side_effects=True, vmem_limit_bytes=limit << 20
        ),
        input_output_aliases=aliases or {},
        cost_estimate=pl.CostEstimate(flops=flops, bytes_accessed=moved, transcendentals=0),
    )(*ins)


def stream(line, groups, gather=None, arrived=None, reduce=None, produce=(), finish=None, lead=0, extra=None):
    hops = line.chips - 1
    produce = list(produce)
    between = len(produce) > 1
    turns = groups + hops + 1 + (lead + 1 if reduce else 0)

    @pl.loop(0, turns)
    def _(i):
        for n in range(hops):
            if gather:
                within(i - hops + n, groups, functools.partial(gather.hop, h=hops - n))
            if reduce:
                d = n + 1
                within(i - lead - 1 - hops + d, groups, functools.partial(reduce.step, d=d))
            if n == hops - 1 and gather:
                within(i, groups, gather.begin)
            if between:
                if n == 0:
                    within(i - hops - 1, groups, arrived)
                for piece in produce[n * len(produce) // hops : (n + 1) * len(produce) // hops]:
                    within(i - lead, groups, piece)
        if not between:
            for piece in produce:
                within(i - lead, groups, piece)
        if reduce:
            within(i - lead, groups, reduce.begin)
        if arrived and not between:
            within(i - hops - 1, groups, arrived)
        if reduce:

            def end(g):
                reduce.last(g)
                finish(g)

            within(i - lead - 2 - hops, groups, end)
        if extra:
            within(i, min(extra[0], turns), extra[1])

    if extra:

        @pl.loop(min(extra[0], turns), extra[0])
        def _(i):
            extra[1](i)

    if gather:
        gather.drain()
    if reduce:
        reduce.drain()


def starts_of(lengths, places):
    end, start = jnp.int32(0), jnp.zeros_like(places)
    for length in lengths:
        end = end + length
        start = start + jnp.where(places >= end, length, 0)
    return start


def softmax_block(q, k, start, first_query, first_key, scaling):
    raw = dot(k, q, NT)
    keys = first_key + lax.broadcasted_iota(jnp.int32, raw.shape, 0)
    queries = first_query + lax.broadcasted_iota(jnp.int32, raw.shape, 1)
    raw = jnp.where((keys <= queries) & (keys >= start), raw * scaling, NEGATIVE)
    exponent = jnp.exp(raw - jnp.max(raw, axis=0, keepdims=True))
    return exponent * (1.0 / jnp.sum(exponent, axis=0, keepdims=True))


def query_starts(lengths, first):
    places = first + lax.broadcasted_iota(jnp.int32, (8, QROWS), 1)
    return starts_of([lengths[0, n] for n in range(lengths.shape[1])], places)[:1]


def put_grouped(out, block, first, own_tokens, rows):
    for at in range(0, block.shape[0], rows):
        rank, inside = divmod(first + at, own_tokens)
        out[inside // rows, rank * rows : (rank + 1) * rows] = block[at : at + rows]


def attend_back(qkv, grad, lengths, active, cosines, sines, width, groups, own_tokens):
    length, heads = qkv.shape[0], width // HDIM
    scaling = HDIM ** (-0.5)
    reach = MAXDOC // QROWS + 1
    rows_own = own_tokens // groups

    def body(live, docs, q, k, v, g, cos, sin, g_q, g_k, g_v, k_t, sum_k, sum_v):
        h = pl.program_id(0)

        @pl.when(live[h] == 0)
        def _():
            g_q[...] = jnp.zeros_like(g_q)
            g_k[...] = jnp.zeros_like(g_k)
            g_v[...] = jnp.zeros_like(g_v)

        def rotate_back(d, rows):
            return (d * cos[rows] + swap_halves(d * sin[rows])).astype(BF)

        @pl.when(live[h] != 0)
        def _():
            k_t[...] = k[...].T
            sum_k[...] = jnp.zeros_like(sum_k)
            sum_v[...] = jnp.zeros_like(sum_v)
            for i in range(length // QROWS):
                low, high = max(0, i + 1 - reach) * QROWS, (i + 1) * QROWS
                rows, keys = slice(i * QROWS, high), slice(low, high)
                start = query_starts(docs, i * QROWS)
                weights = softmax_block(q[rows], k[keys], start, i * QROWS, low, scaling)
                sum_v[keys] += dot(weights.astype(BF), g[rows])
                g_weights = dot(v[keys], g[rows], NT)
                inner = jnp.sum(weights * g_weights, axis=0, keepdims=True)
                g_scores = (weights * (g_weights - inner)).astype(BF)
                sum_k[keys] += dot(g_scores, q[rows])
                back = rotate_back(dot(k_t[:, keys], g_scores).T * scaling, rows)
                put_grouped(g_q, back, i * QROWS, own_tokens, rows_own)
            for i in range(length // QROWS):
                rows = slice(i * QROWS, (i + 1) * QROWS)
                put_grouped(g_k, rotate_back(sum_k[rows] * scaling, rows), i * QROWS, own_tokens, rows_own)
                put_grouped(g_v, sum_v[rows].astype(BF), i * QROWS, own_tokens, rows_own)

    column = lambda n: pl.BlockSpec((length, HDIM), lambda h, live, docs: (0, n * heads + h))
    table = pl.BlockSpec((length, HDIM), lambda h, live, docs: (0, 0))
    return pl.pallas_call(
        body,
        out_shape=[jax.ShapeDtypeStruct((groups, length // groups, width), BF)] * 3,
        grid_spec=pltpu.PrefetchScalarGridSpec(
            num_scalar_prefetch=2,
            grid=(heads,),
            in_specs=[column(0), column(1), column(2), column(0), table, table],
            out_specs=[
                pl.BlockSpec((groups, length // groups, HDIM), lambda h, live, docs: (0, 0, h))
            ]
            * 3,
            scratch_shapes=[
                pltpu.VMEM((HDIM, length), BF),
                pltpu.VMEM((length, HDIM), F32),
                pltpu.VMEM((length, HDIM), F32),
            ],
        ),
        compiler_params=pltpu.CompilerParams(vmem_limit_bytes=48 << 20),
        cost_estimate=pl.CostEstimate(flops=10 << 30, bytes_accessed=8 << 20, transcendentals=0),
    )(active, lengths, qkv, qkv, qkv, grad, cosines, sines)


class Spread:
    def __init__(self, size, out, land, send, recv, rows=None):
        self.size, self.out, self.land, self.send, self.recv = size, out, land, send, recv
        self.rows = rows
        self.me = lax.axis_index("dp")

    def target(self, n):
        return lax.rem(self.me + n, self.size)

    def copy(self, n, source=None):
        return pltpu.make_async_remote_copy(
            src_ref=self.out.at[n],
            dst_ref=self.place(self.me if source is None else source),
            send_sem=self.send.at[n],
            recv_sem=self.recv.at[n],
            device_id={"dp": self.target(n)},
            device_id_type=MESH,
        )

    def place(self, source):
        return self.land.at[source] if self.rows is None else self.land.at[source, self.rows]

    def own(self):
        return pltpu.make_async_copy(self.out.at[0], self.place(self.me), self.send.at[0])

    def begin(self, n):
        @pl.when(n == 0)
        def _():
            self.own().start()

        @pl.when(n != 0)
        def _():
            self.copy(n).start()

    def end(self):
        self.own().wait()

        @pl.loop(1, self.size)
        def _(n):
            self.copy(n).wait_send()
            self.copy(n, lax.rem(self.me + self.size - n, self.size)).wait_recv()

    @staticmethod
    def scratch(size, shape):
        return [pltpu.VMEM((size, *shape), BF), DMA((size,)), DMA((size,))]


class Loads:
    def __init__(self, pairs, sems):
        self.copies = [
            pltpu.make_async_copy(source, held, sems.at[n]) for n, (source, held) in enumerate(pairs)
        ]

    def begin(self, first, *which):
        @pl.when(first)
        def _():
            for n in which:
                self.copies[n].start()

    def need(self, first, *which):
        @pl.when(first)
        def _():
            for n in which:
                self.copies[n].wait()


class Store:
    def __init__(self, held, out, sems, at=lambda ref, g: ref.at[g]):
        self.held, self.out, self.sems, self.at = held, out, sems, at

    def copy(self, g):
        return pltpu.make_async_copy(self.at(self.held, g), self.at(self.out, g), self.sems.at[g])

    def put(self, g):
        self.copy(g).start()

    def end(self, g):
        self.copy(g).wait()


def scratch_of(*arrays):
    return [pltpu.VMEM(a.shape, a.dtype) for a in arrays]


def row_mean(field):
    return jnp.mean(field, axis=1, keepdims=True)


def layer_norm(resid):
    centred = resid - row_mean(resid)
    inv_std = lax.rsqrt(row_mean(centred * centred) + EPSILON)
    return centred * inv_std, inv_std


def front(
    tokens, cotangent, probs, gain, lengths, frequency, live, w_qkv, w_out, g_ln, b_ln, ranks, width
):
    groups, rows, model = tokens.shape
    heads = width // HDIM
    chips = ranks // 2
    own_tokens = groups * rows
    length = ranks * own_tokens
    shift = rows.bit_length() - 1
    scaling = HDIM ** (-0.5)
    reach = MAXDOC // QROWS + 1
    span = QROWS // own_tokens
    blocks = length // QROWS
    lead = 2

    def body(
        x_ref, dy, p, gain_ref, docs, freq, live_ref, w, wo, gain2, bias2,
        qkv, kept_x, cos_out, sin_out, attended, resid, normed, kept_grad,
        full, w_v, wo_v, dy_v, qkv_v, cos_v, sin_v, v_t, attended_v, own_grad, resid_v, normed_v,
        a_send, a_recv, a_across, b_send, b_recv, b_across, part, near, far, acc, s1, s2, s3,
        load_sem, kept_sem, out_sem, grad_sem, attended_sem, resid_sem, normed_sem,
    ):
        line = Line(ranks, rows)
        loads = Loads([(w, w_v), (wo, wo_v), (dy, dy_v)], load_sem)

        @pl.loop(0, groups)
        def _(g):
            x = x_ref[g].astype(F32)
            normal = x * lax.rsqrt(row_mean(x * x) + EPSILON) * gain_ref[...]
            full[g, line.z, line.c] = normal.astype(BF)

        line.barrier()
        gather = Gather(line, full, a_send, a_recv, a_across)
        stores = [Store(full, kept_x, kept_sem)] + [
            Store(held, out, out_sem.at[n], lambda ref, g: ref.at[:, g])
            for n, (held, out) in enumerate(((qkv_v, qkv), (cos_v, cos_out), (sin_v, sin_out)))
        ]
        place_grad = pltpu.make_async_copy(own_grad, kept_grad.at[:, line.z, line.c], grad_sem)

        def scale_grad(turn):
            loads.begin(turn == 0, 0, 1, 2)

            @pl.when(turn == 1)
            def _():
                loads.need(True, 2)

                @pl.loop(0, groups)
                def _(g):
                    own_grad[g] = (dy_v[g].astype(F32) * p[g, :, :1]).astype(BF)

                place_grad.start()

        def project(g):
            r = lax.broadcasted_iota(jnp.int32, (ranks * rows, HDIM), 0)
            lane = lax.broadcasted_iota(jnp.int32, (ranks * rows, HDIM), 1)
            places = lax.shift_right_logical(r, shift) * own_tokens + g * rows + (r & (rows - 1))
            starts = starts_of([docs[0, n] for n in range(docs.shape[1])], places)
            angles = (places - starts).astype(F32) * freq[...]
            c = jnp.cos(angles)
            s = jnp.sin(angles)
            s = jnp.where(lane < HDIM // 2, -s, s)
            for rank in range(ranks):
                cos_v[rank, g] = c[rank * rows : (rank + 1) * rows]
                sin_v[rank, g] = s[rank * rows : (rank + 1) * rows]
            gather.arrived(g)
            loads.need(g == 0, 0)
            x = full[g].reshape(ranks * rows, model)
            for which in range(3):
                out = dot(x, w_v[which])
                for h in range(heads):
                    u = out[:, h * HDIM : (h + 1) * HDIM]
                    if which < 2:
                        u = u * c + swap_halves(u) * s
                    u = u.astype(BF)
                    at = (which * heads + h) * HDIM
                    for rank in range(ranks):
                        qkv_v[rank, g, :, at : at + HDIM] = u[rank * rows : (rank + 1) * rows]
            for store in stores:
                store.put(g)

        stream(line, groups, gather, arrived=project, extra=(2, scale_grad))

        second = Gather(line, kept_grad, b_send, b_recv, b_across)
        reduce = Reduce(line, part, near, far, acc, s1, s2, s3)
        keep = Store(attended_v, attended, attended_sem)
        results = [Store(resid_v, resid, resid_sem), Store(normed_v, normed, normed_sem)]
        place_grad.wait()

        def columns(which, h):
            at = (which * heads + h) * HDIM
            return slice(at, at + HDIM)

        def attend_block(i):
            low, high = max(0, i + 1 - reach), i + 1
            start = query_starts(docs, i * QROWS)
            for h in range(heads):
                q = qkv_v[i * span : high * span, :, :, columns(0, h)].reshape(QROWS, HDIM)
                k = qkv_v[low * span : high * span, :, :, columns(1, h)].reshape((high - low) * QROWS, HDIM)
                weights = softmax_block(q, k, start, i * QROWS, low * QROWS, scaling)
                done = dot(v_t[h, :, low * QROWS : high * QROWS], weights.astype(BF)).T
                at = slice(h * HDIM, (h + 1) * HDIM)
                done = (done * live_ref[:, at]).astype(BF)
                for n in range(0, QROWS, rows):
                    rank, inside = divmod(i * QROWS + n, own_tokens)
                    attended_v[inside // rows, rank * rows : (rank + 1) * rows, at] = done[n : n + rows]

        def attention(turn):
            @pl.when(turn == 0)
            def _():
                for h in range(heads):
                    v_t[h] = qkv_v[:, :, :, columns(2, h)].reshape(length, HDIM).T

            for n in range(lead):

                @pl.when(turn == n)
                def _():
                    for i in range(n * blocks // lead, (n + 1) * blocks // lead):
                        attend_block(i)

        def produce(g):
            keep.put(g)
            loads.need(g == 0, 1)
            for n in range(0, model, 512):
                out = dot(attended_v[g], wo_v[:, n : n + 512]).astype(BF)
                part[g, ..., n : n + 512] = out.reshape(chips, 2, rows, 512)

        def finish(g):
            total = x_ref[g].astype(F32) + acc[...]
            resid_v[g] = total
            lhat, _ = layer_norm(total)
            normed_v[g] = (lhat * gain2[...] + bias2[...]).astype(BF)
            for store in results:
                store.put(g)

        stream(
            line, groups, second, second.arrived, reduce, [produce], finish, lead, extra=(lead, attention)
        )

        @pl.loop(0, groups)
        def _(g):
            for store in (*stores, keep, *results):
                store.end(g)

    table = jax.ShapeDtypeStruct((ranks, groups, rows, HDIM), F32)
    projected = jax.ShapeDtypeStruct((ranks, groups, rows, 3 * width), BF)
    full = jax.ShapeDtypeStruct((groups, chips, 2, rows, model), BF)
    attended = jax.ShapeDtypeStruct((groups, ranks * rows, width), BF)
    resid = jax.ShapeDtypeStruct((groups, rows, model), F32)
    own = jax.ShapeDtypeStruct((groups, rows, model), BF)
    return call(
        body,
        [tokens, cotangent, probs, gain, lengths, frequency, live, w_qkv, w_out, g_ln, b_ln],
        [projected, full, table, table, attended, resid, own, full],
        [
            *scratch_of(full, w_qkv, w_out, cotangent, projected, table, table),
            pltpu.VMEM((heads, HDIM, length), BF),
            *scratch_of(attended, own, resid, own),
            *Gather.scratch(ranks, groups),
            *Gather.scratch(ranks, groups),
            *Reduce.scratch(ranks, groups, rows, model),
            DMA((3,)),
            DMA((groups,)),
            DMA((3, groups)),
            DMA,
            *[DMA((groups,))] * 3,
        ],
        0,
        in_specs=[VM, ANY, VM, VM, pl.BlockSpec(memory_space=pltpu.SMEM), VM, VM, ANY, ANY, VM, VM],
        out_specs=[ANY] * 8,
        flops=2 * length * model * 4 * width,
        moved=160 << 20,
    )


def feed(own_ln, branch_grad, w_up, w_down, widths, resid, cotangent, g_ln, ranks):
    groups, rows, model = own_ln.shape
    columns = w_up.shape[1]
    tile = min(256, columns)
    tokens = ranks * rows

    def body(
        own, grad, up, down, wide, res, dy, gain, grad_resid, grad_low, gains, kept, squared, hidden_grad,
        full, g_send, g_recv, g_across, part, near, far, acc, s1, s2, s3,
        up_v, down_v, res_v, dy_v, grad_v, lifted, squared_v, hidden_v, high_v, low_v, w_sem, grad_sem, out_sem,
    ):
        line = Line(ranks, rows)
        loads = Loads(
            [(own, full.at[:, line.z, line.c]), (up, up_v), (down, down_v), (res, res_v), (dy, dy_v)], w_sem
        )
        loads.begin(True, 0)
        gains[...] = jnp.zeros_like(gains)
        line.barrier()
        loads.need(True, 0)
        gather = Gather(line, full, g_send, g_recv, g_across)
        reduce = Reduce(line, part, near, far, acc, s1, s2, s3)
        first_column = line.t * columns
        keep, keep_squared, keep_hidden, keep_high, keep_low = (
            Store(held, out, out_sem.at[n])
            for n, (held, out) in enumerate(
                (
                    (full, kept),
                    (squared_v, squared),
                    (hidden_v, hidden_grad),
                    (high_v, grad_resid),
                    (low_v, grad_low),
                )
            )
        )

        def fetch(g):
            slot = lax.rem(g, 2)
            return pltpu.make_async_copy(grad.at[g], grad_v.at[slot], grad_sem.at[slot])

        def later(turn):
            loads.begin(turn == 0, 1, 2)
            loads.begin(turn == 2, 3, 4)

            @pl.when(turn == 1)
            def _():
                fetch(0).start()

        def arrived(g):
            gather.arrived(g)
            keep.put(g)
            fetch(g).wait()

            @pl.when(g + 1 < groups)
            def _():
                fetch(g + 1).start()

            loads.need(g == 0, 1, 2)

        def forward(g):
            limit = (jnp.broadcast_to(wide[pl.ds(g, 1), :], (HDIM, tokens)).T[:, :1] + 1) * (FF // 4)

            @pl.loop(0, columns // tile)
            def _(n):
                at = pl.ds(pl.multiple_of(n * tile, tile), tile)
                hidden = dot(full[g].reshape(tokens, model), up_v[:, at])
                ids = first_column + n * tile + lax.broadcasted_iota(jnp.int32, hidden.shape, 1)
                live = jnp.where(ids < limit, jnp.maximum(hidden, 0.0), 0.0)
                lifted[:, at] = live
                squared_v[g, :, at] = (live * live).astype(BF)

            keep_squared.put(g)

        def backward(g):
            slot = lax.rem(g, 2)

            @pl.loop(0, columns // tile)
            def _(n):
                at = pl.ds(pl.multiple_of(n * tile, tile), tile)
                back = dot(grad_v[slot], down_v[at, :], NT)
                hidden_v[g, :, at] = (back * (2.0 * lifted[:, at])).astype(BF)

            keep_hidden.put(g)

        def lower(g):
            @pl.loop(0, model // 256)
            def _(n):
                at = pl.ds(pl.multiple_of(n * 256, 256), 256)
                out = dot(hidden_v[g], up_v[at, :], NT).astype(BF)
                part[g, :, :, :, at] = out.reshape(ranks // 2, 2, rows, 256)

        def finish(g):
            loads.need(g == 0, 3, 4)
            lhat, inv_std = layer_norm(res_v[g])
            back = acc[...]
            gains[0:1] += jnp.sum(back * lhat, axis=0, keepdims=True)
            gains[1:2] += jnp.sum(back, axis=0, keepdims=True)
            back = back * gain[...]
            back = dy_v[g].astype(F32) + inv_std * (back - row_mean(back) - lhat * row_mean(back * lhat))
            high_v[g] = back
            low_v[g] = back.astype(BF)
            keep_high.put(g)
            keep_low.put(g)

        stream(line, groups, gather, arrived, reduce, [forward, backward, lower], finish, line.chips, (3, later))

        @pl.loop(0, groups)
        def _(g):
            for store in (keep, keep_squared, keep_hidden, keep_high, keep_low):
                store.end(g)

    high = jax.ShapeDtypeStruct((groups, rows, model), F32)
    low = jax.ShapeDtypeStruct((groups, rows, model), BF)
    kept = jax.ShapeDtypeStruct((groups, ranks // 2, 2, rows, model), BF)
    hidden = jax.ShapeDtypeStruct((groups, tokens, columns), BF)
    return call(
        body,
        [own_ln, branch_grad, w_up, w_down, widths, resid, cotangent, g_ln],
        [high, low, jax.ShapeDtypeStruct((2, model), F32), kept, hidden, hidden],
        [
            *scratch_of(kept),
            *Gather.scratch(ranks, groups),
            *Reduce.scratch(ranks, groups, rows, model),
            *scratch_of(w_up, w_down, resid, cotangent),
            pltpu.VMEM((2, tokens, model), BF),
            pltpu.VMEM((tokens, columns), F32),
            *scratch_of(hidden, hidden, high, low),
            DMA((5,)),
            DMA((2,)),
            DMA((5, groups)),
        ],
        2,
        in_specs=[ANY, ANY, ANY, ANY, VM, ANY, ANY, VM],
        out_specs=[ANY, ANY, VM, ANY, ANY, ANY],
        flops=6 * groups * tokens * model * columns,
        moved=100 << 20,
    )


def hidden_weights(spread, inputs, hidden, first, turn_of, columns):
    n = turn_of
    side = min(256, spread.out.shape[1])

    @pl.loop(0, spread.out.shape[1] // side)
    def _(m):
        at = pl.ds(pl.multiple_of(first + m * side, side), side)
        to = pl.ds(pl.multiple_of(m * side, side), side)
        x = inputs[:, :, at]
        spread.out[n, to] = dot(
            x.reshape(x.shape[0] * x.shape[1], side), hidden[...].reshape(-1, columns), TN
        ).astype(BF)

    spread.begin(n)


def feed_out(
    own_grad, squared, hidden_grad, kept_ln, branch_grad, w_down, w_out, active, resid, cotangent, probs, ranks, sequences
):
    groups, rows, model = own_grad.shape
    columns, width = w_down.shape[0], w_out.shape[0]
    tokens = ranks * rows
    share = model // sequences
    half = share // 2

    def body(
        own, sq, hg, ln, bg, down, w, live, res, dy, p, result, probs_grad, kept, grad, land_down, land_up,
        full, g_send, g_recv, g_across, part, near, far, acc, s1, s2, s3, kept_sem,
        out_down, down_send, down_recv, out_up, up_send, up_recv, ln_v, bg_v, fetch_sem,
        sq_v, hg_v, down_v, res_v, dy_v, load_sem, result_v, back_v, result_sem, back_sem,
    ):
        line = Line(ranks, rows)
        gather = Gather(line, full, g_send, g_recv, g_across)
        reduce = Reduce(line, part, near, far, acc, s1, s2, s3)
        to_down = Spread(sequences, out_down, land_down, down_send, down_recv)
        to_up = Spread(sequences, out_up, land_up, up_send, up_recv, pl.ds(0, half))
        keep = Store(full, kept, kept_sem)
        keep_result = Store(result_v, result, result_sem)
        keep_back = Store(back_v, grad, back_sem, lambda ref, g: ref.at[:, g])

        def arrived(g):
            gather.arrived(g)
            keep.put(g)
            back = (dot(full[g].reshape(tokens, model), w[...], NT) * live[...]).astype(BF)
            for rank in range(ranks):
                back_v[rank, g] = back[rank * rows : (rank + 1) * rows]
            keep_back.put(g)

        def produce(g):
            loads.need(g == 0, 0, 1)

            @pl.loop(0, model // 256)
            def _(n):
                at = pl.ds(pl.multiple_of(n * 256, 256), 256)
                out = dot(sq_v[g], down_v[:, at]).astype(BF)
                part[g, :, :, :, at] = out.reshape(ranks // 2, 2, rows, 256)

        def finish(g):
            loads.need(g == 0, 3, 4)
            ffn = acc[...]
            result_v[g] = (res_v[g] + p[g, :, :1] * ffn).astype(BF)
            keep_result.put(g)
            probs_grad[g] = jnp.broadcast_to(
                jnp.sum(dy_v[g].astype(F32) * ffn, axis=1, keepdims=True), (rows, HDIM)
            )

        def fetches(step):
            at = pl.multiple_of(to_up.target(lax.rem(step + 1, sequences)) * share, share)
            return [
                pltpu.make_async_copy(ln.at[:, :, pl.ds(at, half)], ln_v, fetch_sem.at[0]),
                pltpu.make_async_copy(bg.at[:, :, pl.ds(at, share)], bg_v, fetch_sem.at[1]),
            ]

        def weights(step):
            n = lax.rem(step + 1, sequences)
            loads.need(step == 0, 2)
            for fetch in fetches(step):
                fetch.wait()
            side = min(256, columns)

            @pl.loop(0, columns // side)
            def _(m):
                at = pl.ds(pl.multiple_of(m * side, side), side)
                out_down[n, at] = dot(
                    sq_v[:, :, at].reshape(groups * tokens, side), bg_v[...].reshape(groups * tokens, share), TN
                ).astype(BF)

            to_down.begin(n)
            hidden_weights(to_up, ln_v, hg_v, 0, n, columns)

            @pl.when(step + 1 < sequences)
            def _():
                for fetch in fetches(step + 1):
                    fetch.start()

        def beside(turn):
            loads.begin(turn == 0, 0, 1, 2)

            @pl.when(turn == 0)
            def _():
                for fetch in fetches(0):
                    fetch.start()

            loads.begin(turn == 3, 3, 4)
            within(turn - 1, sequences, weights)

        loads = Loads(
            [
                (sq, sq_v),
                (down, down_v),
                (hg, hg_v),
                (res, res_v),
                (dy, dy_v),
                (own, full.at[:, line.z, line.c]),
            ],
            load_sem,
        )
        loads.begin(True, 5)
        line.barrier(sequences)
        loads.need(True, 5)
        stream(
            line, groups, gather, arrived, reduce, [produce], finish, 1, (max(sequences + 1, 4), beside)
        )

        @pl.loop(0, groups)
        def _(g):
            for store in (keep, keep_result, keep_back):
                store.end(g)

        to_down.end()
        to_up.end()

    kept = jax.ShapeDtypeStruct((groups, ranks // 2, 2, rows, model), BF)
    low = jax.ShapeDtypeStruct((groups, rows, model), BF)
    back = jax.ShapeDtypeStruct((ranks, groups, rows, width), BF)
    return call(
        body,
        [own_grad, squared, hidden_grad, kept_ln, branch_grad, w_down, w_out, active, resid, cotangent, probs],
        [
            low,
            jax.ShapeDtypeStruct((groups, rows, HDIM), F32),
            kept,
            back,
            jax.ShapeDtypeStruct((sequences, columns, share), BF),
            jax.ShapeDtypeStruct((sequences, share, columns), BF),
        ],
        [
            *scratch_of(kept),
            *Gather.scratch(ranks, groups),
            *Reduce.scratch(ranks, groups, rows, model),
            DMA((groups,)),
            *Spread.scratch(sequences, (columns, share)),
            *Spread.scratch(sequences, (half, columns)),
            pltpu.VMEM((groups, tokens, half), BF),
            pltpu.VMEM((groups, tokens, share), BF),
            DMA((2,)),
            *scratch_of(squared, hidden_grad, w_down, resid, cotangent),
            DMA((6,)),
            *scratch_of(low, back),
            DMA((groups,)),
            DMA((groups,)),
        ],
        3,
        in_specs=[ANY, ANY, ANY, ANY, ANY, ANY, VM, VM, ANY, ANY, VM],
        out_specs=[ANY, VM, ANY, ANY, ANY, ANY],
        flops=2 * groups * tokens * model * (3 * columns + width),
        moved=100 << 20,
    )


def project_back(
    grads, w_qkv, kept_x, attended, attn_grad, kept_ln, hidden_grad, landed_up, tokens, gain, grad_resid, gains, ranks, sequences
):
    groups, tokens_all, width = grads[0].shape
    rows = tokens_all // ranks
    model = w_qkv.shape[1]
    columns = hidden_grad.shape[2]
    share = model // sequences
    half = share // 2

    def body(
        gq, gk, gv, w, xs, a, ga, ln, hg, up_in, x_ref, gain_ref, g_res, gain_parts,
        tokens_grad, totals, land_qkv, land_out, land_up,
        part, near, far, acc, s1, s2, s3,
        out_qkv, qkv_send, qkv_recv, out_out, out_send, out_recv, out_up, up_send, up_recv,
        x_v, ga_v, ln_v, fetch_sem, group_v, group_sem, w_v, a_v, hg_v, own_v, res_v, load_sem,
        mine, terms, t_send, t_recv, sums, d_send, d_recv, g_q, g_k, g_v, grad_v, grad_sem,
    ):
        line = Line(ranks, rows)
        me = lax.axis_index("dp")
        reduce = Reduce(line, part, near, far, acc, s1, s2, s3)
        to_qkv = Spread(sequences, out_qkv, land_qkv, qkv_send, qkv_recv)
        to_out = Spread(sequences, out_out, land_out, out_send, out_recv)
        to_up = Spread(sequences, out_up, land_up, up_send, up_recv, pl.ds(half, half))
        parts = (g_q, g_k, g_v)
        loads = Loads(
            [(w, w_v), (a, a_v), (hg, hg_v), (x_ref, own_v), (g_res, res_v), (gq, g_q), (gk, g_k), (gv, g_v)],
            load_sem,
        )
        keep_grad = Store(grad_v, tokens_grad, grad_sem)

        def group_fetch(g):
            slot = lax.rem(g, 2)
            return pltpu.make_async_copy(xs.at[g], group_v.at[slot], group_sem.at[slot])

        loads.begin(True, 0, 5, 6, 7)
        group_fetch(0).start()
        mine[0:1] = jnp.zeros((1, model), F32)
        mine[1:3] = gain_parts[...]

        def produce(g):
            loads.need(g == 0, 0, 5, 6, 7)
            group_fetch(g).wait()

            @pl.when(g + 1 < groups)
            def _():
                group_fetch(g + 1).start()

            slot = lax.rem(g, 2)

            @pl.loop(0, model // 256)
            def _(n):
                at = pl.ds(pl.multiple_of(n * 256, 256), 256)
                out = dot(g_q[g], w_v[0, at], NT)
                out += dot(g_k[g], w_v[1, at], NT)
                out += dot(g_v[g], w_v[2, at], NT)
                part[g, :, :, :, at] = out.astype(BF).reshape(ranks // 2, 2, rows, 256)
                mine[0:1, at] += jnp.sum(out * group_v[slot, :, at].astype(F32), axis=0, keepdims=True)

        def finish(g):
            loads.need(g == 0, 3, 4)
            x = own_v[g].astype(F32)
            scale = lax.rsqrt(row_mean(x * x) + EPSILON)
            hat = x * scale
            back = acc[...] * gain_ref[...]
            grad_v[g] = res_v[g] + scale * (back - hat * row_mean(back * hat))
            keep_grad.put(g)

        def fetches(step):
            at = pl.multiple_of(to_qkv.target(lax.rem(step + 1, sequences)) * share, share)
            return [
                pltpu.make_async_copy(ln.at[:, :, pl.ds(at + half, half)], ln_v, fetch_sem.at[0]),
                pltpu.make_async_copy(xs.at[:, :, pl.ds(at, share)], x_v, fetch_sem.at[1]),
                pltpu.make_async_copy(ga.at[:, :, pl.ds(at, share)], ga_v, fetch_sem.at[2]),
            ]

        def weights(piece):
            step = piece // 2
            n = lax.rem(step + 1, sequences)

            @pl.when(lax.rem(piece, 2) == 0)
            def _():
                loads.need(step == 0, 1, 2)
                fetches(step)[0].wait()
                hidden_weights(to_up, ln_v, hg_v, 0, n, columns)

                @pl.when(step + 1 < sequences)
                def _():
                    fetches(step + 1)[0].start()

            @pl.when(lax.rem(piece, 2) == 1)
            def _():
                for fetch in fetches(step)[1:]:
                    fetch.wait()

                @pl.loop(0, share // 256)
                def _(m):
                    at = pl.ds(pl.multiple_of(m * 256, 256), 256)
                    x = x_v[:, :, at].reshape(groups * tokens_all, 256)
                    for which in range(3):
                        out_qkv[n, which, at] = dot(
                            x, parts[which][...].reshape(groups * tokens_all, width), TN
                        ).astype(BF)

                to_qkv.begin(n)
                out_out[n] = dot(
                    a_v[...].reshape(groups * tokens_all, width), ga_v[...].reshape(groups * tokens_all, share), TN
                ).astype(BF)
                to_out.begin(n)

                @pl.when(step + 1 < sequences)
                def _():
                    for fetch in fetches(step + 1)[1:]:
                        fetch.start()

        def to_rank(n, source=None):
            return copy_to(
                mine,
                terms.at[line.t if source is None else source],
                t_send.at[n],
                t_recv.at[n],
                lax.rem(line.t + n, ranks),
            )

        def to_sequence(n, source=None):
            return pltpu.make_async_remote_copy(
                src_ref=sums.at[me],
                dst_ref=sums.at[me if source is None else source],
                send_sem=d_send.at[n],
                recv_sem=d_recv.at[n],
                device_id={"dp": lax.rem(me + n, sequences)},
                device_id_type=MESH,
            )

        def beside(turn):
            loads.begin(turn == 0, 1, 2)
            loads.begin(turn == 2, 3, 4)

            @pl.when(turn == 0)
            def _():
                for fetch in fetches(0):
                    fetch.start()

            within(turn - 1, 2 * sequences, weights)

            @pl.when(turn == groups)
            def _():
                mine[0:1] = mine[0:1] / gain_ref[...]
                terms[line.t] = mine[...]

                @pl.loop(1, ranks)
                def _(n):
                    to_rank(n).start()

            @pl.when(turn == groups + 1)
            def _():
                @pl.loop(1, ranks)
                def _(n):
                    to_rank(n).wait_send()
                    to_rank(n, lax.rem(line.t + ranks - n, ranks)).wait_recv()

                total = terms[0]
                for n in range(1, ranks):
                    total += terms[n]
                sums[me] = total

                @pl.loop(1, sequences)
                def _(n):
                    to_sequence(n).start()

            @pl.when(turn == groups + 2)
            def _():
                @pl.loop(1, sequences)
                def _(n):
                    to_sequence(n).wait_send()
                    to_sequence(n, lax.rem(me + sequences - n, sequences)).wait_recv()

                total = sums[0]
                for n in range(1, sequences):
                    total += sums[n]
                totals[...] = total

        line.barrier_all(sequences)
        stream(
            line, groups, None, None, reduce, [produce], finish, extra=(max(groups + 3, 2 * sequences + 1), beside)
        )

        @pl.loop(0, groups)
        def _(g):
            keep_grad.end(g)

        to_qkv.end()
        to_out.end()
        to_up.end()

    return call(
        body,
        [*grads, w_qkv, kept_x, attended, attn_grad, kept_ln, hidden_grad, landed_up, tokens, gain, grad_resid, gains],
        [
            jax.ShapeDtypeStruct((groups, rows, model), F32),
            jax.ShapeDtypeStruct((3, model), F32),
            jax.ShapeDtypeStruct((sequences, 3, share, width), BF),
            jax.ShapeDtypeStruct((sequences, width, share), BF),
            jax.ShapeDtypeStruct(landed_up.shape, BF),
        ],
        [
            *Reduce.scratch(ranks, groups, rows, model),
            *Spread.scratch(sequences, (3, share, width)),
            *Spread.scratch(sequences, (width, share)),
            *Spread.scratch(sequences, (half, columns)),
            pltpu.VMEM((groups, tokens_all, share), BF),
            pltpu.VMEM((groups, tokens_all, share), BF),
            pltpu.VMEM((groups, tokens_all, half), BF),
            DMA((3,)),
            pltpu.VMEM((2, tokens_all, model), BF),
            DMA((2,)),
            *scratch_of(w_qkv, attended, hidden_grad, tokens, grad_resid),
            DMA((8,)),
            pltpu.VMEM((3, model), F32),
            pltpu.VMEM((ranks, 3, model), F32),
            DMA((ranks,)),
            DMA((ranks,)),
            pltpu.VMEM((sequences, 3, model), F32),
            DMA((sequences,)),
            DMA((sequences,)),
            *scratch_of(*grads, grad_resid),
            DMA((groups,)),
        ],
        4,
        in_specs=[ANY] * 11 + [VM, ANY, VM],
        out_specs=[ANY, VM, ANY, ANY, ANY],
        flops=12 * groups * tokens_all * model * width,
        moved=60 << 20,
        aliases={9: 4},
    )


def shards(
    tokens,
    cotangent,
    first_norm_gain,
    w_qkv,
    w_out,
    g_ln,
    b_ln,
    w_up,
    w_down,
    probs,
    lengths,
    head_count,
    widths,
):
    length_all = widths.shape[0]
    own_tokens, model = tokens.shape
    ranks = length_all // own_tokens
    sequences = lax.axis_size("dp")
    groups, rows = GROUPS, own_tokens // GROUPS
    width = w_out.shape[0]
    heads_here = width // HDIM
    half = HDIM // 2
    frequency = 10000.0 ** (-jnp.arange(half, dtype=F32) / half)
    frequency = jnp.concatenate([frequency, frequency]).reshape(1, HDIM)
    w_qkv_t = w_qkv.transpose(1, 0, 2)
    x = tokens.reshape(groups, rows, model)
    dy = cotangent.reshape(groups, rows, model)
    first_norm_gain, g_ln, b_ln = (v.reshape(1, model) for v in (first_norm_gain, g_ln, b_ln))
    p = jnp.broadcast_to(probs.reshape(groups, rows, 1), (groups, rows, HDIM))
    head_ids = lax.axis_index("tensor") * heads_here + jnp.arange(heads_here, dtype=jnp.int32)
    active = (head_ids < head_count[0]).astype(jnp.int32)
    live = jnp.repeat(active.astype(F32), HDIM).reshape(1, width)
    wide = widths.reshape(ranks, groups, rows).swapaxes(0, 1).reshape(groups, ranks * rows)

    qkv, kept_x, cosines, sines, attended, resid, normed_ln, kept_ffn_grad = front(
        x, dy, p, first_norm_gain, lengths, frequency, live, w_qkv_t, w_out, g_ln, b_ln, ranks, width
    )
    qkv = qkv.reshape(length_all, 3 * width)
    cosines, sines = cosines.reshape(length_all, HDIM), sines.reshape(length_all, HDIM)
    whole = lambda kept: kept.reshape(groups, ranks * rows, model)
    grad_resid, grad_low, gains, kept_ln, squared, grad_hidden = feed(
        normed_ln, whole(kept_ffn_grad), w_up, w_down, wide, resid, dy, g_ln, ranks
    )
    result, probs_grad, kept_attn_grad, grad_attended, land_down, land_up = feed_out(
        grad_low, squared, grad_hidden, whole(kept_ln), whole(kept_ffn_grad), w_down, w_out, live, resid, dy, p, ranks, sequences
    )
    grad_proj = attend_back(
        qkv,
        grad_attended.reshape(length_all, width),
        lengths,
        active,
        cosines,
        sines,
        width,
        groups,
        own_tokens,
    )
    tokens_grad, totals, land_qkv, land_out, land_up = project_back(
        grad_proj, w_qkv_t, whole(kept_x), attended, whole(kept_attn_grad), whole(kept_ln), grad_hidden, land_up, x, first_norm_gain,
        grad_resid, gains, ranks, sequences,
    )
    add_up = lambda landed: jnp.sum(landed.astype(F32), axis=0)
    return (
        result.reshape(own_tokens, model),
        tokens_grad.reshape(own_tokens, model),
        probs_grad[:, :, 0].reshape(own_tokens),
        totals[0],
        add_up(land_qkv).transpose(1, 0, 2),
        add_up(land_out),
        totals[1],
        totals[2],
        add_up(land_up),
        add_up(land_down),
    )


def solution(mesh):
    placed = (
        P(("dp", "tensor"), None),
        P(("dp", "tensor"), None),
        P(),
        P(None, None, "tensor"),
        P("tensor", None),
        P(),
        P(),
        P(None, "tensor"),
        P("tensor", None),
        P(("dp", "tensor")),
        P("dp", None),
        P("dp"),
        P("dp"),
    )
    return jax.shard_map(
        shards,
        mesh=mesh,
        in_specs=placed,
        out_specs=(
            P(("dp", "tensor"), None),
            P(("dp", "tensor"), None),
            P(("dp", "tensor")),
            P(),
            P("dp", None, "tensor"),
            P("tensor", "dp"),
            P(),
            P(),
            P("dp", "tensor"),
            P("tensor", "dp"),
        ),
        check_vma=False,
    )
```

```python
import functools

import jax
import jax.numpy as jnp
from jax import lax
from jax.experimental import pallas as pl
from jax.experimental.pallas import tpu as pltpu
from jax.sharding import PartitionSpec as P

HDIM = 128
FF = 8192
EPSILON = 1e-05
NEGATIVE = -1e30
MAXDOC = 1024
GROUPS = 8
QROWS = 256
MESH = pl.DeviceIdType.MESH
BF = jnp.bfloat16
F32 = jnp.float32
ANY = pl.BlockSpec(memory_space=pl.ANY)
VM = pl.BlockSpec(memory_space=pltpu.VMEM)
DMA = pltpu.SemaphoreType.DMA
NT = (((1,), (1,)), ((), ()))
TN = (((0,), (0,)), ((), ()))


def dot(a, b, dims=(((1,), (0,)), ((), ()))):
    return lax.dot_general(a, b, dims, preferred_element_type=F32)


class Line:
    def __init__(self, ranks, rows):
        self.ranks, self.chips, self.rows = ranks, ranks // 2, rows
        self.t = lax.axis_index("tensor")
        self.z, self.c = self.t // 2, lax.rem(self.t, 2)
        self.has_up, self.has_down = self.z < self.chips - 1, self.z > 0
        self.up = jnp.minimum(self.t + 2, ranks - 1)
        self.down = jnp.maximum(self.t - 2, 0)
        self.partner = self.t + 1 - 2 * self.c

    def barrier(self, dp_size=0):
        sem = pltpu.get_barrier_semaphore()
        pl.semaphore_signal(sem, inc=1, device_id={"tensor": self.partner}, device_id_type=MESH)

        @pl.when(self.has_up)
        def _():
            pl.semaphore_signal(sem, inc=1, device_id={"tensor": self.up}, device_id_type=MESH)

        @pl.when(self.has_down)
        def _():
            pl.semaphore_signal(sem, inc=1, device_id={"tensor": self.down}, device_id_type=MESH)

        d = lax.axis_index("dp")
        for step in range(1, dp_size):
            pl.semaphore_signal(
                sem, inc=1, device_id={"dp": lax.rem(d + step, dp_size)}, device_id_type=MESH
            )
        links = self.has_up.astype(jnp.int32) + self.has_down.astype(jnp.int32)
        pl.semaphore_wait(sem, 1 + max(dp_size - 1, 0) + links)

    def barrier_all(self, dp_size):
        sem = pltpu.get_barrier_semaphore()
        for n in range(1, self.ranks):
            pl.semaphore_signal(
                sem, inc=1, device_id={"tensor": lax.rem(self.t + n, self.ranks)}, device_id_type=MESH
            )
        d = lax.axis_index("dp")
        for n in range(1, dp_size):
            pl.semaphore_signal(
                sem, inc=1, device_id={"dp": lax.rem(d + n, dp_size)}, device_id_type=MESH
            )
        pl.semaphore_wait(sem, self.ranks - 1 + dp_size - 1)


def copy_to(src, dst, send, recv, rank):
    return pltpu.make_async_remote_copy(
        src_ref=src,
        dst_ref=dst,
        send_sem=send,
        recv_sem=recv,
        device_id={"tensor": rank},
        device_id_type=MESH,
    )


class Gather:
    def __init__(self, line, full, send, recv, across_recv):
        self.l, self.full, self.send, self.recv, self.across_recv = line, full, send, recv, across_recv

    @staticmethod
    def scratch(ranks, groups):
        return [DMA((3, ranks // 2)), DMA((groups, ranks // 2)), DMA((groups,))]

    def along(self, g, z, up):
        l = self.l
        place = self.full.at[g, z, l.c]
        return copy_to(
            place,
            place,
            self.send.at[0 if up else 1, z],
            self.recv.at[0 if g == slice(None) else g, z],
            l.up if up else l.down,
        )

    def across(self, g, column):
        place = self.full.at[g, :, column]
        return copy_to(
            place, place, self.send.at[2, 0], self.across_recv.at[0 if g == slice(None) else g], self.l.partner
        )

    def pass_on(self, g, z, up):
        @pl.when(self.l.has_up if up else self.l.has_down)
        def _():
            self.along(g, z, up).start()

    def begin(self, g):
        self.pass_on(g, self.l.z, True)
        self.pass_on(g, self.l.z, False)

    def hop(self, g, h):
        l = self.l

        @pl.when(l.z - h >= 0)
        def _():
            self.along(g, l.z - h, True).wait_recv()
            self.pass_on(g, l.z - h, True)

        @pl.when(l.z + h <= l.chips - 1)
        def _():
            self.along(g, l.z + h, False).wait_recv()
            self.pass_on(g, l.z + h, False)

        if h == l.chips - 1:
            self.across(g, l.c).start()

    def arrived(self, g):
        self.across(g, 1 - self.l.c).wait_recv()

    def drain(self):
        l, every = self.l, slice(None)
        for z in range(l.chips):

            @pl.when(l.has_up & (l.z >= z))
            def _():
                self.along(every, z, True).wait_send()

            @pl.when(l.has_down & (l.z <= z))
            def _():
                self.along(every, z, False).wait_send()

        self.across(every, l.c).wait_send()


class Reduce:
    def __init__(self, line, part, near, far, acc, send, near_recv, far_recv):
        self.l, self.part, self.near, self.far, self.acc = line, part, near, far, acc
        self.send, self.near_recv, self.far_recv = send, near_recv, far_recv

    @staticmethod
    def scratch(ranks, groups, rows, width):
        chips = ranks // 2
        return [
            pltpu.VMEM((groups, chips, 2, rows, width), BF),
            pltpu.VMEM((groups, chips, rows, width), BF),
            pltpu.VMEM((groups, chips + 1, rows, width), BF),
            pltpu.VMEM((rows, width), F32),
            DMA((groups, chips + 1)),
            DMA((groups,)),
            DMA((groups, chips + 1)),
        ]

    def across(self, g):
        l = self.l
        return copy_to(
            self.part.at[g, :, 1 - l.c],
            self.near.at[g],
            self.send.at[g, l.chips],
            self.near_recv.at[g],
            l.partner,
        )

    def along(self, g, z, up, receive=False):
        l = self.l
        at = l.z if receive else jnp.where(up, l.z + 1, l.z - 1)
        slot = z if up else jnp.where(z == at, l.chips, z)
        return copy_to(
            self.part.at[g, z, l.c],
            self.far.at[g, slot],
            self.send.at[g, z],
            self.far_recv.at[g, slot],
            l.up if up else l.down,
        ), slot

    def begin(self, g):
        self.across(g).start()

    def add(self, g, z, slots, total=None):
        side = 512

        @pl.loop(0, self.part.shape[-1] // side)
        def _(n):
            at = pl.ds(pl.multiple_of(n * side, side), side)
            value = self.part[g, z, self.l.c, :, at].astype(F32) + self.near[g, z, :, at].astype(F32)
            for slot in slots:
                value += self.far[g, slot, :, at].astype(F32)
            if total is None:
                self.part[g, z, self.l.c, :, at] = value.astype(BF)
            else:
                total[:, at] = value

    def step(self, g, d):
        l = self.l
        if d == l.chips - 1:
            self.across(g).wait_recv()

        def send(z, up):
            further = l.has_down if up else l.has_up

            @pl.when(further)
            def _():
                copy, slot = self.along(g, z, up, receive=True)
                copy.wait_recv()
                self.add(g, z, [slot])

            @pl.when(jnp.logical_not(further))
            def _():
                self.add(g, z, [])

            self.along(g, z, up)[0].start()

        @pl.when(l.z + d <= l.chips - 1)
        def _():
            send(l.z + d, True)

        @pl.when(l.z - d >= 0)
        def _():
            send(l.z - d, False)

    def last(self, g):
        l = self.l

        @pl.when(l.has_down & l.has_up)
        def _():
            self.along(g, l.z, True, receive=True)[0].wait_recv()
            self.along(g, l.z, False, receive=True)[0].wait_recv()
            self.add(g, l.z, [l.z, l.chips], self.acc)

        @pl.when(jnp.logical_not(l.has_up))
        def _():
            self.along(g, l.z, True, receive=True)[0].wait_recv()
            self.add(g, l.z, [l.z], self.acc)

        @pl.when(jnp.logical_not(l.has_down))
        def _():
            self.along(g, l.z, False, receive=True)[0].wait_recv()
            self.add(g, l.z, [l.chips], self.acc)

    def drain(self, g):
        l = self.l
        self.across(g).wait_send()
        for z in range(l.chips):

            @pl.when(l.z != z)
            def _():
                copy_to(
                    self.part.at[g, z, l.c],
                    self.far.at[g, z],
                    self.send.at[g, z],
                    self.far_recv.at[g, z],
                    l.partner,
                ).wait_send()


def within(value, limit, body):
    pl.when((value >= 0) & (value < limit))(lambda: body(value))


def swap_halves(field):
    return pltpu.roll(field, HDIM // 2, axis=1)


def call(body, ins, outs, scratch, ident, in_specs=None, out_specs=None, limit=60, flops=0, moved=0, aliases=None):
    return pl.pallas_call(
        body,
        out_shape=outs,
        in_specs=in_specs or [VM] * len(ins),
        out_specs=out_specs or [VM] * len(outs),
        scratch_shapes=scratch,
        compiler_params=pltpu.CompilerParams(
            collective_id=ident, has_side_effects=True, vmem_limit_bytes=limit << 20
        ),
        input_output_aliases=aliases or {},
        cost_estimate=pl.CostEstimate(flops=flops, bytes_accessed=moved, transcendentals=0),
    )(*ins)


def stream(line, groups, gather=None, arrived=None, reduce=None, produce=(), finish=None, lead=0, extra=None):
    hops = line.chips - 1
    produce = list(produce)
    between = len(produce) > 1
    turns = groups + hops + 1 + (lead + 1 if reduce else 0)

    @pl.loop(0, turns)
    def _(i):
        for n in range(hops):
            if gather:
                within(i - hops + n, groups, functools.partial(gather.hop, h=hops - n))
            if reduce:
                d = n + 1
                within(i - lead - 1 - hops + d, groups, functools.partial(reduce.step, d=d))
            if n == hops - 1 and gather:
                within(i, groups, gather.begin)
            if between:
                if n == 0:
                    within(i - hops - 1, groups, arrived)
                for piece in produce[n * len(produce) // hops : (n + 1) * len(produce) // hops]:
                    within(i - lead, groups, piece)
        if not between:
            for piece in produce:
                within(i - lead, groups, piece)
        if reduce:
            within(i - lead, groups, reduce.begin)
        if arrived and not between:
            within(i - hops - 1, groups, arrived)
        if reduce:

            def end(g):
                reduce.last(g)
                finish(g)

            within(i - lead - 2 - hops, groups, end)
        if extra:
            within(i, min(extra[0], turns), extra[1])

    if extra:

        @pl.loop(min(extra[0], turns), extra[0])
        def _(i):
            extra[1](i)

    if gather:
        gather.drain()
    if reduce:
        pl.loop(0, groups)(reduce.drain)


def starts_of(lengths, places):
    end, start = jnp.int32(0), jnp.zeros_like(places)
    for length in lengths:
        end = end + length
        start = start + jnp.where(places >= end, length, 0)
    return start


def softmax_block(q, k, start, first_query, first_key, scaling):
    raw = dot(k, q, NT)
    keys = first_key + lax.broadcasted_iota(jnp.int32, raw.shape, 0)
    queries = first_query + lax.broadcasted_iota(jnp.int32, raw.shape, 1)
    raw = jnp.where((keys <= queries) & (keys >= start), raw * scaling, NEGATIVE)
    exponent = jnp.exp(raw - jnp.max(raw, axis=0, keepdims=True))
    return exponent * (1.0 / jnp.sum(exponent, axis=0, keepdims=True))


def query_starts(lengths, first):
    places = first + lax.broadcasted_iota(jnp.int32, (8, QROWS), 1)
    return starts_of([lengths[0, n] for n in range(lengths.shape[1])], places)[:1]


def put_grouped(out, block, i, own_tokens, rows, at=slice(None)):
    for n in range(0, QROWS, rows):
        rank, inside = divmod(n, own_tokens)
        rank += i * (QROWS // own_tokens)
        out[inside // rows, pl.ds(pl.multiple_of(rank * rows, rows), rows), at] = block[n : n + rows]


def attend_back(qkv, grad, lengths, active, cosines, sines, width, groups, own_tokens):
    length, heads = qkv.shape[0], width // HDIM
    scaling = HDIM ** (-0.5)
    reach = MAXDOC // QROWS + 1
    rows_own = own_tokens // groups

    def body(live, docs, q, k, v, g, cos, sin, g_q, g_k, g_v, k_t, sum_k, sum_v):
        h = pl.program_id(0)

        @pl.when(live[h] == 0)
        def _():
            g_q[...] = jnp.zeros_like(g_q)
            g_k[...] = jnp.zeros_like(g_k)
            g_v[...] = jnp.zeros_like(g_v)

        def rotate_back(d, rows):
            return (d * cos[rows] + swap_halves(d * sin[rows])).astype(BF)

        @pl.when(live[h] != 0)
        def _():
            k_t[...] = k[...].T
            sum_k[...] = jnp.zeros_like(sum_k)
            sum_v[...] = jnp.zeros_like(sum_v)
            def back_block(i, count):
                low = i + 1 - count
                rows = pl.ds(pl.multiple_of(i * QROWS, QROWS), QROWS)
                keys = pl.ds(pl.multiple_of(low * QROWS, QROWS), count * QROWS)
                start = query_starts(docs, i * QROWS)
                weights = softmax_block(q[rows], k[keys], start, i * QROWS, low * QROWS, scaling)
                sum_v[keys] += dot(weights.astype(BF), g[rows])
                g_weights = dot(v[keys], g[rows], NT)
                inner = jnp.sum(weights * g_weights, axis=0, keepdims=True)
                g_scores = (weights * (g_weights - inner)).astype(BF)
                sum_k[keys] += dot(g_scores, q[rows])
                back = rotate_back(dot(k_t[:, keys], g_scores).T * scaling, rows)
                put_grouped(g_q, back, i, own_tokens, rows_own)

            for i in range(length // QROWS):
                back_block(i, min(i + 1, reach))

            for i in range(length // QROWS):
                rows = pl.ds(pl.multiple_of(i * QROWS, QROWS), QROWS)
                put_grouped(g_k, rotate_back(sum_k[rows] * scaling, rows), i, own_tokens, rows_own)
                put_grouped(g_v, sum_v[rows].astype(BF), i, own_tokens, rows_own)

    column = lambda n: pl.BlockSpec((length, HDIM), lambda h, live, docs: (0, n * heads + h))
    table = pl.BlockSpec((length, HDIM), lambda h, live, docs: (0, 0))
    return pl.pallas_call(
        body,
        out_shape=[jax.ShapeDtypeStruct((groups, length // groups, width), BF)] * 3,
        grid_spec=pltpu.PrefetchScalarGridSpec(
            num_scalar_prefetch=2,
            grid=(heads,),
            in_specs=[column(0), column(1), column(2), column(0), table, table],
            out_specs=[
                pl.BlockSpec((groups, length // groups, HDIM), lambda h, live, docs: (0, 0, h))
            ]
            * 3,
            scratch_shapes=[
                pltpu.VMEM((HDIM, length), BF),
                pltpu.VMEM((length, HDIM), F32),
                pltpu.VMEM((length, HDIM), F32),
            ],
        ),
        compiler_params=pltpu.CompilerParams(vmem_limit_bytes=48 << 20),
        cost_estimate=pl.CostEstimate(flops=10 << 30, bytes_accessed=8 << 20, transcendentals=0),
    )(active, lengths, qkv, qkv, qkv, grad, cosines, sines)


class Spread:
    def __init__(self, size, out, land, send, recv, rows=None):
        self.size, self.out, self.land, self.send, self.recv = size, out, land, send, recv
        self.rows = rows
        self.me = lax.axis_index("dp")

    def target(self, n):
        return lax.rem(self.me + n, self.size)

    def copy(self, n, source=None):
        return pltpu.make_async_remote_copy(
            src_ref=self.out.at[n],
            dst_ref=self.place(self.me if source is None else source),
            send_sem=self.send.at[n],
            recv_sem=self.recv.at[n],
            device_id={"dp": self.target(n)},
            device_id_type=MESH,
        )

    def place(self, source):
        return self.land.at[source] if self.rows is None else self.land.at[source, self.rows]

    def own(self):
        return pltpu.make_async_copy(self.out.at[0], self.place(self.me), self.send.at[0])

    def begin(self, n):
        @pl.when(n == 0)
        def _():
            self.own().start()

        @pl.when(n != 0)
        def _():
            self.copy(n).start()

    def end(self):
        self.own().wait()

        @pl.loop(1, self.size)
        def _(n):
            self.copy(n).wait_send()
            self.copy(n, lax.rem(self.me + self.size - n, self.size)).wait_recv()

    @staticmethod
    def scratch(size, shape):
        return [pltpu.VMEM((size, *shape), BF), DMA((size,)), DMA((size,))]


class Loads:
    def __init__(self, pairs, sems):
        self.copies = [
            pltpu.make_async_copy(source, held, sems.at[n]) for n, (source, held) in enumerate(pairs)
        ]

    def begin(self, first, *which):
        @pl.when(first)
        def _():
            for n in which:
                self.copies[n].start()

    def need(self, first, *which):
        @pl.when(first)
        def _():
            for n in which:
                self.copies[n].wait()


class Store:
    def __init__(self, held, out, sems, at=lambda ref, g: ref.at[g]):
        self.held, self.out, self.sems, self.at = held, out, sems, at

    def copy(self, g):
        return pltpu.make_async_copy(self.at(self.held, g), self.at(self.out, g), self.sems.at[g])

    def put(self, g):
        self.copy(g).start()

    def end(self, g):
        self.copy(g).wait()


class Turns:
    def __init__(self, pairs, sems, at=lambda ref, g: ref.at[g]):
        self.pairs, self.sems, self.at = pairs, sems, at

    def each(self, g):
        return [
            pltpu.make_async_copy(held.at[lax.rem(g, 2)], self.at(out, g), self.sems.at[n, g])
            for n, (held, out) in enumerate(self.pairs)
        ]

    def free(self, g):
        @pl.when(g >= 2)
        def _():
            for copy in self.each(g - 2):
                copy.wait()

        return lax.rem(g, 2)

    def put(self, g):
        for copy in self.each(g):
            copy.start()

    def end(self, groups):
        for g in range(max(groups - 2, 0), groups):
            for copy in self.each(g):
                copy.wait()


def scratch_of(*arrays):
    return [pltpu.VMEM(a.shape, a.dtype) for a in arrays]


def row_mean(field):
    return jnp.mean(field, axis=1, keepdims=True)


def layer_norm(resid):
    centred = resid - row_mean(resid)
    inv_std = lax.rsqrt(row_mean(centred * centred) + EPSILON)
    return centred * inv_std, inv_std


def front(
    tokens, cotangent, probs, gain, lengths, frequency, live, w_qkv, w_out, g_ln, b_ln, w_up, w_down, widths, ranks
):
    width, columns = w_out.shape[0], w_up.shape[1]
    tile = min(256, columns)
    groups, rows, model = tokens.shape
    heads = width // HDIM
    chips = ranks // 2
    own_tokens = groups * rows
    length = ranks * own_tokens
    shift = rows.bit_length() - 1
    scaling = HDIM ** (-0.5)
    reach = MAXDOC // QROWS + 1
    span = QROWS // own_tokens
    blocks = length // QROWS
    lead = 2
    hops = chips - 1
    tokens_all = ranks * rows
    normed_at = lead + 2 + hops
    hidden_at = normed_at + hops + 1
    back_at = hidden_at + 2 + hops

    def body(
        x_ref, dy, p, gain_ref, docs, freq, live_ref, w, wo, gain2, bias2, up, down, wide,
        qkv, kept_x, cos_out, sin_out, attended, resid, kept_grad, grad_resid, grad_low, gains, kept_ln, squared,
        hidden_grad,
        full, w_v, wo_v, dy_v, up_v, down_v, qkv_v, cos_v, sin_v, v_t, attended_v, low_v, resid_v, high_v, grad_v,
        lifted, squared_v, hidden_v,
        a_send, a_recv, a_across, b_send, b_recv, b_across, c_send, c_recv, c_across,
        part, near, far, acc, s1, s2, s3, t1, t2, t3,
        load_sem, kept_sem, out_sem, place_sem, attended_sem, resid_sem, result_sem, tile_sem,
    ):
        line = Line(ranks, rows)
        loads = Loads([(w, w_v), (wo, wo_v), (dy, dy_v), (up, up_v), (down, down_v)], load_sem)

        @pl.loop(0, groups)
        def _(g):
            x = x_ref[g].astype(F32)
            normal = x * lax.rsqrt(row_mean(x * x) + EPSILON) * gain_ref[...]
            full[g, line.z, line.c] = normal.astype(BF)

        line.barrier()
        gather = Gather(line, full, a_send, a_recv, a_across)
        tables = Turns([(cos_v, cos_out), (sin_v, sin_out)], out_sem.at[pl.ds(1, 2)], lambda ref, g: ref.at[:, g])
        stores = [
            Store(full, kept_x, kept_sem.at[0]),
            Store(qkv_v, qkv, out_sem.at[0], lambda ref, g: ref.at[:, g]),
        ]
        place_grad = pltpu.make_async_copy(low_v, kept_grad.at[:, line.z, line.c], place_sem)

        def scale_grad(turn):
            loads.begin(turn == 0, 0, 1, 2)

            @pl.when(turn == 1)
            def _():
                loads.need(True, 2)

                @pl.loop(0, groups)
                def _(g):
                    low_v[g] = (dy_v[g].astype(F32) * p[g, :, :1]).astype(BF)

                place_grad.start()

        def project(g):
            r = lax.broadcasted_iota(jnp.int32, (ranks * rows, HDIM), 0)
            lane = lax.broadcasted_iota(jnp.int32, (ranks * rows, HDIM), 1)
            places = lax.shift_right_logical(r, shift) * own_tokens + g * rows + (r & (rows - 1))
            starts = starts_of([docs[0, n] for n in range(docs.shape[1])], places)
            angles = (places - starts).astype(F32) * freq[...]
            c = jnp.cos(angles)
            s = jnp.sin(angles)
            s = jnp.where(lane < HDIM // 2, -s, s)
            slot = tables.free(g)
            for rank in range(ranks):
                cos_v[slot, rank] = c[rank * rows : (rank + 1) * rows]
                sin_v[slot, rank] = s[rank * rows : (rank + 1) * rows]
            tables.put(g)
            gather.arrived(g)
            loads.need(g == 0, 0)
            x = full[g].reshape(ranks * rows, model)
            for which in range(3):
                out = dot(x, w_v[which])
                for h in range(heads):
                    u = out[:, h * HDIM : (h + 1) * HDIM]
                    if which < 2:
                        u = u * c + swap_halves(u) * s
                    u = u.astype(BF)
                    at = (which * heads + h) * HDIM
                    for rank in range(ranks):
                        qkv_v[rank, g, :, at : at + HDIM] = u[rank * rows : (rank + 1) * rows]
            for store in stores:
                store.put(g)

        stream(line, groups, gather, arrived=project, extra=(2, scale_grad))

        @pl.loop(0, groups)
        def _(g):
            for store in stores:
                store.end(g)

        tables.end(groups)
        loads.begin(True, 3, 4)
        second = Gather(line, kept_grad, b_send, b_recv, b_across)
        third = Gather(line, full, c_send, c_recv, c_across)
        reduce = Reduce(line, part, near, far, acc, s1, s2, s3)
        reduce_back = Reduce(line, part, near, far, acc, t1, t2, t3)
        keep = Store(attended_v, attended, attended_sem)
        keep_ln = Store(full, kept_ln, kept_sem.at[1])
        keep_resid = Store(resid_v, resid, resid_sem)
        keep_low = Store(low_v, grad_low, result_sem)
        highs = Turns([(high_v, grad_resid)], tile_sem.at[pl.ds(1, 1)])
        hiddens = Turns([(squared_v, squared), (hidden_v, hidden_grad)], tile_sem.at[pl.ds(2, 2)])
        gains[...] = jnp.zeros_like(gains)
        first_column = line.t * columns
        place_grad.wait()

        def fetch(g):
            slot = lax.rem(g, 2)
            return pltpu.make_async_copy(kept_grad.at[g], grad_v.at[slot], tile_sem.at[0, slot])

        def part_of(which, h):
            return pl.ds(pl.multiple_of((which * heads + h) * HDIM, HDIM), HDIM)

        def attend_block(i, count):
            low = i + 1 - count
            start = query_starts(docs, i * QROWS)

            @pl.loop(0, heads)
            def _(h):
                q = qkv_v[pl.ds(i * span, span), :, :, part_of(0, h)].reshape(QROWS, HDIM)
                k = qkv_v[pl.ds(low * span, count * span), :, :, part_of(1, h)].reshape(count * QROWS, HDIM)
                weights = softmax_block(q, k, start, i * QROWS, low * QROWS, scaling)
                keys = pl.ds(pl.multiple_of(low * QROWS, QROWS), count * QROWS)
                done = dot(v_t[h, :, keys], weights.astype(BF)).T
                done = (done * live_ref[:, part_of(0, h)]).astype(BF)
                put_grouped(attended_v, done, i, own_tokens, rows, part_of(0, h))

        def attention(turn):
            @pl.when(turn == 0)
            def _():
                @pl.loop(0, heads)
                def _(h):
                    v_t[h] = qkv_v[:, :, :, part_of(2, h)].reshape(length, HDIM).T

                for i in range(min(reach - 1, blocks)):
                    attend_block(i, i + 1)

            @pl.when(turn == 1)
            def _():
                @pl.loop(reach - 1, blocks)
                def _(i):
                    attend_block(i, reach)

        def produce(g):
            keep.put(g)
            loads.need(g == 0, 1)
            for n in range(0, model, 512):
                out = dot(attended_v[g], wo_v[:, n : n + 512]).astype(BF)
                part[g, ..., n : n + 512] = out.reshape(chips, 2, rows, 512)

        def norm(g):
            reduce.last(g)
            total = x_ref[g].astype(F32) + acc[...]
            resid_v[g] = total
            keep_resid.put(g)
            lhat, _ = layer_norm(total)
            full[g, line.z, line.c] = (lhat * gain2[...] + bias2[...]).astype(BF)
            third.begin(g)

        def arrived(g):
            third.arrived(g)
            keep_ln.put(g)
            reduce.drain(g)

            @pl.when(g == 0)
            def _():
                fetch(0).start()

            fetch(g).wait()

            @pl.when(g + 1 < groups)
            def _():
                fetch(g + 1).start()

            loads.need(g == 0, 3, 4)

        def forward(g):
            slot = hiddens.free(g)
            limit = (jnp.broadcast_to(wide[pl.ds(g, 1), :], (HDIM, tokens_all)).T[:, :1] + 1) * (FF // 4)

            @pl.loop(0, columns // tile)
            def _(n):
                at = pl.ds(pl.multiple_of(n * tile, tile), tile)
                hidden = dot(full[g].reshape(tokens_all, model), up_v[:, at])
                ids = first_column + n * tile + lax.broadcasted_iota(jnp.int32, hidden.shape, 1)
                live = jnp.where(ids < limit, jnp.maximum(hidden, 0.0), 0.0)
                lifted[:, at] = live
                squared_v[slot, :, at] = (live * live).astype(BF)

        def backward(g):
            slot = lax.rem(g, 2)

            @pl.loop(0, columns // tile)
            def _(n):
                at = pl.ds(pl.multiple_of(n * tile, tile), tile)
                back = dot(grad_v[slot].reshape(tokens_all, model), down_v[at, :], NT)
                hidden_v[slot, :, at] = (back * (2.0 * lifted[:, at])).astype(BF)

            hiddens.put(g)

        def lower(g):
            slot = lax.rem(g, 2)

            @pl.loop(0, model // 256)
            def _(n):
                at = pl.ds(pl.multiple_of(n * 256, 256), 256)
                out = dot(hidden_v[slot], up_v[at, :], NT).astype(BF)
                part[g, :, :, :, at] = out.reshape(chips, 2, rows, 256)

        def finish(g):
            reduce_back.last(g)
            lhat, inv_std = layer_norm(resid_v[g])
            back = acc[...]
            gains[0:1] += jnp.sum(back * lhat, axis=0, keepdims=True)
            gains[1:2] += jnp.sum(back, axis=0, keepdims=True)
            back = back * gain2[...]
            back = dy_v[g].astype(F32) + inv_std * (back - row_mean(back) - lhat * row_mean(back * lhat))
            high_v[highs.free(g)] = back
            low_v[g] = back.astype(BF)
            highs.put(g)
            keep_low.put(g)

        @pl.loop(0, groups + back_at)
        def _(i):
            for n in range(hops):
                h, d = hops - n, n + 1
                within(i - hidden_at - 1 - hops + d, groups, functools.partial(reduce_back.step, d=d))
                within(i - normed_at - h, groups, functools.partial(third.hop, h=h))
                within(i - lead - 1 - hops + d, groups, functools.partial(reduce.step, d=d))
                within(i - h, groups, functools.partial(second.hop, h=h))
                if n == 0:
                    within(i - hidden_at, groups, arrived)
                for piece in (forward, backward, lower)[n * 3 // hops : (n + 1) * 3 // hops]:
                    within(i - hidden_at, groups, piece)
            within(i, groups, second.begin)
            within(i - hidden_at, groups, reduce_back.begin)
            within(i - normed_at, groups, norm)
            within(i - lead, groups, produce)
            within(i - lead, groups, reduce.begin)
            within(i - hops - 1, groups, second.arrived)
            within(i - back_at, groups, finish)
            within(i, lead, attention)

        second.drain()
        third.drain()
        pl.loop(0, groups)(reduce_back.drain)

        @pl.loop(0, groups)
        def _(g):
            for store in (keep, keep_ln, keep_resid, keep_low):
                store.end(g)

        highs.end(groups)
        hiddens.end(groups)

    table = jax.ShapeDtypeStruct((ranks, groups, rows, HDIM), F32)
    projected = jax.ShapeDtypeStruct((ranks, groups, rows, 3 * width), BF)
    full = jax.ShapeDtypeStruct((groups, chips, 2, rows, model), BF)
    attended = jax.ShapeDtypeStruct((groups, tokens_all, width), BF)
    high = jax.ShapeDtypeStruct((groups, rows, model), F32)
    low = jax.ShapeDtypeStruct((groups, rows, model), BF)
    hidden = jax.ShapeDtypeStruct((groups, tokens_all, columns), BF)
    return call(
        body,
        [tokens, cotangent, probs, gain, lengths, frequency, live, w_qkv, w_out, g_ln, b_ln, w_up, w_down, widths],
        [
            projected,
            full,
            table,
            table,
            attended,
            high,
            full,
            high,
            low,
            jax.ShapeDtypeStruct((2, model), F32),
            full,
            hidden,
            hidden,
        ],
        [
            *scratch_of(full, w_qkv, w_out, cotangent, w_up, w_down, projected),
            pltpu.VMEM((2, ranks, rows, HDIM), F32),
            pltpu.VMEM((2, ranks, rows, HDIM), F32),
            pltpu.VMEM((heads, HDIM, length), BF),
            *scratch_of(attended, low, high),
            pltpu.VMEM((2, rows, model), F32),
            pltpu.VMEM((2, chips, 2, rows, model), BF),
            pltpu.VMEM((tokens_all, columns), F32),
            pltpu.VMEM((2, tokens_all, columns), BF),
            pltpu.VMEM((2, tokens_all, columns), BF),
            *Gather.scratch(ranks, groups) * 3,
            *Reduce.scratch(ranks, groups, rows, model),
            *Reduce.scratch(ranks, groups, rows, model)[-3:],
            DMA((5,)),
            DMA((2, groups)),
            DMA((3, groups)),
            DMA,
            *[DMA((groups,))] * 3,
            DMA((4, groups)),
        ],
        0,
        in_specs=[VM, ANY, VM, VM, pl.BlockSpec(memory_space=pltpu.SMEM), VM, VM, ANY, ANY, VM, VM, ANY, ANY, VM],
        out_specs=[ANY] * 9 + [VM] + [ANY] * 3,
        flops=8 * length * model * (width + columns),
        moved=160 << 20,
    )


def hidden_weights(spread, inputs, hidden, first, turn_of, columns):
    n = turn_of
    side = min(256, spread.out.shape[1])

    @pl.loop(0, spread.out.shape[1] // side)
    def _(m):
        at = pl.ds(pl.multiple_of(first + m * side, side), side)
        to = pl.ds(pl.multiple_of(m * side, side), side)
        x = inputs[:, :, at]
        spread.out[n, to] = dot(
            x.reshape(x.shape[0] * x.shape[1], side), hidden[...].reshape(-1, columns), TN
        ).astype(BF)

    spread.begin(n)


def feed_out(
    own_grad, squared, hidden_grad, kept_ln, branch_grad, w_down, w_out, active, resid, cotangent, probs, ranks, sequences
):
    groups, rows, model = own_grad.shape
    columns, width = w_down.shape[0], w_out.shape[0]
    tokens = ranks * rows
    share = model // sequences
    half = share // 2

    def body(
        own, sq, hg, ln, bg, down, w, live, res, dy, p, result, probs_grad, kept, grad, land_down, land_up,
        full, g_send, g_recv, g_across, part, near, far, acc, s1, s2, s3, kept_sem,
        out_down, down_send, down_recv, out_up, up_send, up_recv, ln_v, bg_v, fetch_sem,
        sq_v, hg_v, down_v, res_v, dy_v, load_sem, result_v, back_v, result_sem, back_sem,
    ):
        line = Line(ranks, rows)
        gather = Gather(line, full, g_send, g_recv, g_across)
        reduce = Reduce(line, part, near, far, acc, s1, s2, s3)
        to_down = Spread(sequences, out_down, land_down, down_send, down_recv)
        to_up = Spread(sequences, out_up, land_up, up_send, up_recv, pl.ds(0, half))
        keep = Store(full, kept, kept_sem)
        keep_result = Store(result_v, result, result_sem)
        keep_back = Store(back_v, grad, back_sem, lambda ref, g: ref.at[:, g])

        def arrived(g):
            gather.arrived(g)
            keep.put(g)
            back = (dot(full[g].reshape(tokens, model), w[...], NT) * live[...]).astype(BF)
            for rank in range(ranks):
                back_v[rank, g] = back[rank * rows : (rank + 1) * rows]
            keep_back.put(g)

        def produce(g):
            loads.need(g == 0, 0, 1)

            @pl.loop(0, model // 256)
            def _(n):
                at = pl.ds(pl.multiple_of(n * 256, 256), 256)
                out = dot(sq_v[g], down_v[:, at]).astype(BF)
                part[g, :, :, :, at] = out.reshape(ranks // 2, 2, rows, 256)

        def finish(g):
            loads.need(g == 0, 3, 4)
            ffn = acc[...]
            result_v[g] = (res_v[g] + p[g, :, :1] * ffn).astype(BF)
            keep_result.put(g)
            probs_grad[g] = jnp.broadcast_to(
                jnp.sum(dy_v[g].astype(F32) * ffn, axis=1, keepdims=True), (rows, HDIM)
            )

        def fetches(step):
            at = pl.multiple_of(to_up.target(lax.rem(step + 1, sequences)) * share, share)
            return [
                pltpu.make_async_copy(ln.at[:, :, pl.ds(at, half)], ln_v, fetch_sem.at[0]),
                pltpu.make_async_copy(bg.at[:, :, pl.ds(at, share)], bg_v, fetch_sem.at[1]),
            ]

        def weights(step):
            n = lax.rem(step + 1, sequences)
            loads.need(step == 0, 2)
            for fetch in fetches(step):
                fetch.wait()
            side = min(256, columns)

            @pl.loop(0, columns // side)
            def _(m):
                at = pl.ds(pl.multiple_of(m * side, side), side)
                out_down[n, at] = dot(
                    sq_v[:, :, at].reshape(groups * tokens, side), bg_v[...].reshape(groups * tokens, share), TN
                ).astype(BF)

            to_down.begin(n)
            hidden_weights(to_up, ln_v, hg_v, 0, n, columns)

            @pl.when(step + 1 < sequences)
            def _():
                for fetch in fetches(step + 1):
                    fetch.start()

        def beside(turn):
            loads.begin(turn == 0, 0, 1, 2)

            @pl.when(turn == 0)
            def _():
                for fetch in fetches(0):
                    fetch.start()

            loads.begin(turn == 3, 3, 4)
            within(turn - 1, sequences, weights)

        loads = Loads(
            [
                (sq, sq_v),
                (down, down_v),
                (hg, hg_v),
                (res, res_v),
                (dy, dy_v),
                (own, full.at[:, line.z, line.c]),
            ],
            load_sem,
        )
        loads.begin(True, 5)
        line.barrier(sequences)
        loads.need(True, 5)
        stream(
            line, groups, gather, arrived, reduce, [produce], finish, 1, (max(sequences + 1, 4), beside)
        )

        @pl.loop(0, groups)
        def _(g):
            for store in (keep, keep_result, keep_back):
                store.end(g)

        to_down.end()
        to_up.end()

    kept = jax.ShapeDtypeStruct((groups, ranks // 2, 2, rows, model), BF)
    low = jax.ShapeDtypeStruct((groups, rows, model), BF)
    back = jax.ShapeDtypeStruct((ranks, groups, rows, width), BF)
    return call(
        body,
        [own_grad, squared, hidden_grad, kept_ln, branch_grad, w_down, w_out, active, resid, cotangent, probs],
        [
            low,
            jax.ShapeDtypeStruct((groups, rows, HDIM), F32),
            kept,
            back,
            jax.ShapeDtypeStruct((sequences, columns, share), BF),
            jax.ShapeDtypeStruct((sequences, share, columns), BF),
        ],
        [
            *scratch_of(kept),
            *Gather.scratch(ranks, groups),
            *Reduce.scratch(ranks, groups, rows, model),
            DMA((groups,)),
            *Spread.scratch(sequences, (columns, share)),
            *Spread.scratch(sequences, (half, columns)),
            pltpu.VMEM((groups, tokens, half), BF),
            pltpu.VMEM((groups, tokens, share), BF),
            DMA((2,)),
            *scratch_of(squared, hidden_grad, w_down, resid, cotangent),
            DMA((6,)),
            *scratch_of(low, back),
            DMA((groups,)),
            DMA((groups,)),
        ],
        3,
        in_specs=[ANY, ANY, ANY, ANY, ANY, ANY, VM, VM, ANY, ANY, VM],
        out_specs=[ANY, VM, ANY, ANY, ANY, ANY],
        flops=2 * groups * tokens * model * (3 * columns + width),
        moved=100 << 20,
    )


def project_back(
    grads, w_qkv, kept_x, attended, attn_grad, kept_ln, hidden_grad, landed_up, tokens, gain, grad_resid, gains, ranks, sequences
):
    groups, tokens_all, width = grads[0].shape
    rows = tokens_all // ranks
    model = w_qkv.shape[1]
    columns = hidden_grad.shape[2]
    share = model // sequences
    half = share // 2

    def body(
        gq, gk, gv, w, xs, a, ga, ln, hg, up_in, x_ref, gain_ref, g_res, gain_parts,
        tokens_grad, totals, land_qkv, land_out, land_up,
        part, near, far, acc, s1, s2, s3,
        out_qkv, qkv_send, qkv_recv, out_out, out_send, out_recv, out_up, up_send, up_recv,
        x_v, ga_v, ln_v, fetch_sem, group_v, group_sem, w_v, a_v, hg_v, own_v, res_v, load_sem,
        mine, terms, t_send, t_recv, sums, d_send, d_recv, g_q, g_k, g_v, grad_v, grad_sem,
    ):
        line = Line(ranks, rows)
        me = lax.axis_index("dp")
        reduce = Reduce(line, part, near, far, acc, s1, s2, s3)
        to_qkv = Spread(sequences, out_qkv, land_qkv, qkv_send, qkv_recv)
        to_out = Spread(sequences, out_out, land_out, out_send, out_recv)
        to_up = Spread(sequences, out_up, land_up, up_send, up_recv, pl.ds(half, half))
        parts = (g_q, g_k, g_v)
        loads = Loads(
            [(w, w_v), (a, a_v), (hg, hg_v), (x_ref, own_v), (g_res, res_v), (gq, g_q), (gk, g_k), (gv, g_v)],
            load_sem,
        )
        keep_grad = Store(grad_v, tokens_grad, grad_sem)

        def group_fetch(g):
            slot = lax.rem(g, 2)
            return pltpu.make_async_copy(xs.at[g], group_v.at[slot], group_sem.at[slot])

        loads.begin(True, 0, 5, 6, 7)
        group_fetch(0).start()
        mine[0:1] = jnp.zeros((1, model), F32)
        mine[1:3] = gain_parts[...]

        def produce(g):
            loads.need(g == 0, 0, 5, 6, 7)
            group_fetch(g).wait()

            @pl.when(g + 1 < groups)
            def _():
                group_fetch(g + 1).start()

            slot = lax.rem(g, 2)

            @pl.loop(0, model // 256)
            def _(n):
                at = pl.ds(pl.multiple_of(n * 256, 256), 256)
                out = dot(g_q[g], w_v[0, at], NT)
                out += dot(g_k[g], w_v[1, at], NT)
                out += dot(g_v[g], w_v[2, at], NT)
                part[g, :, :, :, at] = out.astype(BF).reshape(ranks // 2, 2, rows, 256)
                mine[0:1, at] += jnp.sum(out * group_v[slot, :, at].astype(F32), axis=0, keepdims=True)

        def finish(g):
            loads.need(g == 0, 3, 4)
            x = own_v[g].astype(F32)
            scale = lax.rsqrt(row_mean(x * x) + EPSILON)
            hat = x * scale
            back = acc[...] * gain_ref[...]
            grad_v[g] = res_v[g] + scale * (back - hat * row_mean(back * hat))
            keep_grad.put(g)

        def fetches(step):
            at = pl.multiple_of(to_qkv.target(lax.rem(step + 1, sequences)) * share, share)
            return [
                pltpu.make_async_copy(ln.at[:, :, pl.ds(at + half, half)], ln_v, fetch_sem.at[0]),
                pltpu.make_async_copy(xs.at[:, :, pl.ds(at, share)], x_v, fetch_sem.at[1]),
                pltpu.make_async_copy(ga.at[:, :, pl.ds(at, share)], ga_v, fetch_sem.at[2]),
            ]

        def weights(piece):
            step = piece // 2
            n = lax.rem(step + 1, sequences)

            @pl.when(lax.rem(piece, 2) == 0)
            def _():
                loads.need(step == 0, 1, 2)
                fetches(step)[0].wait()
                hidden_weights(to_up, ln_v, hg_v, 0, n, columns)

                @pl.when(step + 1 < sequences)
                def _():
                    fetches(step + 1)[0].start()

            @pl.when(lax.rem(piece, 2) == 1)
            def _():
                for fetch in fetches(step)[1:]:
                    fetch.wait()

                @pl.loop(0, share // 256)
                def _(m):
                    at = pl.ds(pl.multiple_of(m * 256, 256), 256)
                    x = x_v[:, :, at].reshape(groups * tokens_all, 256)
                    for which in range(3):
                        out_qkv[n, which, at] = dot(
                            x, parts[which][...].reshape(groups * tokens_all, width), TN
                        ).astype(BF)

                to_qkv.begin(n)
                out_out[n] = dot(
                    a_v[...].reshape(groups * tokens_all, width), ga_v[...].reshape(groups * tokens_all, share), TN
                ).astype(BF)
                to_out.begin(n)

                @pl.when(step + 1 < sequences)
                def _():
                    for fetch in fetches(step + 1)[1:]:
                        fetch.start()

        def to_rank(n, source=None):
            return copy_to(
                mine,
                terms.at[line.t if source is None else source],
                t_send.at[n],
                t_recv.at[n],
                lax.rem(line.t + n, ranks),
            )

        def to_sequence(n, source=None):
            return pltpu.make_async_remote_copy(
                src_ref=sums.at[me],
                dst_ref=sums.at[me if source is None else source],
                send_sem=d_send.at[n],
                recv_sem=d_recv.at[n],
                device_id={"dp": lax.rem(me + n, sequences)},
                device_id_type=MESH,
            )

        def beside(turn):
            loads.begin(turn == 0, 1, 2)
            loads.begin(turn == 2, 3, 4)

            @pl.when(turn == 0)
            def _():
                for fetch in fetches(0):
                    fetch.start()

            within(turn - 1, 2 * sequences, weights)

            @pl.when(turn == groups)
            def _():
                mine[0:1] = mine[0:1] / gain_ref[...]
                terms[line.t] = mine[...]

                @pl.loop(1, ranks)
                def _(n):
                    to_rank(n).start()

            @pl.when(turn == groups + 1)
            def _():
                @pl.loop(1, ranks)
                def _(n):
                    to_rank(n).wait_send()
                    to_rank(n, lax.rem(line.t + ranks - n, ranks)).wait_recv()

                total = terms[0]
                for n in range(1, ranks):
                    total += terms[n]
                sums[me] = total

                @pl.loop(1, sequences)
                def _(n):
                    to_sequence(n).start()

            @pl.when(turn == groups + 2)
            def _():
                @pl.loop(1, sequences)
                def _(n):
                    to_sequence(n).wait_send()
                    to_sequence(n, lax.rem(me + sequences - n, sequences)).wait_recv()

                total = sums[0]
                for n in range(1, sequences):
                    total += sums[n]
                totals[...] = total

        line.barrier_all(sequences)
        stream(
            line, groups, None, None, reduce, [produce], finish, extra=(max(groups + 3, 2 * sequences + 1), beside)
        )

        @pl.loop(0, groups)
        def _(g):
            keep_grad.end(g)

        to_qkv.end()
        to_out.end()
        to_up.end()

    return call(
        body,
        [*grads, w_qkv, kept_x, attended, attn_grad, kept_ln, hidden_grad, landed_up, tokens, gain, grad_resid, gains],
        [
            jax.ShapeDtypeStruct((groups, rows, model), F32),
            jax.ShapeDtypeStruct((3, model), F32),
            jax.ShapeDtypeStruct((sequences, 3, share, width), BF),
            jax.ShapeDtypeStruct((sequences, width, share), BF),
            jax.ShapeDtypeStruct(landed_up.shape, BF),
        ],
        [
            *Reduce.scratch(ranks, groups, rows, model),
            *Spread.scratch(sequences, (3, share, width)),
            *Spread.scratch(sequences, (width, share)),
            *Spread.scratch(sequences, (half, columns)),
            pltpu.VMEM((groups, tokens_all, share), BF),
            pltpu.VMEM((groups, tokens_all, share), BF),
            pltpu.VMEM((groups, tokens_all, half), BF),
            DMA((3,)),
            pltpu.VMEM((2, tokens_all, model), BF),
            DMA((2,)),
            *scratch_of(w_qkv, attended, hidden_grad, tokens, grad_resid),
            DMA((8,)),
            pltpu.VMEM((3, model), F32),
            pltpu.VMEM((ranks, 3, model), F32),
            DMA((ranks,)),
            DMA((ranks,)),
            pltpu.VMEM((sequences, 3, model), F32),
            DMA((sequences,)),
            DMA((sequences,)),
            *scratch_of(*grads, grad_resid),
            DMA((groups,)),
        ],
        4,
        in_specs=[ANY] * 11 + [VM, ANY, VM],
        out_specs=[ANY, VM, ANY, ANY, ANY],
        flops=12 * groups * tokens_all * model * width,
        moved=60 << 20,
        aliases={9: 4},
    )


def shards(
    tokens,
    cotangent,
    first_norm_gain,
    w_qkv,
    w_out,
    g_ln,
    b_ln,
    w_up,
    w_down,
    probs,
    lengths,
    head_count,
    widths,
):
    length_all = widths.shape[0]
    own_tokens, model = tokens.shape
    ranks = length_all // own_tokens
    sequences = lax.axis_size("dp")
    groups, rows = GROUPS, own_tokens // GROUPS
    width = w_out.shape[0]
    heads_here = width // HDIM
    half = HDIM // 2
    frequency = 10000.0 ** (-jnp.arange(half, dtype=F32) / half)
    frequency = jnp.concatenate([frequency, frequency]).reshape(1, HDIM)
    w_qkv_t = w_qkv.transpose(1, 0, 2)
    x = tokens.reshape(groups, rows, model)
    dy = cotangent.reshape(groups, rows, model)
    first_norm_gain, g_ln, b_ln = (v.reshape(1, model) for v in (first_norm_gain, g_ln, b_ln))
    p = jnp.broadcast_to(probs.reshape(groups, rows, 1), (groups, rows, HDIM))
    head_ids = lax.axis_index("tensor") * heads_here + jnp.arange(heads_here, dtype=jnp.int32)
    active = (head_ids < head_count[0]).astype(jnp.int32)
    live = jnp.repeat(active.astype(F32), HDIM).reshape(1, width)
    wide = widths.reshape(ranks, groups, rows).swapaxes(0, 1).reshape(groups, ranks * rows)

    (
        qkv, kept_x, cosines, sines, attended, resid, kept_ffn_grad, grad_resid, grad_low, gains, kept_ln, squared,
        grad_hidden,
    ) = front(
        x, dy, p, first_norm_gain, lengths, frequency, live, w_qkv_t, w_out, g_ln, b_ln, w_up, w_down, wide, ranks
    )
    qkv = qkv.reshape(length_all, 3 * width)
    cosines, sines = cosines.reshape(length_all, HDIM), sines.reshape(length_all, HDIM)
    whole = lambda kept: kept.reshape(groups, ranks * rows, model)
    result, probs_grad, kept_attn_grad, grad_attended, land_down, land_up = feed_out(
        grad_low, squared, grad_hidden, whole(kept_ln), whole(kept_ffn_grad), w_down, w_out, live, resid, dy, p, ranks, sequences
    )
    grad_proj = attend_back(
        qkv,
        grad_attended.reshape(length_all, width),
        lengths,
        active,
        cosines,
        sines,
        width,
        groups,
        own_tokens,
    )
    tokens_grad, totals, land_qkv, land_out, land_up = project_back(
        grad_proj, w_qkv_t, whole(kept_x), attended, whole(kept_attn_grad), whole(kept_ln), grad_hidden, land_up, x, first_norm_gain,
        grad_resid, gains, ranks, sequences,
    )
    add_up = lambda landed: jnp.sum(landed.astype(F32), axis=0)
    return (
        result.reshape(own_tokens, model),
        tokens_grad.reshape(own_tokens, model),
        probs_grad[:, :, 0].reshape(own_tokens),
        totals[0],
        add_up(land_qkv).transpose(1, 0, 2),
        add_up(land_out),
        totals[1],
        totals[2],
        add_up(land_up),
        add_up(land_down),
    )


def solution(mesh):
    placed = (
        P(("dp", "tensor"), None),
        P(("dp", "tensor"), None),
        P(),
        P(None, None, "tensor"),
        P("tensor", None),
        P(),
        P(),
        P(None, "tensor"),
        P("tensor", None),
        P(("dp", "tensor")),
        P("dp", None),
        P("dp"),
        P("dp"),
    )
    return jax.shard_map(
        shards,
        mesh=mesh,
        in_specs=placed,
        out_specs=(
            P(("dp", "tensor"), None),
            P(("dp", "tensor"), None),
            P(("dp", "tensor")),
            P(),
            P("dp", None, "tensor"),
            P("tensor", "dp"),
            P(),
            P(),
            P("dp", "tensor"),
            P("tensor", "dp"),
        ),
        check_vma=False,
    )
```

```python
import functools

import jax
import jax.numpy as jnp
import numpy as np
from jax import lax
from jax.experimental import pallas as pl
from jax.experimental.pallas import tpu as pltpu
from jax.sharding import PartitionSpec as P

HDIM = 128
FF = 8192
EPSILON = 1e-05
NEGATIVE = -1e30
MAXDOC = 1024
GROUPS = 8
QROWS = 256
MESH = pl.DeviceIdType.MESH
BF = jnp.bfloat16
F32 = jnp.float32
ANY = pl.BlockSpec(memory_space=pl.ANY)
VM = pl.BlockSpec(memory_space=pltpu.VMEM)
SM = pl.BlockSpec(memory_space=pltpu.SMEM)
DMA = pltpu.SemaphoreType.DMA
NT = (((1,), (1,)), ((), ()))
TN = (((0,), (0,)), ((), ()))


def dot(a, b, dims=(((1,), (0,)), ((), ()))):
    return lax.dot_general(a, b, dims, preferred_element_type=F32)


class Line:
    def __init__(self, ranks, rows):
        self.ranks, self.chips, self.rows = ranks, ranks // 2, rows
        self.t = lax.axis_index("tensor")
        self.z, self.c = self.t // 2, lax.rem(self.t, 2)
        self.has_up, self.has_down = self.z < self.chips - 1, self.z > 0
        self.up = jnp.minimum(self.t + 2, ranks - 1)
        self.down = jnp.maximum(self.t - 2, 0)
        self.partner = self.t + 1 - 2 * self.c

    def barrier(self, dp_size=0):
        sem = pltpu.get_barrier_semaphore()
        pl.semaphore_signal(sem, inc=1, device_id={"tensor": self.partner}, device_id_type=MESH)

        @pl.when(self.has_up)
        def _():
            pl.semaphore_signal(sem, inc=1, device_id={"tensor": self.up}, device_id_type=MESH)

        @pl.when(self.has_down)
        def _():
            pl.semaphore_signal(sem, inc=1, device_id={"tensor": self.down}, device_id_type=MESH)

        d = lax.axis_index("dp")
        for step in range(1, dp_size):
            pl.semaphore_signal(
                sem, inc=1, device_id={"dp": lax.rem(d + step, dp_size)}, device_id_type=MESH
            )
        links = self.has_up.astype(jnp.int32) + self.has_down.astype(jnp.int32)
        pl.semaphore_wait(sem, 1 + max(dp_size - 1, 0) + links)

    def barrier_all(self, dp_size):
        sem = pltpu.get_barrier_semaphore()
        for n in range(1, self.ranks):
            pl.semaphore_signal(
                sem, inc=1, device_id={"tensor": lax.rem(self.t + n, self.ranks)}, device_id_type=MESH
            )
        d = lax.axis_index("dp")
        for n in range(1, dp_size):
            pl.semaphore_signal(
                sem, inc=1, device_id={"dp": lax.rem(d + n, dp_size)}, device_id_type=MESH
            )
        pl.semaphore_wait(sem, self.ranks - 1 + dp_size - 1)


def copy_to(src, dst, send, recv, rank):
    return pltpu.make_async_remote_copy(
        src_ref=src,
        dst_ref=dst,
        send_sem=send,
        recv_sem=recv,
        device_id={"tensor": rank},
        device_id_type=MESH,
    )


class Gather:
    def __init__(self, line, full, send, recv, across_recv):
        self.l, self.full, self.send, self.recv, self.across_recv = line, full, send, recv, across_recv

    @staticmethod
    def scratch(ranks, groups):
        return [DMA((3, ranks // 2)), DMA((groups, ranks // 2)), DMA((groups,))]

    def along(self, g, z, up):
        l = self.l
        place = self.full.at[g, z, l.c]
        return copy_to(
            place,
            place,
            self.send.at[0 if up else 1, z],
            self.recv.at[0 if g == slice(None) else g, z],
            l.up if up else l.down,
        )

    def across(self, g, column):
        place = self.full.at[g, :, column]
        return copy_to(
            place, place, self.send.at[2, 0], self.across_recv.at[0 if g == slice(None) else g], self.l.partner
        )

    def pass_on(self, g, z, up):
        @pl.when(self.l.has_up if up else self.l.has_down)
        def _():
            self.along(g, z, up).start()

    def begin(self, g):
        self.pass_on(g, self.l.z, True)
        self.pass_on(g, self.l.z, False)

    def hop(self, g, h):
        l = self.l

        @pl.when(l.z - h >= 0)
        def _():
            self.along(g, l.z - h, True).wait_recv()
            self.pass_on(g, l.z - h, True)

        @pl.when(l.z + h <= l.chips - 1)
        def _():
            self.along(g, l.z + h, False).wait_recv()
            self.pass_on(g, l.z + h, False)

        if h == l.chips - 1:
            self.across(g, l.c).start()

    def arrived(self, g):
        self.across(g, 1 - self.l.c).wait_recv()

    def drain(self):
        l, every = self.l, slice(None)
        for z in range(l.chips):

            @pl.when(l.has_up & (l.z >= z))
            def _():
                self.along(every, z, True).wait_send()

            @pl.when(l.has_down & (l.z <= z))
            def _():
                self.along(every, z, False).wait_send()

        self.across(every, l.c).wait_send()


class Reduce:
    def __init__(self, line, part, near, far, acc, send, near_recv, far_recv):
        self.l, self.part, self.near, self.far, self.acc = line, part, near, far, acc
        self.send, self.near_recv, self.far_recv = send, near_recv, far_recv

    @staticmethod
    def scratch(ranks, groups, rows, width):
        chips = ranks // 2
        return [
            pltpu.VMEM((groups, chips, 2, rows, width), BF),
            pltpu.VMEM((groups, chips, rows, width), BF),
            pltpu.VMEM((groups, chips + 1, rows, width), BF),
            pltpu.VMEM((rows, width), F32),
            DMA((groups, chips + 1)),
            DMA((groups,)),
            DMA((groups, chips + 1)),
        ]

    def across(self, g):
        l = self.l
        return copy_to(
            self.part.at[g, :, 1 - l.c],
            self.near.at[g],
            self.send.at[g, l.chips],
            self.near_recv.at[g],
            l.partner,
        )

    def along(self, g, z, up, receive=False):
        l = self.l
        at = l.z if receive else jnp.where(up, l.z + 1, l.z - 1)
        slot = z if up else jnp.where(z == at, l.chips, z)
        return copy_to(
            self.part.at[g, z, l.c],
            self.far.at[g, slot],
            self.send.at[g, z],
            self.far_recv.at[g, slot],
            l.up if up else l.down,
        ), slot

    def begin(self, g):
        self.across(g).start()

    def add(self, g, z, slots, total=None):
        side = 512

        @pl.loop(0, self.part.shape[-1] // side)
        def _(n):
            at = pl.ds(pl.multiple_of(n * side, side), side)
            value = self.part[g, z, self.l.c, :, at].astype(F32) + self.near[g, z, :, at].astype(F32)
            for slot in slots:
                value += self.far[g, slot, :, at].astype(F32)
            if total is None:
                self.part[g, z, self.l.c, :, at] = value.astype(BF)
            else:
                total[:, at] = value

    def step(self, g, d):
        l = self.l
        if d == l.chips - 1:
            self.across(g).wait_recv()

        def send(z, up):
            further = l.has_down if up else l.has_up

            @pl.when(further)
            def _():
                copy, slot = self.along(g, z, up, receive=True)
                copy.wait_recv()
                self.add(g, z, [slot])

            @pl.when(jnp.logical_not(further))
            def _():
                self.add(g, z, [])

            self.along(g, z, up)[0].start()

        @pl.when(l.z + d <= l.chips - 1)
        def _():
            send(l.z + d, True)

        @pl.when(l.z - d >= 0)
        def _():
            send(l.z - d, False)

    def last(self, g):
        l = self.l

        @pl.when(l.has_down & l.has_up)
        def _():
            self.along(g, l.z, True, receive=True)[0].wait_recv()
            self.along(g, l.z, False, receive=True)[0].wait_recv()
            self.add(g, l.z, [l.z, l.chips], self.acc)

        @pl.when(jnp.logical_not(l.has_up))
        def _():
            self.along(g, l.z, True, receive=True)[0].wait_recv()
            self.add(g, l.z, [l.z], self.acc)

        @pl.when(jnp.logical_not(l.has_down))
        def _():
            self.along(g, l.z, False, receive=True)[0].wait_recv()
            self.add(g, l.z, [l.chips], self.acc)

    def drain(self, g):
        l = self.l
        self.across(g).wait_send()
        for z in range(l.chips):

            @pl.when(l.z != z)
            def _():
                copy_to(
                    self.part.at[g, z, l.c],
                    self.far.at[g, z],
                    self.send.at[g, z],
                    self.far_recv.at[g, z],
                    l.partner,
                ).wait_send()


def within(value, limit, body):
    pl.when((value >= 0) & (value < limit))(lambda: body(value))


def swap_halves(field):
    return pltpu.roll(field, HDIM // 2, axis=1)


def call(body, ins, outs, scratch, ident, in_specs=None, out_specs=None, limit=60, flops=0, moved=0, aliases=None):
    return pl.pallas_call(
        body,
        out_shape=outs,
        in_specs=in_specs or [VM] * len(ins),
        out_specs=out_specs or [VM] * len(outs),
        scratch_shapes=scratch,
        compiler_params=pltpu.CompilerParams(
            collective_id=ident, has_side_effects=True, vmem_limit_bytes=limit << 20
        ),
        input_output_aliases=aliases or {},
        cost_estimate=pl.CostEstimate(flops=flops, bytes_accessed=moved, transcendentals=0),
    )(*ins)


def stream(line, groups, gather=None, arrived=None, reduce=None, produce=(), finish=None, lead=0, extra=None):
    hops = line.chips - 1
    produce = list(produce)
    between = len(produce) > 1
    turns = groups + hops + 1 + (lead + 1 if reduce else 0)

    @pl.loop(0, turns)
    def _(i):
        for n in range(hops):
            if gather:
                within(i - hops + n, groups, functools.partial(gather.hop, h=hops - n))
            if reduce:
                d = n + 1
                within(i - lead - 1 - hops + d, groups, functools.partial(reduce.step, d=d))
            if n == hops - 1 and gather:
                within(i, groups, gather.begin)
            if between:
                if n == 0:
                    within(i - hops - 1, groups, arrived)
                for piece in produce[n * len(produce) // hops : (n + 1) * len(produce) // hops]:
                    within(i - lead, groups, piece)
        if not between:
            for piece in produce:
                within(i - lead, groups, piece)
        if reduce:
            within(i - lead, groups, reduce.begin)
        if arrived and not between:
            within(i - hops - 1, groups, arrived)
        if reduce:

            def end(g):
                reduce.last(g)
                finish(g)

            within(i - lead - 2 - hops, groups, end)
        if extra:
            within(i, min(extra[0], turns), extra[1])

    if extra:

        @pl.loop(min(extra[0], turns), extra[0])
        def _(i):
            extra[1](i)

    if gather:
        gather.drain()
    if reduce:
        pl.loop(0, groups)(reduce.drain)


def starts_of(lengths, places):
    end, start = jnp.int32(0), jnp.zeros_like(places)
    for length in lengths:
        end = end + length
        start = start + jnp.where(places >= end, length, 0)
    return start


def softmax_block(q, k, start, first_query, first_key, scaling):
    raw = dot(k, q, NT)
    keys = first_key + lax.broadcasted_iota(jnp.int32, raw.shape, 0)
    queries = first_query + lax.broadcasted_iota(jnp.int32, raw.shape, 1)
    raw = jnp.where((keys <= queries) & (keys >= start), raw * scaling, NEGATIVE)
    exponent = jnp.exp(raw - jnp.max(raw, axis=0, keepdims=True))
    return exponent * (1.0 / jnp.sum(exponent, axis=0, keepdims=True))


def query_starts(lengths, first):
    places = first + lax.broadcasted_iota(jnp.int32, (8, QROWS), 1)
    return starts_of([lengths[0, n] for n in range(lengths.shape[1])], places)[:1]


def weight_rows(i, reach):
    ramp = reach * (reach - 1) // 2
    if isinstance(i, int) and i < reach:
        return i * (i + 1) // 2 * QROWS
    return (ramp + (i - reach + 1) * reach) * QROWS


def put_grouped(out, block, i, own_tokens, rows, at=slice(None)):
    for n in range(0, QROWS, rows):
        rank, inside = divmod(n, own_tokens)
        rank += i * (QROWS // own_tokens)
        out[inside // rows, pl.ds(pl.multiple_of(rank * rows, rows), rows), at] = block[n : n + rows]


def attend_back(qkv, grad, kept_weights, count, cosines, sines, width, groups, own_tokens):
    length, heads = qkv.shape[0], width // HDIM
    scaling = HDIM ** (-0.5)
    reach = MAXDOC // QROWS + 1
    rows_own = own_tokens // groups

    def body(active, q, k, v, g, cos, sin, kept, g_q, g_k, g_v, k_t, sum_k, sum_v):
        live = lax.axis_index("tensor") * heads + pl.program_id(0) < active[0]

        @pl.when(jnp.logical_not(live))
        def _():
            g_q[...] = jnp.zeros_like(g_q)
            g_k[...] = jnp.zeros_like(g_k)
            g_v[...] = jnp.zeros_like(g_v)

        def rotate_back(d, rows):
            return (d * cos[rows] + swap_halves(d * sin[rows])).astype(BF)

        @pl.when(live)
        def _():
            k_t[...] = k[...].T
            sum_k[...] = jnp.zeros_like(sum_k)
            sum_v[...] = jnp.zeros_like(sum_v)
            def back_block(i, count):
                low = i + 1 - count
                rows = pl.ds(pl.multiple_of(i * QROWS, QROWS), QROWS)
                keys = pl.ds(pl.multiple_of(low * QROWS, QROWS), count * QROWS)
                weights = kept[0, pl.ds(weight_rows(i, reach), count * QROWS)]
                sum_v[keys] += dot(weights, g[rows])
                weights = weights.astype(F32)
                g_weights = dot(v[keys], g[rows], NT)
                inner = jnp.sum(weights * g_weights, axis=0, keepdims=True)
                g_scores = (weights * (g_weights - inner)).astype(BF)
                sum_k[keys] += dot(g_scores, q[rows])
                back = rotate_back(dot(k_t[:, keys], g_scores).T * scaling, rows)
                put_grouped(g_q, back, i, own_tokens, rows_own)

            for i in range(length // QROWS):
                back_block(i, min(i + 1, reach))

            for i in range(length // QROWS):
                rows = pl.ds(pl.multiple_of(i * QROWS, QROWS), QROWS)
                put_grouped(g_k, rotate_back(sum_k[rows] * scaling, rows), i, own_tokens, rows_own)
                put_grouped(g_v, sum_v[rows].astype(BF), i, own_tokens, rows_own)

    column = lambda n: pl.BlockSpec((length, HDIM), lambda h, live: (0, n * heads + h))
    table = pl.BlockSpec((length, HDIM), lambda h, live: (0, 0))
    return pl.pallas_call(
        body,
        out_shape=[jax.ShapeDtypeStruct((groups, length // groups, width), BF)] * 3,
        grid_spec=pltpu.PrefetchScalarGridSpec(
            num_scalar_prefetch=1,
            grid=(heads,),
            in_specs=[
                column(0),
                column(1),
                column(2),
                column(0),
                table,
                table,
                pl.BlockSpec((1, *kept_weights.shape[1:]), lambda h, live: (h, 0, 0)),
            ],
            out_specs=[pl.BlockSpec((groups, length // groups, HDIM), lambda h, live: (0, 0, h))] * 3,
            scratch_shapes=[
                pltpu.VMEM((HDIM, length), BF),
                pltpu.VMEM((length, HDIM), F32),
                pltpu.VMEM((length, HDIM), F32),
            ],
        ),
        compiler_params=pltpu.CompilerParams(vmem_limit_bytes=60 << 20),
        cost_estimate=pl.CostEstimate(flops=10 << 30, bytes_accessed=16 << 20, transcendentals=0),
    )(count, qkv, qkv, qkv, grad, cosines, sines, kept_weights)


class Spread:
    def __init__(self, size, out, land, send, recv, rows=None):
        self.size, self.out, self.land, self.send, self.recv = size, out, land, send, recv
        self.rows = rows
        self.me = lax.axis_index("dp")

    def target(self, n):
        return lax.rem(self.me + n, self.size)

    def copy(self, n, source=None):
        return pltpu.make_async_remote_copy(
            src_ref=self.out.at[n],
            dst_ref=self.place(self.me if source is None else source),
            send_sem=self.send.at[n],
            recv_sem=self.recv.at[n],
            device_id={"dp": self.target(n)},
            device_id_type=MESH,
        )

    def place(self, source):
        return self.land.at[source] if self.rows is None else self.land.at[source, self.rows]

    def own(self):
        return pltpu.make_async_copy(self.out.at[0], self.place(self.me), self.send.at[0])

    def begin(self, n):
        @pl.when(n == 0)
        def _():
            self.own().start()

        @pl.when(n != 0)
        def _():
            self.copy(n).start()

    def end(self):
        self.own().wait()

        @pl.loop(1, self.size)
        def _(n):
            self.copy(n).wait_send()
            self.copy(n, lax.rem(self.me + self.size - n, self.size)).wait_recv()

    @staticmethod
    def scratch(size, shape):
        return [pltpu.VMEM((size, *shape), BF), DMA((size,)), DMA((size,))]


class Loads:
    def __init__(self, pairs, sems):
        self.copies = [
            pltpu.make_async_copy(source, held, sems.at[n]) for n, (source, held) in enumerate(pairs)
        ]

    def begin(self, first, *which):
        @pl.when(first)
        def _():
            for n in which:
                self.copies[n].start()

    def need(self, first, *which):
        @pl.when(first)
        def _():
            for n in which:
                self.copies[n].wait()


class Store:
    def __init__(self, held, out, sems, at=lambda ref, g: ref.at[g]):
        self.held, self.out, self.sems, self.at = held, out, sems, at

    def copy(self, g):
        return pltpu.make_async_copy(self.at(self.held, g), self.at(self.out, g), self.sems.at[g])

    def put(self, g):
        self.copy(g).start()

    def end(self, g):
        self.copy(g).wait()


class Turns:
    def __init__(self, pairs, sems, at=lambda ref, g: ref.at[g]):
        self.pairs, self.sems, self.at = pairs, sems, at

    def each(self, g):
        return [
            pltpu.make_async_copy(held.at[lax.rem(g, 2)], self.at(out, g), self.sems.at[n, g])
            for n, (held, out) in enumerate(self.pairs)
        ]

    def free(self, g):
        @pl.when(g >= 2)
        def _():
            for copy in self.each(g - 2):
                copy.wait()

        return lax.rem(g, 2)

    def put(self, g):
        for copy in self.each(g):
            copy.start()

    def end(self, groups):
        for g in range(max(groups - 2, 0), groups):
            for copy in self.each(g):
                copy.wait()


def scratch_of(*arrays):
    return [pltpu.VMEM(a.shape, a.dtype) for a in arrays]


def row_mean(field):
    return jnp.mean(field, axis=1, keepdims=True)


def layer_norm(resid):
    centred = resid - row_mean(resid)
    inv_std = lax.rsqrt(row_mean(centred * centred) + EPSILON)
    return centred * inv_std, inv_std


def front(
    tokens, cotangent, probs, gain, lengths, frequency, count, w_qkv, w_out, g_ln, b_ln, w_up, w_down, widths, ranks
):
    width, columns = w_out.shape[0], w_up.shape[1]
    tile = min(256, columns)
    groups, rows, model = tokens.shape
    heads = width // HDIM
    chips = ranks // 2
    own_tokens = groups * rows
    length = ranks * own_tokens
    shift = rows.bit_length() - 1
    scaling = HDIM ** (-0.5)
    reach = MAXDOC // QROWS + 1
    span = QROWS // own_tokens
    blocks = length // QROWS
    lead = 2
    hops = chips - 1
    tokens_all = ranks * rows
    normed_at = lead + 2 + hops
    hidden_at = normed_at + hops + 1
    back_at = hidden_at + 2 + hops

    def body(
        x_ref, dy, p, gain_ref, docs, freq, active, w, wo, gain2, bias2, up, down, wide,
        qkv, kept_x, cos_out, sin_out, attended, resid, kept_grad, grad_resid, grad_low, gains, kept_ln, squared,
        hidden_grad, kept_weights,
        full, w_v, wo_v, dy_v, up_v, down_v, qkv_v, cos_v, sin_v, v_t, attended_v, low_v, resid_v, high_v, grad_v,
        lifted, squared_v, hidden_v,
        a_send, a_recv, a_across, b_send, b_recv, b_across, c_send, c_recv, c_across,
        part, near, far, acc, s1, s2, s3, t1, t2, t3,
        load_sem, kept_sem, out_sem, place_sem, attended_sem, resid_sem, result_sem, tile_sem, weights_v, weights_sem,
    ):
        line = Line(ranks, rows)
        loads = Loads([(w, w_v), (wo, wo_v), (dy, dy_v), (up, up_v), (down, down_v)], load_sem)

        @pl.loop(0, groups)
        def _(g):
            x = x_ref[g].astype(F32)
            normal = x * lax.rsqrt(row_mean(x * x) + EPSILON) * gain_ref[...]
            full[g, line.z, line.c] = normal.astype(BF)

        line.barrier()
        gather = Gather(line, full, a_send, a_recv, a_across)
        tables = Turns([(cos_v, cos_out), (sin_v, sin_out)], out_sem.at[pl.ds(1, 2)], lambda ref, g: ref.at[:, g])
        stores = [
            Store(full, kept_x, kept_sem.at[0]),
            Store(qkv_v, qkv, out_sem.at[0], lambda ref, g: ref.at[:, g]),
        ]
        place_grad = pltpu.make_async_copy(low_v, kept_grad.at[:, line.z, line.c], place_sem)

        def scale_grad(turn):
            loads.begin(turn == 0, 0, 1, 2)

            @pl.when(turn == 1)
            def _():
                loads.need(True, 2)

                @pl.loop(0, groups)
                def _(g):
                    low_v[g] = (dy_v[g].astype(F32) * p[g, :, :1]).astype(BF)

                place_grad.start()

        def project(g):
            r = lax.broadcasted_iota(jnp.int32, (ranks * rows, HDIM), 0)
            lane = lax.broadcasted_iota(jnp.int32, (ranks * rows, HDIM), 1)
            places = lax.shift_right_logical(r, shift) * own_tokens + g * rows + (r & (rows - 1))
            starts = starts_of([docs[0, n] for n in range(docs.shape[1])], places)
            angles = (places - starts).astype(F32) * freq[...]
            c = jnp.cos(angles)
            s = jnp.sin(angles)
            s = jnp.where(lane < HDIM // 2, -s, s)
            slot = tables.free(g)
            for rank in range(ranks):
                cos_v[slot, rank] = c[rank * rows : (rank + 1) * rows]
                sin_v[slot, rank] = s[rank * rows : (rank + 1) * rows]
            tables.put(g)
            gather.arrived(g)
            loads.need(g == 0, 0)
            x = full[g].reshape(ranks * rows, model)
            for which in range(3):
                out = dot(x, w_v[which])
                for h in range(heads):
                    u = out[:, h * HDIM : (h + 1) * HDIM]
                    if which < 2:
                        u = u * c + swap_halves(u) * s
                    u = u.astype(BF)
                    at = (which * heads + h) * HDIM
                    for rank in range(ranks):
                        qkv_v[rank, g, :, at : at + HDIM] = u[rank * rows : (rank + 1) * rows]
            for store in stores:
                store.put(g)

        stream(line, groups, gather, arrived=project, extra=(2, scale_grad))

        @pl.loop(0, groups)
        def _(g):
            for store in stores:
                store.end(g)

        tables.end(groups)
        loads.begin(True, 3, 4)
        second = Gather(line, kept_grad, b_send, b_recv, b_across)
        third = Gather(line, full, c_send, c_recv, c_across)
        reduce = Reduce(line, part, near, far, acc, s1, s2, s3)
        reduce_back = Reduce(line, part, near, far, acc, t1, t2, t3)
        keep = Store(attended_v, attended, attended_sem)
        keep_ln = Store(full, kept_ln, kept_sem.at[1])
        keep_resid = Store(resid_v, resid, resid_sem)
        keep_low = Store(low_v, grad_low, result_sem)
        highs = Turns([(high_v, grad_resid)], tile_sem.at[pl.ds(1, 1)])
        hiddens = Turns([(squared_v, squared), (hidden_v, hidden_grad)], tile_sem.at[pl.ds(2, 2)])
        gains[...] = jnp.zeros_like(gains)
        first_column = line.t * columns
        place_grad.wait()

        def fetch(g):
            slot = lax.rem(g, 2)
            return pltpu.make_async_copy(kept_grad.at[g], grad_v.at[slot], tile_sem.at[0, slot])

        def part_of(which, h):
            return pl.ds(pl.multiple_of((which * heads + h) * HDIM, HDIM), HDIM)

        def keep_weights(i, count, h):
            rows_kept = weight_rows(i if count == reach else count - 1, reach)
            return pltpu.make_async_copy(
                weights_v.at[h, pl.ds(0, count * QROWS)],
                kept_weights.at[h, pl.ds(pl.multiple_of(rows_kept, QROWS), count * QROWS)],
                weights_sem.at[h],
            )

        def attend_block(i, count):
            low = i + 1 - count
            start = query_starts(docs, i * QROWS)

            @pl.loop(0, heads)
            def _(h):
                q = qkv_v[pl.ds(i * span, span), :, :, part_of(0, h)].reshape(QROWS, HDIM)
                k = qkv_v[pl.ds(low * span, count * span), :, :, part_of(1, h)].reshape(count * QROWS, HDIM)
                weights = softmax_block(q, k, start, i * QROWS, low * QROWS, scaling).astype(BF)
                keys = pl.ds(pl.multiple_of(low * QROWS, QROWS), count * QROWS)
                done = dot(v_t[h, :, keys], weights).T
                done = (done * jnp.where(line.t * heads + h < active[0], 1.0, 0.0)).astype(BF)
                put_grouped(attended_v, done, i, own_tokens, rows, part_of(0, h))
                if not isinstance(i, int):
                    pl.when(i == reach - 1)(lambda: keep_weights(i - 1, reach - 1, h).wait())
                    pl.when(i > reach - 1)(lambda: keep_weights(i - 1, reach, h).wait())
                elif i:
                    keep_weights(i - 1, count - 1, h).wait()
                weights_v[h, : count * QROWS] = weights
                keep_weights(i, count, h).start()

        def attention(turn):
            @pl.when(turn == 0)
            def _():
                @pl.loop(0, heads)
                def _(h):
                    v_t[h] = qkv_v[:, :, :, part_of(2, h)].reshape(length, HDIM).T

                for i in range(min(reach - 1, blocks)):
                    attend_block(i, i + 1)

            @pl.when(turn == 1)
            def _():
                @pl.loop(reach - 1, blocks)
                def _(i):
                    attend_block(i, reach)

        def produce(g):
            keep.put(g)
            loads.need(g == 0, 1)
            for n in range(0, model, 512):
                out = dot(attended_v[g], wo_v[:, n : n + 512]).astype(BF)
                part[g, ..., n : n + 512] = out.reshape(chips, 2, rows, 512)

        def norm(g):
            reduce.last(g)
            total = x_ref[g].astype(F32) + acc[...]
            resid_v[g] = total
            keep_resid.put(g)
            lhat, _ = layer_norm(total)
            full[g, line.z, line.c] = (lhat * gain2[...] + bias2[...]).astype(BF)
            third.begin(g)

        def arrived(g):
            third.arrived(g)
            keep_ln.put(g)
            reduce.drain(g)

            @pl.when(g == 0)
            def _():
                fetch(0).start()

            fetch(g).wait()

            @pl.when(g + 1 < groups)
            def _():
                fetch(g + 1).start()

            loads.need(g == 0, 3, 4)

        def forward(g):
            slot = hiddens.free(g)
            limit = (jnp.broadcast_to(wide[pl.ds(g, 1), :], (HDIM, tokens_all)).T[:, :1] + 1) * (FF // 4)

            @pl.loop(0, columns // tile)
            def _(n):
                at = pl.ds(pl.multiple_of(n * tile, tile), tile)
                hidden = dot(full[g].reshape(tokens_all, model), up_v[:, at])
                ids = first_column + n * tile + lax.broadcasted_iota(jnp.int32, hidden.shape, 1)
                live = jnp.where(ids < limit, jnp.maximum(hidden, 0.0), 0.0)
                lifted[:, at] = live
                squared_v[slot, :, at] = (live * live).astype(BF)

        def backward(g):
            slot = lax.rem(g, 2)

            @pl.loop(0, columns // tile)
            def _(n):
                at = pl.ds(pl.multiple_of(n * tile, tile), tile)
                back = dot(grad_v[slot].reshape(tokens_all, model), down_v[at, :], NT)
                hidden_v[slot, :, at] = (back * (2.0 * lifted[:, at])).astype(BF)

            hiddens.put(g)

        def lower(g):
            slot = lax.rem(g, 2)

            @pl.loop(0, model // 256)
            def _(n):
                at = pl.ds(pl.multiple_of(n * 256, 256), 256)
                out = dot(hidden_v[slot], up_v[at, :], NT).astype(BF)
                part[g, :, :, :, at] = out.reshape(chips, 2, rows, 256)

        def finish(g):
            reduce_back.last(g)
            lhat, inv_std = layer_norm(resid_v[g])
            back = acc[...]
            gains[0:1] += jnp.sum(back * lhat, axis=0, keepdims=True)
            gains[1:2] += jnp.sum(back, axis=0, keepdims=True)
            back = back * gain2[...]
            back = dy_v[g].astype(F32) + inv_std * (back - row_mean(back) - lhat * row_mean(back * lhat))
            high_v[highs.free(g)] = back
            low_v[g] = back.astype(BF)
            highs.put(g)
            keep_low.put(g)

        @pl.loop(0, groups + back_at)
        def _(i):
            for n in range(hops):
                h, d = hops - n, n + 1
                within(i - hidden_at - 1 - hops + d, groups, functools.partial(reduce_back.step, d=d))
                within(i - normed_at - h, groups, functools.partial(third.hop, h=h))
                within(i - lead - 1 - hops + d, groups, functools.partial(reduce.step, d=d))
                within(i - h, groups, functools.partial(second.hop, h=h))
                if n == 0:
                    within(i - hidden_at, groups, arrived)
                for piece in (forward, backward, lower)[n * 3 // hops : (n + 1) * 3 // hops]:
                    within(i - hidden_at, groups, piece)
            within(i, groups, second.begin)
            within(i - hidden_at, groups, reduce_back.begin)
            within(i - normed_at, groups, norm)
            within(i - lead, groups, produce)
            within(i - lead, groups, reduce.begin)
            within(i - hops - 1, groups, second.arrived)
            within(i - back_at, groups, finish)
            within(i, lead, attention)

        for h in range(heads):
            keep_weights(blocks - 1, reach, h).wait()
        second.drain()
        third.drain()
        pl.loop(0, groups)(reduce_back.drain)

        @pl.loop(0, groups)
        def _(g):
            for store in (keep, keep_ln, keep_resid, keep_low):
                store.end(g)

        highs.end(groups)
        hiddens.end(groups)

    table = jax.ShapeDtypeStruct((ranks, groups, rows, HDIM), F32)
    projected = jax.ShapeDtypeStruct((ranks, groups, rows, 3 * width), BF)
    full = jax.ShapeDtypeStruct((groups, chips, 2, rows, model), BF)
    attended = jax.ShapeDtypeStruct((groups, tokens_all, width), BF)
    high = jax.ShapeDtypeStruct((groups, rows, model), F32)
    low = jax.ShapeDtypeStruct((groups, rows, model), BF)
    hidden = jax.ShapeDtypeStruct((groups, tokens_all, columns), BF)
    return call(
        body,
        [tokens, cotangent, probs, gain, lengths, frequency, count, w_qkv, w_out, g_ln, b_ln, w_up, w_down, widths],
        [
            projected,
            full,
            table,
            table,
            attended,
            high,
            full,
            high,
            low,
            jax.ShapeDtypeStruct((2, model), F32),
            full,
            hidden,
            hidden,
            jax.ShapeDtypeStruct((heads, weight_rows(blocks, reach), QROWS), BF),
        ],
        [
            *scratch_of(full, w_qkv, w_out, cotangent, w_up, w_down, projected),
            pltpu.VMEM((2, ranks, rows, HDIM), F32),
            pltpu.VMEM((2, ranks, rows, HDIM), F32),
            pltpu.VMEM((heads, HDIM, length), BF),
            *scratch_of(attended, low, high),
            pltpu.VMEM((2, rows, model), F32),
            pltpu.VMEM((2, chips, 2, rows, model), BF),
            pltpu.VMEM((tokens_all, columns), F32),
            pltpu.VMEM((2, tokens_all, columns), BF),
            pltpu.VMEM((2, tokens_all, columns), BF),
            *Gather.scratch(ranks, groups) * 3,
            *Reduce.scratch(ranks, groups, rows, model),
            *Reduce.scratch(ranks, groups, rows, model)[-3:],
            DMA((5,)),
            DMA((2, groups)),
            DMA((3, groups)),
            DMA,
            *[DMA((groups,))] * 3,
            DMA((4, groups)),
            pltpu.VMEM((heads, reach * QROWS, QROWS), BF),
            DMA((heads,)),
        ],
        0,
        in_specs=[VM, ANY, VM, VM, SM, VM, SM, ANY, ANY, VM, VM, ANY, ANY, VM],
        out_specs=[ANY] * 9 + [VM] + [ANY] * 4,
        flops=8 * length * model * (width + columns),
        moved=160 << 20,
    )


def hidden_weights(spread, inputs, hidden, first, turn_of, columns):
    n = turn_of
    side = min(256, spread.out.shape[1])

    @pl.loop(0, spread.out.shape[1] // side)
    def _(m):
        at = pl.ds(pl.multiple_of(first + m * side, side), side)
        to = pl.ds(pl.multiple_of(m * side, side), side)
        x = inputs[:, :, at]
        spread.out[n, to] = dot(
            x.reshape(x.shape[0] * x.shape[1], side), hidden[...].reshape(-1, columns), TN
        ).astype(BF)

    spread.begin(n)


def feed_out(
    own_grad, squared, hidden_grad, kept_ln, branch_grad, w_down, w_out, count, resid, cotangent, probs, ranks, sequences
):
    groups, rows, model = own_grad.shape
    columns, width = w_down.shape[0], w_out.shape[0]
    tokens = ranks * rows
    share = model // sequences
    half = share // 2

    def body(
        own, sq, hg, ln, bg, down, w, active, res, dy, p, result, probs_grad, kept, grad, land_down, land_up,
        full, g_send, g_recv, g_across, part, near, far, acc, s1, s2, s3, kept_sem,
        out_down, down_send, down_recv, out_up, up_send, up_recv, ln_v, bg_v, fetch_sem,
        sq_v, hg_v, down_v, res_v, dy_v, load_sem, result_v, back_v, result_sem, back_sem,
    ):
        line = Line(ranks, rows)
        gather = Gather(line, full, g_send, g_recv, g_across)
        reduce = Reduce(line, part, near, far, acc, s1, s2, s3)
        to_down = Spread(sequences, out_down, land_down, down_send, down_recv)
        to_up = Spread(sequences, out_up, land_up, up_send, up_recv, pl.ds(0, half))
        keep = Store(full, kept, kept_sem)
        keep_result = Store(result_v, result, result_sem)
        keep_back = Store(back_v, grad, back_sem, lambda ref, g: ref.at[:, g])

        def arrived(g):
            gather.arrived(g)
            keep.put(g)
            heads = line.t * (width // HDIM) + lax.broadcasted_iota(jnp.int32, (1, width), 1) // HDIM
            live = jnp.where(heads < active[0], 1.0, 0.0)
            back = (dot(full[g].reshape(tokens, model), w[...], NT) * live).astype(BF)
            for rank in range(ranks):
                back_v[rank, g] = back[rank * rows : (rank + 1) * rows]
            keep_back.put(g)

        def produce(g):
            loads.need(g == 0, 0, 1)

            @pl.loop(0, model // 256)
            def _(n):
                at = pl.ds(pl.multiple_of(n * 256, 256), 256)
                out = dot(sq_v[g], down_v[:, at]).astype(BF)
                part[g, :, :, :, at] = out.reshape(ranks // 2, 2, rows, 256)

        def finish(g):
            loads.need(g == 0, 3, 4)
            ffn = acc[...]
            result_v[g] = (res_v[g] + p[g, :, :1] * ffn).astype(BF)
            keep_result.put(g)
            scores = jnp.sum(dy_v[g].astype(F32) * ffn, axis=1, keepdims=True)
            probs_grad[pl.ds(g, 1)] = jnp.broadcast_to(scores, (rows, HDIM)).T[:1]

        def fetches(step):
            at = pl.multiple_of(to_up.target(lax.rem(step + 1, sequences)) * share, share)
            return [
                pltpu.make_async_copy(ln.at[:, :, pl.ds(at, half)], ln_v, fetch_sem.at[0]),
                pltpu.make_async_copy(bg.at[:, :, pl.ds(at, share)], bg_v, fetch_sem.at[1]),
            ]

        def weights(step):
            n = lax.rem(step + 1, sequences)
            loads.need(step == 0, 2)
            for fetch in fetches(step):
                fetch.wait()
            side = min(256, columns)

            @pl.loop(0, columns // side)
            def _(m):
                at = pl.ds(pl.multiple_of(m * side, side), side)
                out_down[n, at] = dot(
                    sq_v[:, :, at].reshape(groups * tokens, side), bg_v[...].reshape(groups * tokens, share), TN
                ).astype(BF)

            to_down.begin(n)
            hidden_weights(to_up, ln_v, hg_v, 0, n, columns)

            @pl.when(step + 1 < sequences)
            def _():
                for fetch in fetches(step + 1):
                    fetch.start()

        def beside(turn):
            loads.begin(turn == 0, 0, 1, 2)

            @pl.when(turn == 0)
            def _():
                for fetch in fetches(0):
                    fetch.start()

            loads.begin(turn == 3, 3, 4)
            within(turn - 1, sequences, weights)

        loads = Loads(
            [
                (sq, sq_v),
                (down, down_v),
                (hg, hg_v),
                (res, res_v),
                (dy, dy_v),
                (own, full.at[:, line.z, line.c]),
            ],
            load_sem,
        )
        loads.begin(True, 5)
        line.barrier(sequences)
        loads.need(True, 5)
        stream(
            line, groups, gather, arrived, reduce, [produce], finish, 1, (max(sequences + 1, 4), beside)
        )

        @pl.loop(0, groups)
        def _(g):
            for store in (keep, keep_result, keep_back):
                store.end(g)

        to_down.end()
        to_up.end()

    kept = jax.ShapeDtypeStruct((groups, ranks // 2, 2, rows, model), BF)
    low = jax.ShapeDtypeStruct((groups, rows, model), BF)
    back = jax.ShapeDtypeStruct((ranks, groups, rows, width), BF)
    return call(
        body,
        [own_grad, squared, hidden_grad, kept_ln, branch_grad, w_down, w_out, count, resid, cotangent, probs],
        [
            low,
            jax.ShapeDtypeStruct((groups, rows), F32),
            kept,
            back,
            jax.ShapeDtypeStruct((sequences, columns, share), BF),
            jax.ShapeDtypeStruct((sequences, share, columns), BF),
        ],
        [
            *scratch_of(kept),
            *Gather.scratch(ranks, groups),
            *Reduce.scratch(ranks, groups, rows, model),
            DMA((groups,)),
            *Spread.scratch(sequences, (columns, share)),
            *Spread.scratch(sequences, (half, columns)),
            pltpu.VMEM((groups, tokens, half), BF),
            pltpu.VMEM((groups, tokens, share), BF),
            DMA((2,)),
            *scratch_of(squared, hidden_grad, w_down, resid, cotangent),
            DMA((6,)),
            *scratch_of(low, back),
            DMA((groups,)),
            DMA((groups,)),
        ],
        3,
        in_specs=[ANY, ANY, ANY, ANY, ANY, ANY, VM, SM, ANY, ANY, VM],
        out_specs=[ANY, VM, ANY, ANY, ANY, ANY],
        flops=2 * groups * tokens * model * (3 * columns + width),
        moved=100 << 20,
    )


def project_back(
    grads, w_qkv, kept_x, attended, attn_grad, kept_ln, hidden_grad, landed_up, tokens, gain, grad_resid, gains, ranks, sequences
):
    groups, tokens_all, width = grads[0].shape
    rows = tokens_all // ranks
    model = w_qkv.shape[1]
    columns = hidden_grad.shape[2]
    share = model // sequences
    half = share // 2

    def body(
        gq, gk, gv, w, xs, a, ga, ln, hg, up_in, x_ref, gain_ref, g_res, gain_parts,
        tokens_grad, totals, land_qkv, land_out, land_up,
        part, near, far, acc, s1, s2, s3,
        out_qkv, qkv_send, qkv_recv, out_out, out_send, out_recv, out_up, up_send, up_recv,
        x_v, ga_v, ln_v, fetch_sem, group_v, group_sem, w_v, a_v, hg_v, own_v, res_v, load_sem,
        mine, terms, t_send, t_recv, sums, d_send, d_recv, g_q, g_k, g_v, grad_v, grad_sem,
    ):
        line = Line(ranks, rows)
        me = lax.axis_index("dp")
        reduce = Reduce(line, part, near, far, acc, s1, s2, s3)
        to_qkv = Spread(sequences, out_qkv, land_qkv, qkv_send, qkv_recv)
        to_out = Spread(sequences, out_out, land_out, out_send, out_recv)
        to_up = Spread(sequences, out_up, land_up, up_send, up_recv, pl.ds(half, half))
        parts = (g_q, g_k, g_v)
        loads = Loads(
            [(w, w_v), (a, a_v), (hg, hg_v), (x_ref, own_v), (g_res, res_v), (gq, g_q), (gk, g_k), (gv, g_v)],
            load_sem,
        )
        keep_grad = Store(grad_v, tokens_grad, grad_sem)

        def group_fetch(g):
            slot = lax.rem(g, 2)
            return pltpu.make_async_copy(xs.at[g], group_v.at[slot], group_sem.at[slot])

        loads.begin(True, 0, 5, 6, 7)
        group_fetch(0).start()
        mine[0:1] = jnp.zeros((1, model), F32)
        mine[1:3] = gain_parts[...]

        def produce(g):
            loads.need(g == 0, 0, 5, 6, 7)
            group_fetch(g).wait()

            @pl.when(g + 1 < groups)
            def _():
                group_fetch(g + 1).start()

            slot = lax.rem(g, 2)

            @pl.loop(0, model // 256)
            def _(n):
                at = pl.ds(pl.multiple_of(n * 256, 256), 256)
                out = dot(g_q[g], w_v[0, at], NT)
                out += dot(g_k[g], w_v[1, at], NT)
                out += dot(g_v[g], w_v[2, at], NT)
                part[g, :, :, :, at] = out.astype(BF).reshape(ranks // 2, 2, rows, 256)
                mine[0:1, at] += jnp.sum(out * group_v[slot, :, at].astype(F32), axis=0, keepdims=True)

        def finish(g):
            loads.need(g == 0, 3, 4)
            x = own_v[g].astype(F32)
            scale = lax.rsqrt(row_mean(x * x) + EPSILON)
            hat = x * scale
            back = acc[...] * gain_ref[...]
            grad_v[g] = res_v[g] + scale * (back - hat * row_mean(back * hat))
            keep_grad.put(g)

        def fetches(step):
            at = pl.multiple_of(to_qkv.target(lax.rem(step + 1, sequences)) * share, share)
            return [
                pltpu.make_async_copy(ln.at[:, :, pl.ds(at + half, half)], ln_v, fetch_sem.at[0]),
                pltpu.make_async_copy(xs.at[:, :, pl.ds(at, share)], x_v, fetch_sem.at[1]),
                pltpu.make_async_copy(ga.at[:, :, pl.ds(at, share)], ga_v, fetch_sem.at[2]),
            ]

        def weights(piece):
            step = piece // 2
            n = lax.rem(step + 1, sequences)

            @pl.when(lax.rem(piece, 2) == 0)
            def _():
                loads.need(step == 0, 1, 2)
                fetches(step)[0].wait()
                hidden_weights(to_up, ln_v, hg_v, 0, n, columns)

                @pl.when(step + 1 < sequences)
                def _():
                    fetches(step + 1)[0].start()

            @pl.when(lax.rem(piece, 2) == 1)
            def _():
                for fetch in fetches(step)[1:]:
                    fetch.wait()

                @pl.loop(0, share // 256)
                def _(m):
                    at = pl.ds(pl.multiple_of(m * 256, 256), 256)
                    x = x_v[:, :, at].reshape(groups * tokens_all, 256)
                    for which in range(3):
                        out_qkv[n, which, at] = dot(
                            x, parts[which][...].reshape(groups * tokens_all, width), TN
                        ).astype(BF)

                to_qkv.begin(n)
                out_out[n] = dot(
                    a_v[...].reshape(groups * tokens_all, width), ga_v[...].reshape(groups * tokens_all, share), TN
                ).astype(BF)
                to_out.begin(n)

                @pl.when(step + 1 < sequences)
                def _():
                    for fetch in fetches(step + 1)[1:]:
                        fetch.start()

        def to_rank(n, source=None):
            return copy_to(
                mine,
                terms.at[line.t if source is None else source],
                t_send.at[n],
                t_recv.at[n],
                lax.rem(line.t + n, ranks),
            )

        def to_sequence(n, source=None):
            return pltpu.make_async_remote_copy(
                src_ref=sums.at[me],
                dst_ref=sums.at[me if source is None else source],
                send_sem=d_send.at[n],
                recv_sem=d_recv.at[n],
                device_id={"dp": lax.rem(me + n, sequences)},
                device_id_type=MESH,
            )

        def beside(turn):
            loads.begin(turn == 0, 1, 2)
            loads.begin(turn == 2, 3, 4)

            @pl.when(turn == 0)
            def _():
                for fetch in fetches(0):
                    fetch.start()

            within(turn - 1, 2 * sequences, weights)

            @pl.when(turn == groups)
            def _():
                mine[0:1] = mine[0:1] / gain_ref[...]
                terms[line.t] = mine[...]

                @pl.loop(1, ranks)
                def _(n):
                    to_rank(n).start()

            @pl.when(turn == groups + 1)
            def _():
                @pl.loop(1, ranks)
                def _(n):
                    to_rank(n).wait_send()
                    to_rank(n, lax.rem(line.t + ranks - n, ranks)).wait_recv()

                total = terms[0]
                for n in range(1, ranks):
                    total += terms[n]
                sums[me] = total

                @pl.loop(1, sequences)
                def _(n):
                    to_sequence(n).start()

            @pl.when(turn == groups + 2)
            def _():
                @pl.loop(1, sequences)
                def _(n):
                    to_sequence(n).wait_send()
                    to_sequence(n, lax.rem(me + sequences - n, sequences)).wait_recv()

                total = sums[0]
                for n in range(1, sequences):
                    total += sums[n]
                totals[...] = total

        line.barrier_all(sequences)
        stream(
            line, groups, None, None, reduce, [produce], finish, extra=(max(groups + 3, 2 * sequences + 1), beside)
        )

        @pl.loop(0, groups)
        def _(g):
            keep_grad.end(g)

        to_qkv.end()
        to_out.end()

        to_up.end()

    return call(
        body,
        [*grads, w_qkv, kept_x, attended, attn_grad, kept_ln, hidden_grad, landed_up, tokens, gain, grad_resid, gains],
        [
            jax.ShapeDtypeStruct((groups, rows, model), F32),
            jax.ShapeDtypeStruct((3, model), F32),
            jax.ShapeDtypeStruct((sequences, 3, share, width), BF),
            jax.ShapeDtypeStruct((sequences, width, share), BF),
            jax.ShapeDtypeStruct(landed_up.shape, BF),
        ],
        [
            *Reduce.scratch(ranks, groups, rows, model),
            *Spread.scratch(sequences, (3, share, width)),
            *Spread.scratch(sequences, (width, share)),
            *Spread.scratch(sequences, (half, columns)),
            pltpu.VMEM((groups, tokens_all, share), BF),
            pltpu.VMEM((groups, tokens_all, share), BF),
            pltpu.VMEM((groups, tokens_all, half), BF),
            DMA((3,)),
            pltpu.VMEM((2, tokens_all, model), BF),
            DMA((2,)),
            *scratch_of(w_qkv, attended, hidden_grad, tokens, grad_resid),
            DMA((8,)),
            pltpu.VMEM((3, model), F32),
            pltpu.VMEM((ranks, 3, model), F32),
            DMA((ranks,)),
            DMA((ranks,)),
            pltpu.VMEM((sequences, 3, model), F32),
            DMA((sequences,)),
            DMA((sequences,)),
            *scratch_of(*grads, grad_resid),
            DMA((groups,)),
        ],
        4,
        in_specs=[ANY] * 11 + [VM, ANY, VM],
        out_specs=[ANY, VM, ANY, ANY, ANY],
        flops=12 * groups * tokens_all * model * width,
        moved=60 << 20,
        aliases={9: 4},
    )


def collect(result, tokens_grad, totals, *landed):
    steps = result.shape[0]

    def body(result_in, tokens_in, totals_in, *refs):
        pieces, outs = refs[: len(landed)], refs[len(landed) :]
        outs[0][...] = result_in[...]
        outs[1][...] = tokens_in[...]
        for n in range(3):
            outs[2 + n][...] = totals_in[n : n + 1]
        for piece, out in zip(pieces, outs[5:]):
            total = piece[0].astype(F32)
            for n in range(1, piece.shape[0]):
                total += piece[n].astype(F32)
            out[...] = total

    def split(a, at):
        block = list(a.shape)
        block[at] //= steps
        return pl.BlockSpec(tuple(block), lambda i: tuple(i if n == at else 0 for n in range(len(block))))

    sums = [jax.ShapeDtypeStruct(a.shape[1:], F32) for a in landed]
    row = jax.ShapeDtypeStruct((1, totals.shape[1]), F32)
    fixed = lambda a: pl.BlockSpec(a.shape, lambda i: (0, 0))
    return pl.pallas_call(
        body,
        out_shape=[
            jax.ShapeDtypeStruct(result.shape, BF),
            jax.ShapeDtypeStruct(tokens_grad.shape, F32),
            row,
            row,
            row,
            *sums,
        ],
        grid=(steps,),
        in_specs=[split(result, 0), split(tokens_grad, 0), fixed(totals)]
        + [split(a, a.ndim - 2) for a in landed],
        out_specs=[split(result, 0), split(tokens_grad, 0), fixed(row), fixed(row), fixed(row)]
        + [split(a, len(a.shape) - 2) for a in sums],
        compiler_params=pltpu.CompilerParams(vmem_limit_bytes=60 << 20),
        cost_estimate=pl.CostEstimate(flops=1 << 24, bytes_accessed=24 << 20, transcendentals=0),
    )(result, tokens_grad, totals, *landed)


def shards(
    tokens,
    cotangent,
    first_norm_gain,
    w_qkv,
    w_out,
    g_ln,
    b_ln,
    w_up,
    w_down,
    probs,
    lengths,
    head_count,
    widths,
):
    length_all = widths.shape[0]
    own_tokens, model = tokens.shape
    ranks = length_all // own_tokens
    sequences = lax.axis_size("dp")
    groups, rows = GROUPS, own_tokens // GROUPS
    width = w_out.shape[0]
    half = HDIM // 2
    frequency = 10000.0 ** (-np.arange(half) / half)
    frequency = jnp.asarray(np.concatenate([frequency, frequency]).reshape(1, HDIM), F32)
    w_qkv_t = w_qkv.transpose(1, 0, 2)
    x = tokens.reshape(groups, rows, model)
    dy = cotangent.reshape(groups, rows, model)
    first_norm_gain, g_ln, b_ln = (v.reshape(1, model) for v in (first_norm_gain, g_ln, b_ln))
    p = jnp.broadcast_to(probs.reshape(groups, rows, 1), (groups, rows, HDIM))
    wide = widths.reshape(ranks, groups, rows).swapaxes(0, 1).reshape(groups, ranks * rows)

    (
        qkv, kept_x, cosines, sines, attended, resid, kept_ffn_grad, grad_resid, grad_low, gains, kept_ln, squared,
        grad_hidden, kept_weights,
    ) = front(
        x, dy, p, first_norm_gain, lengths, frequency, head_count, w_qkv_t, w_out, g_ln, b_ln, w_up, w_down, wide, ranks
    )
    qkv = qkv.reshape(length_all, 3 * width)
    cosines, sines = cosines.reshape(length_all, HDIM), sines.reshape(length_all, HDIM)
    whole = lambda kept: kept.reshape(groups, ranks * rows, model)
    result, probs_grad, kept_attn_grad, grad_attended, land_down, land_up = feed_out(
        grad_low, squared, grad_hidden, whole(kept_ln), whole(kept_ffn_grad), w_down, w_out, head_count, resid, dy, p, ranks, sequences
    )
    grad_proj = attend_back(
        qkv,
        grad_attended.reshape(length_all, width),
        kept_weights,
        head_count,
        cosines,
        sines,
        width,
        groups,
        own_tokens,
    )
    tokens_grad, totals, land_qkv, land_out, land_up = project_back(
        grad_proj, w_qkv_t, whole(kept_x), attended, whole(kept_attn_grad), whole(kept_ln), grad_hidden, land_up, x, first_norm_gain,
        grad_resid, gains, ranks, sequences,
    )
    result, tokens_grad, rms, gain, bias, g_qkv, g_out, g_up, g_down = collect(
        result, tokens_grad, totals, land_qkv, land_out, land_up, land_down
    )
    return (
        result.reshape(own_tokens, model),
        tokens_grad.reshape(own_tokens, model),
        probs_grad.reshape(own_tokens),
        rms.reshape(model),
        g_qkv.transpose(1, 0, 2),
        g_out,
        gain.reshape(model),
        bias.reshape(model),
        g_up,
        g_down,
    )


def solution(mesh):
    placed = (
        P(("dp", "tensor"), None),
        P(("dp", "tensor"), None),
        P(),
        P(None, None, "tensor"),
        P("tensor", None),
        P(),
        P(),
        P(None, "tensor"),
        P("tensor", None),
        P(("dp", "tensor")),
        P("dp", None),
        P("dp"),
        P("dp"),
    )
    return jax.shard_map(
        shards,
        mesh=mesh,
        in_specs=placed,
        out_specs=(
            P(("dp", "tensor"), None),
            P(("dp", "tensor"), None),
            P(("dp", "tensor")),
            P(),
            P("dp", None, "tensor"),
            P("tensor", "dp"),
            P(),
            P(),
            P("dp", "tensor"),
            P("tensor", "dp"),
        ),
        check_vma=False,
    )
```

```python
import functools

import jax
import jax.numpy as jnp
import numpy as np
from jax import lax
from jax.experimental import pallas as pl
from jax.experimental.pallas import tpu as pltpu
from jax.sharding import PartitionSpec as P

HDIM = 128
FF = 8192
EPSILON = 1e-05
NEGATIVE = -1e30
MAXDOC = 1024
GROUPS = 8
QROWS = 256
MESH = pl.DeviceIdType.MESH
BF = jnp.bfloat16
F32 = jnp.float32
ANY = pl.BlockSpec(memory_space=pl.ANY)
VM = pl.BlockSpec(memory_space=pltpu.VMEM)
SM = pl.BlockSpec(memory_space=pltpu.SMEM)
DMA = pltpu.SemaphoreType.DMA
NT = (((1,), (1,)), ((), ()))
TN = (((0,), (0,)), ((), ()))


def dot(a, b, dims=(((1,), (0,)), ((), ()))):
    return lax.dot_general(a, b, dims, preferred_element_type=F32)


class Line:
    def __init__(self, ranks, rows):
        self.ranks, self.chips, self.rows = ranks, ranks // 2, rows
        self.t = lax.axis_index("tensor")
        self.z, self.c = self.t // 2, lax.rem(self.t, 2)
        self.has_up, self.has_down = self.z < self.chips - 1, self.z > 0
        self.up = jnp.minimum(self.t + 2, ranks - 1)
        self.down = jnp.maximum(self.t - 2, 0)
        self.partner = self.t + 1 - 2 * self.c

    def barrier(self, dp_size=0):
        sem = pltpu.get_barrier_semaphore()
        pl.semaphore_signal(sem, inc=1, device_id={"tensor": self.partner}, device_id_type=MESH)

        @pl.when(self.has_up)
        def _():
            pl.semaphore_signal(sem, inc=1, device_id={"tensor": self.up}, device_id_type=MESH)

        @pl.when(self.has_down)
        def _():
            pl.semaphore_signal(sem, inc=1, device_id={"tensor": self.down}, device_id_type=MESH)

        d = lax.axis_index("dp")
        for step in range(1, dp_size):
            pl.semaphore_signal(
                sem, inc=1, device_id={"dp": lax.rem(d + step, dp_size)}, device_id_type=MESH
            )
        links = self.has_up.astype(jnp.int32) + self.has_down.astype(jnp.int32)
        pl.semaphore_wait(sem, 1 + max(dp_size - 1, 0) + links)

    def barrier_all(self, dp_size):
        sem = pltpu.get_barrier_semaphore()
        for n in range(1, self.ranks):
            pl.semaphore_signal(
                sem, inc=1, device_id={"tensor": lax.rem(self.t + n, self.ranks)}, device_id_type=MESH
            )
        d = lax.axis_index("dp")
        for n in range(1, dp_size):
            pl.semaphore_signal(
                sem, inc=1, device_id={"dp": lax.rem(d + n, dp_size)}, device_id_type=MESH
            )
        pl.semaphore_wait(sem, self.ranks - 1 + dp_size - 1)


def copy_to(src, dst, send, recv, rank):
    return pltpu.make_async_remote_copy(
        src_ref=src,
        dst_ref=dst,
        send_sem=send,
        recv_sem=recv,
        device_id={"tensor": rank},
        device_id_type=MESH,
    )


class Gather:
    def __init__(self, line, full, send, recv, across_recv):
        self.l, self.full, self.send, self.recv, self.across_recv = line, full, send, recv, across_recv

    @staticmethod
    def scratch(ranks, groups):
        return [DMA((3, ranks // 2)), DMA((groups, ranks // 2)), DMA((groups,))]

    def along(self, g, z, up):
        l = self.l
        place = self.full.at[g, z, l.c]
        return copy_to(
            place,
            place,
            self.send.at[0 if up else 1, z],
            self.recv.at[0 if g == slice(None) else g, z],
            l.up if up else l.down,
        )

    def across(self, g, column):
        place = self.full.at[g, :, column]
        return copy_to(
            place, place, self.send.at[2, 0], self.across_recv.at[0 if g == slice(None) else g], self.l.partner
        )

    def pass_on(self, g, z, up):
        @pl.when(self.l.has_up if up else self.l.has_down)
        def _():
            self.along(g, z, up).start()

    def begin(self, g):
        self.pass_on(g, self.l.z, True)
        self.pass_on(g, self.l.z, False)

    def hop(self, g, h):
        l = self.l

        @pl.when(l.z - h >= 0)
        def _():
            self.along(g, l.z - h, True).wait_recv()
            self.pass_on(g, l.z - h, True)

        @pl.when(l.z + h <= l.chips - 1)
        def _():
            self.along(g, l.z + h, False).wait_recv()
            self.pass_on(g, l.z + h, False)

        if h == l.chips - 1:
            self.across(g, l.c).start()

    def arrived(self, g):
        self.across(g, 1 - self.l.c).wait_recv()

    def drain(self):
        l, every = self.l, slice(None)
        for z in range(l.chips):

            @pl.when(l.has_up & (l.z >= z))
            def _():
                self.along(every, z, True).wait_send()

            @pl.when(l.has_down & (l.z <= z))
            def _():
                self.along(every, z, False).wait_send()

        self.across(every, l.c).wait_send()


class Reduce:
    def __init__(self, line, part, near, far, acc, send, near_recv, far_recv):
        self.l, self.part, self.near, self.far, self.acc = line, part, near, far, acc
        self.send, self.near_recv, self.far_recv = send, near_recv, far_recv

    @staticmethod
    def scratch(ranks, groups, rows, width):
        chips = ranks // 2
        return [
            pltpu.VMEM((groups, chips, 2, rows, width), BF),
            pltpu.VMEM((groups, chips, rows, width), BF),
            pltpu.VMEM((groups, chips + 1, rows, width), BF),
            pltpu.VMEM((rows, width), F32),
            DMA((groups, chips + 1)),
            DMA((groups,)),
            DMA((groups, chips + 1)),
        ]

    def across(self, g):
        l = self.l
        return copy_to(
            self.part.at[g, :, 1 - l.c],
            self.near.at[g],
            self.send.at[g, l.chips],
            self.near_recv.at[g],
            l.partner,
        )

    def along(self, g, z, up, receive=False):
        l = self.l
        at = l.z if receive else jnp.where(up, l.z + 1, l.z - 1)
        slot = z if up else jnp.where(z == at, l.chips, z)
        return copy_to(
            self.part.at[g, z, l.c],
            self.far.at[g, slot],
            self.send.at[g, z],
            self.far_recv.at[g, slot],
            l.up if up else l.down,
        ), slot

    def begin(self, g):
        self.across(g).start()

    def add(self, g, z, slots, total=None):
        side = 512

        @pl.loop(0, self.part.shape[-1] // side)
        def _(n):
            at = pl.ds(pl.multiple_of(n * side, side), side)
            value = self.part[g, z, self.l.c, :, at].astype(F32) + self.near[g, z, :, at].astype(F32)
            for slot in slots:
                value += self.far[g, slot, :, at].astype(F32)
            if total is None:
                self.part[g, z, self.l.c, :, at] = value.astype(BF)
            else:
                total[:, at] = value

    def step(self, g, d):
        l = self.l
        if d == l.chips - 1:
            self.across(g).wait_recv()

        def send(z, up):
            further = l.has_down if up else l.has_up

            @pl.when(further)
            def _():
                copy, slot = self.along(g, z, up, receive=True)
                copy.wait_recv()
                self.add(g, z, [slot])

            @pl.when(jnp.logical_not(further))
            def _():
                self.add(g, z, [])

            self.along(g, z, up)[0].start()

        @pl.when(l.z + d <= l.chips - 1)
        def _():
            send(l.z + d, True)

        @pl.when(l.z - d >= 0)
        def _():
            send(l.z - d, False)

    def last(self, g):
        l = self.l

        @pl.when(l.has_down & l.has_up)
        def _():
            self.along(g, l.z, True, receive=True)[0].wait_recv()
            self.along(g, l.z, False, receive=True)[0].wait_recv()
            self.add(g, l.z, [l.z, l.chips], self.acc)

        @pl.when(jnp.logical_not(l.has_up))
        def _():
            self.along(g, l.z, True, receive=True)[0].wait_recv()
            self.add(g, l.z, [l.z], self.acc)

        @pl.when(jnp.logical_not(l.has_down))
        def _():
            self.along(g, l.z, False, receive=True)[0].wait_recv()
            self.add(g, l.z, [l.chips], self.acc)

    def drain(self, g):
        l = self.l
        self.across(g).wait_send()
        for z in range(l.chips):

            @pl.when(l.z != z)
            def _():
                copy_to(
                    self.part.at[g, z, l.c],
                    self.far.at[g, z],
                    self.send.at[g, z],
                    self.far_recv.at[g, z],
                    l.partner,
                ).wait_send()


def within(value, limit, body):
    pl.when((value >= 0) & (value < limit))(lambda: body(value))


def swap_halves(field):
    return pltpu.roll(field, HDIM // 2, axis=1)


def call(body, ins, outs, scratch, ident, in_specs=None, out_specs=None, limit=60, flops=0, moved=0, aliases=None):
    return pl.pallas_call(
        body,
        out_shape=outs,
        in_specs=in_specs or [VM] * len(ins),
        out_specs=out_specs or [VM] * len(outs),
        scratch_shapes=scratch,
        compiler_params=pltpu.CompilerParams(
            collective_id=ident, has_side_effects=True, vmem_limit_bytes=limit << 20
        ),
        input_output_aliases=aliases or {},
        cost_estimate=pl.CostEstimate(flops=flops, bytes_accessed=moved, transcendentals=0),
    )(*ins)


def stream(line, groups, gather=None, arrived=None, reduce=None, produce=(), finish=None, lead=0, extra=None):
    hops = line.chips - 1
    produce = list(produce)
    between = len(produce) > 1
    turns = groups + hops + 1 + (lead if reduce else 0)

    @pl.loop(0, turns)
    def _(i):
        for n in range(hops):
            if gather:
                within(i - hops + n, groups, functools.partial(gather.hop, h=hops - n))
            if reduce:
                d = n + 1
                within(i - lead - 1 - hops + d, groups, functools.partial(reduce.step, d=d))
            if n == hops - 1 and gather:
                within(i, groups, gather.begin)
            if between:
                if n == 0:
                    within(i - hops - 1, groups, arrived)
                for piece in produce[n * len(produce) // hops : (n + 1) * len(produce) // hops]:
                    within(i - lead, groups, piece)
        if not between:
            for piece in produce:
                within(i - lead, groups, piece)
        if reduce:
            within(i - lead, groups, reduce.begin)
        if arrived and not between:
            within(i - hops - 1, groups, arrived)
        if reduce:

            def end(g):
                reduce.last(g)
                finish(g)

            within(i - lead - 1 - hops, groups, end)
        if extra:
            within(i, min(extra[0], turns), extra[1])

    if extra:

        @pl.loop(min(extra[0], turns), extra[0])
        def _(i):
            extra[1](i)

    if gather:
        gather.drain()
    if reduce:
        pl.loop(0, groups)(reduce.drain)


def starts_of(lengths, places):
    end, start = jnp.int32(0), jnp.zeros_like(places)
    for length in lengths:
        end = end + length
        start = start + jnp.where(places >= end, length, 0)
    return start


def softmax_block(q, k, start, first_query, first_key, scaling):
    raw = dot(k, q, NT)
    keys = first_key + lax.broadcasted_iota(jnp.int32, raw.shape, 0)
    queries = first_query + lax.broadcasted_iota(jnp.int32, raw.shape, 1)
    raw = jnp.where((keys <= queries) & (keys >= start), raw * scaling, NEGATIVE)
    exponent = jnp.exp(raw - jnp.max(raw, axis=0, keepdims=True))
    return exponent * (1.0 / jnp.sum(exponent, axis=0, keepdims=True))


def query_starts(lengths, first):
    places = first + lax.broadcasted_iota(jnp.int32, (8, QROWS), 1)
    return starts_of([lengths[0, n] for n in range(lengths.shape[1])], places)[:1]


def weight_rows(i, reach):
    ramp = reach * (reach - 1) // 2
    if isinstance(i, int) and i < reach:
        return i * (i + 1) // 2 * QROWS
    return (ramp + (i - reach + 1) * reach) * QROWS


def put_grouped(out, block, i, own_tokens, rows, at=slice(None)):
    for n in range(0, QROWS, rows):
        rank, inside = divmod(n, own_tokens)
        rank += i * (QROWS // own_tokens)
        out[inside // rows, pl.ds(pl.multiple_of(rank * rows, rows), rows), at] = block[n : n + rows]


def attend_back(qkv, grad, kept_weights, count, cosines, sines, width, groups, own_tokens):
    length, heads = qkv.shape[0], width // HDIM
    scaling = HDIM ** (-0.5)
    reach = MAXDOC // QROWS + 1
    rows_own = own_tokens // groups

    def body(active, q, k, v, g, cos, sin, kept, g_q, g_k, g_v, k_t, sum_k, sum_v):
        live = lax.axis_index("tensor") * heads + pl.program_id(0) < active[0]

        @pl.when(jnp.logical_not(live))
        def _():
            g_q[...] = jnp.zeros_like(g_q)
            g_k[...] = jnp.zeros_like(g_k)
            g_v[...] = jnp.zeros_like(g_v)

        def rotate_back(d, rows):
            return (d * cos[rows] + swap_halves(d * sin[rows])).astype(BF)

        @pl.when(live)
        def _():
            k_t[...] = k[...].T
            sum_k[...] = jnp.zeros_like(sum_k)
            sum_v[...] = jnp.zeros_like(sum_v)
            def back_block(i, count):
                low = i + 1 - count
                rows = pl.ds(pl.multiple_of(i * QROWS, QROWS), QROWS)
                keys = pl.ds(pl.multiple_of(low * QROWS, QROWS), count * QROWS)
                weights = kept[0, pl.ds(weight_rows(i, reach), count * QROWS)]
                sum_v[keys] += dot(weights, g[rows])
                weights = weights.astype(F32)
                g_weights = dot(v[keys], g[rows], NT)
                inner = jnp.sum(weights * g_weights, axis=0, keepdims=True)
                g_scores = (weights * (g_weights - inner)).astype(BF)
                sum_k[keys] += dot(g_scores, q[rows])
                back = rotate_back(dot(k_t[:, keys], g_scores).T * scaling, rows)
                put_grouped(g_q, back, i, own_tokens, rows_own)

            for i in range(length // QROWS):
                back_block(i, min(i + 1, reach))

            for i in range(length // QROWS):
                rows = pl.ds(pl.multiple_of(i * QROWS, QROWS), QROWS)
                put_grouped(g_k, rotate_back(sum_k[rows] * scaling, rows), i, own_tokens, rows_own)
                put_grouped(g_v, sum_v[rows].astype(BF), i, own_tokens, rows_own)

    column = lambda n: pl.BlockSpec((length, HDIM), lambda h, live: (0, n * heads + h))
    table = pl.BlockSpec((length, HDIM), lambda h, live: (0, 0))
    return pl.pallas_call(
        body,
        out_shape=[jax.ShapeDtypeStruct((groups, length // groups, width), BF)] * 3,
        grid_spec=pltpu.PrefetchScalarGridSpec(
            num_scalar_prefetch=1,
            grid=(heads,),
            in_specs=[
                column(0),
                column(1),
                column(2),
                column(0),
                table,
                table,
                pl.BlockSpec((1, *kept_weights.shape[1:]), lambda h, live: (h, 0, 0)),
            ],
            out_specs=[pl.BlockSpec((groups, length // groups, HDIM), lambda h, live: (0, 0, h))] * 3,
            scratch_shapes=[
                pltpu.VMEM((HDIM, length), BF),
                pltpu.VMEM((length, HDIM), F32),
                pltpu.VMEM((length, HDIM), F32),
            ],
        ),
        compiler_params=pltpu.CompilerParams(vmem_limit_bytes=60 << 20),
        cost_estimate=pl.CostEstimate(flops=10 << 30, bytes_accessed=16 << 20, transcendentals=0),
    )(count, qkv, qkv, qkv, grad, cosines, sines, kept_weights)


class Spread:
    def __init__(self, size, out, land, send, recv, rows=None):
        self.size, self.out, self.land, self.send, self.recv = size, out, land, send, recv
        self.rows = rows
        self.me = lax.axis_index("dp")

    def target(self, n):
        return lax.rem(self.me + n, self.size)

    def copy(self, n, source=None):
        return pltpu.make_async_remote_copy(
            src_ref=self.out.at[n],
            dst_ref=self.place(self.me if source is None else source),
            send_sem=self.send.at[n],
            recv_sem=self.recv.at[n],
            device_id={"dp": self.target(n)},
            device_id_type=MESH,
        )

    def place(self, source):
        return self.land.at[source] if self.rows is None else self.land.at[source, self.rows]

    def own(self):
        return pltpu.make_async_copy(self.out.at[0], self.place(self.me), self.send.at[0])

    def begin(self, n):
        @pl.when(n == 0)
        def _():
            self.own().start()

        @pl.when(n != 0)
        def _():
            self.copy(n).start()

    def end(self):
        self.own().wait()

        @pl.loop(1, self.size)
        def _(n):
            self.copy(n).wait_send()
            self.copy(n, lax.rem(self.me + self.size - n, self.size)).wait_recv()

    @staticmethod
    def scratch(size, shape):
        return [pltpu.VMEM((size, *shape), BF), DMA((size,)), DMA((size,))]


class Loads:
    def __init__(self, pairs, sems):
        self.copies = [
            pltpu.make_async_copy(source, held, sems.at[n]) for n, (source, held) in enumerate(pairs)
        ]

    def begin(self, first, *which):
        @pl.when(first)
        def _():
            for n in which:
                self.copies[n].start()

    def need(self, first, *which):
        @pl.when(first)
        def _():
            for n in which:
                self.copies[n].wait()


class Store:
    def __init__(self, held, out, sems, at=lambda ref, g: ref.at[g]):
        self.held, self.out, self.sems, self.at = held, out, sems, at

    def copy(self, g):
        return pltpu.make_async_copy(self.at(self.held, g), self.at(self.out, g), self.sems.at[g])

    def put(self, g):
        self.copy(g).start()

    def end(self, g):
        self.copy(g).wait()


class Turns:
    def __init__(self, pairs, sems, at=lambda ref, g: ref.at[g]):
        self.pairs, self.sems, self.at = pairs, sems, at

    def each(self, g):
        return [
            pltpu.make_async_copy(held.at[lax.rem(g, 2)], self.at(out, g), self.sems.at[n, g])
            for n, (held, out) in enumerate(self.pairs)
        ]

    def free(self, g):
        @pl.when(g >= 2)
        def _():
            for copy in self.each(g - 2):
                copy.wait()

        return lax.rem(g, 2)

    def put(self, g):
        for copy in self.each(g):
            copy.start()

    def end(self, groups):
        for g in range(max(groups - 2, 0), groups):
            for copy in self.each(g):
                copy.wait()


def scratch_of(*arrays):
    return [pltpu.VMEM(a.shape, a.dtype) for a in arrays]


def row_mean(field):
    return jnp.mean(field, axis=1, keepdims=True)


def layer_norm(resid):
    centred = resid - row_mean(resid)
    inv_std = lax.rsqrt(row_mean(centred * centred) + EPSILON)
    return centred * inv_std, inv_std


def front(
    tokens, cotangent, probs, gain, lengths, frequency, count, w_qkv, w_out, g_ln, b_ln, w_up, w_down, widths, ranks
):
    width, columns = w_out.shape[0], w_up.shape[1]
    tile = min(256, columns)
    groups, rows, model = tokens.shape
    heads = width // HDIM
    chips = ranks // 2
    own_tokens = groups * rows
    length = ranks * own_tokens
    shift = rows.bit_length() - 1
    scaling = HDIM ** (-0.5)
    reach = MAXDOC // QROWS + 1
    span = QROWS // own_tokens
    blocks = length // QROWS
    lead, ahead = 2, 3
    hops = chips - 1
    tokens_all = ranks * rows
    normed_at = lead + 1 + hops
    hidden_at = normed_at + hops + 1
    back_at = hidden_at + 1 + hops

    def body(
        x_ref, dy, p, gain_ref, docs, freq, active, w, wo, gain2, bias2, up, down, wide,
        qkv, kept_x, cos_out, sin_out, attended, resid, kept_grad, grad_resid, grad_low, gains, kept_ln, squared,
        hidden_grad, kept_weights,
        full, w_v, wo_v, dy_v, up_v, down_v, qkv_v, cos_v, sin_v, v_t, attended_v, low_v, resid_v, high_v, grad_v,
        lifted, squared_v, hidden_v,
        a_send, a_recv, a_across, b_send, b_recv, b_across, c_send, c_recv, c_across,
        part, near, far, acc, s1, s2, s3, t1, t2, t3,
        load_sem, kept_sem, out_sem, place_sem, attended_sem, resid_sem, result_sem, tile_sem, weights_v, weights_sem,
    ):
        line = Line(ranks, rows)
        loads = Loads([(w, w_v), (wo, wo_v), (dy, dy_v), (up, up_v), (down, down_v)], load_sem)

        @pl.loop(0, groups)
        def _(g):
            x = x_ref[g].astype(F32)
            normal = x * lax.rsqrt(row_mean(x * x) + EPSILON) * gain_ref[...]
            full[g, line.z, line.c] = normal.astype(BF)

        line.barrier()
        gather = Gather(line, full, a_send, a_recv, a_across)
        tables = Turns([(cos_v, cos_out), (sin_v, sin_out)], out_sem.at[pl.ds(1, 2)], lambda ref, g: ref.at[:, g])
        stores = [
            Store(full, kept_x, kept_sem.at[0]),
            Store(qkv_v, qkv, out_sem.at[0], lambda ref, g: ref.at[:, g]),
        ]
        place_grad = pltpu.make_async_copy(low_v, kept_grad.at[:, line.z, line.c], place_sem)

        second = Gather(line, kept_grad, b_send, b_recv, b_across)

        def second_turn(j):
            for h in range(hops, 0, -1):
                within(j - h, groups, functools.partial(second.hop, h=h))
            within(j, groups, second.begin)

        def scale_grad(turn):
            loads.begin(turn == 0, 0, 1, 2)

            @pl.when(turn == 1)
            def _():
                loads.need(True, 2)

                @pl.loop(0, groups)
                def _(g):
                    low_v[g] = (dy_v[g].astype(F32) * p[g, :, :1]).astype(BF)

                place_grad.start()

            pl.when(turn == 2)(place_grad.wait)
            second_turn(turn - groups - hops - 1 + ahead)

        def project(g):
            r = lax.broadcasted_iota(jnp.int32, (ranks * rows, HDIM), 0)
            lane = lax.broadcasted_iota(jnp.int32, (ranks * rows, HDIM), 1)
            places = lax.shift_right_logical(r, shift) * own_tokens + g * rows + (r & (rows - 1))
            starts = starts_of([docs[0, n] for n in range(docs.shape[1])], places)
            angles = (places - starts).astype(F32) * freq[...]
            c = jnp.cos(angles)
            s = jnp.sin(angles)
            s = jnp.where(lane < HDIM // 2, -s, s)
            slot = tables.free(g)
            for rank in range(ranks):
                cos_v[slot, rank] = c[rank * rows : (rank + 1) * rows]
                sin_v[slot, rank] = s[rank * rows : (rank + 1) * rows]
            tables.put(g)
            gather.arrived(g)
            loads.need(g == 0, 0)
            x = full[g].reshape(ranks * rows, model)
            for which in range(3):
                out = dot(x, w_v[which])
                for h in range(heads):
                    u = out[:, h * HDIM : (h + 1) * HDIM]
                    if which < 2:
                        u = u * c + swap_halves(u) * s
                    u = u.astype(BF)
                    at = (which * heads + h) * HDIM
                    for rank in range(ranks):
                        qkv_v[rank, g, :, at : at + HDIM] = u[rank * rows : (rank + 1) * rows]
            for store in stores:
                store.put(g)

        stream(line, groups, gather, arrived=project, extra=(groups + hops + 1, scale_grad))

        @pl.loop(0, groups)
        def _(g):
            for store in stores:
                store.end(g)

        tables.end(groups)
        loads.begin(True, 3, 4)
        third = Gather(line, full, c_send, c_recv, c_across)
        reduce = Reduce(line, part, near, far, acc, s1, s2, s3)
        reduce_back = Reduce(line, part, near, far, acc, t1, t2, t3)
        keep = Store(attended_v, attended, attended_sem)
        keep_ln = Store(full, kept_ln, kept_sem.at[1])
        keep_resid = Store(resid_v, resid, resid_sem)
        keep_low = Store(low_v, grad_low, result_sem)
        highs = Turns([(high_v, grad_resid)], tile_sem.at[pl.ds(1, 1)])
        hiddens = Turns([(squared_v, squared), (hidden_v, hidden_grad)], tile_sem.at[pl.ds(2, 2)])
        gains[...] = jnp.zeros_like(gains)
        first_column = line.t * columns

        def fetch(g):
            slot = lax.rem(g, 2)
            return pltpu.make_async_copy(kept_grad.at[g], grad_v.at[slot], tile_sem.at[0, slot])

        def part_of(which, h):
            return pl.ds(pl.multiple_of((which * heads + h) * HDIM, HDIM), HDIM)

        def keep_weights(i, count, h):
            rows_kept = weight_rows(i if count == reach else count - 1, reach)
            return pltpu.make_async_copy(
                weights_v.at[h, pl.ds(0, count * QROWS)],
                kept_weights.at[h, pl.ds(pl.multiple_of(rows_kept, QROWS), count * QROWS)],
                weights_sem.at[h],
            )

        def attend_block(i, count):
            low = i + 1 - count
            start = query_starts(docs, i * QROWS)

            @pl.loop(0, heads)
            def _(h):
                q = qkv_v[pl.ds(i * span, span), :, :, part_of(0, h)].reshape(QROWS, HDIM)
                k = qkv_v[pl.ds(low * span, count * span), :, :, part_of(1, h)].reshape(count * QROWS, HDIM)
                weights = softmax_block(q, k, start, i * QROWS, low * QROWS, scaling).astype(BF)
                keys = pl.ds(pl.multiple_of(low * QROWS, QROWS), count * QROWS)
                done = dot(v_t[h, :, keys], weights).T
                done = (done * jnp.where(line.t * heads + h < active[0], 1.0, 0.0)).astype(BF)
                put_grouped(attended_v, done, i, own_tokens, rows, part_of(0, h))
                if not isinstance(i, int):
                    pl.when(i == reach - 1)(lambda: keep_weights(i - 1, reach - 1, h).wait())
                    pl.when(i > reach - 1)(lambda: keep_weights(i - 1, reach, h).wait())
                elif i:
                    keep_weights(i - 1, count - 1, h).wait()
                weights_v[h, : count * QROWS] = weights
                keep_weights(i, count, h).start()

        def attention(turn):
            @pl.when(turn == 0)
            def _():
                @pl.loop(0, heads)
                def _(h):
                    v_t[h] = qkv_v[:, :, :, part_of(2, h)].reshape(length, HDIM).T

                for i in range(min(reach - 1, blocks)):
                    attend_block(i, i + 1)

            @pl.when(turn == 1)
            def _():
                @pl.loop(reach - 1, blocks)
                def _(i):
                    attend_block(i, reach)

        def produce(g):
            keep.put(g)
            loads.need(g == 0, 1)
            for n in range(0, model, 512):
                out = dot(attended_v[g], wo_v[:, n : n + 512]).astype(BF)
                part[g, ..., n : n + 512] = out.reshape(chips, 2, rows, 512)

        def norm(g):
            reduce.last(g)
            total = x_ref[g].astype(F32) + acc[...]
            resid_v[g] = total
            keep_resid.put(g)
            lhat, _ = layer_norm(total)
            full[g, line.z, line.c] = (lhat * gain2[...] + bias2[...]).astype(BF)
            third.begin(g)

        def arrived(g):
            third.arrived(g)
            keep_ln.put(g)
            reduce.drain(g)

            @pl.when(g == 0)
            def _():
                fetch(0).start()

            fetch(g).wait()

            @pl.when(g + 1 < groups)
            def _():
                fetch(g + 1).start()

            loads.need(g == 0, 3, 4)

        def forward(g):
            slot = hiddens.free(g)
            limit = (jnp.broadcast_to(wide[pl.ds(g, 1), :], (HDIM, tokens_all)).T[:, :1] + 1) * (FF // 4)

            @pl.loop(0, columns // tile)
            def _(n):
                at = pl.ds(pl.multiple_of(n * tile, tile), tile)
                hidden = dot(full[g].reshape(tokens_all, model), up_v[:, at])
                ids = first_column + n * tile + lax.broadcasted_iota(jnp.int32, hidden.shape, 1)
                live = jnp.where(ids < limit, jnp.maximum(hidden, 0.0), 0.0)
                lifted[:, at] = live
                squared_v[slot, :, at] = (live * live).astype(BF)

        def backward(g):
            slot = lax.rem(g, 2)

            @pl.loop(0, columns // tile)
            def _(n):
                at = pl.ds(pl.multiple_of(n * tile, tile), tile)
                back = dot(grad_v[slot].reshape(tokens_all, model), down_v[at, :], NT)
                hidden_v[slot, :, at] = (back * (2.0 * lifted[:, at])).astype(BF)

            hiddens.put(g)

        def lower(g):
            slot = lax.rem(g, 2)

            @pl.loop(0, model // 256)
            def _(n):
                at = pl.ds(pl.multiple_of(n * 256, 256), 256)
                out = dot(hidden_v[slot], up_v[at, :], NT).astype(BF)
                part[g, :, :, :, at] = out.reshape(chips, 2, rows, 256)

        def finish(g):
            reduce_back.last(g)
            lhat, inv_std = layer_norm(resid_v[g])
            back = acc[...]
            gains[0:1] += jnp.sum(back * lhat, axis=0, keepdims=True)
            gains[1:2] += jnp.sum(back, axis=0, keepdims=True)
            back = back * gain2[...]
            back = dy_v[g].astype(F32) + inv_std * (back - row_mean(back) - lhat * row_mean(back * lhat))
            high_v[highs.free(g)] = back
            low_v[g] = back.astype(BF)
            highs.put(g)
            keep_low.put(g)

        @pl.loop(0, groups + back_at)
        def _(i):
            for n in range(hops):
                h, d = hops - n, n + 1
                within(i - hidden_at - 1 - hops + d, groups, functools.partial(reduce_back.step, d=d))
                within(i - normed_at - h, groups, functools.partial(third.hop, h=h))
                within(i - lead - 1 - hops + d, groups, functools.partial(reduce.step, d=d))
                within(i + ahead - h, groups, functools.partial(second.hop, h=h))
                if n == 0:
                    within(i - hidden_at, groups, arrived)
                for piece in (forward, backward, lower)[n * 3 // hops : (n + 1) * 3 // hops]:
                    within(i - hidden_at, groups, piece)
            within(i + ahead, groups, second.begin)
            within(i - hidden_at, groups, reduce_back.begin)
            within(i - normed_at, groups, norm)
            within(i - lead, groups, produce)
            within(i - lead, groups, reduce.begin)
            within(i + ahead - hops - 1, groups, second.arrived)
            within(i - back_at, groups, finish)
            within(i, lead, attention)

        for h in range(heads):
            keep_weights(blocks - 1, reach, h).wait()
        second.drain()
        third.drain()
        pl.loop(0, groups)(reduce_back.drain)

        @pl.loop(0, groups)
        def _(g):
            for store in (keep, keep_ln, keep_resid, keep_low):
                store.end(g)

        highs.end(groups)
        hiddens.end(groups)

    table = jax.ShapeDtypeStruct((ranks, groups, rows, HDIM), F32)
    projected = jax.ShapeDtypeStruct((ranks, groups, rows, 3 * width), BF)
    full = jax.ShapeDtypeStruct((groups, chips, 2, rows, model), BF)
    attended = jax.ShapeDtypeStruct((groups, tokens_all, width), BF)
    high = jax.ShapeDtypeStruct((groups, rows, model), F32)
    low = jax.ShapeDtypeStruct((groups, rows, model), BF)
    hidden = jax.ShapeDtypeStruct((groups, tokens_all, columns), BF)
    return call(
        body,
        [tokens, cotangent, probs, gain, lengths, frequency, count, w_qkv, w_out, g_ln, b_ln, w_up, w_down, widths],
        [
            projected,
            full,
            table,
            table,
            attended,
            high,
            full,
            high,
            low,
            jax.ShapeDtypeStruct((2, model), F32),
            full,
            hidden,
            hidden,
            jax.ShapeDtypeStruct((heads, weight_rows(blocks, reach), QROWS), BF),
        ],
        [
            *scratch_of(full, w_qkv, w_out, cotangent, w_up, w_down, projected),
            pltpu.VMEM((2, ranks, rows, HDIM), F32),
            pltpu.VMEM((2, ranks, rows, HDIM), F32),
            pltpu.VMEM((heads, HDIM, length), BF),
            *scratch_of(attended, low, high),
            pltpu.VMEM((2, rows, model), F32),
            pltpu.VMEM((2, chips, 2, rows, model), BF),
            pltpu.VMEM((tokens_all, columns), F32),
            pltpu.VMEM((2, tokens_all, columns), BF),
            pltpu.VMEM((2, tokens_all, columns), BF),
            *Gather.scratch(ranks, groups) * 3,
            *Reduce.scratch(ranks, groups, rows, model),
            *Reduce.scratch(ranks, groups, rows, model)[-3:],
            DMA((5,)),
            DMA((2, groups)),
            DMA((3, groups)),
            DMA,
            *[DMA((groups,))] * 3,
            DMA((4, groups)),
            pltpu.VMEM((heads, reach * QROWS, QROWS), BF),
            DMA((heads,)),
        ],
        0,
        in_specs=[VM, ANY, VM, VM, SM, VM, SM, ANY, ANY, VM, VM, ANY, ANY, VM],
        out_specs=[ANY] * 9 + [VM] + [ANY] * 4,
        flops=8 * length * model * (width + columns),
        moved=160 << 20,
    )


def hidden_weights(spread, inputs, hidden, first, turn_of, columns):
    n = turn_of
    side = min(256, spread.out.shape[1])

    @pl.loop(0, spread.out.shape[1] // side)
    def _(m):
        at = pl.ds(pl.multiple_of(first + m * side, side), side)
        to = pl.ds(pl.multiple_of(m * side, side), side)
        x = inputs[:, :, at]
        spread.out[n, to] = dot(
            x.reshape(x.shape[0] * x.shape[1], side), hidden[...].reshape(-1, columns), TN
        ).astype(BF)

    spread.begin(n)


def feed_out(
    own_grad, squared, hidden_grad, kept_ln, branch_grad, w_down, w_out, count, resid, cotangent, probs, ranks, sequences
):
    groups, rows, model = own_grad.shape
    columns, width = w_down.shape[0], w_out.shape[0]
    tokens = ranks * rows
    share = model // sequences
    half = share // 2

    def body(
        own, sq, hg, ln, bg, down, w, active, res, dy, p, result, probs_grad, kept, grad, land_down, land_up,
        full, g_send, g_recv, g_across, part, near, far, acc, s1, s2, s3, kept_sem,
        out_down, down_send, down_recv, out_up, up_send, up_recv, ln_v, bg_v, fetch_sem,
        sq_v, hg_v, down_v, res_v, dy_v, load_sem, result_v, back_v, result_sem, back_sem,
    ):
        line = Line(ranks, rows)
        gather = Gather(line, full, g_send, g_recv, g_across)
        reduce = Reduce(line, part, near, far, acc, s1, s2, s3)
        to_down = Spread(sequences, out_down, land_down, down_send, down_recv)
        to_up = Spread(sequences, out_up, land_up, up_send, up_recv, pl.ds(0, half))
        keep = Store(full, kept, kept_sem)
        keep_result = Store(result_v, result, result_sem)
        keep_back = Store(back_v, grad, back_sem, lambda ref, g: ref.at[:, g])

        def arrived(g):
            gather.arrived(g)
            keep.put(g)
            heads = line.t * (width // HDIM) + lax.broadcasted_iota(jnp.int32, (1, width), 1) // HDIM
            live = jnp.where(heads < active[0], 1.0, 0.0)
            back = (dot(full[g].reshape(tokens, model), w[...], NT) * live).astype(BF)
            for rank in range(ranks):
                back_v[rank, g] = back[rank * rows : (rank + 1) * rows]
            keep_back.put(g)

        def produce(g):
            loads.need(g == 0, 0, 1)

            @pl.loop(0, model // 256)
            def _(n):
                at = pl.ds(pl.multiple_of(n * 256, 256), 256)
                out = dot(sq_v[g], down_v[:, at]).astype(BF)
                part[g, :, :, :, at] = out.reshape(ranks // 2, 2, rows, 256)

        def finish(g):
            loads.need(g == 0, 3, 4)
            ffn = acc[...]
            result_v[g] = (res_v[g] + p[g, :, :1] * ffn).astype(BF)
            keep_result.put(g)
            scores = jnp.sum(dy_v[g].astype(F32) * ffn, axis=1, keepdims=True)
            probs_grad[pl.ds(g, 1)] = jnp.broadcast_to(scores, (rows, HDIM)).T[:1]

        def fetches(step):
            at = pl.multiple_of(to_up.target(lax.rem(step + 1, sequences)) * share, share)
            return [
                pltpu.make_async_copy(ln.at[:, :, pl.ds(at, half)], ln_v, fetch_sem.at[0]),
                pltpu.make_async_copy(bg.at[:, :, pl.ds(at, share)], bg_v, fetch_sem.at[1]),
            ]

        def weights(step):
            n = lax.rem(step + 1, sequences)
            loads.need(step == 0, 2)
            for fetch in fetches(step):
                fetch.wait()
            side = min(256, columns)

            @pl.loop(0, columns // side)
            def _(m):
                at = pl.ds(pl.multiple_of(m * side, side), side)
                out_down[n, at] = dot(
                    sq_v[:, :, at].reshape(groups * tokens, side), bg_v[...].reshape(groups * tokens, share), TN
                ).astype(BF)

            to_down.begin(n)
            hidden_weights(to_up, ln_v, hg_v, 0, n, columns)

            @pl.when(step + 1 < sequences)
            def _():
                for fetch in fetches(step + 1):
                    fetch.start()

        def beside(turn):
            loads.begin(turn == 0, 0, 1, 2)

            @pl.when(turn == 0)
            def _():
                for fetch in fetches(0):
                    fetch.start()

            loads.begin(turn == 3, 3, 4)
            within(turn - 1, sequences, weights)

        loads = Loads(
            [
                (sq, sq_v),
                (down, down_v),
                (hg, hg_v),
                (res, res_v),
                (dy, dy_v),
                (own, full.at[:, line.z, line.c]),
            ],
            load_sem,
        )
        loads.begin(True, 5)
        line.barrier(sequences)
        loads.need(True, 5)
        stream(
            line, groups, gather, arrived, reduce, [produce], finish, 1, (max(sequences + 1, 4), beside)
        )

        @pl.loop(0, groups)
        def _(g):
            for store in (keep, keep_result, keep_back):
                store.end(g)

        to_down.end()
        to_up.end()

    kept = jax.ShapeDtypeStruct((groups, ranks // 2, 2, rows, model), BF)
    low = jax.ShapeDtypeStruct((groups, rows, model), BF)
    back = jax.ShapeDtypeStruct((ranks, groups, rows, width), BF)
    return call(
        body,
        [own_grad, squared, hidden_grad, kept_ln, branch_grad, w_down, w_out, count, resid, cotangent, probs],
        [
            low,
            jax.ShapeDtypeStruct((groups, rows), F32),
            kept,
            back,
            jax.ShapeDtypeStruct((sequences, columns, share), BF),
            jax.ShapeDtypeStruct((sequences, share, columns), BF),
        ],
        [
            *scratch_of(kept),
            *Gather.scratch(ranks, groups),
            *Reduce.scratch(ranks, groups, rows, model),
            DMA((groups,)),
            *Spread.scratch(sequences, (columns, share)),
            *Spread.scratch(sequences, (half, columns)),
            pltpu.VMEM((groups, tokens, half), BF),
            pltpu.VMEM((groups, tokens, share), BF),
            DMA((2,)),
            *scratch_of(squared, hidden_grad, w_down, resid, cotangent),
            DMA((6,)),
            *scratch_of(low, back),
            DMA((groups,)),
            DMA((groups,)),
        ],
        3,
        in_specs=[ANY, ANY, ANY, ANY, ANY, ANY, VM, SM, ANY, ANY, VM],
        out_specs=[ANY, VM, ANY, ANY, ANY, ANY],
        flops=2 * groups * tokens * model * (3 * columns + width),
        moved=100 << 20,
    )


def project_back(
    grads, w_qkv, kept_x, attended, attn_grad, kept_ln, hidden_grad, landed_up, tokens, gain, grad_resid, gains, ranks, sequences
):
    groups, tokens_all, width = grads[0].shape
    rows = tokens_all // ranks
    model = w_qkv.shape[1]
    columns = hidden_grad.shape[2]
    share = model // sequences
    half = share // 2

    def body(
        gq, gk, gv, w, xs, a, ga, ln, hg, up_in, x_ref, gain_ref, g_res, gain_parts,
        tokens_grad, totals, land_qkv, land_out, land_up,
        part, near, far, acc, s1, s2, s3,
        out_qkv, qkv_send, qkv_recv, out_out, out_send, out_recv, out_up, up_send, up_recv,
        x_v, ga_v, ln_v, fetch_sem, group_v, group_sem, w_v, a_v, hg_v, own_v, res_v, load_sem,
        mine, terms, t_send, t_recv, sums, d_send, d_recv, g_q, g_k, g_v, grad_v, grad_sem,
    ):
        line = Line(ranks, rows)
        me = lax.axis_index("dp")
        reduce = Reduce(line, part, near, far, acc, s1, s2, s3)
        to_qkv = Spread(sequences, out_qkv, land_qkv, qkv_send, qkv_recv)
        to_out = Spread(sequences, out_out, land_out, out_send, out_recv)
        to_up = Spread(sequences, out_up, land_up, up_send, up_recv, pl.ds(half, half))
        parts = (g_q, g_k, g_v)
        loads = Loads(
            [(w, w_v), (a, a_v), (hg, hg_v), (x_ref, own_v), (g_res, res_v), (gq, g_q), (gk, g_k), (gv, g_v)],
            load_sem,
        )
        keep_grad = Store(grad_v, tokens_grad, grad_sem)

        def group_fetch(g):
            slot = lax.rem(g, 2)
            return pltpu.make_async_copy(xs.at[g], group_v.at[slot], group_sem.at[slot])

        loads.begin(True, 0, 5, 6, 7)
        group_fetch(0).start()
        mine[0:1] = jnp.zeros((1, model), F32)
        mine[1:3] = gain_parts[...]

        def produce(g):
            loads.need(g == 0, 0, 5, 6, 7)
            group_fetch(g).wait()

            @pl.when(g + 1 < groups)
            def _():
                group_fetch(g + 1).start()

            slot = lax.rem(g, 2)

            @pl.loop(0, model // 256)
            def _(n):
                at = pl.ds(pl.multiple_of(n * 256, 256), 256)
                out = dot(g_q[g], w_v[0, at], NT)
                out += dot(g_k[g], w_v[1, at], NT)
                out += dot(g_v[g], w_v[2, at], NT)
                part[g, :, :, :, at] = out.astype(BF).reshape(ranks // 2, 2, rows, 256)
                mine[0:1, at] += jnp.sum(out * group_v[slot, :, at].astype(F32), axis=0, keepdims=True)

        def finish(g):
            loads.need(g == 0, 3, 4)
            x = own_v[g].astype(F32)
            scale = lax.rsqrt(row_mean(x * x) + EPSILON)
            hat = x * scale
            back = acc[...] * gain_ref[...]
            grad_v[g] = res_v[g] + scale * (back - hat * row_mean(back * hat))
            keep_grad.put(g)

        def fetches(step):
            at = pl.multiple_of(to_qkv.target(lax.rem(step + 1, sequences)) * share, share)
            return [
                pltpu.make_async_copy(ln.at[:, :, pl.ds(at + half, half)], ln_v, fetch_sem.at[0]),
                pltpu.make_async_copy(xs.at[:, :, pl.ds(at, share)], x_v, fetch_sem.at[1]),
                pltpu.make_async_copy(ga.at[:, :, pl.ds(at, share)], ga_v, fetch_sem.at[2]),
            ]

        def weights(piece):
            step = piece // 2
            n = lax.rem(step + 1, sequences)

            @pl.when(lax.rem(piece, 2) == 0)
            def _():
                loads.need(step == 0, 1, 2)
                fetches(step)[0].wait()
                hidden_weights(to_up, ln_v, hg_v, 0, n, columns)

                @pl.when(step + 1 < sequences)
                def _():
                    fetches(step + 1)[0].start()

            @pl.when(lax.rem(piece, 2) == 1)
            def _():
                for fetch in fetches(step)[1:]:
                    fetch.wait()

                @pl.loop(0, share // 256)
                def _(m):
                    at = pl.ds(pl.multiple_of(m * 256, 256), 256)
                    x = x_v[:, :, at].reshape(groups * tokens_all, 256)
                    for which in range(3):
                        out_qkv[n, which, at] = dot(
                            x, parts[which][...].reshape(groups * tokens_all, width), TN
                        ).astype(BF)

                to_qkv.begin(n)
                out_out[n] = dot(
                    a_v[...].reshape(groups * tokens_all, width), ga_v[...].reshape(groups * tokens_all, share), TN
                ).astype(BF)
                to_out.begin(n)

                @pl.when(step + 1 < sequences)
                def _():
                    for fetch in fetches(step + 1)[1:]:
                        fetch.start()

        def to_rank(n, source=None):
            return copy_to(
                mine,
                terms.at[line.t if source is None else source],
                t_send.at[n],
                t_recv.at[n],
                lax.rem(line.t + n, ranks),
            )

        def to_sequence(n, source=None):
            return pltpu.make_async_remote_copy(
                src_ref=sums.at[me],
                dst_ref=sums.at[me if source is None else source],
                send_sem=d_send.at[n],
                recv_sem=d_recv.at[n],
                device_id={"dp": lax.rem(me + n, sequences)},
                device_id_type=MESH,
            )

        def beside(turn):
            loads.begin(turn == 0, 1, 2)
            loads.begin(turn == 2, 3, 4)

            @pl.when(turn == 0)
            def _():
                for fetch in fetches(0):
                    fetch.start()

            within(turn - 1, 2 * sequences, weights)

            @pl.when(turn == groups)
            def _():
                mine[0:1] = mine[0:1] / gain_ref[...]
                terms[line.t] = mine[...]

                @pl.loop(1, ranks)
                def _(n):
                    to_rank(n).start()

            @pl.when(turn == groups + 1)
            def _():
                @pl.loop(1, ranks)
                def _(n):
                    to_rank(n).wait_send()
                    to_rank(n, lax.rem(line.t + ranks - n, ranks)).wait_recv()

                total = terms[0]
                for n in range(1, ranks):
                    total += terms[n]
                sums[me] = total

                @pl.loop(1, sequences)
                def _(n):
                    to_sequence(n).start()

            @pl.when(turn == groups + 2)
            def _():
                @pl.loop(1, sequences)
                def _(n):
                    to_sequence(n).wait_send()
                    to_sequence(n, lax.rem(me + sequences - n, sequences)).wait_recv()

                total = sums[0]
                for n in range(1, sequences):
                    total += sums[n]
                totals[...] = total

        line.barrier_all(sequences)
        stream(
            line, groups, None, None, reduce, [produce], finish, extra=(max(groups + 3, 2 * sequences + 1), beside)
        )

        @pl.loop(0, groups)
        def _(g):
            keep_grad.end(g)

        to_qkv.end()
        to_out.end()

        to_up.end()

    return call(
        body,
        [*grads, w_qkv, kept_x, attended, attn_grad, kept_ln, hidden_grad, landed_up, tokens, gain, grad_resid, gains],
        [
            jax.ShapeDtypeStruct((groups, rows, model), F32),
            jax.ShapeDtypeStruct((3, model), F32),
            jax.ShapeDtypeStruct((sequences, 3, share, width), BF),
            jax.ShapeDtypeStruct((sequences, width, share), BF),
            jax.ShapeDtypeStruct(landed_up.shape, BF),
        ],
        [
            *Reduce.scratch(ranks, groups, rows, model),
            *Spread.scratch(sequences, (3, share, width)),
            *Spread.scratch(sequences, (width, share)),
            *Spread.scratch(sequences, (half, columns)),
            pltpu.VMEM((groups, tokens_all, share), BF),
            pltpu.VMEM((groups, tokens_all, share), BF),
            pltpu.VMEM((groups, tokens_all, half), BF),
            DMA((3,)),
            pltpu.VMEM((2, tokens_all, model), BF),
            DMA((2,)),
            *scratch_of(w_qkv, attended, hidden_grad, tokens, grad_resid),
            DMA((8,)),
            pltpu.VMEM((3, model), F32),
            pltpu.VMEM((ranks, 3, model), F32),
            DMA((ranks,)),
            DMA((ranks,)),
            pltpu.VMEM((sequences, 3, model), F32),
            DMA((sequences,)),
            DMA((sequences,)),
            *scratch_of(*grads, grad_resid),
            DMA((groups,)),
        ],
        4,
        in_specs=[ANY] * 11 + [VM, ANY, VM],
        out_specs=[ANY, VM, ANY, ANY, ANY],
        flops=12 * groups * tokens_all * model * width,
        moved=60 << 20,
        aliases={9: 4},
    )


def collect(result, tokens_grad, totals, *landed):
    steps = result.shape[0]

    def body(result_in, tokens_in, totals_in, *refs):
        pieces, outs = refs[: len(landed)], refs[len(landed) :]
        outs[0][...] = result_in[...]
        outs[1][...] = tokens_in[...]
        for n in range(3):
            outs[2 + n][...] = totals_in[n : n + 1]
        for piece, out in zip(pieces, outs[5:]):
            total = piece[0].astype(F32)
            for n in range(1, piece.shape[0]):
                total += piece[n].astype(F32)
            out[...] = total

    def split(a, at):
        block = list(a.shape)
        block[at] //= steps
        return pl.BlockSpec(tuple(block), lambda i: tuple(i if n == at else 0 for n in range(len(block))))

    sums = [jax.ShapeDtypeStruct(a.shape[1:], F32) for a in landed]
    row = jax.ShapeDtypeStruct((1, totals.shape[1]), F32)
    fixed = lambda a: pl.BlockSpec(a.shape, lambda i: (0, 0))
    return pl.pallas_call(
        body,
        out_shape=[
            jax.ShapeDtypeStruct(result.shape, BF),
            jax.ShapeDtypeStruct(tokens_grad.shape, F32),
            row,
            row,
            row,
            *sums,
        ],
        grid=(steps,),
        in_specs=[split(result, 0), split(tokens_grad, 0), fixed(totals)]
        + [split(a, a.ndim - 2) for a in landed],
        out_specs=[split(result, 0), split(tokens_grad, 0), fixed(row), fixed(row), fixed(row)]
        + [split(a, len(a.shape) - 2) for a in sums],
        compiler_params=pltpu.CompilerParams(vmem_limit_bytes=60 << 20),
        cost_estimate=pl.CostEstimate(flops=1 << 24, bytes_accessed=24 << 20, transcendentals=0),
    )(result, tokens_grad, totals, *landed)


def shards(
    tokens,
    cotangent,
    first_norm_gain,
    w_qkv,
    w_out,
    g_ln,
    b_ln,
    w_up,
    w_down,
    probs,
    lengths,
    head_count,
    widths,
):
    length_all = widths.shape[0]
    own_tokens, model = tokens.shape
    ranks = length_all // own_tokens
    sequences = lax.axis_size("dp")
    groups, rows = GROUPS, own_tokens // GROUPS
    width = w_out.shape[0]
    half = HDIM // 2
    frequency = 10000.0 ** (-np.arange(half) / half)
    frequency = jnp.asarray(np.concatenate([frequency, frequency]).reshape(1, HDIM), F32)
    w_qkv_t = w_qkv.transpose(1, 0, 2)
    x = tokens.reshape(groups, rows, model)
    dy = cotangent.reshape(groups, rows, model)
    first_norm_gain, g_ln, b_ln = (v.reshape(1, model) for v in (first_norm_gain, g_ln, b_ln))
    p = jnp.broadcast_to(probs.reshape(groups, rows, 1), (groups, rows, HDIM))
    wide = widths.reshape(ranks, groups, rows).swapaxes(0, 1).reshape(groups, ranks * rows)

    (
        qkv, kept_x, cosines, sines, attended, resid, kept_ffn_grad, grad_resid, grad_low, gains, kept_ln, squared,
        grad_hidden, kept_weights,
    ) = front(
        x, dy, p, first_norm_gain, lengths, frequency, head_count, w_qkv_t, w_out, g_ln, b_ln, w_up, w_down, wide, ranks
    )
    qkv = qkv.reshape(length_all, 3 * width)
    cosines, sines = cosines.reshape(length_all, HDIM), sines.reshape(length_all, HDIM)
    whole = lambda kept: kept.reshape(groups, ranks * rows, model)
    result, probs_grad, kept_attn_grad, grad_attended, land_down, land_up = feed_out(
        grad_low, squared, grad_hidden, whole(kept_ln), whole(kept_ffn_grad), w_down, w_out, head_count, resid, dy, p, ranks, sequences
    )
    grad_proj = attend_back(
        qkv,
        grad_attended.reshape(length_all, width),
        kept_weights,
        head_count,
        cosines,
        sines,
        width,
        groups,
        own_tokens,
    )
    tokens_grad, totals, land_qkv, land_out, land_up = project_back(
        grad_proj, w_qkv_t, whole(kept_x), attended, whole(kept_attn_grad), whole(kept_ln), grad_hidden, land_up, x, first_norm_gain,
        grad_resid, gains, ranks, sequences,
    )
    result, tokens_grad, rms, gain, bias, g_qkv, g_out, g_up, g_down = collect(
        result, tokens_grad, totals, land_qkv, land_out, land_up, land_down
    )
    return (
        result.reshape(own_tokens, model),
        tokens_grad.reshape(own_tokens, model),
        probs_grad.reshape(own_tokens),
        rms.reshape(model),
        g_qkv.transpose(1, 0, 2),
        g_out,
        gain.reshape(model),
        bias.reshape(model),
        g_up,
        g_down,
    )


def solution(mesh):
    placed = (
        P(("dp", "tensor"), None),
        P(("dp", "tensor"), None),
        P(),
        P(None, None, "tensor"),
        P("tensor", None),
        P(),
        P(),
        P(None, "tensor"),
        P("tensor", None),
        P(("dp", "tensor")),
        P("dp", None),
        P("dp"),
        P("dp"),
    )
    return jax.shard_map(
        shards,
        mesh=mesh,
        in_specs=placed,
        out_specs=(
            P(("dp", "tensor"), None),
            P(("dp", "tensor"), None),
            P(("dp", "tensor")),
            P(),
            P("dp", None, "tensor"),
            P("tensor", "dp"),
            P(),
            P(),
            P("dp", "tensor"),
            P("tensor", "dp"),
        ),
        check_vma=False,
    )
```

```python
import functools

import jax
import jax.numpy as jnp
import numpy as np
from jax import lax
from jax.experimental import pallas as pl
from jax.experimental.pallas import tpu as pltpu
from jax.sharding import PartitionSpec as P

HDIM = 128
FF = 8192
EPSILON = 1e-05
NEGATIVE = -1e30
MAXDOC = 1024
GROUPS = 8
QROWS = 256
MESH = pl.DeviceIdType.MESH
BF = jnp.bfloat16
F32 = jnp.float32
ANY = pl.BlockSpec(memory_space=pl.ANY)
VM = pl.BlockSpec(memory_space=pltpu.VMEM)
SM = pl.BlockSpec(memory_space=pltpu.SMEM)
DMA = pltpu.SemaphoreType.DMA
NT = (((1,), (1,)), ((), ()))
TN = (((0,), (0,)), ((), ()))


def dot(a, b, dims=(((1,), (0,)), ((), ()))):
    return lax.dot_general(a, b, dims, preferred_element_type=F32)


class Line:
    def __init__(self, ranks, rows):
        self.ranks, self.chips, self.rows = ranks, ranks // 2, rows
        self.t = lax.axis_index("tensor")
        self.z, self.c = self.t // 2, lax.rem(self.t, 2)
        self.has_up, self.has_down = self.z < self.chips - 1, self.z > 0
        self.up = jnp.minimum(self.t + 2, ranks - 1)
        self.down = jnp.maximum(self.t - 2, 0)
        self.partner = self.t + 1 - 2 * self.c

    def greet(self, dp_size=0):
        sem = pltpu.get_barrier_semaphore()
        pl.semaphore_signal(sem, inc=1, device_id={"tensor": self.partner}, device_id_type=MESH)

        @pl.when(self.has_up)
        def _():
            pl.semaphore_signal(sem, inc=1, device_id={"tensor": self.up}, device_id_type=MESH)

        @pl.when(self.has_down)
        def _():
            pl.semaphore_signal(sem, inc=1, device_id={"tensor": self.down}, device_id_type=MESH)

        d = lax.axis_index("dp")
        for step in range(1, dp_size):
            pl.semaphore_signal(
                sem, inc=1, device_id={"dp": lax.rem(d + step, dp_size)}, device_id_type=MESH
            )

    def meet(self, dp_size=0):
        links = self.has_up.astype(jnp.int32) + self.has_down.astype(jnp.int32)
        pl.semaphore_wait(pltpu.get_barrier_semaphore(), 1 + max(dp_size - 1, 0) + links)

    def greet_all(self, dp_size):
        sem = pltpu.get_barrier_semaphore()
        for n in range(1, self.ranks):
            pl.semaphore_signal(
                sem, inc=1, device_id={"tensor": lax.rem(self.t + n, self.ranks)}, device_id_type=MESH
            )
        d = lax.axis_index("dp")
        for n in range(1, dp_size):
            pl.semaphore_signal(
                sem, inc=1, device_id={"dp": lax.rem(d + n, dp_size)}, device_id_type=MESH
            )

    def meet_all(self, dp_size):
        pl.semaphore_wait(pltpu.get_barrier_semaphore(), self.ranks - 1 + dp_size - 1)


def copy_to(src, dst, send, recv, rank):
    return pltpu.make_async_remote_copy(
        src_ref=src,
        dst_ref=dst,
        send_sem=send,
        recv_sem=recv,
        device_id={"tensor": rank},
        device_id_type=MESH,
    )


class Gather:
    def __init__(self, line, full, send, recv, across_recv):
        self.l, self.full, self.send, self.recv, self.across_recv = line, full, send, recv, across_recv

    @staticmethod
    def scratch(ranks, groups):
        return [DMA((3, ranks // 2)), DMA((groups, ranks // 2)), DMA((groups,))]

    def along(self, g, z, up):
        l = self.l
        place = self.full.at[g, z, l.c]
        return copy_to(
            place,
            place,
            self.send.at[0 if up else 1, z],
            self.recv.at[0 if g == slice(None) else g, z],
            l.up if up else l.down,
        )

    def across(self, g, column):
        place = self.full.at[g, :, column]
        return copy_to(
            place, place, self.send.at[2, 0], self.across_recv.at[0 if g == slice(None) else g], self.l.partner
        )

    def pass_on(self, g, z, up):
        @pl.when(self.l.has_up if up else self.l.has_down)
        def _():
            self.along(g, z, up).start()

    def begin(self, g):
        self.pass_on(g, self.l.z, True)
        self.pass_on(g, self.l.z, False)

    def hop(self, g, h):
        l = self.l

        @pl.when(l.z - h >= 0)
        def _():
            self.along(g, l.z - h, True).wait_recv()
            self.pass_on(g, l.z - h, True)

        @pl.when(l.z + h <= l.chips - 1)
        def _():
            self.along(g, l.z + h, False).wait_recv()
            self.pass_on(g, l.z + h, False)

        if h == l.chips - 1:
            self.across(g, l.c).start()

    def arrived(self, g):
        self.across(g, 1 - self.l.c).wait_recv()

    def drain(self):
        l, every = self.l, slice(None)
        for z in range(l.chips):

            @pl.when(l.has_up & (l.z >= z))
            def _():
                self.along(every, z, True).wait_send()

            @pl.when(l.has_down & (l.z <= z))
            def _():
                self.along(every, z, False).wait_send()

        self.across(every, l.c).wait_send()


class Reduce:
    def __init__(self, line, part, near, far, acc, send, near_recv, far_recv):
        self.l, self.part, self.near, self.far, self.acc = line, part, near, far, acc
        self.send, self.near_recv, self.far_recv = send, near_recv, far_recv

    @staticmethod
    def scratch(ranks, groups, rows, width):
        chips = ranks // 2
        return [
            pltpu.VMEM((groups, chips, 2, rows, width), BF),
            pltpu.VMEM((groups, chips, rows, width), BF),
            pltpu.VMEM((groups, chips + 1, rows, width), BF),
            pltpu.VMEM((rows, width), F32),
            DMA((groups, chips + 1)),
            DMA((groups,)),
            DMA((groups, chips + 1)),
        ]

    def across(self, g):
        l = self.l
        return copy_to(
            self.part.at[g, :, 1 - l.c],
            self.near.at[g],
            self.send.at[g, l.chips],
            self.near_recv.at[g],
            l.partner,
        )

    def along(self, g, z, up, receive=False):
        l = self.l
        at = l.z if receive else jnp.where(up, l.z + 1, l.z - 1)
        slot = z if up else jnp.where(z == at, l.chips, z)
        return copy_to(
            self.part.at[g, z, l.c],
            self.far.at[g, slot],
            self.send.at[g, z],
            self.far_recv.at[g, slot],
            l.up if up else l.down,
        ), slot

    def begin(self, g):
        self.across(g).start()

    def add(self, g, z, slots, total=None):
        side = 512

        @pl.loop(0, self.part.shape[-1] // side)
        def _(n):
            at = pl.ds(pl.multiple_of(n * side, side), side)
            value = self.part[g, z, self.l.c, :, at].astype(F32) + self.near[g, z, :, at].astype(F32)
            for slot in slots:
                value += self.far[g, slot, :, at].astype(F32)
            if total is None:
                self.part[g, z, self.l.c, :, at] = value.astype(BF)
            else:
                total[:, at] = value

    def step(self, g, d):
        l = self.l
        if d == l.chips - 1:
            self.across(g).wait_recv()

        def send(z, up):
            further = l.has_down if up else l.has_up

            @pl.when(further)
            def _():
                copy, slot = self.along(g, z, up, receive=True)
                copy.wait_recv()
                self.add(g, z, [slot])

            @pl.when(jnp.logical_not(further))
            def _():
                self.add(g, z, [])

            self.along(g, z, up)[0].start()

        @pl.when(l.z + d <= l.chips - 1)
        def _():
            send(l.z + d, True)

        @pl.when(l.z - d >= 0)
        def _():
            send(l.z - d, False)

    def last(self, g):
        l = self.l

        @pl.when(l.has_down & l.has_up)
        def _():
            self.along(g, l.z, True, receive=True)[0].wait_recv()
            self.along(g, l.z, False, receive=True)[0].wait_recv()
            self.add(g, l.z, [l.z, l.chips], self.acc)

        @pl.when(jnp.logical_not(l.has_up))
        def _():
            self.along(g, l.z, True, receive=True)[0].wait_recv()
            self.add(g, l.z, [l.z], self.acc)

        @pl.when(jnp.logical_not(l.has_down))
        def _():
            self.along(g, l.z, False, receive=True)[0].wait_recv()
            self.add(g, l.z, [l.chips], self.acc)

    def drain(self, g):
        l = self.l
        self.across(g).wait_send()
        for z in range(l.chips):

            @pl.when(l.z != z)
            def _():
                copy_to(
                    self.part.at[g, z, l.c],
                    self.far.at[g, z],
                    self.send.at[g, z],
                    self.far_recv.at[g, z],
                    l.partner,
                ).wait_send()


def within(value, limit, body):
    pl.when((value >= 0) & (value < limit))(lambda: body(value))


def swap_halves(field):
    return pltpu.roll(field, HDIM // 2, axis=1)


def call(body, ins, outs, scratch, ident, in_specs=None, out_specs=None, limit=60, flops=0, moved=0, aliases=None):
    return pl.pallas_call(
        body,
        out_shape=outs,
        in_specs=in_specs or [VM] * len(ins),
        out_specs=out_specs or [VM] * len(outs),
        scratch_shapes=scratch,
        compiler_params=pltpu.CompilerParams(
            collective_id=ident, has_side_effects=True, vmem_limit_bytes=limit << 20
        ),
        input_output_aliases=aliases or {},
        cost_estimate=pl.CostEstimate(flops=flops, bytes_accessed=moved, transcendentals=0),
    )(*ins)


def stream(line, groups, gather=None, arrived=None, reduce=None, produce=(), finish=None, lead=0, extra=None):
    hops = line.chips - 1
    produce = list(produce)
    between = len(produce) > 1
    turns = groups + hops + 1 + (lead if reduce else 0)

    @pl.loop(0, turns)
    def _(i):
        for n in range(hops):
            if gather:
                within(i - hops + n, groups, functools.partial(gather.hop, h=hops - n))
            if reduce:
                d = n + 1
                within(i - lead - 1 - hops + d, groups, functools.partial(reduce.step, d=d))
            if n == hops - 1 and gather:
                within(i, groups, gather.begin)
            if between:
                if n == 0:
                    within(i - hops - 1, groups, arrived)
                for piece in produce[n * len(produce) // hops : (n + 1) * len(produce) // hops]:
                    within(i - lead, groups, piece)
        if not between:
            for piece in produce:
                within(i - lead, groups, piece)
        if reduce:
            within(i - lead, groups, reduce.begin)
        if arrived and not between:
            within(i - hops - 1, groups, arrived)
        if reduce:

            def end(g):
                reduce.last(g)
                finish(g)

            within(i - lead - 1 - hops, groups, end)
        if extra:
            within(i, min(extra[0], turns), extra[1])

    if extra:

        @pl.loop(min(extra[0], turns), extra[0])
        def _(i):
            extra[1](i)

    if gather:
        gather.drain()
    if reduce:
        pl.loop(0, groups)(reduce.drain)


def starts_of(lengths, places):
    end, start = jnp.int32(0), jnp.zeros_like(places)
    for length in lengths:
        end = end + length
        start = start + jnp.where(places >= end, length, 0)
    return start


def softmax_block(q, k, start, first_query, first_key, scaling):
    raw = dot(k, q, NT)
    keys = first_key + lax.broadcasted_iota(jnp.int32, raw.shape, 0)
    queries = first_query + lax.broadcasted_iota(jnp.int32, raw.shape, 1)
    raw = jnp.where((keys <= queries) & (keys >= start), raw * scaling, NEGATIVE)
    exponent = jnp.exp(raw - jnp.max(raw, axis=0, keepdims=True))
    return exponent * (1.0 / jnp.sum(exponent, axis=0, keepdims=True))


def query_starts(lengths, first):
    places = first + lax.broadcasted_iota(jnp.int32, (8, QROWS), 1)
    return starts_of([lengths[0, n] for n in range(lengths.shape[1])], places)[:1]


def weight_rows(i, reach):
    ramp = reach * (reach - 1) // 2
    if isinstance(i, int) and i < reach:
        return i * (i + 1) // 2 * QROWS
    return (ramp + (i - reach + 1) * reach) * QROWS


def put_grouped(out, block, i, own_tokens, rows, at=slice(None)):
    for n in range(0, QROWS, rows):
        rank, inside = divmod(n, own_tokens)
        rank += i * (QROWS // own_tokens)
        out[inside // rows, pl.ds(pl.multiple_of(rank * rows, rows), rows), at] = block[n : n + rows]


def attend_back(qkv, grad, kept_weights, count, cosines, sines, width, groups, own_tokens):
    length, heads = qkv.shape[0], width // HDIM
    scaling = HDIM ** (-0.5)
    reach = MAXDOC // QROWS + 1
    rows_own = own_tokens // groups

    def body(active, q, k, v, g, cos, sin, kept, g_q, g_k, g_v, k_t, sum_k, sum_v):
        live = lax.axis_index("tensor") * heads + pl.program_id(0) < active[0]

        @pl.when(jnp.logical_not(live))
        def _():
            g_q[...] = jnp.zeros_like(g_q)
            g_k[...] = jnp.zeros_like(g_k)
            g_v[...] = jnp.zeros_like(g_v)

        def rotate_back(d, rows):
            return (d * cos[rows] + swap_halves(d * sin[rows])).astype(BF)

        @pl.when(live)
        def _():
            k_t[...] = k[...].T
            sum_k[...] = jnp.zeros_like(sum_k)
            sum_v[...] = jnp.zeros_like(sum_v)
            def back_block(i, count):
                low = i + 1 - count
                rows = pl.ds(pl.multiple_of(i * QROWS, QROWS), QROWS)
                keys = pl.ds(pl.multiple_of(low * QROWS, QROWS), count * QROWS)
                weights = kept[0, pl.ds(weight_rows(i, reach), count * QROWS)]
                sum_v[keys] += dot(weights, g[rows])
                weights = weights.astype(F32)
                g_weights = dot(v[keys], g[rows], NT)
                inner = jnp.sum(weights * g_weights, axis=0, keepdims=True)
                g_scores = (weights * (g_weights - inner)).astype(BF)
                sum_k[keys] += dot(g_scores, q[rows])
                back = rotate_back(dot(k_t[:, keys], g_scores).T * scaling, rows)
                put_grouped(g_q, back, i, own_tokens, rows_own)

            for i in range(length // QROWS):
                back_block(i, min(i + 1, reach))

            for i in range(length // QROWS):
                rows = pl.ds(pl.multiple_of(i * QROWS, QROWS), QROWS)
                put_grouped(g_k, rotate_back(sum_k[rows] * scaling, rows), i, own_tokens, rows_own)
                put_grouped(g_v, sum_v[rows].astype(BF), i, own_tokens, rows_own)

    column = lambda n: pl.BlockSpec((length, HDIM), lambda h, live: (0, n * heads + h))
    table = pl.BlockSpec((length, HDIM), lambda h, live: (0, 0))
    return pl.pallas_call(
        body,
        out_shape=[jax.ShapeDtypeStruct((groups, length // groups, width), BF)] * 3,
        grid_spec=pltpu.PrefetchScalarGridSpec(
            num_scalar_prefetch=1,
            grid=(heads,),
            in_specs=[
                column(0),
                column(1),
                column(2),
                column(0),
                table,
                table,
                pl.BlockSpec((1, *kept_weights.shape[1:]), lambda h, live: (h, 0, 0)),
            ],
            out_specs=[pl.BlockSpec((groups, length // groups, HDIM), lambda h, live: (0, 0, h))] * 3,
            scratch_shapes=[
                pltpu.VMEM((HDIM, length), BF),
                pltpu.VMEM((length, HDIM), F32),
                pltpu.VMEM((length, HDIM), F32),
            ],
        ),
        compiler_params=pltpu.CompilerParams(vmem_limit_bytes=60 << 20),
        cost_estimate=pl.CostEstimate(flops=10 << 30, bytes_accessed=16 << 20, transcendentals=0),
    )(count, qkv, qkv, qkv, grad, cosines, sines, kept_weights)


class Spread:
    def __init__(self, size, out, land, send, recv, rows=None):
        self.size, self.out, self.land, self.send, self.recv = size, out, land, send, recv
        self.rows = rows
        self.me = lax.axis_index("dp")

    def target(self, n):
        return lax.rem(self.me + n, self.size)

    def copy(self, n, source=None):
        return pltpu.make_async_remote_copy(
            src_ref=self.out.at[n],
            dst_ref=self.place(self.me if source is None else source),
            send_sem=self.send.at[n],
            recv_sem=self.recv.at[n],
            device_id={"dp": self.target(n)},
            device_id_type=MESH,
        )

    def place(self, source):
        return self.land.at[source] if self.rows is None else self.land.at[source, self.rows]

    def own(self):
        return pltpu.make_async_copy(self.out.at[0], self.place(self.me), self.send.at[0])

    def begin(self, n):
        @pl.when(n == 0)
        def _():
            self.own().start()

        @pl.when(n != 0)
        def _():
            self.copy(n).start()

    def end(self):
        self.own().wait()

        @pl.loop(1, self.size)
        def _(n):
            self.copy(n).wait_send()
            self.copy(n, lax.rem(self.me + self.size - n, self.size)).wait_recv()

    @staticmethod
    def scratch(size, shape):
        return [pltpu.VMEM((size, *shape), BF), DMA((size,)), DMA((size,))]


class Loads:
    def __init__(self, pairs, sems):
        self.copies = [
            pltpu.make_async_copy(source, held, sems.at[n]) for n, (source, held) in enumerate(pairs)
        ]

    def begin(self, first, *which):
        @pl.when(first)
        def _():
            for n in which:
                self.copies[n].start()

    def need(self, first, *which):
        @pl.when(first)
        def _():
            for n in which:
                self.copies[n].wait()


class Store:
    def __init__(self, held, out, sems, at=lambda ref, g: ref.at[g]):
        self.held, self.out, self.sems, self.at = held, out, sems, at

    def copy(self, g):
        return pltpu.make_async_copy(self.at(self.held, g), self.at(self.out, g), self.sems.at[g])

    def put(self, g):
        self.copy(g).start()

    def end(self, g):
        self.copy(g).wait()


class Turns:
    def __init__(self, pairs, sems, at=lambda ref, g: ref.at[g]):
        self.pairs, self.sems, self.at = pairs, sems, at

    def each(self, g):
        return [
            pltpu.make_async_copy(held.at[lax.rem(g, 2)], self.at(out, g), self.sems.at[n, g])
            for n, (held, out) in enumerate(self.pairs)
        ]

    def free(self, g):
        @pl.when(g >= 2)
        def _():
            for copy in self.each(g - 2):
                copy.wait()

        return lax.rem(g, 2)

    def put(self, g):
        for copy in self.each(g):
            copy.start()

    def end(self, groups):
        for g in range(max(groups - 2, 0), groups):
            for copy in self.each(g):
                copy.wait()


def scratch_of(*arrays):
    return [pltpu.VMEM(a.shape, a.dtype) for a in arrays]


def row_mean(field):
    return jnp.mean(field, axis=1, keepdims=True)


def layer_norm(resid):
    centred = resid - row_mean(resid)
    inv_std = lax.rsqrt(row_mean(centred * centred) + EPSILON)
    return centred * inv_std, inv_std


def front(
    tokens, cotangent, probs, gain, lengths, frequency, count, w_qkv, w_out, g_ln, b_ln, w_up, w_down, widths, ranks
):
    width, columns = w_out.shape[0], w_up.shape[1]
    tile = min(256, columns)
    groups, rows, model = tokens.shape
    heads = width // HDIM
    chips = ranks // 2
    own_tokens = groups * rows
    length = ranks * own_tokens
    shift = rows.bit_length() - 1
    scaling = HDIM ** (-0.5)
    reach = MAXDOC // QROWS + 1
    span = QROWS // own_tokens
    blocks = length // QROWS
    lead, ahead = 2, 3
    hops = chips - 1
    tokens_all = ranks * rows
    normed_at = lead + 1 + hops
    hidden_at = normed_at + hops + 1
    back_at = hidden_at + 1 + hops

    def body(
        x_ref, dy, p, gain_ref, docs, freq, active, w, wo, gain2, bias2, up, down, wide,
        qkv, kept_x, cos_out, sin_out, attended, resid, kept_grad, grad_resid, grad_low, gains, kept_ln, squared,
        hidden_grad, kept_weights,
        full, w_v, wo_v, dy_v, up_v, down_v, qkv_v, cos_v, sin_v, v_t, attended_v, low_v, resid_v, high_v, grad_v,
        lifted, squared_v, hidden_v,
        a_send, a_recv, a_across, b_send, b_recv, b_across, c_send, c_recv, c_across,
        part, near, far, acc, s1, s2, s3, t1, t2, t3,
        load_sem, kept_sem, out_sem, place_sem, attended_sem, resid_sem, result_sem, tile_sem, weights_v, weights_sem,
    ):
        line = Line(ranks, rows)
        line.greet()
        loads = Loads([(w, w_v), (wo, wo_v), (dy, dy_v), (up, up_v), (down, down_v)], load_sem)

        gather = Gather(line, full, a_send, a_recv, a_across)

        class NormedFirst:
            hop, drain = gather.hop, gather.drain

            def begin(g):
                x = x_ref[g].astype(F32)
                normal = x * lax.rsqrt(row_mean(x * x) + EPSILON) * gain_ref[...]
                full[g, line.z, line.c] = normal.astype(BF)
                gather.begin(g)

        line.meet()
        tables = Turns([(cos_v, cos_out), (sin_v, sin_out)], out_sem.at[pl.ds(1, 2)], lambda ref, g: ref.at[:, g])
        stores = [
            Store(full, kept_x, kept_sem.at[0]),
            Store(qkv_v, qkv, out_sem.at[0], lambda ref, g: ref.at[:, g]),
        ]
        place_grad = pltpu.make_async_copy(low_v, kept_grad.at[:, line.z, line.c], place_sem)

        second = Gather(line, kept_grad, b_send, b_recv, b_across)

        def second_turn(j):
            for h in range(hops, 0, -1):
                within(j - h, groups, functools.partial(second.hop, h=h))
            within(j, groups, second.begin)

        def scale_grad(turn):
            loads.begin(turn == 0, 0, 1, 2)

            @pl.when(turn == 1)
            def _():
                loads.need(True, 2)

                @pl.loop(0, groups)
                def _(g):
                    low_v[g] = (dy_v[g].astype(F32) * p[g, :, :1]).astype(BF)

                place_grad.start()

            pl.when(turn == 2)(place_grad.wait)
            second_turn(turn - groups - hops - 1 + ahead)

        def project(g):
            r = lax.broadcasted_iota(jnp.int32, (ranks * rows, HDIM), 0)
            lane = lax.broadcasted_iota(jnp.int32, (ranks * rows, HDIM), 1)
            places = lax.shift_right_logical(r, shift) * own_tokens + g * rows + (r & (rows - 1))
            starts = starts_of([docs[0, n] for n in range(docs.shape[1])], places)
            angles = (places - starts).astype(F32) * freq[...]
            c = jnp.cos(angles)
            s = jnp.sin(angles)
            s = jnp.where(lane < HDIM // 2, -s, s)
            slot = tables.free(g)
            for rank in range(ranks):
                cos_v[slot, rank] = c[rank * rows : (rank + 1) * rows]
                sin_v[slot, rank] = s[rank * rows : (rank + 1) * rows]
            tables.put(g)
            gather.arrived(g)
            loads.need(g == 0, 0)
            x = full[g].reshape(ranks * rows, model)
            for which in range(3):
                out = dot(x, w_v[which])
                for h in range(heads):
                    u = out[:, h * HDIM : (h + 1) * HDIM]
                    if which < 2:
                        u = u * c + swap_halves(u) * s
                    u = u.astype(BF)
                    at = (which * heads + h) * HDIM
                    for rank in range(ranks):
                        qkv_v[rank, g, :, at : at + HDIM] = u[rank * rows : (rank + 1) * rows]
            for store in stores:
                store.put(g)

        stream(line, groups, NormedFirst, arrived=project, extra=(groups + hops + 1, scale_grad))

        @pl.loop(0, groups)
        def _(g):
            for store in stores:
                store.end(g)

        tables.end(groups)
        loads.begin(True, 3, 4)
        third = Gather(line, full, c_send, c_recv, c_across)
        reduce = Reduce(line, part, near, far, acc, s1, s2, s3)
        reduce_back = Reduce(line, part, near, far, acc, t1, t2, t3)
        keep = Store(attended_v, attended, attended_sem)
        keep_ln = Store(full, kept_ln, kept_sem.at[1])
        keep_resid = Store(resid_v, resid, resid_sem)
        keep_low = Store(low_v, grad_low, result_sem)
        highs = Turns([(high_v, grad_resid)], tile_sem.at[pl.ds(1, 1)])
        hiddens = Turns([(squared_v, squared), (hidden_v, hidden_grad)], tile_sem.at[pl.ds(2, 2)])
        gains[...] = jnp.zeros_like(gains)
        first_column = line.t * columns

        def fetch(g):
            slot = lax.rem(g, 2)
            return pltpu.make_async_copy(kept_grad.at[g], grad_v.at[slot], tile_sem.at[0, slot])

        def part_of(which, h):
            return pl.ds(pl.multiple_of((which * heads + h) * HDIM, HDIM), HDIM)

        def keep_weights(i, count, h):
            rows_kept = weight_rows(i if count == reach else count - 1, reach)
            return pltpu.make_async_copy(
                weights_v.at[h, pl.ds(0, count * QROWS)],
                kept_weights.at[h, pl.ds(pl.multiple_of(rows_kept, QROWS), count * QROWS)],
                weights_sem.at[h],
            )

        def attend_block(i, count):
            low = i + 1 - count
            start = query_starts(docs, i * QROWS)

            @pl.loop(0, heads)
            def _(h):
                q = qkv_v[pl.ds(i * span, span), :, :, part_of(0, h)].reshape(QROWS, HDIM)
                k = qkv_v[pl.ds(low * span, count * span), :, :, part_of(1, h)].reshape(count * QROWS, HDIM)
                weights = softmax_block(q, k, start, i * QROWS, low * QROWS, scaling).astype(BF)
                keys = pl.ds(pl.multiple_of(low * QROWS, QROWS), count * QROWS)
                done = dot(v_t[h, :, keys], weights).T
                done = (done * jnp.where(line.t * heads + h < active[0], 1.0, 0.0)).astype(BF)
                put_grouped(attended_v, done, i, own_tokens, rows, part_of(0, h))
                if not isinstance(i, int):
                    pl.when(i == reach - 1)(lambda: keep_weights(i - 1, reach - 1, h).wait())
                    pl.when(i > reach - 1)(lambda: keep_weights(i - 1, reach, h).wait())
                elif i:
                    keep_weights(i - 1, count - 1, h).wait()
                weights_v[h, : count * QROWS] = weights
                keep_weights(i, count, h).start()

        def attention(turn):
            @pl.when(turn == 0)
            def _():
                @pl.loop(0, heads)
                def _(h):
                    v_t[h] = qkv_v[:, :, :, part_of(2, h)].reshape(length, HDIM).T

                for i in range(min(reach - 1, blocks)):
                    attend_block(i, i + 1)

            @pl.when(turn == 1)
            def _():
                @pl.loop(reach - 1, blocks)
                def _(i):
                    attend_block(i, reach)

        def produce(g):
            keep.put(g)
            loads.need(g == 0, 1)
            for n in range(0, model, 512):
                out = dot(attended_v[g], wo_v[:, n : n + 512]).astype(BF)
                part[g, ..., n : n + 512] = out.reshape(chips, 2, rows, 512)

        def norm(g):
            reduce.last(g)
            total = x_ref[g].astype(F32) + acc[...]
            resid_v[g] = total
            keep_resid.put(g)
            lhat, _ = layer_norm(total)
            full[g, line.z, line.c] = (lhat * gain2[...] + bias2[...]).astype(BF)
            third.begin(g)

        def arrived(g):
            third.arrived(g)
            keep_ln.put(g)
            reduce.drain(g)

            @pl.when(g == 0)
            def _():
                fetch(0).start()

            fetch(g).wait()

            @pl.when(g + 1 < groups)
            def _():
                fetch(g + 1).start()

            loads.need(g == 0, 3, 4)

        def forward(g):
            slot = hiddens.free(g)
            limit = (jnp.broadcast_to(wide[pl.ds(g, 1), :], (HDIM, tokens_all)).T[:, :1] + 1) * (FF // 4)

            @pl.loop(0, columns // tile)
            def _(n):
                at = pl.ds(pl.multiple_of(n * tile, tile), tile)
                hidden = dot(full[g].reshape(tokens_all, model), up_v[:, at])
                ids = first_column + n * tile + lax.broadcasted_iota(jnp.int32, hidden.shape, 1)
                live = jnp.where(ids < limit, jnp.maximum(hidden, 0.0), 0.0)
                lifted[:, at] = live
                squared_v[slot, :, at] = (live * live).astype(BF)

        def backward(g):
            slot = lax.rem(g, 2)

            @pl.loop(0, columns // tile)
            def _(n):
                at = pl.ds(pl.multiple_of(n * tile, tile), tile)
                back = dot(grad_v[slot].reshape(tokens_all, model), down_v[at, :], NT)
                hidden_v[slot, :, at] = (back * (2.0 * lifted[:, at])).astype(BF)

            hiddens.put(g)

        def lower(g):
            slot = lax.rem(g, 2)

            @pl.loop(0, model // 256)
            def _(n):
                at = pl.ds(pl.multiple_of(n * 256, 256), 256)
                out = dot(hidden_v[slot], up_v[at, :], NT).astype(BF)
                part[g, :, :, :, at] = out.reshape(chips, 2, rows, 256)

        def finish(g):
            reduce_back.last(g)
            lhat, inv_std = layer_norm(resid_v[g])
            back = acc[...]
            gains[0:1] += jnp.sum(back * lhat, axis=0, keepdims=True)
            gains[1:2] += jnp.sum(back, axis=0, keepdims=True)
            back = back * gain2[...]
            back = dy_v[g].astype(F32) + inv_std * (back - row_mean(back) - lhat * row_mean(back * lhat))
            high_v[highs.free(g)] = back
            low_v[g] = back.astype(BF)
            highs.put(g)
            keep_low.put(g)

        @pl.loop(0, groups + back_at)
        def _(i):
            for n in range(hops):
                h, d = hops - n, n + 1
                within(i - hidden_at - 1 - hops + d, groups, functools.partial(reduce_back.step, d=d))
                within(i - normed_at - h, groups, functools.partial(third.hop, h=h))
                within(i - lead - 1 - hops + d, groups, functools.partial(reduce.step, d=d))
                within(i + ahead - h, groups, functools.partial(second.hop, h=h))
                if n == 0:
                    within(i - hidden_at, groups, arrived)
                for piece in (forward, backward, lower)[n * 3 // hops : (n + 1) * 3 // hops]:
                    within(i - hidden_at, groups, piece)
            within(i + ahead, groups, second.begin)
            within(i - hidden_at, groups, reduce_back.begin)
            within(i - normed_at, groups, norm)
            within(i - lead, groups, produce)
            within(i - lead, groups, reduce.begin)
            within(i + ahead - hops - 1, groups, second.arrived)
            within(i - back_at, groups, finish)
            within(i, lead, attention)

        for h in range(heads):
            keep_weights(blocks - 1, reach, h).wait()
        second.drain()
        third.drain()
        pl.loop(0, groups)(reduce_back.drain)

        @pl.loop(0, groups)
        def _(g):
            for store in (keep, keep_ln, keep_resid, keep_low):
                store.end(g)

        highs.end(groups)
        hiddens.end(groups)

    table = jax.ShapeDtypeStruct((ranks, groups, rows, HDIM), F32)
    projected = jax.ShapeDtypeStruct((ranks, groups, rows, 3 * width), BF)
    full = jax.ShapeDtypeStruct((groups, chips, 2, rows, model), BF)
    attended = jax.ShapeDtypeStruct((groups, tokens_all, width), BF)
    high = jax.ShapeDtypeStruct((groups, rows, model), F32)
    low = jax.ShapeDtypeStruct((groups, rows, model), BF)
    hidden = jax.ShapeDtypeStruct((groups, tokens_all, columns), BF)
    return call(
        body,
        [tokens, cotangent, probs, gain, lengths, frequency, count, w_qkv, w_out, g_ln, b_ln, w_up, w_down, widths],
        [
            projected,
            full,
            table,
            table,
            attended,
            high,
            full,
            high,
            low,
            jax.ShapeDtypeStruct((2, model), F32),
            full,
            hidden,
            hidden,
            jax.ShapeDtypeStruct((heads, weight_rows(blocks, reach), QROWS), BF),
        ],
        [
            *scratch_of(full, w_qkv, w_out, cotangent, w_up, w_down, projected),
            pltpu.VMEM((2, ranks, rows, HDIM), F32),
            pltpu.VMEM((2, ranks, rows, HDIM), F32),
            pltpu.VMEM((heads, HDIM, length), BF),
            *scratch_of(attended, low, high),
            pltpu.VMEM((2, rows, model), F32),
            pltpu.VMEM((2, chips, 2, rows, model), BF),
            pltpu.VMEM((tokens_all, columns), F32),
            pltpu.VMEM((2, tokens_all, columns), BF),
            pltpu.VMEM((2, tokens_all, columns), BF),
            *Gather.scratch(ranks, groups) * 3,
            *Reduce.scratch(ranks, groups, rows, model),
            *Reduce.scratch(ranks, groups, rows, model)[-3:],
            DMA((5,)),
            DMA((2, groups)),
            DMA((3, groups)),
            DMA,
            *[DMA((groups,))] * 3,
            DMA((4, groups)),
            pltpu.VMEM((heads, reach * QROWS, QROWS), BF),
            DMA((heads,)),
        ],
        0,
        in_specs=[VM, ANY, VM, VM, SM, VM, SM, ANY, ANY, VM, VM, ANY, ANY, VM],
        out_specs=[ANY] * 9 + [VM] + [ANY] * 4,
        flops=8 * length * model * (width + columns),
        moved=160 << 20,
    )


def hidden_weights(spread, inputs, hidden, first, turn_of, columns):
    n = turn_of
    side = min(256, spread.out.shape[1])

    @pl.loop(0, spread.out.shape[1] // side)
    def _(m):
        at = pl.ds(pl.multiple_of(first + m * side, side), side)
        to = pl.ds(pl.multiple_of(m * side, side), side)
        x = inputs[:, :, at]
        spread.out[n, to] = dot(
            x.reshape(x.shape[0] * x.shape[1], side), hidden[...].reshape(-1, columns), TN
        ).astype(BF)

    spread.begin(n)


def feed_out(
    own_grad, squared, hidden_grad, kept_ln, branch_grad, w_down, w_out, count, resid, cotangent, probs, ranks, sequences
):
    groups, rows, model = own_grad.shape
    columns, width = w_down.shape[0], w_out.shape[0]
    tokens = ranks * rows
    share = model // sequences
    half = share // 2

    def body(
        own, sq, hg, ln, bg, down, w, active, res, dy, p, result, probs_grad, kept, grad, land_down, land_up,
        full, g_send, g_recv, g_across, part, near, far, acc, s1, s2, s3, kept_sem,
        out_down, down_send, down_recv, out_up, up_send, up_recv, ln_v, bg_v, fetch_sem,
        sq_v, hg_v, down_v, res_v, dy_v, load_sem, result_v, back_v, result_sem, back_sem,
    ):
        line = Line(ranks, rows)
        line.greet(sequences)
        gather = Gather(line, full, g_send, g_recv, g_across)
        reduce = Reduce(line, part, near, far, acc, s1, s2, s3)
        to_down = Spread(sequences, out_down, land_down, down_send, down_recv)
        to_up = Spread(sequences, out_up, land_up, up_send, up_recv, pl.ds(0, half))
        keep = Store(full, kept, kept_sem)
        keep_result = Store(result_v, result, result_sem)
        keep_back = Store(back_v, grad, back_sem, lambda ref, g: ref.at[:, g])

        def arrived(g):
            gather.arrived(g)
            keep.put(g)
            heads = line.t * (width // HDIM) + lax.broadcasted_iota(jnp.int32, (1, width), 1) // HDIM
            live = jnp.where(heads < active[0], 1.0, 0.0)
            back = (dot(full[g].reshape(tokens, model), w[...], NT) * live).astype(BF)
            for rank in range(ranks):
                back_v[rank, g] = back[rank * rows : (rank + 1) * rows]
            keep_back.put(g)

        def produce(g):
            loads.need(g == 0, 0, 1)

            @pl.loop(0, model // 256)
            def _(n):
                at = pl.ds(pl.multiple_of(n * 256, 256), 256)
                out = dot(sq_v[g], down_v[:, at]).astype(BF)
                part[g, :, :, :, at] = out.reshape(ranks // 2, 2, rows, 256)

        def finish(g):
            loads.need(g == 0, 3, 4)
            ffn = acc[...]
            result_v[g] = (res_v[g] + p[g, :, :1] * ffn).astype(BF)
            keep_result.put(g)
            scores = jnp.sum(dy_v[g].astype(F32) * ffn, axis=1, keepdims=True)
            probs_grad[pl.ds(g, 1)] = jnp.broadcast_to(scores, (rows, HDIM)).T[:1]

        def fetches(step):
            at = pl.multiple_of(to_up.target(lax.rem(step + 1, sequences)) * share, share)
            return [
                pltpu.make_async_copy(ln.at[:, :, pl.ds(at, half)], ln_v, fetch_sem.at[0]),
                pltpu.make_async_copy(bg.at[:, :, pl.ds(at, share)], bg_v, fetch_sem.at[1]),
            ]

        def weights(step):
            n = lax.rem(step + 1, sequences)
            loads.need(step == 0, 2)
            for fetch in fetches(step):
                fetch.wait()
            side = min(256, columns)

            @pl.loop(0, columns // side)
            def _(m):
                at = pl.ds(pl.multiple_of(m * side, side), side)
                out_down[n, at] = dot(
                    sq_v[:, :, at].reshape(groups * tokens, side), bg_v[...].reshape(groups * tokens, share), TN
                ).astype(BF)

            to_down.begin(n)
            hidden_weights(to_up, ln_v, hg_v, 0, n, columns)

            @pl.when(step + 1 < sequences)
            def _():
                for fetch in fetches(step + 1):
                    fetch.start()

        def beside(turn):
            loads.begin(turn == 0, 0, 1, 2)

            @pl.when(turn == 0)
            def _():
                for fetch in fetches(0):
                    fetch.start()

            loads.begin(turn == 3, 3, 4)
            within(turn - 1, sequences, weights)

        loads = Loads(
            [
                (sq, sq_v),
                (down, down_v),
                (hg, hg_v),
                (res, res_v),
                (dy, dy_v),
                (own, full.at[:, line.z, line.c]),
            ],
            load_sem,
        )
        loads.begin(True, 5)
        line.meet(sequences)
        loads.need(True, 5)
        stream(
            line, groups, gather, arrived, reduce, [produce], finish, 1, (max(sequences + 1, 4), beside)
        )

        @pl.loop(0, groups)
        def _(g):
            for store in (keep, keep_result, keep_back):
                store.end(g)

        to_down.end()
        to_up.end()

    kept = jax.ShapeDtypeStruct((groups, ranks // 2, 2, rows, model), BF)
    low = jax.ShapeDtypeStruct((groups, rows, model), BF)
    back = jax.ShapeDtypeStruct((ranks, groups, rows, width), BF)
    return call(
        body,
        [own_grad, squared, hidden_grad, kept_ln, branch_grad, w_down, w_out, count, resid, cotangent, probs],
        [
            low,
            jax.ShapeDtypeStruct((groups, rows), F32),
            kept,
            back,
            jax.ShapeDtypeStruct((sequences, columns, share), BF),
            jax.ShapeDtypeStruct((sequences, share, columns), BF),
        ],
        [
            *scratch_of(kept),
            *Gather.scratch(ranks, groups),
            *Reduce.scratch(ranks, groups, rows, model),
            DMA((groups,)),
            *Spread.scratch(sequences, (columns, share)),
            *Spread.scratch(sequences, (half, columns)),
            pltpu.VMEM((groups, tokens, half), BF),
            pltpu.VMEM((groups, tokens, share), BF),
            DMA((2,)),
            *scratch_of(squared, hidden_grad, w_down, resid, cotangent),
            DMA((6,)),
            *scratch_of(low, back),
            DMA((groups,)),
            DMA((groups,)),
        ],
        3,
        in_specs=[ANY, ANY, ANY, ANY, ANY, ANY, VM, SM, ANY, ANY, VM],
        out_specs=[ANY, VM, ANY, ANY, ANY, ANY],
        flops=2 * groups * tokens * model * (3 * columns + width),
        moved=100 << 20,
    )


def project_back(
    grads, w_qkv, kept_x, attended, attn_grad, kept_ln, hidden_grad, landed_up, tokens, gain, grad_resid, gains, ranks, sequences
):
    groups, tokens_all, width = grads[0].shape
    rows = tokens_all // ranks
    model = w_qkv.shape[1]
    columns = hidden_grad.shape[2]
    share = model // sequences
    half = share // 2

    def body(
        gq, gk, gv, w, xs, a, ga, ln, hg, up_in, x_ref, gain_ref, g_res, gain_parts,
        tokens_grad, totals, land_qkv, land_out, land_up,
        part, near, far, acc, s1, s2, s3,
        out_qkv, qkv_send, qkv_recv, out_out, out_send, out_recv, out_up, up_send, up_recv,
        x_v, ga_v, ln_v, fetch_sem, group_v, group_sem, w_v, a_v, hg_v, own_v, res_v, load_sem,
        mine, terms, t_send, t_recv, sums, d_send, d_recv, g_q, g_k, g_v, grad_v, grad_sem,
    ):
        line = Line(ranks, rows)
        line.greet_all(sequences)
        me = lax.axis_index("dp")
        reduce = Reduce(line, part, near, far, acc, s1, s2, s3)
        to_qkv = Spread(sequences, out_qkv, land_qkv, qkv_send, qkv_recv)
        to_out = Spread(sequences, out_out, land_out, out_send, out_recv)
        to_up = Spread(sequences, out_up, land_up, up_send, up_recv, pl.ds(half, half))
        parts = (g_q, g_k, g_v)
        loads = Loads(
            [(w, w_v), (a, a_v), (hg, hg_v), (x_ref, own_v), (g_res, res_v), (gq, g_q), (gk, g_k), (gv, g_v)],
            load_sem,
        )
        keep_grad = Store(grad_v, tokens_grad, grad_sem)

        def group_fetch(g):
            slot = lax.rem(g, 2)
            return pltpu.make_async_copy(xs.at[g], group_v.at[slot], group_sem.at[slot])

        loads.begin(True, 0, 5, 6, 7)
        group_fetch(0).start()
        mine[0:1] = jnp.zeros((1, model), F32)
        mine[1:3] = gain_parts[...]

        def produce(g):
            loads.need(g == 0, 0, 5, 6, 7)
            group_fetch(g).wait()

            @pl.when(g + 1 < groups)
            def _():
                group_fetch(g + 1).start()

            slot = lax.rem(g, 2)

            @pl.loop(0, model // 256)
            def _(n):
                at = pl.ds(pl.multiple_of(n * 256, 256), 256)
                out = dot(g_q[g], w_v[0, at], NT)
                out += dot(g_k[g], w_v[1, at], NT)
                out += dot(g_v[g], w_v[2, at], NT)
                part[g, :, :, :, at] = out.astype(BF).reshape(ranks // 2, 2, rows, 256)
                mine[0:1, at] += jnp.sum(out * group_v[slot, :, at].astype(F32), axis=0, keepdims=True)

        def finish(g):
            loads.need(g == 0, 3, 4)
            x = own_v[g].astype(F32)
            scale = lax.rsqrt(row_mean(x * x) + EPSILON)
            hat = x * scale
            back = acc[...] * gain_ref[...]
            grad_v[g] = res_v[g] + scale * (back - hat * row_mean(back * hat))
            keep_grad.put(g)

        def fetches(step):
            at = pl.multiple_of(to_qkv.target(lax.rem(step + 1, sequences)) * share, share)
            return [
                pltpu.make_async_copy(ln.at[:, :, pl.ds(at + half, half)], ln_v, fetch_sem.at[0]),
                pltpu.make_async_copy(xs.at[:, :, pl.ds(at, share)], x_v, fetch_sem.at[1]),
                pltpu.make_async_copy(ga.at[:, :, pl.ds(at, share)], ga_v, fetch_sem.at[2]),
            ]

        def weights(piece):
            step = piece // 2
            n = lax.rem(step + 1, sequences)

            @pl.when(lax.rem(piece, 2) == 0)
            def _():
                loads.need(step == 0, 1, 2)
                fetches(step)[0].wait()
                hidden_weights(to_up, ln_v, hg_v, 0, n, columns)

                @pl.when(step + 1 < sequences)
                def _():
                    fetches(step + 1)[0].start()

            @pl.when(lax.rem(piece, 2) == 1)
            def _():
                for fetch in fetches(step)[1:]:
                    fetch.wait()

                @pl.loop(0, share // 256)
                def _(m):
                    at = pl.ds(pl.multiple_of(m * 256, 256), 256)
                    x = x_v[:, :, at].reshape(groups * tokens_all, 256)
                    for which in range(3):
                        out_qkv[n, which, at] = dot(
                            x, parts[which][...].reshape(groups * tokens_all, width), TN
                        ).astype(BF)

                to_qkv.begin(n)
                out_out[n] = dot(
                    a_v[...].reshape(groups * tokens_all, width), ga_v[...].reshape(groups * tokens_all, share), TN
                ).astype(BF)
                to_out.begin(n)

                @pl.when(step + 1 < sequences)
                def _():
                    for fetch in fetches(step + 1)[1:]:
                        fetch.start()

        def to_rank(n, source=None):
            return copy_to(
                mine,
                terms.at[line.t if source is None else source],
                t_send.at[n],
                t_recv.at[n],
                lax.rem(line.t + n, ranks),
            )

        def to_sequence(n, source=None):
            return pltpu.make_async_remote_copy(
                src_ref=sums.at[me],
                dst_ref=sums.at[me if source is None else source],
                send_sem=d_send.at[n],
                recv_sem=d_recv.at[n],
                device_id={"dp": lax.rem(me + n, sequences)},
                device_id_type=MESH,
            )

        def beside(turn):
            loads.begin(turn == 0, 1, 2)
            loads.begin(turn == 2, 3, 4)

            @pl.when(turn == 0)
            def _():
                for fetch in fetches(0):
                    fetch.start()

            within(turn - 1, 2 * sequences, weights)

            @pl.when(turn == groups)
            def _():
                mine[0:1] = mine[0:1] / gain_ref[...]
                terms[line.t] = mine[...]

                @pl.loop(1, ranks)
                def _(n):
                    to_rank(n).start()

            @pl.when(turn == groups + 1)
            def _():
                @pl.loop(1, ranks)
                def _(n):
                    to_rank(n).wait_send()
                    to_rank(n, lax.rem(line.t + ranks - n, ranks)).wait_recv()

                total = terms[0]
                for n in range(1, ranks):
                    total += terms[n]
                sums[me] = total

                @pl.loop(1, sequences)
                def _(n):
                    to_sequence(n).start()

            @pl.when(turn == groups + 2)
            def _():
                @pl.loop(1, sequences)
                def _(n):
                    to_sequence(n).wait_send()
                    to_sequence(n, lax.rem(me + sequences - n, sequences)).wait_recv()

                total = sums[0]
                for n in range(1, sequences):
                    total += sums[n]
                totals[...] = total

        produce(0)
        line.meet_all(sequences)

        def next_part(g):
            pl.when(g > 0)(lambda: produce(g))

        stream(
            line, groups, None, None, reduce, [next_part], finish, extra=(max(groups + 3, 2 * sequences + 1), beside)
        )

        @pl.loop(0, groups)
        def _(g):
            keep_grad.end(g)

        to_qkv.end()
        to_out.end()

        to_up.end()

    return call(
        body,
        [*grads, w_qkv, kept_x, attended, attn_grad, kept_ln, hidden_grad, landed_up, tokens, gain, grad_resid, gains],
        [
            jax.ShapeDtypeStruct((groups, rows, model), F32),
            jax.ShapeDtypeStruct((3, model), F32),
            jax.ShapeDtypeStruct((sequences, 3, share, width), BF),
            jax.ShapeDtypeStruct((sequences, width, share), BF),
            jax.ShapeDtypeStruct(landed_up.shape, BF),
        ],
        [
            *Reduce.scratch(ranks, groups, rows, model),
            *Spread.scratch(sequences, (3, share, width)),
            *Spread.scratch(sequences, (width, share)),
            *Spread.scratch(sequences, (half, columns)),
            pltpu.VMEM((groups, tokens_all, share), BF),
            pltpu.VMEM((groups, tokens_all, share), BF),
            pltpu.VMEM((groups, tokens_all, half), BF),
            DMA((3,)),
            pltpu.VMEM((2, tokens_all, model), BF),
            DMA((2,)),
            *scratch_of(w_qkv, attended, hidden_grad, tokens, grad_resid),
            DMA((8,)),
            pltpu.VMEM((3, model), F32),
            pltpu.VMEM((ranks, 3, model), F32),
            DMA((ranks,)),
            DMA((ranks,)),
            pltpu.VMEM((sequences, 3, model), F32),
            DMA((sequences,)),
            DMA((sequences,)),
            *scratch_of(*grads, grad_resid),
            DMA((groups,)),
        ],
        4,
        in_specs=[ANY] * 11 + [VM, ANY, VM],
        out_specs=[ANY, VM, ANY, ANY, ANY],
        flops=12 * groups * tokens_all * model * width,
        moved=60 << 20,
        aliases={9: 4},
    )


def collect(result, tokens_grad, totals, *landed):
    steps = result.shape[0] // 2

    def body(result_in, tokens_in, totals_in, *refs):
        pieces, outs = refs[: len(landed)], refs[len(landed) :]
        outs[0][...] = result_in[...]
        outs[1][...] = tokens_in[...]
        for n in range(3):
            outs[2 + n][...] = totals_in[n : n + 1]
        for piece, out in zip(pieces, outs[5:]):
            total = piece[0].astype(F32)
            for n in range(1, piece.shape[0]):
                total += piece[n].astype(F32)
            out[...] = total

    def split(a, at):
        block = list(a.shape)
        block[at] //= steps
        return pl.BlockSpec(tuple(block), lambda i: tuple(i if n == at else 0 for n in range(len(block))))

    sums = [jax.ShapeDtypeStruct(a.shape[1:], F32) for a in landed]
    row = jax.ShapeDtypeStruct((1, totals.shape[1]), F32)
    fixed = lambda a: pl.BlockSpec(a.shape, lambda i: (0, 0))
    return pl.pallas_call(
        body,
        out_shape=[
            jax.ShapeDtypeStruct(result.shape, BF),
            jax.ShapeDtypeStruct(tokens_grad.shape, F32),
            row,
            row,
            row,
            *sums,
        ],
        grid=(steps,),
        in_specs=[split(result, 0), split(tokens_grad, 0), fixed(totals)]
        + [split(a, a.ndim - 2) for a in landed],
        out_specs=[split(result, 0), split(tokens_grad, 0), fixed(row), fixed(row), fixed(row)]
        + [split(a, len(a.shape) - 2) for a in sums],
        compiler_params=pltpu.CompilerParams(vmem_limit_bytes=60 << 20),
        cost_estimate=pl.CostEstimate(flops=1 << 24, bytes_accessed=24 << 20, transcendentals=0),
    )(result, tokens_grad, totals, *landed)


def shards(
    tokens,
    cotangent,
    first_norm_gain,
    w_qkv,
    w_out,
    g_ln,
    b_ln,
    w_up,
    w_down,
    probs,
    lengths,
    head_count,
    widths,
):
    length_all = widths.shape[0]
    own_tokens, model = tokens.shape
    ranks = length_all // own_tokens
    sequences = lax.axis_size("dp")
    groups, rows = GROUPS, own_tokens // GROUPS
    width = w_out.shape[0]
    half = HDIM // 2
    frequency = 10000.0 ** (-np.arange(half) / half)
    frequency = jnp.asarray(np.concatenate([frequency, frequency]).reshape(1, HDIM), F32)
    w_qkv_t = w_qkv.transpose(1, 0, 2)
    x = tokens.reshape(groups, rows, model)
    dy = cotangent.reshape(groups, rows, model)
    first_norm_gain, g_ln, b_ln = (v.reshape(1, model) for v in (first_norm_gain, g_ln, b_ln))
    p = jnp.broadcast_to(probs.reshape(groups, rows, 1), (groups, rows, HDIM))
    wide = widths.reshape(ranks, groups, rows).swapaxes(0, 1).reshape(groups, ranks * rows)

    (
        qkv, kept_x, cosines, sines, attended, resid, kept_ffn_grad, grad_resid, grad_low, gains, kept_ln, squared,
        grad_hidden, kept_weights,
    ) = front(
        x, dy, p, first_norm_gain, lengths, frequency, head_count, w_qkv_t, w_out, g_ln, b_ln, w_up, w_down, wide, ranks
    )
    qkv = qkv.reshape(length_all, 3 * width)
    cosines, sines = cosines.reshape(length_all, HDIM), sines.reshape(length_all, HDIM)
    whole = lambda kept: kept.reshape(groups, ranks * rows, model)
    result, probs_grad, kept_attn_grad, grad_attended, land_down, land_up = feed_out(
        grad_low, squared, grad_hidden, whole(kept_ln), whole(kept_ffn_grad), w_down, w_out, head_count, resid, dy, p, ranks, sequences
    )
    grad_proj = attend_back(
        qkv,
        grad_attended.reshape(length_all, width),
        kept_weights,
        head_count,
        cosines,
        sines,
        width,
        groups,
        own_tokens,
    )
    tokens_grad, totals, land_qkv, land_out, land_up = project_back(
        grad_proj, w_qkv_t, whole(kept_x), attended, whole(kept_attn_grad), whole(kept_ln), grad_hidden, land_up, x, first_norm_gain,
        grad_resid, gains, ranks, sequences,
    )
    result, tokens_grad, rms, gain, bias, g_qkv, g_out, g_up, g_down = collect(
        result, tokens_grad, totals, land_qkv, land_out, land_up, land_down
    )
    return (
        result.reshape(own_tokens, model),
        tokens_grad.reshape(own_tokens, model),
        probs_grad.reshape(own_tokens),
        rms.reshape(model),
        g_qkv.transpose(1, 0, 2),
        g_out,
        gain.reshape(model),
        bias.reshape(model),
        g_up,
        g_down,
    )


def solution(mesh):
    placed = (
        P(("dp", "tensor"), None),
        P(("dp", "tensor"), None),
        P(),
        P(None, None, "tensor"),
        P("tensor", None),
        P(),
        P(),
        P(None, "tensor"),
        P("tensor", None),
        P(("dp", "tensor")),
        P("dp", None),
        P("dp"),
        P("dp"),
    )
    return jax.shard_map(
        shards,
        mesh=mesh,
        in_specs=placed,
        out_specs=(
            P(("dp", "tensor"), None),
            P(("dp", "tensor"), None),
            P(("dp", "tensor")),
            P(),
            P("dp", None, "tensor"),
            P("tensor", "dp"),
            P(),
            P(),
            P("dp", "tensor"),
            P("tensor", "dp"),
        ),
        check_vma=False,
    )
```

```python
import functools

import jax
import jax.numpy as jnp
import numpy as np
from jax import lax
from jax.experimental import pallas as pl
from jax.experimental.pallas import tpu as pltpu
from jax.sharding import PartitionSpec as P

HDIM = 128
FF = 8192
EPSILON = 1e-05
NEGATIVE = -1e30
MAXDOC = 1024
GROUPS = 8
QROWS = 256
MESH = pl.DeviceIdType.MESH
BF = jnp.bfloat16
F32 = jnp.float32
ANY = pl.BlockSpec(memory_space=pl.ANY)
VM = pl.BlockSpec(memory_space=pltpu.VMEM)
SM = pl.BlockSpec(memory_space=pltpu.SMEM)
DMA = pltpu.SemaphoreType.DMA
NT = (((1,), (1,)), ((), ()))
TN = (((0,), (0,)), ((), ()))


def dot(a, b, dims=(((1,), (0,)), ((), ()))):
    return lax.dot_general(a, b, dims, preferred_element_type=F32)


class Line:
    def __init__(self, ranks, rows):
        self.ranks, self.chips, self.rows = ranks, ranks // 2, rows
        self.t = lax.axis_index("tensor")
        self.z, self.c = self.t // 2, lax.rem(self.t, 2)
        self.has_up, self.has_down = self.z < self.chips - 1, self.z > 0
        self.up = jnp.minimum(self.t + 2, ranks - 1)
        self.down = jnp.maximum(self.t - 2, 0)
        self.partner = self.t + 1 - 2 * self.c

    def greet(self, dp_size=0):
        sem = pltpu.get_barrier_semaphore()
        pl.semaphore_signal(sem, inc=1, device_id={"tensor": self.partner}, device_id_type=MESH)

        @pl.when(self.has_up)
        def _():
            pl.semaphore_signal(sem, inc=1, device_id={"tensor": self.up}, device_id_type=MESH)

        @pl.when(self.has_down)
        def _():
            pl.semaphore_signal(sem, inc=1, device_id={"tensor": self.down}, device_id_type=MESH)

        d = lax.axis_index("dp")
        for step in range(1, dp_size):
            pl.semaphore_signal(
                sem, inc=1, device_id={"dp": lax.rem(d + step, dp_size)}, device_id_type=MESH
            )

    def meet(self, dp_size=0):
        links = self.has_up.astype(jnp.int32) + self.has_down.astype(jnp.int32)
        pl.semaphore_wait(pltpu.get_barrier_semaphore(), 1 + max(dp_size - 1, 0) + links)

    def greet_all(self, dp_size):
        sem = pltpu.get_barrier_semaphore()
        for n in range(1, self.ranks):
            pl.semaphore_signal(
                sem, inc=1, device_id={"tensor": lax.rem(self.t + n, self.ranks)}, device_id_type=MESH
            )
        d = lax.axis_index("dp")
        for n in range(1, dp_size):
            pl.semaphore_signal(
                sem, inc=1, device_id={"dp": lax.rem(d + n, dp_size)}, device_id_type=MESH
            )

    def meet_all(self, dp_size):
        pl.semaphore_wait(pltpu.get_barrier_semaphore(), self.ranks - 1 + dp_size - 1)


def copy_to(src, dst, send, recv, rank):
    return pltpu.make_async_remote_copy(
        src_ref=src,
        dst_ref=dst,
        send_sem=send,
        recv_sem=recv,
        device_id={"tensor": rank},
        device_id_type=MESH,
    )


class Gather:
    def __init__(self, line, full, send, recv, across_recv):
        self.l, self.full, self.send, self.recv, self.across_recv = line, full, send, recv, across_recv

    @staticmethod
    def scratch(ranks, groups):
        return [DMA((3, ranks // 2)), DMA((groups, ranks // 2)), DMA((groups,))]

    def along(self, g, z, up):
        l = self.l
        place = self.full.at[g, z, l.c]
        return copy_to(
            place,
            place,
            self.send.at[0 if up else 1, z],
            self.recv.at[0 if g == slice(None) else g, z],
            l.up if up else l.down,
        )

    def across(self, g, column):
        place = self.full.at[g, :, column]
        return copy_to(
            place, place, self.send.at[2, 0], self.across_recv.at[0 if g == slice(None) else g], self.l.partner
        )

    def pass_on(self, g, z, up):
        @pl.when(self.l.has_up if up else self.l.has_down)
        def _():
            self.along(g, z, up).start()

    def begin(self, g):
        self.pass_on(g, self.l.z, True)
        self.pass_on(g, self.l.z, False)

    def hop(self, g, h):
        l = self.l

        @pl.when(l.z - h >= 0)
        def _():
            self.along(g, l.z - h, True).wait_recv()
            self.pass_on(g, l.z - h, True)

        @pl.when(l.z + h <= l.chips - 1)
        def _():
            self.along(g, l.z + h, False).wait_recv()
            self.pass_on(g, l.z + h, False)

        if h == l.chips - 1:
            self.across(g, l.c).start()

    def arrived(self, g):
        self.across(g, 1 - self.l.c).wait_recv()

    def drain(self):
        l, every = self.l, slice(None)
        for z in range(l.chips):

            @pl.when(l.has_up & (l.z >= z))
            def _():
                self.along(every, z, True).wait_send()

            @pl.when(l.has_down & (l.z <= z))
            def _():
                self.along(every, z, False).wait_send()

        self.across(every, l.c).wait_send()


class Reduce:
    def __init__(self, line, part, near, far, acc, send, near_recv, far_recv):
        self.l, self.part, self.near, self.far, self.acc = line, part, near, far, acc
        self.send, self.near_recv, self.far_recv = send, near_recv, far_recv

    @staticmethod
    def scratch(ranks, groups, rows, width):
        chips = ranks // 2
        return [
            pltpu.VMEM((groups, chips, 2, rows, width), BF),
            pltpu.VMEM((groups, chips, rows, width), BF),
            pltpu.VMEM((groups, chips + 1, rows, width), BF),
            pltpu.VMEM((rows, width), F32),
            DMA((groups, chips + 1)),
            DMA((groups,)),
            DMA((groups, chips + 1)),
        ]

    def across(self, g):
        l = self.l
        return copy_to(
            self.part.at[g, :, 1 - l.c],
            self.near.at[g],
            self.send.at[g, l.chips],
            self.near_recv.at[g],
            l.partner,
        )

    def along(self, g, z, up, receive=False):
        l = self.l
        at = l.z if receive else jnp.where(up, l.z + 1, l.z - 1)
        slot = z if up else jnp.where(z == at, l.chips, z)
        return copy_to(
            self.part.at[g, z, l.c],
            self.far.at[g, slot],
            self.send.at[g, z],
            self.far_recv.at[g, slot],
            l.up if up else l.down,
        ), slot

    def begin(self, g):
        self.across(g).start()

    def add(self, g, z, slots, total=None):
        side = 512

        @pl.loop(0, self.part.shape[-1] // side)
        def _(n):
            at = pl.ds(pl.multiple_of(n * side, side), side)
            value = self.part[g, z, self.l.c, :, at].astype(F32) + self.near[g, z, :, at].astype(F32)
            for slot in slots:
                value += self.far[g, slot, :, at].astype(F32)
            if total is None:
                self.part[g, z, self.l.c, :, at] = value.astype(BF)
            else:
                total[:, at] = value

    def step(self, g, d):
        l = self.l
        if d == l.chips - 1:
            self.across(g).wait_recv()

        def send(z, up):
            further = l.has_down if up else l.has_up

            @pl.when(further)
            def _():
                copy, slot = self.along(g, z, up, receive=True)
                copy.wait_recv()
                self.add(g, z, [slot])

            @pl.when(jnp.logical_not(further))
            def _():
                self.add(g, z, [])

            self.along(g, z, up)[0].start()

        @pl.when(l.z + d <= l.chips - 1)
        def _():
            send(l.z + d, True)

        @pl.when(l.z - d >= 0)
        def _():
            send(l.z - d, False)

    def last(self, g):
        l = self.l

        @pl.when(l.has_down & l.has_up)
        def _():
            self.along(g, l.z, True, receive=True)[0].wait_recv()
            self.along(g, l.z, False, receive=True)[0].wait_recv()
            self.add(g, l.z, [l.z, l.chips], self.acc)

        @pl.when(jnp.logical_not(l.has_up))
        def _():
            self.along(g, l.z, True, receive=True)[0].wait_recv()
            self.add(g, l.z, [l.z], self.acc)

        @pl.when(jnp.logical_not(l.has_down))
        def _():
            self.along(g, l.z, False, receive=True)[0].wait_recv()
            self.add(g, l.z, [l.chips], self.acc)

    def drain(self, g):
        l = self.l
        self.across(g).wait_send()
        for z in range(l.chips):

            @pl.when(l.z != z)
            def _():
                copy_to(
                    self.part.at[g, z, l.c],
                    self.far.at[g, z],
                    self.send.at[g, z],
                    self.far_recv.at[g, z],
                    l.partner,
                ).wait_send()


def within(value, limit, body):
    pl.when((value >= 0) & (value < limit))(lambda: body(value))


def swap_halves(field):
    return pltpu.roll(field, HDIM // 2, axis=1)


def call(body, ins, outs, scratch, ident, in_specs=None, out_specs=None, limit=60, flops=0, moved=0, aliases=None):
    return pl.pallas_call(
        body,
        out_shape=outs,
        in_specs=in_specs or [VM] * len(ins),
        out_specs=out_specs or [VM] * len(outs),
        scratch_shapes=scratch,
        compiler_params=pltpu.CompilerParams(
            collective_id=ident, has_side_effects=True, vmem_limit_bytes=limit << 20
        ),
        input_output_aliases=aliases or {},
        cost_estimate=pl.CostEstimate(flops=flops, bytes_accessed=moved, transcendentals=0),
    )(*ins)


def stream(line, groups, gather=None, arrived=None, reduce=None, produce=(), finish=None, lead=0, extra=None):
    hops = line.chips - 1
    produce = list(produce)
    between = len(produce) > 1
    turns = groups + hops + 1 + (lead if reduce else 0)

    @pl.loop(0, turns)
    def _(i):
        for n in range(hops):
            if gather:
                within(i - hops + n, groups, functools.partial(gather.hop, h=hops - n))
            if reduce:
                d = n + 1
                within(i - lead - 1 - hops + d, groups, functools.partial(reduce.step, d=d))
            if n == hops - 1 and gather:
                within(i, groups, gather.begin)
            if between:
                if n == 0:
                    within(i - hops - 1, groups, arrived)
                for piece in produce[n * len(produce) // hops : (n + 1) * len(produce) // hops]:
                    within(i - lead, groups, piece)
        if not between:
            for piece in produce:
                within(i - lead, groups, piece)
        if reduce:
            within(i - lead, groups, reduce.begin)
        if arrived and not between:
            within(i - hops - 1, groups, arrived)
        if reduce:

            def end(g):
                reduce.last(g)
                finish(g)

            within(i - lead - 1 - hops, groups, end)
        if extra:
            within(i, min(extra[0], turns), extra[1])

    if extra:

        @pl.loop(min(extra[0], turns), extra[0])
        def _(i):
            extra[1](i)

    if gather:
        gather.drain()
    if reduce:
        pl.loop(0, groups)(reduce.drain)


def starts_of(lengths, places):
    end, start = jnp.int32(0), jnp.zeros_like(places)
    for length in lengths:
        end = end + length
        start = start + jnp.where(places >= end, length, 0)
    return start


def softmax_block(q, k, start, first_query, first_key, scaling):
    raw = dot(k, q, NT)
    keys = first_key + lax.broadcasted_iota(jnp.int32, raw.shape, 0)
    queries = first_query + lax.broadcasted_iota(jnp.int32, raw.shape, 1)
    raw = jnp.where((keys <= queries) & (keys >= start), raw * scaling, NEGATIVE)
    exponent = jnp.exp(raw - jnp.max(raw, axis=0, keepdims=True))
    return exponent * (1.0 / jnp.sum(exponent, axis=0, keepdims=True))


def query_starts(lengths, first):
    places = first + lax.broadcasted_iota(jnp.int32, (8, QROWS), 1)
    return starts_of([lengths[0, n] for n in range(lengths.shape[1])], places)[:1]


def weight_rows(i, reach):
    ramp = reach * (reach - 1) // 2
    if isinstance(i, int) and i < reach:
        return i * (i + 1) // 2 * QROWS
    return (ramp + (i - reach + 1) * reach) * QROWS


def put_grouped(out, block, i, own_tokens, rows, at=slice(None)):
    for n in range(0, QROWS, rows):
        rank, inside = divmod(n, own_tokens)
        rank += i * (QROWS // own_tokens)
        out[inside // rows, pl.ds(pl.multiple_of(rank * rows, rows), rows), at] = block[n : n + rows]


def attend_back(qkv, grad, kept_weights, count, cosines, sines, width, groups, own_tokens):
    length, heads = qkv.shape[0], width // HDIM
    scaling = HDIM ** (-0.5)
    reach = MAXDOC // QROWS + 1
    rows_own = own_tokens // groups

    def body(active, q, k, v, g, cos, sin, kept, g_q, g_k, g_v, k_t, sum_k, sum_v):
        live = lax.axis_index("tensor") * heads + pl.program_id(0) < active[0]

        @pl.when(jnp.logical_not(live))
        def _():
            g_q[...] = jnp.zeros_like(g_q)
            g_k[...] = jnp.zeros_like(g_k)
            g_v[...] = jnp.zeros_like(g_v)

        def rotate_back(d, rows):
            return (d * cos[rows] + swap_halves(d * sin[rows])).astype(BF)

        @pl.when(live)
        def _():
            k_t[...] = k[...].T
            sum_k[...] = jnp.zeros_like(sum_k)
            sum_v[...] = jnp.zeros_like(sum_v)
            def back_block(i, count):
                low = i + 1 - count
                rows = pl.ds(pl.multiple_of(i * QROWS, QROWS), QROWS)
                keys = pl.ds(pl.multiple_of(low * QROWS, QROWS), count * QROWS)
                weights = kept[0, pl.ds(weight_rows(i, reach), count * QROWS)]
                sum_v[keys] += dot(weights, g[rows])
                weights = weights.astype(F32)
                g_weights = dot(v[keys], g[rows], NT)
                inner = jnp.sum(weights * g_weights, axis=0, keepdims=True)
                g_scores = (weights * (g_weights - inner)).astype(BF)
                sum_k[keys] += dot(g_scores, q[rows])
                back = rotate_back(dot(k_t[:, keys], g_scores).T * scaling, rows)
                put_grouped(g_q, back, i, own_tokens, rows_own)

            for i in range(length // QROWS):
                back_block(i, min(i + 1, reach))

            for i in range(length // QROWS):
                rows = pl.ds(pl.multiple_of(i * QROWS, QROWS), QROWS)
                put_grouped(g_k, rotate_back(sum_k[rows] * scaling, rows), i, own_tokens, rows_own)
                put_grouped(g_v, sum_v[rows].astype(BF), i, own_tokens, rows_own)

    column = lambda n: pl.BlockSpec((length, HDIM), lambda h, live: (0, n * heads + h))
    table = pl.BlockSpec((length, HDIM), lambda h, live: (0, 0))
    return pl.pallas_call(
        body,
        out_shape=[jax.ShapeDtypeStruct((groups, length // groups, width), BF)] * 3,
        grid_spec=pltpu.PrefetchScalarGridSpec(
            num_scalar_prefetch=1,
            grid=(heads,),
            in_specs=[
                column(0),
                column(1),
                column(2),
                column(0),
                table,
                table,
                pl.BlockSpec((1, *kept_weights.shape[1:]), lambda h, live: (h, 0, 0)),
            ],
            out_specs=[pl.BlockSpec((groups, length // groups, HDIM), lambda h, live: (0, 0, h))] * 3,
            scratch_shapes=[
                pltpu.VMEM((HDIM, length), BF),
                pltpu.VMEM((length, HDIM), F32),
                pltpu.VMEM((length, HDIM), F32),
            ],
        ),
        compiler_params=pltpu.CompilerParams(vmem_limit_bytes=60 << 20),
        cost_estimate=pl.CostEstimate(flops=10 << 30, bytes_accessed=16 << 20, transcendentals=0),
    )(count, qkv, qkv, qkv, grad, cosines, sines, kept_weights)


class Spread:
    def __init__(self, size, out, land, send, recv, rows=None):
        self.size, self.out, self.land, self.send, self.recv = size, out, land, send, recv
        self.rows = rows
        self.me = lax.axis_index("dp")

    def target(self, n):
        return lax.rem(self.me + n, self.size)

    def copy(self, n, source=None):
        return pltpu.make_async_remote_copy(
            src_ref=self.out.at[n],
            dst_ref=self.place(self.me if source is None else source),
            send_sem=self.send.at[n],
            recv_sem=self.recv.at[n],
            device_id={"dp": self.target(n)},
            device_id_type=MESH,
        )

    def place(self, source):
        return self.land.at[source] if self.rows is None else self.land.at[source, self.rows]

    def own(self):
        return pltpu.make_async_copy(self.out.at[0], self.place(self.me), self.send.at[0])

    def begin(self, n):
        @pl.when(n == 0)
        def _():
            self.own().start()

        @pl.when(n != 0)
        def _():
            self.copy(n).start()

    def end(self):
        self.own().wait()

        @pl.loop(1, self.size)
        def _(n):
            self.copy(n).wait_send()
            self.copy(n, lax.rem(self.me + self.size - n, self.size)).wait_recv()

    @staticmethod
    def scratch(size, shape):
        return [pltpu.VMEM((size, *shape), BF), DMA((size,)), DMA((size,))]


class Loads:
    def __init__(self, pairs, sems):
        self.copies = [
            pltpu.make_async_copy(source, held, sems.at[n]) for n, (source, held) in enumerate(pairs)
        ]

    def begin(self, first, *which):
        @pl.when(first)
        def _():
            for n in which:
                self.copies[n].start()

    def need(self, first, *which):
        @pl.when(first)
        def _():
            for n in which:
                self.copies[n].wait()


class Store:
    def __init__(self, held, out, sems, at=lambda ref, g: ref.at[g]):
        self.held, self.out, self.sems, self.at = held, out, sems, at

    def copy(self, g):
        return pltpu.make_async_copy(self.at(self.held, g), self.at(self.out, g), self.sems.at[g])

    def put(self, g):
        self.copy(g).start()

    def end(self, g):
        self.copy(g).wait()


class Turns:
    def __init__(self, pairs, sems, at=lambda ref, g: ref.at[g]):
        self.pairs, self.sems, self.at = pairs, sems, at

    def each(self, g):
        return [
            pltpu.make_async_copy(held.at[lax.rem(g, 2)], self.at(out, g), self.sems.at[n, g])
            for n, (held, out) in enumerate(self.pairs)
        ]

    def free(self, g):
        @pl.when(g >= 2)
        def _():
            for copy in self.each(g - 2):
                copy.wait()

        return lax.rem(g, 2)

    def put(self, g):
        for copy in self.each(g):
            copy.start()

    def end(self, groups):
        for g in range(max(groups - 2, 0), groups):
            for copy in self.each(g):
                copy.wait()


def scratch_of(*arrays):
    return [pltpu.VMEM(a.shape, a.dtype) for a in arrays]


def column_of(ref, g):
    return jnp.broadcast_to(ref[pl.ds(g, 1), :], (HDIM, ref.shape[1])).T[:, :1]


def row_mean(field):
    return jnp.mean(field, axis=1, keepdims=True)


def layer_norm(resid):
    centred = resid - row_mean(resid)
    inv_std = lax.rsqrt(row_mean(centred * centred) + EPSILON)
    return centred * inv_std, inv_std


def front(
    tokens, cotangent, probs, gain, lengths, frequency, count, w_qkv, w_out, g_ln, b_ln, w_up, w_down, widths, ranks
):
    width, columns = w_out.shape[0], w_up.shape[1]
    tile = min(256, columns)
    groups, rows, model = tokens.shape
    heads = width // HDIM
    chips = ranks // 2
    own_tokens = groups * rows
    length = ranks * own_tokens
    shift = rows.bit_length() - 1
    scaling = HDIM ** (-0.5)
    reach = MAXDOC // QROWS + 1
    span = QROWS // own_tokens
    blocks = length // QROWS
    lead, ahead = 2, 3
    hops = chips - 1
    tokens_all = ranks * rows
    normed_at = lead + 1 + hops
    hidden_at = normed_at + hops + 1
    back_at = hidden_at + 1 + hops

    def body(
        x_ref, dy, p, gain_ref, docs, freq, active, w, wo, gain2, bias2, up, down, wide,
        qkv, kept_x, cos_out, sin_out, attended, resid, kept_grad, grad_resid, grad_low, gains, kept_ln, squared,
        hidden_grad, kept_weights,
        full, w_v, wo_v, dy_v, up_v, down_v, qkv_v, cos_v, sin_v, v_t, attended_v, low_v, resid_v, high_v, grad_v,
        lifted, squared_v, hidden_v,
        a_send, a_recv, a_across, b_send, b_recv, b_across, c_send, c_recv, c_across,
        part, near, far, acc, s1, s2, s3, t1, t2, t3,
        load_sem, kept_sem, out_sem, place_sem, attended_sem, resid_sem, result_sem, tile_sem, weights_v, weights_sem,
    ):
        line = Line(ranks, rows)
        line.greet()
        loads = Loads([(w, w_v), (wo, wo_v), (dy, dy_v), (up, up_v), (down, down_v)], load_sem)

        gather = Gather(line, full, a_send, a_recv, a_across)

        class NormedFirst:
            hop, drain = gather.hop, gather.drain

            def begin(g):
                x = x_ref[g].astype(F32)
                normal = x * lax.rsqrt(row_mean(x * x) + EPSILON) * gain_ref[...]
                full[g, line.z, line.c] = normal.astype(BF)
                gather.begin(g)

        line.meet()
        tables = Turns([(cos_v, cos_out), (sin_v, sin_out)], out_sem.at[pl.ds(1, 2)], lambda ref, g: ref.at[:, g])
        stores = [
            Store(full, kept_x, kept_sem.at[0]),
            Store(qkv_v, qkv, out_sem.at[0], lambda ref, g: ref.at[:, g]),
        ]
        place_grad = pltpu.make_async_copy(low_v, kept_grad.at[:, line.z, line.c], place_sem)

        second = Gather(line, kept_grad, b_send, b_recv, b_across)

        def second_turn(j):
            for h in range(hops, 0, -1):
                within(j - h, groups, functools.partial(second.hop, h=h))
            within(j, groups, second.begin)

        def scale_grad(turn):
            loads.begin(turn == 0, 0, 1, 2)

            @pl.when(turn == 1)
            def _():
                loads.need(True, 2)

                @pl.loop(0, groups)
                def _(g):
                    low_v[g] = (dy_v[g].astype(F32) * column_of(p, g)).astype(BF)

                place_grad.start()

            pl.when(turn == 2)(place_grad.wait)
            second_turn(turn - groups - hops - 1 + ahead)

        def project(g):
            r = lax.broadcasted_iota(jnp.int32, (ranks * rows, HDIM), 0)
            lane = lax.broadcasted_iota(jnp.int32, (ranks * rows, HDIM), 1)
            places = lax.shift_right_logical(r, shift) * own_tokens + g * rows + (r & (rows - 1))
            starts = starts_of([docs[0, n] for n in range(docs.shape[1])], places)
            angles = (places - starts).astype(F32) * freq[...]
            c = jnp.cos(angles)
            s = jnp.sin(angles)
            s = jnp.where(lane < HDIM // 2, -s, s)
            slot = tables.free(g)
            for rank in range(ranks):
                cos_v[slot, rank] = c[rank * rows : (rank + 1) * rows]
                sin_v[slot, rank] = s[rank * rows : (rank + 1) * rows]
            tables.put(g)
            gather.arrived(g)
            loads.need(g == 0, 0)
            x = full[g].reshape(ranks * rows, model)
            for which in range(3):
                out = dot(x, w_v[which])
                for h in range(heads):
                    u = out[:, h * HDIM : (h + 1) * HDIM]
                    if which < 2:
                        u = u * c + swap_halves(u) * s
                    u = u.astype(BF)
                    at = (which * heads + h) * HDIM
                    for rank in range(ranks):
                        qkv_v[rank, g, :, at : at + HDIM] = u[rank * rows : (rank + 1) * rows]
            for store in stores:
                store.put(g)

        stream(line, groups, NormedFirst, arrived=project, extra=(groups + hops + 1, scale_grad))

        @pl.loop(0, groups)
        def _(g):
            for store in stores:
                store.end(g)

        tables.end(groups)
        loads.begin(True, 3, 4)
        third = Gather(line, full, c_send, c_recv, c_across)
        reduce = Reduce(line, part, near, far, acc, s1, s2, s3)
        reduce_back = Reduce(line, part, near, far, acc, t1, t2, t3)
        keep = Store(attended_v, attended, attended_sem)
        keep_ln = Store(full, kept_ln, kept_sem.at[1])
        keep_resid = Store(resid_v, resid, resid_sem)
        keep_low = Store(low_v, grad_low, result_sem)
        highs = Turns([(high_v, grad_resid)], tile_sem.at[pl.ds(1, 1)])
        hiddens = Turns([(squared_v, squared), (hidden_v, hidden_grad)], tile_sem.at[pl.ds(2, 2)])
        gains[...] = jnp.zeros_like(gains)
        first_column = line.t * columns

        def fetch(g):
            slot = lax.rem(g, 2)
            return pltpu.make_async_copy(kept_grad.at[g], grad_v.at[slot], tile_sem.at[0, slot])

        def part_of(which, h):
            return pl.ds(pl.multiple_of((which * heads + h) * HDIM, HDIM), HDIM)

        def keep_weights(i, count, h):
            rows_kept = weight_rows(i if count == reach else count - 1, reach)
            return pltpu.make_async_copy(
                weights_v.at[h, pl.ds(0, count * QROWS)],
                kept_weights.at[h, pl.ds(pl.multiple_of(rows_kept, QROWS), count * QROWS)],
                weights_sem.at[h],
            )

        def attend_block(i, count):
            low = i + 1 - count
            start = query_starts(docs, i * QROWS)

            @pl.loop(0, heads)
            def _(h):
                q = qkv_v[pl.ds(i * span, span), :, :, part_of(0, h)].reshape(QROWS, HDIM)
                k = qkv_v[pl.ds(low * span, count * span), :, :, part_of(1, h)].reshape(count * QROWS, HDIM)
                weights = softmax_block(q, k, start, i * QROWS, low * QROWS, scaling).astype(BF)
                keys = pl.ds(pl.multiple_of(low * QROWS, QROWS), count * QROWS)
                done = dot(v_t[h, :, keys], weights).T
                done = (done * jnp.where(line.t * heads + h < active[0], 1.0, 0.0)).astype(BF)
                put_grouped(attended_v, done, i, own_tokens, rows, part_of(0, h))
                if not isinstance(i, int):
                    pl.when(i == reach - 1)(lambda: keep_weights(i - 1, reach - 1, h).wait())
                    pl.when(i > reach - 1)(lambda: keep_weights(i - 1, reach, h).wait())
                elif i:
                    keep_weights(i - 1, count - 1, h).wait()
                weights_v[h, : count * QROWS] = weights
                keep_weights(i, count, h).start()

        def attention(turn):
            @pl.when(turn == 0)
            def _():
                @pl.loop(0, heads)
                def _(h):
                    v_t[h] = qkv_v[:, :, :, part_of(2, h)].reshape(length, HDIM).T

                for i in range(min(reach - 1, blocks)):
                    attend_block(i, i + 1)

            @pl.when(turn == 1)
            def _():
                @pl.loop(reach - 1, blocks)
                def _(i):
                    attend_block(i, reach)

        def produce(g):
            keep.put(g)
            loads.need(g == 0, 1)
            for n in range(0, model, 512):
                out = dot(attended_v[g], wo_v[:, n : n + 512]).astype(BF)
                part[g, ..., n : n + 512] = out.reshape(chips, 2, rows, 512)

        def norm(g):
            reduce.last(g)
            total = x_ref[g].astype(F32) + acc[...]
            resid_v[g] = total
            keep_resid.put(g)
            lhat, _ = layer_norm(total)
            full[g, line.z, line.c] = (lhat * gain2[...] + bias2[...]).astype(BF)
            third.begin(g)

        def arrived(g):
            third.arrived(g)
            keep_ln.put(g)
            reduce.drain(g)

            @pl.when(g == 0)
            def _():
                fetch(0).start()

            fetch(g).wait()

            @pl.when(g + 1 < groups)
            def _():
                fetch(g + 1).start()

            loads.need(g == 0, 3, 4)

        def forward(g):
            slot = hiddens.free(g)
            limit = (jnp.broadcast_to(wide[pl.ds(g, 1), :], (HDIM, tokens_all)).T[:, :1] + 1) * (FF // 4)

            @pl.loop(0, columns // tile)
            def _(n):
                at = pl.ds(pl.multiple_of(n * tile, tile), tile)
                hidden = dot(full[g].reshape(tokens_all, model), up_v[:, at])
                ids = first_column + n * tile + lax.broadcasted_iota(jnp.int32, hidden.shape, 1)
                live = jnp.where(ids < limit, jnp.maximum(hidden, 0.0), 0.0)
                lifted[:, at] = live
                squared_v[slot, :, at] = (live * live).astype(BF)

        def backward(g):
            slot = lax.rem(g, 2)

            @pl.loop(0, columns // tile)
            def _(n):
                at = pl.ds(pl.multiple_of(n * tile, tile), tile)
                back = dot(grad_v[slot].reshape(tokens_all, model), down_v[at, :], NT)
                hidden_v[slot, :, at] = (back * (2.0 * lifted[:, at])).astype(BF)

            hiddens.put(g)

        def lower(g):
            slot = lax.rem(g, 2)

            @pl.loop(0, model // 256)
            def _(n):
                at = pl.ds(pl.multiple_of(n * 256, 256), 256)
                out = dot(hidden_v[slot], up_v[at, :], NT).astype(BF)
                part[g, :, :, :, at] = out.reshape(chips, 2, rows, 256)

        def finish(g):
            reduce_back.last(g)
            lhat, inv_std = layer_norm(resid_v[g])
            back = acc[...]
            gains[0:1] += jnp.sum(back * lhat, axis=0, keepdims=True)
            gains[1:2] += jnp.sum(back, axis=0, keepdims=True)
            back = back * gain2[...]
            back = dy_v[g].astype(F32) + inv_std * (back - row_mean(back) - lhat * row_mean(back * lhat))
            high_v[highs.free(g)] = back
            low_v[g] = back.astype(BF)
            highs.put(g)
            keep_low.put(g)

        @pl.loop(0, groups + back_at)
        def _(i):
            for n in range(hops):
                h, d = hops - n, n + 1
                within(i - hidden_at - 1 - hops + d, groups, functools.partial(reduce_back.step, d=d))
                within(i - lead - 1 - hops + d, groups, functools.partial(reduce.step, d=d))
                within(i - normed_at - h, groups, functools.partial(third.hop, h=h))
                within(i + ahead - h, groups, functools.partial(second.hop, h=h))
                if n == 0:
                    within(i - hidden_at, groups, arrived)
                for piece in (forward, backward, lower)[n * 3 // hops : (n + 1) * 3 // hops]:
                    within(i - hidden_at, groups, piece)
            within(i + ahead, groups, second.begin)
            within(i - hidden_at, groups, reduce_back.begin)
            within(i - normed_at, groups, norm)
            within(i - lead, groups, produce)
            within(i - lead, groups, reduce.begin)
            within(i + ahead - hops - 1, groups, second.arrived)
            within(i - back_at, groups, finish)
            within(i, lead, attention)

        for h in range(heads):
            keep_weights(blocks - 1, reach, h).wait()
        second.drain()
        third.drain()
        pl.loop(0, groups)(reduce_back.drain)

        @pl.loop(0, groups)
        def _(g):
            for store in (keep, keep_ln, keep_resid, keep_low):
                store.end(g)

        highs.end(groups)
        hiddens.end(groups)

    table = jax.ShapeDtypeStruct((ranks, groups, rows, HDIM), F32)
    projected = jax.ShapeDtypeStruct((ranks, groups, rows, 3 * width), BF)
    full = jax.ShapeDtypeStruct((groups, chips, 2, rows, model), BF)
    attended = jax.ShapeDtypeStruct((groups, tokens_all, width), BF)
    high = jax.ShapeDtypeStruct((groups, rows, model), F32)
    low = jax.ShapeDtypeStruct((groups, rows, model), BF)
    hidden = jax.ShapeDtypeStruct((groups, tokens_all, columns), BF)
    return call(
        body,
        [tokens, cotangent, probs, gain, lengths, frequency, count, w_qkv, w_out, g_ln, b_ln, w_up, w_down, widths],
        [
            projected,
            full,
            table,
            table,
            attended,
            high,
            full,
            high,
            low,
            jax.ShapeDtypeStruct((2, model), F32),
            full,
            hidden,
            hidden,
            jax.ShapeDtypeStruct((heads, weight_rows(blocks, reach), QROWS), BF),
        ],
        [
            *scratch_of(full, w_qkv, w_out, cotangent, w_up, w_down, projected),
            pltpu.VMEM((2, ranks, rows, HDIM), F32),
            pltpu.VMEM((2, ranks, rows, HDIM), F32),
            pltpu.VMEM((heads, HDIM, length), BF),
            *scratch_of(attended, low, high),
            pltpu.VMEM((2, rows, model), F32),
            pltpu.VMEM((2, chips, 2, rows, model), BF),
            pltpu.VMEM((tokens_all, columns), F32),
            pltpu.VMEM((2, tokens_all, columns), BF),
            pltpu.VMEM((2, tokens_all, columns), BF),
            *Gather.scratch(ranks, groups) * 3,
            *Reduce.scratch(ranks, groups, rows, model),
            *Reduce.scratch(ranks, groups, rows, model)[-3:],
            DMA((5,)),
            DMA((2, groups)),
            DMA((3, groups)),
            DMA,
            *[DMA((groups,))] * 3,
            DMA((4, groups)),
            pltpu.VMEM((heads, reach * QROWS, QROWS), BF),
            DMA((heads,)),
        ],
        0,
        in_specs=[VM, ANY, VM, VM, SM, VM, SM, ANY, ANY, VM, VM, ANY, ANY, VM],
        out_specs=[ANY] * 9 + [VM] + [ANY] * 4,
        flops=8 * length * model * (width + columns),
        moved=160 << 20,
    )


def hidden_weights(spread, inputs, hidden, first, turn_of, columns):
    n = turn_of
    side = min(256, spread.out.shape[1])

    @pl.loop(0, spread.out.shape[1] // side)
    def _(m):
        at = pl.ds(pl.multiple_of(first + m * side, side), side)
        to = pl.ds(pl.multiple_of(m * side, side), side)
        x = inputs[:, :, at]
        spread.out[n, to] = dot(
            x.reshape(x.shape[0] * x.shape[1], side), hidden[...].reshape(-1, columns), TN
        ).astype(BF)

    spread.begin(n)


def feed_out(
    own_grad, squared, hidden_grad, kept_ln, branch_grad, w_down, w_out, count, resid, cotangent, probs, ranks, sequences
):
    groups, rows, model = own_grad.shape
    columns, width = w_down.shape[0], w_out.shape[0]
    tokens = ranks * rows
    share = model // sequences
    half = share // 2

    def body(
        own, sq, hg, ln, bg, down, w, active, res, dy, p, result, probs_grad, kept, grad, land_down, land_up,
        full, g_send, g_recv, g_across, part, near, far, acc, s1, s2, s3, kept_sem,
        out_down, down_send, down_recv, out_up, up_send, up_recv, ln_v, bg_v, fetch_sem,
        sq_v, hg_v, down_v, res_v, dy_v, load_sem, result_v, back_v, result_sem, back_sem,
    ):
        line = Line(ranks, rows)
        line.greet(sequences)
        gather = Gather(line, full, g_send, g_recv, g_across)
        reduce = Reduce(line, part, near, far, acc, s1, s2, s3)
        to_down = Spread(sequences, out_down, land_down, down_send, down_recv)
        to_up = Spread(sequences, out_up, land_up, up_send, up_recv, pl.ds(0, half))
        keep = Store(full, kept, kept_sem)
        keep_result = Store(result_v, result, result_sem)
        keep_back = Store(back_v, grad, back_sem, lambda ref, g: ref.at[:, g])

        def arrived(g):
            gather.arrived(g)
            keep.put(g)
            heads = line.t * (width // HDIM) + lax.broadcasted_iota(jnp.int32, (1, width), 1) // HDIM
            live = jnp.where(heads < active[0], 1.0, 0.0)
            back = (dot(full[g].reshape(tokens, model), w[...], NT) * live).astype(BF)
            for rank in range(ranks):
                back_v[rank, g] = back[rank * rows : (rank + 1) * rows]
            keep_back.put(g)

        def produce(g):
            loads.need(g == 0, 0, 1)

            @pl.loop(0, model // 256)
            def _(n):
                at = pl.ds(pl.multiple_of(n * 256, 256), 256)
                out = dot(sq_v[g], down_v[:, at]).astype(BF)
                part[g, :, :, :, at] = out.reshape(ranks // 2, 2, rows, 256)

        def finish(g):
            loads.need(g == 0, 3, 4)
            ffn = acc[...]
            result_v[g] = (res_v[g] + column_of(p, g) * ffn).astype(BF)
            keep_result.put(g)
            scores = jnp.sum(dy_v[g].astype(F32) * ffn, axis=1, keepdims=True)
            probs_grad[pl.ds(g, 1)] = jnp.broadcast_to(scores, (rows, HDIM)).T[:1]

        def fetches(step):
            at = pl.multiple_of(to_up.target(lax.rem(step + 1, sequences)) * share, share)
            return [
                pltpu.make_async_copy(ln.at[:, :, pl.ds(at, half)], ln_v, fetch_sem.at[0]),
                pltpu.make_async_copy(bg.at[:, :, pl.ds(at, share)], bg_v, fetch_sem.at[1]),
            ]

        def weights(step):
            n = lax.rem(step + 1, sequences)
            loads.need(step == 0, 2)
            for fetch in fetches(step):
                fetch.wait()
            side = min(256, columns)

            @pl.loop(0, columns // side)
            def _(m):
                at = pl.ds(pl.multiple_of(m * side, side), side)
                out_down[n, at] = dot(
                    sq_v[:, :, at].reshape(groups * tokens, side), bg_v[...].reshape(groups * tokens, share), TN
                ).astype(BF)

            to_down.begin(n)
            hidden_weights(to_up, ln_v, hg_v, 0, n, columns)

            @pl.when(step + 1 < sequences)
            def _():
                for fetch in fetches(step + 1):
                    fetch.start()

        def beside(turn):
            loads.begin(turn == 0, 0, 1, 2)

            @pl.when(turn == 0)
            def _():
                for fetch in fetches(0):
                    fetch.start()

            loads.begin(turn == 3, 3, 4)
            within(turn - 1, sequences, weights)

        loads = Loads(
            [
                (sq, sq_v),
                (down, down_v),
                (hg, hg_v),
                (res, res_v),
                (dy, dy_v),
                (own, full.at[:, line.z, line.c]),
            ],
            load_sem,
        )
        loads.begin(True, 5)
        line.meet(sequences)
        loads.need(True, 5)
        stream(
            line, groups, gather, arrived, reduce, [produce], finish, 1, (max(sequences + 1, 4), beside)
        )

        @pl.loop(0, groups)
        def _(g):
            for store in (keep, keep_result, keep_back):
                store.end(g)

        to_down.end()
        to_up.end()

    kept = jax.ShapeDtypeStruct((groups, ranks // 2, 2, rows, model), BF)
    low = jax.ShapeDtypeStruct((groups, rows, model), BF)
    back = jax.ShapeDtypeStruct((ranks, groups, rows, width), BF)
    return call(
        body,
        [own_grad, squared, hidden_grad, kept_ln, branch_grad, w_down, w_out, count, resid, cotangent, probs],
        [
            low,
            jax.ShapeDtypeStruct((groups, rows), F32),
            kept,
            back,
            jax.ShapeDtypeStruct((sequences, columns, share), BF),
            jax.ShapeDtypeStruct((sequences, share, columns), BF),
        ],
        [
            *scratch_of(kept),
            *Gather.scratch(ranks, groups),
            *Reduce.scratch(ranks, groups, rows, model),
            DMA((groups,)),
            *Spread.scratch(sequences, (columns, share)),
            *Spread.scratch(sequences, (half, columns)),
            pltpu.VMEM((groups, tokens, half), BF),
            pltpu.VMEM((groups, tokens, share), BF),
            DMA((2,)),
            *scratch_of(squared, hidden_grad, w_down, resid, cotangent),
            DMA((6,)),
            *scratch_of(low, back),
            DMA((groups,)),
            DMA((groups,)),
        ],
        3,
        in_specs=[ANY, ANY, ANY, ANY, ANY, ANY, VM, SM, ANY, ANY, VM],
        out_specs=[ANY, VM, ANY, ANY, ANY, ANY],
        flops=2 * groups * tokens * model * (3 * columns + width),
        moved=100 << 20,
    )


def project_back(
    grads, w_qkv, kept_x, attended, attn_grad, kept_ln, hidden_grad, landed_up, tokens, gain, grad_resid, gains, ranks, sequences
):
    groups, tokens_all, width = grads[0].shape
    rows = tokens_all // ranks
    model = w_qkv.shape[1]
    columns = hidden_grad.shape[2]
    share = model // sequences
    half = share // 2

    def body(
        gq, gk, gv, w, xs, a, ga, ln, hg, up_in, x_ref, gain_ref, g_res, gain_parts,
        tokens_grad, totals, land_qkv, land_out, land_up,
        part, near, far, acc, s1, s2, s3,
        out_qkv, qkv_send, qkv_recv, out_out, out_send, out_recv, out_up, up_send, up_recv,
        x_v, ga_v, ln_v, fetch_sem, group_v, group_sem, w_v, a_v, hg_v, own_v, res_v, load_sem,
        mine, terms, t_send, t_recv, sums, d_send, d_recv, g_q, g_k, g_v, grad_v, grad_sem,
    ):
        line = Line(ranks, rows)
        line.greet_all(sequences)
        me = lax.axis_index("dp")
        reduce = Reduce(line, part, near, far, acc, s1, s2, s3)
        to_qkv = Spread(sequences, out_qkv, land_qkv, qkv_send, qkv_recv)
        to_out = Spread(sequences, out_out, land_out, out_send, out_recv)
        to_up = Spread(sequences, out_up, land_up, up_send, up_recv, pl.ds(half, half))
        parts = (g_q, g_k, g_v)
        loads = Loads(
            [(w, w_v), (a, a_v), (hg, hg_v), (x_ref, own_v), (g_res, res_v), (gq, g_q), (gk, g_k), (gv, g_v)],
            load_sem,
        )
        keep_grad = Store(grad_v, tokens_grad, grad_sem)

        def group_fetch(g):
            slot = lax.rem(g, 2)
            return pltpu.make_async_copy(xs.at[g], group_v.at[slot], group_sem.at[slot])

        loads.begin(True, 0, 5, 6, 7)
        group_fetch(0).start()
        mine[0:1] = jnp.zeros((1, model), F32)
        mine[1:3] = gain_parts[...]

        def produce(g):
            loads.need(g == 0, 0, 5, 6, 7)
            group_fetch(g).wait()

            @pl.when(g + 1 < groups)
            def _():
                group_fetch(g + 1).start()

            slot = lax.rem(g, 2)

            @pl.loop(0, model // 256)
            def _(n):
                at = pl.ds(pl.multiple_of(n * 256, 256), 256)
                out = dot(g_q[g], w_v[0, at], NT)
                out += dot(g_k[g], w_v[1, at], NT)
                out += dot(g_v[g], w_v[2, at], NT)
                part[g, :, :, :, at] = out.astype(BF).reshape(ranks // 2, 2, rows, 256)
                mine[0:1, at] += jnp.sum(out * group_v[slot, :, at].astype(F32), axis=0, keepdims=True)

        def finish(g):
            loads.need(g == 0, 3, 4)
            x = own_v[g].astype(F32)
            scale = lax.rsqrt(row_mean(x * x) + EPSILON)
            hat = x * scale
            back = acc[...] * gain_ref[...]
            grad_v[g] = res_v[g] + scale * (back - hat * row_mean(back * hat))
            keep_grad.put(g)

        def fetches(step):
            at = pl.multiple_of(to_qkv.target(lax.rem(step + 1, sequences)) * share, share)
            return [
                pltpu.make_async_copy(ln.at[:, :, pl.ds(at + half, half)], ln_v, fetch_sem.at[0]),
                pltpu.make_async_copy(xs.at[:, :, pl.ds(at, share)], x_v, fetch_sem.at[1]),
                pltpu.make_async_copy(ga.at[:, :, pl.ds(at, share)], ga_v, fetch_sem.at[2]),
            ]

        def weights(piece):
            step = piece // 2
            n = lax.rem(step + 1, sequences)

            @pl.when(lax.rem(piece, 2) == 0)
            def _():
                loads.need(step == 0, 1, 2)
                fetches(step)[0].wait()
                hidden_weights(to_up, ln_v, hg_v, 0, n, columns)

                @pl.when(step + 1 < sequences)
                def _():
                    fetches(step + 1)[0].start()

            @pl.when(lax.rem(piece, 2) == 1)
            def _():
                for fetch in fetches(step)[1:]:
                    fetch.wait()

                @pl.loop(0, share // 256)
                def _(m):
                    at = pl.ds(pl.multiple_of(m * 256, 256), 256)
                    x = x_v[:, :, at].reshape(groups * tokens_all, 256)
                    for which in range(3):
                        out_qkv[n, which, at] = dot(
                            x, parts[which][...].reshape(groups * tokens_all, width), TN
                        ).astype(BF)

                to_qkv.begin(n)
                out_out[n] = dot(
                    a_v[...].reshape(groups * tokens_all, width), ga_v[...].reshape(groups * tokens_all, share), TN
                ).astype(BF)
                to_out.begin(n)

                @pl.when(step + 1 < sequences)
                def _():
                    for fetch in fetches(step + 1)[1:]:
                        fetch.start()

        def to_rank(n, source=None):
            return copy_to(
                mine,
                terms.at[line.t if source is None else source],
                t_send.at[n],
                t_recv.at[n],
                lax.rem(line.t + n, ranks),
            )

        def to_sequence(n, source=None):
            return pltpu.make_async_remote_copy(
                src_ref=sums.at[me],
                dst_ref=sums.at[me if source is None else source],
                send_sem=d_send.at[n],
                recv_sem=d_recv.at[n],
                device_id={"dp": lax.rem(me + n, sequences)},
                device_id_type=MESH,
            )

        def beside(turn):
            loads.begin(turn == 0, 1, 2)
            loads.begin(turn == 2, 3, 4)

            @pl.when(turn == 0)
            def _():
                for fetch in fetches(0):
                    fetch.start()

            within(turn - 1, 2 * sequences, weights)

            @pl.when(turn == groups)
            def _():
                mine[0:1] = mine[0:1] / gain_ref[...]
                terms[line.t] = mine[...]

                @pl.loop(1, ranks)
                def _(n):
                    to_rank(n).start()

            @pl.when(turn == groups + 1)
            def _():
                @pl.loop(1, ranks)
                def _(n):
                    to_rank(n).wait_send()
                    to_rank(n, lax.rem(line.t + ranks - n, ranks)).wait_recv()

                total = terms[0]
                for n in range(1, ranks):
                    total += terms[n]
                sums[me] = total

                @pl.loop(1, sequences)
                def _(n):
                    to_sequence(n).start()

            @pl.when(turn == groups + 2)
            def _():
                @pl.loop(1, sequences)
                def _(n):
                    to_sequence(n).wait_send()
                    to_sequence(n, lax.rem(me + sequences - n, sequences)).wait_recv()

                total = sums[0]
                for n in range(1, sequences):
                    total += sums[n]
                totals[...] = total

        produce(0)
        line.meet_all(sequences)

        def next_part(g):
            pl.when(g > 0)(lambda: produce(g))

        stream(
            line, groups, None, None, reduce, [next_part], finish, extra=(max(groups + 3, 2 * sequences + 1), beside)
        )

        @pl.loop(0, groups)
        def _(g):
            keep_grad.end(g)

        to_qkv.end()
        to_out.end()

        to_up.end()

    return call(
        body,
        [*grads, w_qkv, kept_x, attended, attn_grad, kept_ln, hidden_grad, landed_up, tokens, gain, grad_resid, gains],
        [
            jax.ShapeDtypeStruct((groups, rows, model), F32),
            jax.ShapeDtypeStruct((3, model), F32),
            jax.ShapeDtypeStruct((sequences, 3, share, width), BF),
            jax.ShapeDtypeStruct((sequences, width, share), BF),
            jax.ShapeDtypeStruct(landed_up.shape, BF),
        ],
        [
            *Reduce.scratch(ranks, groups, rows, model),
            *Spread.scratch(sequences, (3, share, width)),
            *Spread.scratch(sequences, (width, share)),
            *Spread.scratch(sequences, (half, columns)),
            pltpu.VMEM((groups, tokens_all, share), BF),
            pltpu.VMEM((groups, tokens_all, share), BF),
            pltpu.VMEM((groups, tokens_all, half), BF),
            DMA((3,)),
            pltpu.VMEM((2, tokens_all, model), BF),
            DMA((2,)),
            *scratch_of(w_qkv, attended, hidden_grad, tokens, grad_resid),
            DMA((8,)),
            pltpu.VMEM((3, model), F32),
            pltpu.VMEM((ranks, 3, model), F32),
            DMA((ranks,)),
            DMA((ranks,)),
            pltpu.VMEM((sequences, 3, model), F32),
            DMA((sequences,)),
            DMA((sequences,)),
            *scratch_of(*grads, grad_resid),
            DMA((groups,)),
        ],
        4,
        in_specs=[ANY] * 11 + [VM, ANY, VM],
        out_specs=[ANY, VM, ANY, ANY, ANY],
        flops=12 * groups * tokens_all * model * width,
        moved=60 << 20,
        aliases={9: 4},
    )


def collect(result, tokens_grad, totals, *landed):
    steps = result.shape[0] // 2

    def body(result_in, tokens_in, totals_in, *refs):
        pieces, outs = refs[: len(landed)], refs[len(landed) :]
        outs[0][...] = result_in[...]
        outs[1][...] = tokens_in[...]
        for n in range(3):
            outs[2 + n][...] = totals_in[n : n + 1]
        for piece, out in zip(pieces, outs[5:]):
            total = piece[0].astype(F32)
            for n in range(1, piece.shape[0]):
                total += piece[n].astype(F32)
            out[...] = total

    def split(a, at):
        block = list(a.shape)
        block[at] //= steps
        return pl.BlockSpec(tuple(block), lambda i: tuple(i if n == at else 0 for n in range(len(block))))

    sums = [jax.ShapeDtypeStruct(a.shape[1:], F32) for a in landed]
    row = jax.ShapeDtypeStruct((1, totals.shape[1]), F32)
    fixed = lambda a: pl.BlockSpec(a.shape, lambda i: (0, 0))
    return pl.pallas_call(
        body,
        out_shape=[
            jax.ShapeDtypeStruct(result.shape, BF),
            jax.ShapeDtypeStruct(tokens_grad.shape, F32),
            row,
            row,
            row,
            *sums,
        ],
        grid=(steps,),
        in_specs=[split(result, 0), split(tokens_grad, 0), fixed(totals)]
        + [split(a, a.ndim - 2) for a in landed],
        out_specs=[split(result, 0), split(tokens_grad, 0), fixed(row), fixed(row), fixed(row)]
        + [split(a, len(a.shape) - 2) for a in sums],
        compiler_params=pltpu.CompilerParams(vmem_limit_bytes=60 << 20),
        cost_estimate=pl.CostEstimate(flops=1 << 24, bytes_accessed=24 << 20, transcendentals=0),
    )(result, tokens_grad, totals, *landed)


def shards(
    tokens,
    cotangent,
    first_norm_gain,
    w_qkv,
    w_out,
    g_ln,
    b_ln,
    w_up,
    w_down,
    probs,
    lengths,
    head_count,
    widths,
):
    length_all = widths.shape[0]
    own_tokens, model = tokens.shape
    ranks = length_all // own_tokens
    sequences = lax.axis_size("dp")
    groups, rows = GROUPS, own_tokens // GROUPS
    width = w_out.shape[0]
    half = HDIM // 2
    frequency = 10000.0 ** (-np.arange(half) / half)
    frequency = jnp.asarray(np.concatenate([frequency, frequency]).reshape(1, HDIM), F32)
    w_qkv_t = w_qkv.transpose(1, 0, 2)
    x = tokens.reshape(groups, rows, model)
    dy = cotangent.reshape(groups, rows, model)
    first_norm_gain, g_ln, b_ln = (v.reshape(1, model) for v in (first_norm_gain, g_ln, b_ln))
    p = probs.reshape(groups, rows)
    wide = widths.reshape(ranks, groups, rows).swapaxes(0, 1).reshape(groups, ranks * rows)

    (
        qkv, kept_x, cosines, sines, attended, resid, kept_ffn_grad, grad_resid, grad_low, gains, kept_ln, squared,
        grad_hidden, kept_weights,
    ) = front(
        x, dy, p, first_norm_gain, lengths, frequency, head_count, w_qkv_t, w_out, g_ln, b_ln, w_up, w_down, wide, ranks
    )
    qkv = qkv.reshape(length_all, 3 * width)
    cosines, sines = cosines.reshape(length_all, HDIM), sines.reshape(length_all, HDIM)
    whole = lambda kept: kept.reshape(groups, ranks * rows, model)
    result, probs_grad, kept_attn_grad, grad_attended, land_down, land_up = feed_out(
        grad_low, squared, grad_hidden, whole(kept_ln), whole(kept_ffn_grad), w_down, w_out, head_count, resid, dy, p, ranks, sequences
    )
    grad_proj = attend_back(
        qkv,
        grad_attended.reshape(length_all, width),
        kept_weights,
        head_count,
        cosines,
        sines,
        width,
        groups,
        own_tokens,
    )
    tokens_grad, totals, land_qkv, land_out, land_up = project_back(
        grad_proj, w_qkv_t, whole(kept_x), attended, whole(kept_attn_grad), whole(kept_ln), grad_hidden, land_up, x, first_norm_gain,
        grad_resid, gains, ranks, sequences,
    )
    result, tokens_grad, rms, gain, bias, g_qkv, g_out, g_up, g_down = collect(
        result, tokens_grad, totals, land_qkv, land_out, land_up, land_down
    )
    return (
        result.reshape(own_tokens, model),
        tokens_grad.reshape(own_tokens, model),
        probs_grad.reshape(own_tokens),
        rms.reshape(model),
        g_qkv.transpose(1, 0, 2),
        g_out,
        gain.reshape(model),
        bias.reshape(model),
        g_up,
        g_down,
    )


def solution(mesh):
    placed = (
        P(("dp", "tensor"), None),
        P(("dp", "tensor"), None),
        P(),
        P(None, None, "tensor"),
        P("tensor", None),
        P(),
        P(),
        P(None, "tensor"),
        P("tensor", None),
        P(("dp", "tensor")),
        P("dp", None),
        P("dp"),
        P("dp"),
    )
    return jax.shard_map(
        shards,
        mesh=mesh,
        in_specs=placed,
        out_specs=(
            P(("dp", "tensor"), None),
            P(("dp", "tensor"), None),
            P(("dp", "tensor")),
            P(),
            P("dp", None, "tensor"),
            P("tensor", "dp"),
            P(),
            P(),
            P("dp", "tensor"),
            P("tensor", "dp"),
        ),
        check_vma=False,
    )
```
